32 devices in a mesh: ctx: 8 (over z, y), fsdp: 4 (over x, core).
Axes of the slice: x: 2, y: 2, z: 4, core: 2. Of those that a mesh axis runs over, the one named last changes fastest.
Arguments:
- tokens: bfloat16 [6144, 768], P(('ctx', 'fsdp')), may hold values from -6 to 6
- document_starts: int32 [8], replicated, may hold values from 0 to 6143, as said below
- attend_weight: bfloat16 [768, 2304], P('fsdp'), may hold values from -0.3125 to 0.3125
- attend_bias: bfloat16 [1536], P('fsdp'), may hold values from -3 to 3
- project_weight: bfloat16 [768, 768], P('fsdp'), may hold values from -4 to 4
- project_bias: bfloat16 [768], P('fsdp'), may hold values from -4 to 4
- expand_weight: bfloat16 [768, 3072], P('fsdp'), may hold values from -0.21875 to 0.21875
- expand_bias: bfloat16 [3072], P('fsdp'), may hold values from -3 to 3
- contract_weight: bfloat16 [3072, 768], P('fsdp'), may hold values from -0.75 to 0.75
- contract_bias: bfloat16 [768], P('fsdp'), may hold values from -4 to 4
- gain_first: bfloat16 [768], P('fsdp'), may hold values from 0.5 to 1.5
- shift_first: bfloat16 [768], P('fsdp'), may hold values from -2 to 2
- gain_second: bfloat16 [768], P('fsdp'), may hold values from 0.5 to 1.5
- shift_second: bfloat16 [768], P('fsdp'), may hold values from -2 to 2
- cotangent: bfloat16 [6144, 768], P(('ctx', 'fsdp')), may hold values from -6 to 6
Outputs:
- block_output: bfloat16 [6144, 768], P(('ctx', 'fsdp'))
- tokens_grad: bfloat16 [6144, 768], P(('ctx', 'fsdp'))
- attend_grad: float32 [768, 2304], P('fsdp')
- attbias_grad: float32 [1536], P('fsdp')
- project_grad: float32 [768, 768], P('fsdp')
- projbias_grad: float32 [768], P('fsdp')
- expand_grad: float32 [768, 3072], P('fsdp')
- expbias_grad: float32 [3072], P('fsdp')
- contract_grad: float32 [3072, 768], P('fsdp')
- conbias_grad: float32 [768], P('fsdp')
- gainone_grad: float32 [768], P('fsdp')
- shiftone_grad: float32 [768], P('fsdp')
- gaintwo_grad: float32 [768], P('fsdp')
- shifttwo_grad: float32 [768], P('fsdp')
The draws below stay inside these ranges and needn't reach their ends.
Inputs may be any that keep to these rules, and one draw needn't show every extreme that they name: document_starts is strictly increasing and its first entry is 0; a document runs from its start to the next start, the last one to the end of the stream.
All inputs are finite; a program needn't handle non-finite values.
Results may differ from the reference program's by a relative error of at most 0.017.
Values may be sent and summed in bfloat16 or wider, within the bound.
A program may use at most 320 MiB of HBM per device.

```python
import math
from functools import partial
import jax
import jax.numpy as jnp
from jax import lax

D = 768
H = 12
HD = 64
FF = 3072
DOCS = 8
TOKENS = 6144
BLOCK_TOK = 768


def draw_document_starts(key, part):
    key_place, key_rest = jax.random.split(jax.random.fold_in(key, 17))
    long_length = TOKENS // 2 + BLOCK_TOK
    spare_count = TOKENS - long_length - 2 * BLOCK_TOK - 1
    opening = jax.random.randint(key_place, (1,), BLOCK_TOK + 1, TOKENS - long_length - BLOCK_TOK + 1, dtype=jnp.int32)
    chosen = jax.random.permutation(key_rest, spare_count)[:DOCS - 3].astype(jnp.int32)
    before = opening - BLOCK_TOK - 1
    placed = jnp.where(chosen < before, chosen + BLOCK_TOK + 1, chosen - before + opening + long_length + 1)
    leading = jnp.zeros((1,), jnp.int32)
    joined = jnp.concatenate([leading, opening, opening + long_length, placed.astype(jnp.int32)])
    return jnp.sort(joined).astype(jnp.int32)


def levels(own_key, extent, cuts, smallest, top_value):
    loudness = 1.0
    for position, parts in cuts:
        heights = jax.random.uniform(jax.random.fold_in(jax.random.fold_in(own_key, 6), position), (parts,), jnp.float32, smallest / len(cuts), top_value / len(cuts))
        loudness = loudness * jnp.repeat(jnp.exp(heights), extent[position] // parts).reshape((-1,) + (1,) * (len(extent) - 1 - position))
    return loudness


def bell_draw(key, dims, scale, limit, cuts=(), kind=jnp.bfloat16):
    loudness = levels(key, dims, cuts, -0.22, 0.18) if cuts else 1.0
    drawn = jax.random.normal(key, dims, jnp.float32) * scale * loudness
    return jnp.minimum(jnp.maximum(drawn, -limit), limit).astype(kind)


def setup_inputs(seed: int = 0) -> dict:
    arg_keys = jax.random.split(jax.random.key(seed), 16)
    return {
        "tokens": bell_draw(arg_keys[0], (TOKENS, D), 1.0, 6.0, ((0, 32),)),
        "document_starts": draw_document_starts(jax.random.fold_in(arg_keys[15], 71), 0),
        "attend_weight": bell_draw(arg_keys[2], (D, 3 * D), (D // 2) ** -0.5, 0.3125, ((0, 4),)),
        "attend_bias": bell_draw(arg_keys[3], (2 * D,), 0.5, 3.0, ((0, 4),)),
        "project_weight": bell_draw(arg_keys[4], (D, D), 2 ** -0.5, 4.0, ((0, 4),)),
        "project_bias": bell_draw(arg_keys[5], (D,), 1.0, 4.0, ((0, 4),)),
        "expand_weight": bell_draw(arg_keys[6], (D, FF), D ** -0.5, 0.21875, ((0, 4),)),
        "expand_bias": bell_draw(arg_keys[7], (FF,), 0.5, 3.0, ((0, 4),)),
        "contract_weight": bell_draw(arg_keys[8], (FF, D), (FF // 48) ** -0.5, 0.75, ((0, 4),)),
        "contract_bias": bell_draw(arg_keys[9], (D,), 1.0, 4.0, ((0, 4),)),
        "gain_first": jnp.clip(1.0 + 0.1 * jax.random.normal(arg_keys[10], (D,), jnp.float32), 0.5, 1.5).astype(jnp.bfloat16),
        "shift_first": bell_draw(arg_keys[11], (D,), 0.3, 2.0, ((0, 4),)),
        "gain_second": jnp.clip(1.0 + 0.1 * jax.random.normal(arg_keys[12], (D,), jnp.float32), 0.5, 1.5).astype(jnp.bfloat16),
        "shift_second": bell_draw(arg_keys[13], (D,), 0.3, 2.0, ((0, 4),)),
        "cotangent": bell_draw(arg_keys[14], (TOKENS, D), 1.0, 6.0, ((0, 32),)),
    }


EPS = 1e-05
SCALE = 0.125
BRANCH = 48.0 ** (-0.5)
NEG = -1e+30

@jax.custom_vjp
def low(v):
    return lax.optimization_barrier(v.astype(jnp.bfloat16)).astype(jnp.float32)

@jax.custom_vjp
def low_back(v):
    return v

def low_keep(v):
    return (low(v), None)

def low_pass(kept, grad):
    return (grad,)

def back_keep(v):
    return (v, None)

def back_low(kept, grad):
    return (low(grad),)
low.defvjp(low_keep, low_pass)
low_back.defvjp(back_keep, back_low)

def matmul(left, right):
    return jnp.dot(left, right, precision=lax.Precision.HIGHEST, preferred_element_type=jnp.float32)

def layer_norm(rows_in, gain, shift):
    mean = lax.optimization_barrier(jnp.mean(rows_in, axis=-1, keepdims=True))
    centered = rows_in - mean
    variance = lax.optimization_barrier(jnp.mean(centered * centered, axis=-1, keepdims=True))
    return centered * lax.rsqrt(variance + EPS) * gain + shift

def first_position(places, starts):
    below = starts[None, :] <= places[:, None]
    return lax.optimization_barrier(jnp.max(jnp.where(below, starts[None, :], 0), axis=1)).astype(jnp.int32)

def attend(queries, keys, values, places, begins):
    block_size = math.gcd(TOKENS, 512)
    block_count = TOKENS // block_size

    def one_block(operands):
        query_block, place_block, begin_block = operands
        scores = jnp.einsum('qhd,khd->hqk', query_block, keys, precision=lax.Precision.HIGHEST) * SCALE
        allowed = (places[None, :] <= place_block[:, None]) & (places[None, :] >= begin_block[:, None])
        scores = low_back(jnp.where(allowed[None], scores, NEG))
        peak = lax.optimization_barrier(jnp.max(scores, axis=-1, keepdims=True))
        raised = jnp.exp(scores - peak)
        probs = raised / lax.optimization_barrier(jnp.sum(raised, axis=-1, keepdims=True))
        return jnp.einsum('hqk,khd->qhd', low(probs), values, precision=lax.Precision.HIGHEST)
    results = lax.map(jax.checkpoint(one_block), (queries.reshape(block_count, block_size, H, HD), places.reshape(block_count, block_size), begins.reshape(block_count, block_size)))
    return results.reshape(TOKENS, H * HD)

def block_forward(starts, hidden_in, attend_weight, attend_bias, project_weight, project_bias, expand_weight, expand_bias, contract_weight, contract_bias, gain_first, shift_first, gain_second, shift_second):
    normed = low(layer_norm(hidden_in, gain_first, shift_first))
    zero_part = jnp.zeros((D,), jnp.float32)
    offsets = jnp.concatenate([attend_bias[:D], zero_part, attend_bias[D:]])
    triple = low(low_back(matmul(normed, attend_weight) + offsets))
    queries = triple[:, :D].reshape(TOKENS, H, HD)
    keys = triple[:, D:2 * D].reshape(TOKENS, H, HD)
    values = triple[:, 2 * D:].reshape(TOKENS, H, HD)
    places = jnp.arange(TOKENS, dtype=jnp.int32)
    begins = first_position(places, starts)
    attended = low(low_back(attend(queries, keys, values, places, begins)))
    branch_one = low_back(matmul(attended, project_weight) + project_bias)
    middle = hidden_in + BRANCH * branch_one
    normed_two = low(layer_norm(middle, gain_second, shift_second))
    expanded = low_back(matmul(normed_two, expand_weight) + expand_bias)
    activated = low(jax.nn.gelu(expanded, approximate=True))
    branch_two = low_back(matmul(activated, contract_weight) + contract_bias)
    return middle + BRANCH * branch_two

def reference(tokens, document_starts, attend_weight, attend_bias, project_weight, project_bias, expand_weight, expand_bias, contract_weight, contract_bias, gain_first, shift_first, gain_second, shift_second, cotangent):
    inputs = (tokens, attend_weight, attend_bias, project_weight, project_bias, expand_weight, expand_bias, contract_weight, contract_bias, gain_first, shift_first, gain_second, shift_second)
    widened = tuple((array_in.astype(jnp.float32) for array_in in inputs))
    output, pullback = jax.vjp(partial(block_forward, document_starts), *widened)
    gradients = pullback(cotangent.astype(jnp.float32))
    return (output.astype(jnp.bfloat16), gradients[0].astype(jnp.bfloat16), gradients[1], gradients[2], gradients[3], gradients[4], gradients[5], gradients[6], gradients[7], gradients[8], gradients[9], gradients[10], gradients[11], gradients[12])
```

```python
import functools
import jax
import jax.numpy as jnp
from jax import lax
from jax.experimental import pallas as pl
from jax.experimental.pallas import tpu as pltpu
from jax.sharding import PartitionSpec as P

D = 768
H = 12
HD = 64
EPS = 1e-05
SCALE = 0.125
BRANCH = 48.0 ** (-0.5)
NEG = -1e30
SUB = 256
BF = jnp.bfloat16
F32 = jnp.float32


def mm(a, b):
    return jnp.dot(a, b, preferred_element_type=F32)


def mm_nt(a, b):
    return lax.dot_general(a, b, (((1,), (1,)), ((), ())), preferred_element_type=F32)


def mm_tn(a, b):
    return lax.dot_general(a, b, (((0,), (0,)), ((), ())), preferred_element_type=F32)


def head_lanes(head):
    return slice(0, 128) if head < 2 else slice(128, 192)


def fill_masked_columns(target, flipped):
    zero = jnp.zeros((HD, flipped.shape[1]), BF)
    target[0, 0:HD, :] = flipped[0:HD]
    target[0, HD : 2 * HD, :] = zero
    target[1, 0:HD, :] = zero
    target[1, HD : 2 * HD, :] = flipped[HD : 2 * HD]
    target[2, 0:HD, :] = flipped[2 * HD : 3 * HD]


def masked_rows(array_in, head):
    if head == 2:
        return array_in[:, 128:192]
    pair = array_in[:, 0:128]
    lane = lax.broadcasted_iota(jnp.int32, pair.shape, 1)
    return jnp.where((lane < HD) if head == 0 else (lane >= HD), pair, jnp.zeros_like(pair))


def allowed_pairs(first_key, first_query, begins, shape):
    key_places = first_key + lax.broadcasted_iota(jnp.int32, shape, 0)
    query_places = first_query + lax.broadcasted_iota(jnp.int32, shape, 1)
    return (key_places <= query_places) & (key_places >= begins)


def attend_forward_kernel(
    where_ref, rows_ref, own_ref, wq_ref, wk_ref, wv_ref, bias_ref, begins_ref,
    q_out, k_out, v_out, o_out, lse_out,
    qm, vt, peak, total, acc,
):
    turn = pl.program_id(0)
    block = own_ref.shape[0]
    mine, begin_low, begin_high = where_ref[0], where_ref[1], where_ref[2]
    first_query = mine * block
    needed = (turn <= mine) & ((turn + 1) * block - 1 >= begin_low)

    @pl.when(turn == 0)
    def _():
        query = (mm(own_ref[...], wq_ref[...]) + bias_ref[0:1, :]).astype(BF)
        q_out[...] = query
        fill_masked_columns(qm, (query.astype(F32) * SCALE).T.astype(BF))
        peak[...] = jnp.full(peak.shape, NEG, F32)
        total[...] = jnp.zeros(total.shape, F32)
        acc[...] = jnp.zeros(acc.shape, F32)

    @pl.when(needed)
    def _():
        rows = rows_ref[...]
        k_out[...] = mm(rows, wk_ref[...]).astype(BF)
        value = (mm(rows, wv_ref[...]) + bias_ref[1:2, :]).astype(BF)
        v_out[...] = value
        vt[...] = value.astype(F32).T.astype(BF)

        def one(step, masked):
            at = pl.ds(pl.multiple_of(step * SUB, SUB), SUB)
            first_key = turn * block + step * SUB
            if masked:
                allowed = allowed_pairs(first_key, first_query, begins_ref[...], (SUB, block))
            for head in range(3):
                depth = 128 if head < 2 else HD
                scores = mm(k_out[at, head_lanes(head)], qm[head, 0:depth, :])
                if masked:
                    scores = jnp.where(allowed, scores, NEG)
                old = peak[head : head + 1, :]
                new = jnp.maximum(old, jnp.max(scores, axis=0, keepdims=True))
                weights = jnp.exp(scores - new)
                if masked:
                    weights = jnp.where(allowed, weights, 0.0)
                factor = jnp.exp(old - new)
                peak[head : head + 1, :] = new
                total[head : head + 1, :] = total[head : head + 1, :] * factor + jnp.sum(
                    weights, axis=0, keepdims=True
                )
                part = slice(head * HD, head * HD + HD)
                acc[part, :] = acc[part, :] * factor + mm(vt[part, at], weights.astype(BF))

        @pl.loop(0, block // SUB)
        def _(step):
            first_key = turn * block + step * SUB
            inner = (first_key + SUB - 1 <= first_query) & (first_key >= begin_high)
            touched = first_key + SUB - 1 >= begin_low

            @pl.when(inner)
            def _():
                one(step, False)

            @pl.when(jnp.logical_not(inner) & touched)
            def _():
                one(step, True)

    @pl.when(turn == mine)
    def _():
        for head in range(3):
            part = slice(head * HD, head * HD + HD)
            o_out[part, :] = acc[part, :] / total[head : head + 1, :]
        lse_out[...] = peak[...] + jnp.log(jnp.maximum(total[...], 1e-30))


def attend_forward(where, rows_all, own, wq, wk, wv, bias, begins):
    block = own.shape[0]
    count = rows_all.shape[0] // block

    def seen(turn, where_ref):
        return (jnp.minimum(turn, where_ref[0]), 0)

    def fixed(turn, where_ref):
        return (0, 0)

    return pl.pallas_call(
        attend_forward_kernel,
        grid_spec=pltpu.PrefetchScalarGridSpec(
            num_scalar_prefetch=1,
            grid=(count,),
            in_specs=[
                pl.BlockSpec((block, D), seen),
                pl.BlockSpec((block, D), fixed),
                pl.BlockSpec((D, 192), fixed),
                pl.BlockSpec((D, 192), fixed),
                pl.BlockSpec((D, 192), fixed),
                pl.BlockSpec((2, 192), fixed),
                pl.BlockSpec((1, block), fixed),
            ],
            out_specs=[
                pl.BlockSpec((block, 192), fixed),
                pl.BlockSpec((block, 192), seen),
                pl.BlockSpec((block, 192), seen),
                pl.BlockSpec((192, block), fixed),
                pl.BlockSpec((8, block), fixed),
            ],
            scratch_shapes=[
                pltpu.VMEM((3, 128, block), BF),
                pltpu.VMEM((192, block), BF),
                pltpu.VMEM((8, block), F32),
                pltpu.VMEM((8, block), F32),
                pltpu.VMEM((192, block), F32),
            ],
        ),
        out_shape=[
            jax.ShapeDtypeStruct((block, 192), BF),
            jax.ShapeDtypeStruct((block * count, 192), BF),
            jax.ShapeDtypeStruct((block * count, 192), BF),
            jax.ShapeDtypeStruct((192, block), F32),
            jax.ShapeDtypeStruct((8, block), F32),
        ],
        compiler_params=pltpu.CompilerParams(vmem_limit_bytes=48 << 20),
        name="attend_forward",
    )(where, rows_all, own, wq, wk, wv, bias, begins)


def attend_backward_kernel(
    where_ref, rows_ref, k_ref, v_ref, own_ref, q_ref, o_ref, lse_ref, g_ref, wp_ref,
    wq_ref, wk_ref, wv_ref, begins_ref,
    dn_out, grad_out, proj_out, sums_out,
    qm, dm, qn, dn, delta, dqt, kt, dk, dv,
):
    turn = pl.program_id(0)
    block = own_ref.shape[0]
    mine, begin_low, begin_high = where_ref[0], where_ref[1], where_ref[2]
    first_query = mine * block
    needed = (turn <= mine) & ((turn + 1) * block - 1 >= begin_low)

    @pl.when(turn == 0)
    def _():
        grads = g_ref[...]
        exact = o_ref[...]
        proj_out[...] = mm(exact.astype(BF), grads)
        outer = mm_nt(grads, wp_ref[...]).astype(BF)
        flipped = outer.astype(F32).T
        product = flipped * exact
        for head in range(3):
            delta[head : head + 1, :] = jnp.sum(
                product[head * HD : head * HD + HD], axis=0, keepdims=True
            )
        fill_masked_columns(dm, flipped.astype(BF))
        scaled = (q_ref[...].astype(F32) * SCALE)
        fill_masked_columns(qm, scaled.T.astype(BF))
        scaled = scaled.astype(BF)
        for head in range(3):
            depth = 128 if head < 2 else HD
            qn[head, :, 0:depth] = masked_rows(scaled, head)
            dn[head, :, 0:depth] = masked_rows(outer, head)
        dqt[...] = jnp.zeros(dqt.shape, F32)
        grad_out[...] = jnp.zeros(grad_out.shape, F32)
        sums_out[...] = jnp.zeros(sums_out.shape, F32)

    @pl.when(jnp.logical_not(needed))
    def _():
        dn_out[...] = jnp.zeros(dn_out.shape, BF)

    @pl.when(needed)
    def _():
        kt[...] = k_ref[...].astype(F32).T.astype(BF)
        dk[...] = jnp.zeros(dk.shape, F32)
        dv[...] = jnp.zeros(dv.shape, F32)

        def one(step, masked):
            at = pl.ds(pl.multiple_of(step * SUB, SUB), SUB)
            first_key = turn * block + step * SUB
            if masked:
                allowed = allowed_pairs(first_key, first_query, begins_ref[...], (SUB, block))
            for head in range(3):
                depth = 128 if head < 2 else HD
                lanes = head_lanes(head)
                scores = mm(k_ref[at, lanes], qm[head, 0:depth, :])
                probs = jnp.exp(scores - lse_ref[head : head + 1, :])
                if masked:
                    probs = jnp.where(allowed, probs, 0.0)
                outer = mm(v_ref[at, lanes], dm[head, 0:depth, :])
                inner = (probs * (outer - delta[head : head + 1, :])).astype(BF)
                dv[at, lanes] += mm(probs.astype(BF), dn[head, :, 0:depth])
                dk[at, lanes] += mm(inner, qn[head, :, 0:depth])
                part = slice(head * HD, head * HD + HD)
                dqt[part, :] += mm(kt[part, at], inner)

        @pl.loop(0, block // SUB)
        def _(step):
            first_key = turn * block + step * SUB
            inner = (first_key + SUB - 1 <= first_query) & (first_key >= begin_high)
            touched = first_key + SUB - 1 >= begin_low

            @pl.when(inner)
            def _():
                one(step, False)

            @pl.when(jnp.logical_not(inner) & touched)
            def _():
                one(step, True)

        rows = rows_ref[...]
        low_k = dk[...].astype(BF)
        low_v = dv[...].astype(BF)
        grad_out[192:384, :] += mm(low_k.astype(F32).T.astype(BF), rows)
        grad_out[384:576, :] += mm(low_v.astype(F32).T.astype(BF), rows)
        sums_out[1:2, :] += jnp.sum(low_v.astype(F32), axis=0, keepdims=True)
        through = mm_nt(low_k, wk_ref[...]) + mm_nt(low_v, wv_ref[...])

        @pl.when(turn < mine)
        def _():
            dn_out[...] = through.astype(BF)

        @pl.when(turn == mine)
        def _():
            flipped = dqt[...] * SCALE
            low_q = flipped.T.astype(BF)
            grad_out[0:192, :] += mm(flipped.astype(BF), own_ref[...])
            sums_out[0:1, :] += jnp.sum(low_q.astype(F32), axis=0, keepdims=True)
            dn_out[...] = (through + mm_nt(low_q, wq_ref[...])).astype(BF)


def attend_backward(where, rows_all, k, v, own, q, o, lse, g, wp, wq, wk, wv, begins):
    block = own.shape[0]
    count = rows_all.shape[0] // block

    def seen(turn, where_ref):
        return (jnp.minimum(turn, where_ref[0]), 0)

    def each(turn, where_ref):
        return (turn, 0)

    def fixed(turn, where_ref):
        return (0, 0)

    return pl.pallas_call(
        attend_backward_kernel,
        grid_spec=pltpu.PrefetchScalarGridSpec(
            num_scalar_prefetch=1,
            grid=(count,),
            in_specs=[
                pl.BlockSpec((block, D), seen),
                pl.BlockSpec((block, 192), seen),
                pl.BlockSpec((block, 192), seen),
                pl.BlockSpec((block, D), fixed),
                pl.BlockSpec((block, 192), fixed),
                pl.BlockSpec((192, block), fixed),
                pl.BlockSpec((8, block), fixed),
                pl.BlockSpec((block, D), fixed),
                pl.BlockSpec((192, D), fixed),
                pl.BlockSpec((D, 192), fixed),
                pl.BlockSpec((D, 192), fixed),
                pl.BlockSpec((D, 192), fixed),
                pl.BlockSpec((1, block), fixed),
            ],
            out_specs=[
                pl.BlockSpec((block, D), each),
                pl.BlockSpec((576, D), fixed),
                pl.BlockSpec((192, D), fixed),
                pl.BlockSpec((8, 192), fixed),
            ],
            scratch_shapes=[
                pltpu.VMEM((3, 128, block), BF),
                pltpu.VMEM((3, 128, block), BF),
                pltpu.VMEM((3, block, 128), BF),
                pltpu.VMEM((3, block, 128), BF),
                pltpu.VMEM((8, block), F32),
                pltpu.VMEM((192, block), F32),
                pltpu.VMEM((192, block), BF),
                pltpu.VMEM((block, 192), F32),
                pltpu.VMEM((block, 192), F32),
            ],
        ),
        out_shape=[
            jax.ShapeDtypeStruct((block * count, D), BF),
            jax.ShapeDtypeStruct((576, D), F32),
            jax.ShapeDtypeStruct((192, D), F32),
            jax.ShapeDtypeStruct((8, 192), F32),
        ],
        compiler_params=pltpu.CompilerParams(vmem_limit_bytes=48 << 20),
        name="attend_backward",
    )(where, rows_all, k, v, own, q, o, lse, g, wp, wq, wk, wv, begins)


MESH = pl.DeviceIdType.MESH


class Place:
    def __init__(self):
        ctx = lax.axis_index("ctx")
        part = lax.axis_index("fsdp")
        self.levels = lax.axis_size("ctx") // 2
        self.ctx, self.part = ctx, part
        self.level, self.side = ctx // 2, ctx % 2
        self.half, self.core = part // 2, part % 2

    def at(self, level=None, side=None, half=None, core=None):
        level = self.level if level is None else level
        side = self.side if side is None else side
        half = self.half if half is None else half
        core = self.core if core is None else core
        return (level * 2 + side, half * 2 + core)

    @property
    def twin(self):
        return self.at(core=1 - self.core)

    @property
    def across(self):
        return self.at(half=1 - self.half)

    @property
    def corner(self):
        return self.at(half=1 - self.half, core=1 - self.core)

    @property
    def beside(self):
        return self.at(side=1 - self.side)


def remote(source, target, send, recv, device):
    return pltpu.make_async_remote_copy(
        src_ref=source, dst_ref=target, send_sem=send, recv_sem=recv, device_id=device, device_id_type=MESH
    )


def signal(sem, device):
    pl.semaphore_signal(sem, inc=1, device_id=device, device_id_type=MESH)


def piece(ref, ctx, part):
    rows = 192
    return ref.at[pl.ds(pl.multiple_of((ctx * 4 + part) * rows, rows), rows)]


def rows_of(ref, part):
    return ref.at[pl.ds(pl.multiple_of(part * 192, 192), 192)]


def layer_norm(rows_in, gain, shift):
    mean = jnp.mean(rows_in, axis=1, keepdims=True)
    centered = rows_in - mean
    inverse = lax.rsqrt(jnp.mean(centered * centered, axis=1, keepdims=True) + EPS)
    unit = centered * inverse
    return unit * gain + shift, unit, inverse


def gather_kernel(
    levels, tok_ref, vec_ref, acol_ref, ecol_ref, cot_ref,
    all_ref, attend_ref, expand_ref, gtwo_ref, vec_out,
    normed, gtwo, vec_in,
    vec_send, vec_recv, att_send, att_recv, exp_send, exp_recv, two_send, two_recv,
    x_send, x_recv, z_send, z_recv, y_send, y_recv, core_send, core_recv, local_sem,
):
    me = Place()
    mine = me.part
    barrier = pltpu.get_barrier_semaphore()
    for device in (me.twin, me.across, me.corner, me.beside):
        signal(barrier, device)

    @pl.when(me.level > 0)
    def _():
        signal(barrier, me.at(level=me.level - 1))

    @pl.when(me.level < levels - 1)
    def _():
        signal(barrier, me.at(level=me.level + 1))

    ends = (me.level == 0).astype(jnp.int32) + (me.level == levels - 1).astype(jnp.int32)
    pl.semaphore_wait(barrier, 6 - ends)

    peers = (
        (me.twin, me.half * 2 + 1 - me.core),
        (me.across, (1 - me.half) * 2 + me.core),
        (me.corner, (1 - me.half) * 2 + 1 - me.core),
    )
    vecs = [remote(vec_ref, vec_in.at[i], vec_send.at[i], vec_recv.at[i], d) for i, (d, p) in enumerate(peers)]
    for copy in vecs:
        copy.start()
    atts = [
        remote(acol_ref.at[p], rows_of(attend_ref, mine), att_send.at[i], att_recv.at[i], d)
        for i, (d, p) in enumerate(peers)
    ]
    for copy in atts:
        copy.start()
    local = [
        pltpu.make_async_copy(acol_ref.at[mine], rows_of(attend_ref, mine), local_sem.at[0]),
        pltpu.make_async_copy(ecol_ref.at[:, pl.ds(pl.multiple_of(mine * D, D), D)], rows_of(expand_ref, mine), local_sem.at[1]),
    ]
    for copy in local:
        copy.start()
    gtwo[...] = (BRANCH * cot_ref[...].astype(F32)).astype(BF)
    for copy in vecs:
        copy.wait_recv()
    vec_out[...] = vec_ref[...] + vec_in[0] + vec_in[1] + vec_in[2]
    out, unit, inverse = layer_norm(tok_ref[...].astype(F32), vec_out[4:5, :], vec_out[5:6, :])
    normed[...] = out.astype(BF)

    def go(copy):
        copy.start()
        return copy

    ctx = me.ctx
    across = go(remote(normed, piece(all_ref, ctx, mine), x_send.at[0], x_recv.at[0], me.across))
    keep = go(pltpu.make_async_copy(normed, piece(all_ref, ctx, mine), local_sem.at[2]))
    keep_two = go(pltpu.make_async_copy(gtwo, rows_of(gtwo_ref, mine), local_sem.at[3]))
    local += [keep, keep_two]

    def spread_static(source, distance, slot):
        level = me.level - distance
        where = level * 2 + me.side
        half = me.half if slot == 0 else 1 - me.half
        part = half * 2 + me.core

        @pl.when(me.level < levels - 1)
        def _():
            remote(source, piece(all_ref, where, part), z_send.at[distance, slot], z_recv.at[distance + 1, slot], me.at(level=me.level + 1)).start()

        remote(source, piece(all_ref, where, part), y_send.at[distance, slot], y_recv.at[distance, slot], me.beside).start()
        remote(source, piece(all_ref, where, part), core_send.at[distance, 0, slot], core_recv.at[distance, 0, slot], me.twin).start()

    spread_static(normed, 0, 0)
    exps = [
        go(remote(ecol_ref.at[:, pl.ds(pl.multiple_of(p * D, D), D)], rows_of(expand_ref, mine), exp_send.at[i], exp_recv.at[i], d))
        for i, (d, p) in enumerate(peers)
    ]
    two_x = go(remote(gtwo, rows_of(gtwo_ref, mine), two_send.at[0], two_recv.at[0], me.across))
    two_c = go(remote(gtwo, rows_of(gtwo_ref, mine), two_send.at[1], two_recv.at[1], me.twin))

    other = (1 - me.half) * 2 + me.core

    def held(distance, slot, side):
        half = me.half if slot == 0 else 1 - me.half
        return piece(all_ref, (me.level - distance) * 2 + side, half * 2 + me.core)

    def take_y(distance):
        for slot in range(2):
            got = held(distance, slot, 1 - me.side)
            remote(got, got, y_send.at[distance, slot], y_recv.at[distance, slot], me.beside).wait_recv()
            remote(got, got, core_send.at[distance, 1, slot], core_recv.at[distance, 1, slot], me.twin).start()

    got = piece(all_ref, ctx, other)
    remote(normed, got, x_send.at[0], x_recv.at[0], me.across).wait_recv()
    spread_static(got, 0, 1)
    for distance in range(1, levels):

        @pl.when(me.level >= distance)
        def _():
            for slot in range(2):
                got = held(distance, slot, me.side)
                remote(got, got, z_send.at[distance, slot], z_recv.at[distance, slot], me.twin).wait_recv()
                spread_static(got, distance, slot)

        if distance == 1:
            take_y(0)
        else:

            @pl.when(me.level >= distance - 1)
            def _():
                take_y(distance - 1)

    @pl.when(me.level >= levels - 1)
    def _():
        take_y(levels - 1)

    got = rows_of(gtwo_ref, other)
    remote(gtwo, got, two_send.at[0], two_recv.at[0], me.across).wait_recv()
    two_f = go(remote(got, got, two_send.at[2], two_recv.at[2], me.twin))
    for copy in local:
        copy.wait()
    for copy in vecs:
        copy.wait_send()
    for copy in atts + exps + [two_c, two_f]:
        copy.wait()
    two_x.wait_send()
    across.wait_send()
    for distance in range(levels):

        @pl.when(me.level >= distance)
        def _():
            for slot in range(2):
                got = held(distance, slot, me.side)

                @pl.when(me.level < levels - 1)
                def _():
                    remote(got, got, z_send.at[distance, slot], z_recv.at[distance, slot], me.twin).wait_send()

                remote(got, got, y_send.at[distance, slot], y_recv.at[distance, slot], me.beside).wait_send()
                for side in range(2):
                    remote(got, got, core_send.at[distance, side, slot], core_recv.at[distance, side, slot], me.twin).wait()


def gather_inputs(tokens, vectors, attend_cols, expand_weight, cotangent):
    levels = lax.axis_size("ctx") // 2
    rows = tokens.shape[0]
    block = rows * 4
    vmem = pl.BlockSpec(memory_space=pltpu.VMEM)
    anywhere = pl.BlockSpec(memory_space=pl.ANY)
    dma = pltpu.SemaphoreType.DMA
    return pl.pallas_call(
        functools.partial(gather_kernel, levels),
        in_specs=[vmem, vmem, anywhere, anywhere, vmem],
        out_specs=[anywhere, anywhere, anywhere, anywhere, vmem],
        out_shape=[
            jax.ShapeDtypeStruct((block * levels * 2, D), BF),
            jax.ShapeDtypeStruct((D, 576), BF),
            jax.ShapeDtypeStruct((D, D), BF),
            jax.ShapeDtypeStruct((block, D), BF),
            jax.ShapeDtypeStruct((8, D), F32),
        ],
        scratch_shapes=[
            pltpu.VMEM((rows, D), BF),
            pltpu.VMEM((rows, D), BF),
            pltpu.VMEM((3, 8, D), F32),
            dma((3,)), dma((3,)), dma((3,)), dma((3,)), dma((3,)), dma((3,)), dma((3,)), dma((3,)),
            dma((1,)), dma((1,)),
            dma((levels, 2)), dma((levels + 1, 2)),
            dma((levels, 2)), dma((levels, 2)),
            dma((levels, 2, 2)), dma((levels, 2, 2)),
            dma((4,)),
        ],
        compiler_params=pltpu.CompilerParams(collective_id=1, has_side_effects=True, vmem_limit_bytes=16 << 20),
        name="gather_inputs",
    )(tokens, vectors, attend_cols, expand_weight, cotangent)


def gelu_pair(t):
    slope = 0.7978845608028654
    square = t * t
    bend = jnp.tanh(slope * t * (1.0 + 0.044715 * square))
    half = 0.5 * (1.0 + bend)
    return t * half, half + 0.5 * t * (1.0 - bend * bend) * (slope * (1.0 + 0.134145 * square))


def mlp_kernel(
    o_ref, wp_ref, expand_ref, contract_ref, ebias_ref, tok_ref, cot_ref, gtwo_ref, vec_ref,
    block_out, gmid_out, gone_out, cpart_out, epart_out, sums_out,
    o_rows, gact, n2, act, gexp, held, unit,
    c_send_buf, c_recv_buf, x_send_buf, x_recv_buf,
    c_send, c_recv, x_send, x_recv, ag_send, ag_recv,
):
    me = Place()
    mine = me.part
    barrier = pltpu.get_barrier_semaphore()
    signal(barrier, me.twin)
    signal(barrier, me.across)
    pl.semaphore_wait(barrier, 2)
    p_across = (1 - me.half) * 2 + me.core
    p_twin = me.half * 2 + 1 - me.core
    p_corner = (1 - me.half) * 2 + 1 - me.core

    def part(ref, p):
        return ref[pl.ds(pl.multiple_of(p * 192, 192), 192), :]

    def to_twin(i, slot, value):
        c_send_buf[i, slot] = value.astype(BF)
        remote(c_send_buf.at[i, slot], c_recv_buf.at[i, slot], c_send.at[i, slot], c_recv.at[i, slot], me.twin).start()

    def from_twin(i, slot):
        remote(c_send_buf.at[i, slot], c_recv_buf.at[i, slot], c_send.at[i, slot], c_recv.at[i, slot], me.twin).wait_recv()
        return c_recv_buf[i, slot].astype(F32)

    def to_across(i, value):
        x_send_buf[i] = value.astype(BF)
        remote(x_send_buf.at[i], x_recv_buf.at[i], x_send.at[i], x_recv.at[i], me.across).start()

    def from_across(i):
        remote(x_send_buf.at[i], x_recv_buf.at[i], x_send.at[i], x_recv.at[i], me.across).wait_recv()
        return x_recv_buf[i].astype(F32)

    def share(i, ref):
        own = rows_of(ref, mine)
        remote(own, own, ag_send.at[i, 0], ag_recv.at[i, 0], me.across).start()
        remote(own, own, ag_send.at[i, 1], ag_recv.at[i, 1], me.twin).start()

    def share_across(i, ref):
        got = rows_of(ref, p_across)
        remote(got, got, ag_send.at[i, 0], ag_recv.at[i, 0], me.across).wait_recv()
        remote(got, got, ag_send.at[i, 2], ag_recv.at[i, 2], me.twin).start()

    def share_twin(i, ref):
        got = rows_of(ref, p_twin)
        remote(got, got, ag_send.at[i, 1], ag_recv.at[i, 1], me.twin).wait_recv()

    def share_corner(i, ref):
        got = rows_of(ref, p_corner)
        remote(got, got, ag_send.at[i, 2], ag_recv.at[i, 2], me.twin).wait_recv()

    o_rows[...] = o_ref[...].T.astype(BF)
    to_twin(0, 0, mm(part(o_rows, p_corner), wp_ref[...]))
    to_twin(0, 1, mm(part(o_rows, p_twin), wp_ref[...]))
    value = mm(part(o_rows, p_across), wp_ref[...])
    to_across(0, value + from_twin(0, 0))
    for p in range(4):
        gact[p * 192 : p * 192 + 192, :] = mm_nt(gtwo_ref[p * 192 : p * 192 + 192, :], contract_ref[...])
    value = mm(part(o_rows, mine), wp_ref[...]) + from_twin(0, 1)
    value = value + from_across(0)
    middle = tok_ref[...].astype(F32) + BRANCH * (value + vec_ref[2:3, :])
    out, unit_two, inverse = layer_norm(middle, vec_ref[6:7, :], vec_ref[7:8, :])
    n2[pl.ds(pl.multiple_of(mine * 192, 192), 192), :] = out.astype(BF)
    share(0, n2)
    unit[...] = unit_two
    held[...] = middle

    def through(p):
        at = pl.ds(pl.multiple_of(p * 192, 192), 192)
        expanded = mm(n2[at, :], expand_ref[...]) + ebias_ref[...]
        activation, slope = gelu_pair(expanded)
        act[at, :] = activation.astype(BF)
        low = (gact[at, :] * slope).astype(BF)
        gexp[at, :] = low
        return mm_nt(low, expand_ref[...])

    own_value = through(mine)
    share_twin(0, n2)
    to_twin(1, 1, through(p_twin))
    share_across(0, n2)
    across_value = through(p_across)
    share_corner(0, n2)
    to_twin(1, 0, through(p_corner))
    to_across(1, across_value + from_twin(1, 0))
    own_value = own_value + from_twin(1, 1)
    to_twin(2, 0, mm(part(act, p_corner), contract_ref[...]))
    to_twin(2, 1, mm(part(act, p_twin), contract_ref[...]))
    to_across(2, mm(part(act, p_across), contract_ref[...]) + from_twin(2, 0))
    cpart_out[...] = mm_tn(act[...], gtwo_ref[...]).astype(BF)
    grad = own_value + from_across(1)
    unit_two = unit[...]
    scaled = grad * vec_ref[6:7, :]
    spread = (
        scaled
        - jnp.mean(scaled, axis=1, keepdims=True)
        - unit_two * jnp.mean(scaled * unit_two, axis=1, keepdims=True)
    )
    grad_middle = cot_ref[...].astype(F32) + inverse * spread
    gmid_out[...] = grad_middle
    low = (BRANCH * grad_middle).astype(BF)
    gone_out[pl.ds(pl.multiple_of(mine * 192, 192), 192), :] = low
    share(1, gone_out)
    sums_out[0:1, :] = jnp.sum(low.astype(F32), axis=0, keepdims=True)
    sums_out[1:2, :] = jnp.sum(part(gtwo_ref, mine).astype(F32), axis=0, keepdims=True)
    sums_out[2:3, :] = jnp.sum(grad * unit_two, axis=0, keepdims=True)
    sums_out[3:4, :] = jnp.sum(grad, axis=0, keepdims=True)
    sums_out[4:5, :] = jnp.sum(gexp[...].astype(F32), axis=0, keepdims=True)
    sums_out[5:8, :] = jnp.zeros((3, D), F32)
    epart_out[...] = mm_tn(n2[...], gexp[...]).astype(BF)
    value = mm(part(act, mine), contract_ref[...]) + from_twin(2, 1)
    value = value + from_across(2)
    block_out[...] = (held[...] + BRANCH * (value + vec_ref[3:4, :])).astype(BF)
    share_across(1, gone_out)
    share_twin(1, gone_out)
    share_corner(1, gone_out)
    for i in range(3):
        for slot in range(2):
            remote(c_send_buf.at[i, slot], c_recv_buf.at[i, slot], c_send.at[i, slot], c_recv.at[i, slot], me.twin).wait_send()
        remote(x_send_buf.at[i], x_recv_buf.at[i], x_send.at[i], x_recv.at[i], me.across).wait_send()
    for i, ref in ((0, n2), (1, gone_out)):
        own = rows_of(ref, mine)
        for j in range(3):
            remote(own, own, ag_send.at[i, j], ag_recv.at[i, j], me.twin).wait_send()


def feed_forward(o, wp, expand, contract, ebias, tokens, cotangent, gtwo, vectors):
    rows = tokens.shape[0]
    block = rows * 4
    vmem = pl.BlockSpec(memory_space=pltpu.VMEM)
    dma = pltpu.SemaphoreType.DMA
    return pl.pallas_call(
        mlp_kernel,
        in_specs=[vmem] * 9,
        out_specs=[vmem] * 6,
        out_shape=[
            jax.ShapeDtypeStruct((rows, D), BF),
            jax.ShapeDtypeStruct((rows, D), F32),
            jax.ShapeDtypeStruct((block, D), BF),
            jax.ShapeDtypeStruct((D, D), BF),
            jax.ShapeDtypeStruct((D, D), BF),
            jax.ShapeDtypeStruct((8, D), F32),
        ],
        scratch_shapes=[
            pltpu.VMEM((block, 192), BF),
            pltpu.VMEM((block, D), F32),
            pltpu.VMEM((block, D), BF),
            pltpu.VMEM((block, D), BF),
            pltpu.VMEM((block, D), BF),
            pltpu.VMEM((rows, D), F32),
            pltpu.VMEM((rows, D), F32),
            pltpu.VMEM((3, 2, rows, D), BF),
            pltpu.VMEM((3, 2, rows, D), BF),
            pltpu.VMEM((3, rows, D), BF),
            pltpu.VMEM((3, rows, D), BF),
            dma((3, 2)), dma((3, 2)), dma((3,)), dma((3,)), dma((2, 3)), dma((2, 3)),
        ],
        compiler_params=pltpu.CompilerParams(collective_id=2, has_side_effects=True, vmem_limit_bytes=48 << 20),
        name="feed_forward",
    )(o, wp, expand, contract, ebias, tokens, cotangent, gtwo, vectors)


def normalize(rows_in, gain, shift):
    mean = jnp.mean(rows_in, axis=1, keepdims=True)
    centered = rows_in - mean
    inverse = lax.rsqrt(jnp.mean(centered * centered, axis=1, keepdims=True) + EPS)
    unit = centered * inverse
    return (unit * gain + shift, unit, inverse)


def normalize_back(incoming, unit, inverse, gain):
    scaled = incoming * gain
    spread = (
        scaled
        - jnp.mean(scaled, axis=1, keepdims=True)
        - unit * jnp.mean(scaled * unit, axis=1, keepdims=True)
    )
    return (inverse * spread, jnp.sum(incoming * unit, axis=0), jnp.sum(incoming, axis=0))


def first_position(places, starts):
    below = starts[None, :] <= places[:, None]
    return jnp.max(jnp.where(below, starts[None, :], 0), axis=1)


def per_device(
    tokens, document_starts, attend_weight, attend_bias, project_weight, project_bias,
    expand_weight, expand_bias, contract_weight, contract_bias,
    gain_first, shift_first, gain_second, shift_second, cotangent,
):
    both = ("ctx", "fsdp")
    rows = tokens.shape[0]
    ways = lax.axis_size("fsdp")
    block = rows * ways
    ctx = lax.axis_index("ctx")
    part = lax.axis_index("fsdp")

    def whole(array_in):
        return lax.all_gather(array_in, "fsdp", axis=0, tiled=True)

    own_vectors = jnp.stack([project_bias, contract_bias, gain_first, shift_first, gain_second, shift_second])
    vectors = lax.dynamic_update_slice(jnp.zeros((6, D), F32), own_vectors.astype(F32), (0, part * rows))
    biases = lax.dynamic_update_slice(jnp.zeros((2 * D,), F32), attend_bias.astype(F32), (part * 2 * rows,))
    vectors = jnp.concatenate([biases.reshape(2, D), vectors])
    attend_cols = attend_weight.reshape(rows, 3, ways, 192).transpose(2, 0, 1, 3).reshape(ways, rows, 576)
    normed_all, attend_cols, expand_cols, g2, vectors = gather_inputs(
        tokens, vectors, attend_cols, expand_weight, cotangent
    )
    project_b, contract_b, gain_one, shift_one, gain_two, shift_two = [vectors[i] for i in range(2, 8)]
    wq, wk, wv = attend_cols[:, :192], attend_cols[:, 192:384], attend_cols[:, 384:]
    bias = lax.dynamic_slice(vectors, (0, part * 192), (2, 192))

    hidden_in = tokens.astype(F32)
    normed, unit_one, inverse_one = normalize(hidden_in, gain_one, shift_one)
    own = lax.dynamic_slice(normed_all, (ctx * block, 0), (block, D))
    places = ctx * block + jnp.arange(block, dtype=jnp.int32)
    begins = first_position(places, document_starts)
    where = jnp.stack([ctx, begins[0], begins[-1]]).astype(jnp.int32)
    begins_row = begins.reshape(1, block)
    q, k, v, o, lse = attend_forward(where, normed_all, own, wq, wk, wv, bias, begins_row)
    block_output, grad_middle, g1, contract_part, expand_part, mlp_sums = feed_forward(
        o, project_weight, expand_cols, contract_weight, expand_bias.astype(F32).reshape(1, D), tokens, cotangent, g2, vectors
    )
    dn, attend_t, project_part, sums = attend_backward(
        where, normed_all, k, v, own, q, o, lse, g1, project_weight, wq, wk, wv, begins_row
    )
    grad_normed = lax.psum_scatter(dn.astype(F32), both, scatter_dimension=0, tiled=True)
    first_part, gainone_grad, shiftone_grad = normalize_back(grad_normed, unit_one, inverse_one, gain_one)
    tokens_grad = grad_middle + first_part

    def summed(array_in):
        return lax.psum(array_in.astype(BF), "ctx").astype(F32)

    contract_grad = summed(contract_part)
    project_grad = summed(project_part)
    expand_grad = lax.all_to_all(summed(expand_part).reshape(ways, rows, D), "fsdp", 0, 0)
    expand_grad = expand_grad.transpose(1, 0, 2).reshape(rows, ways * D)
    attend_grad = lax.all_to_all(summed(attend_t.T).reshape(ways, rows, 576), "fsdp", 0, 0)
    attend_grad = attend_grad.reshape(ways, rows, 3, 192).transpose(1, 2, 0, 3).reshape(rows, 3 * D)
    expbias_grad = lax.psum(mlp_sums[4], "ctx")
    spread = jnp.zeros((2, D), F32)
    spread = lax.dynamic_update_slice(spread, sums[:2], (0, part * 192))
    vectors = jnp.concatenate([
        spread.reshape(-1),
        mlp_sums[0], mlp_sums[1], gainone_grad, shiftone_grad, mlp_sums[2], mlp_sums[3],
    ])
    vectors = lax.psum(vectors, both)

    def mine_of(start, length):
        return lax.dynamic_slice(vectors, (start + part * (length // ways),), (length // ways,))

    return (
        block_output.astype(BF), tokens_grad.astype(BF),
        attend_grad, mine_of(0, 2 * D), project_grad, mine_of(2 * D, D), expand_grad, expbias_grad,
        contract_grad, mine_of(3 * D, D), mine_of(4 * D, D), mine_of(5 * D, D), mine_of(6 * D, D), mine_of(7 * D, D),
    )


def solution(mesh):
    tok, row, vec = P(("ctx", "fsdp"), None), P("fsdp", None), P("fsdp")
    in_specs = (tok, P(), row, vec, row, vec, row, vec, row, vec, vec, vec, vec, vec, tok)
    out_specs = (tok, tok, row, vec, row, vec, row, vec, row, vec, vec, vec, vec, vec)
    return jax.shard_map(per_device, mesh=mesh, in_specs=in_specs, out_specs=out_specs, check_vma=False)
```

```python
import functools
import jax
import jax.numpy as jnp
from jax import lax
from jax.experimental import pallas as pl
from jax.experimental.pallas import tpu as pltpu
from jax.sharding import PartitionSpec as P

D = 768
H = 12
HD = 64
EPS = 1e-05
SCALE = 0.125
BRANCH = 48.0 ** (-0.5)
NEG = -1e30
SUB = 256
BF = jnp.bfloat16
F32 = jnp.float32


def mm(a, b):
    return jnp.dot(a, b, preferred_element_type=F32)


def mm_nt(a, b):
    return lax.dot_general(a, b, (((1,), (1,)), ((), ())), preferred_element_type=F32)


def mm_tn(a, b):
    return lax.dot_general(a, b, (((0,), (0,)), ((), ())), preferred_element_type=F32)


def head_lanes(head):
    return slice(0, 128) if head < 2 else slice(128, 192)


def fill_masked_columns(target, flipped):
    zero = jnp.zeros((HD, flipped.shape[1]), BF)
    target[0, 0:HD, :] = flipped[0:HD]
    target[0, HD : 2 * HD, :] = zero
    target[1, 0:HD, :] = zero
    target[1, HD : 2 * HD, :] = flipped[HD : 2 * HD]
    target[2, 0:HD, :] = flipped[2 * HD : 3 * HD]


def masked_rows(array_in, head):
    if head == 2:
        return array_in[:, 128:192]
    pair = array_in[:, 0:128]
    lane = lax.broadcasted_iota(jnp.int32, pair.shape, 1)
    return jnp.where((lane < HD) if head == 0 else (lane >= HD), pair, jnp.zeros_like(pair))


def allowed_pairs(first_key, first_query, begins, shape):
    key_places = first_key + lax.broadcasted_iota(jnp.int32, shape, 0)
    query_places = first_query + lax.broadcasted_iota(jnp.int32, shape, 1)
    return (key_places <= query_places) & (key_places >= begins)


def attend_forward_kernel(
    where_ref, rows_ref, own_ref, wq_ref, wk_ref, wv_ref, bias_ref, begins_ref,
    q_out, k_out, v_out, o_out, lse_out,
    qm, vt, peak, total, acc,
):
    turn = pl.program_id(0)
    block = own_ref.shape[0]
    mine, begin_low, begin_high = where_ref[0], where_ref[1], where_ref[2]
    first_query = mine * block
    needed = (turn <= mine) & ((turn + 1) * block - 1 >= begin_low)

    @pl.when(turn == 0)
    def _():
        query = (mm(own_ref[...], wq_ref[...]) + bias_ref[0:1, :]).astype(BF)
        q_out[...] = query
        fill_masked_columns(qm, (query.astype(F32) * SCALE).T.astype(BF))
        peak[...] = jnp.full(peak.shape, NEG, F32)
        total[...] = jnp.zeros(total.shape, F32)
        acc[...] = jnp.zeros(acc.shape, F32)

    @pl.when(needed)
    def _():
        rows = rows_ref[...]
        k_out[...] = mm(rows, wk_ref[...]).astype(BF)
        value = (mm(rows, wv_ref[...]) + bias_ref[1:2, :]).astype(BF)
        v_out[...] = value
        vt[...] = value.astype(F32).T.astype(BF)

        def one(step, masked):
            at = pl.ds(pl.multiple_of(step * SUB, SUB), SUB)
            first_key = turn * block + step * SUB
            if masked:
                allowed = allowed_pairs(first_key, first_query, begins_ref[...], (SUB, block))
            for head in range(3):
                depth = 128 if head < 2 else HD
                scores = mm(k_out[at, head_lanes(head)], qm[head, 0:depth, :])
                if masked:
                    scores = jnp.where(allowed, scores, NEG)
                old = peak[head : head + 1, :]
                new = jnp.maximum(old, jnp.max(scores, axis=0, keepdims=True))
                weights = jnp.exp(scores - new)
                if masked:
                    weights = jnp.where(allowed, weights, 0.0)
                factor = jnp.exp(old - new)
                peak[head : head + 1, :] = new
                total[head : head + 1, :] = total[head : head + 1, :] * factor + jnp.sum(
                    weights, axis=0, keepdims=True
                )
                part = slice(head * HD, head * HD + HD)
                acc[part, :] = acc[part, :] * factor + mm(vt[part, at], weights.astype(BF))

        @pl.loop(0, block // SUB)
        def _(step):
            first_key = turn * block + step * SUB
            inner = (first_key + SUB - 1 <= first_query) & (first_key >= begin_high)
            touched = first_key + SUB - 1 >= begin_low

            @pl.when(inner)
            def _():
                one(step, False)

            @pl.when(jnp.logical_not(inner) & touched)
            def _():
                one(step, True)

    @pl.when(turn == mine)
    def _():
        for head in range(3):
            part = slice(head * HD, head * HD + HD)
            o_out[part, :] = acc[part, :] / total[head : head + 1, :]
        lse_out[...] = peak[...] + jnp.log(jnp.maximum(total[...], 1e-30))


def attend_forward(where, rows_all, own, wq, wk, wv, bias, begins):
    block = own.shape[0]
    count = rows_all.shape[0] // block

    def seen(turn, where_ref):
        return (jnp.minimum(turn, where_ref[0]), 0)

    def fixed(turn, where_ref):
        return (0, 0)

    return pl.pallas_call(
        attend_forward_kernel,
        grid_spec=pltpu.PrefetchScalarGridSpec(
            num_scalar_prefetch=1,
            grid=(count,),
            in_specs=[
                pl.BlockSpec((block, D), seen),
                pl.BlockSpec((block, D), fixed),
                pl.BlockSpec((D, 192), fixed),
                pl.BlockSpec((D, 192), fixed),
                pl.BlockSpec((D, 192), fixed),
                pl.BlockSpec((2, 192), fixed),
                pl.BlockSpec((1, block), fixed),
            ],
            out_specs=[
                pl.BlockSpec((block, 192), fixed),
                pl.BlockSpec((block, 192), seen),
                pl.BlockSpec((block, 192), seen),
                pl.BlockSpec((192, block), fixed),
                pl.BlockSpec((8, block), fixed),
            ],
            scratch_shapes=[
                pltpu.VMEM((3, 128, block), BF),
                pltpu.VMEM((192, block), BF),
                pltpu.VMEM((8, block), F32),
                pltpu.VMEM((8, block), F32),
                pltpu.VMEM((192, block), F32),
            ],
        ),
        out_shape=[
            jax.ShapeDtypeStruct((block, 192), BF),
            jax.ShapeDtypeStruct((block * count, 192), BF),
            jax.ShapeDtypeStruct((block * count, 192), BF),
            jax.ShapeDtypeStruct((192, block), F32),
            jax.ShapeDtypeStruct((8, block), F32),
        ],
        compiler_params=pltpu.CompilerParams(vmem_limit_bytes=48 << 20),
        name="attend_forward",
    )(where, rows_all, own, wq, wk, wv, bias, begins)


def attend_backward_kernel(
    where_ref, rows_ref, k_ref, v_ref, own_ref, q_ref, o_ref, lse_ref, g_ref, wp_ref,
    wq_ref, wk_ref, wv_ref, begins_ref,
    dn_out, grad_out, proj_out, sums_out,
    qm, dm, qn, dn, delta, dqt, kt, dk, dv,
):
    turn = pl.program_id(0)
    block = own_ref.shape[0]
    mine, begin_low, begin_high = where_ref[0], where_ref[1], where_ref[2]
    first_query = mine * block
    needed = (turn <= mine) & ((turn + 1) * block - 1 >= begin_low)

    @pl.when(turn == 0)
    def _():
        grads = g_ref[...]
        exact = o_ref[...]
        proj_out[...] = mm(exact.astype(BF), grads)
        outer = mm_nt(grads, wp_ref[...]).astype(BF)
        flipped = outer.astype(F32).T
        product = flipped * exact
        for head in range(3):
            delta[head : head + 1, :] = jnp.sum(
                product[head * HD : head * HD + HD], axis=0, keepdims=True
            )
        fill_masked_columns(dm, flipped.astype(BF))
        scaled = (q_ref[...].astype(F32) * SCALE)
        fill_masked_columns(qm, scaled.T.astype(BF))
        scaled = scaled.astype(BF)
        for head in range(3):
            depth = 128 if head < 2 else HD
            qn[head, :, 0:depth] = masked_rows(scaled, head)
            dn[head, :, 0:depth] = masked_rows(outer, head)
        dqt[...] = jnp.zeros(dqt.shape, F32)
        grad_out[...] = jnp.zeros(grad_out.shape, F32)
        sums_out[...] = jnp.zeros(sums_out.shape, F32)

    @pl.when(jnp.logical_not(needed))
    def _():
        dn_out[...] = jnp.zeros(dn_out.shape, BF)

    @pl.when(needed)
    def _():
        kt[...] = k_ref[...].astype(F32).T.astype(BF)
        dk[...] = jnp.zeros(dk.shape, F32)
        dv[...] = jnp.zeros(dv.shape, F32)

        def one(step, masked):
            at = pl.ds(pl.multiple_of(step * SUB, SUB), SUB)
            first_key = turn * block + step * SUB
            if masked:
                allowed = allowed_pairs(first_key, first_query, begins_ref[...], (SUB, block))
            for head in range(3):
                depth = 128 if head < 2 else HD
                lanes = head_lanes(head)
                scores = mm(k_ref[at, lanes], qm[head, 0:depth, :])
                probs = jnp.exp(scores - lse_ref[head : head + 1, :])
                if masked:
                    probs = jnp.where(allowed, probs, 0.0)
                outer = mm(v_ref[at, lanes], dm[head, 0:depth, :])
                inner = (probs * (outer - delta[head : head + 1, :])).astype(BF)
                dv[at, lanes] += mm(probs.astype(BF), dn[head, :, 0:depth])
                dk[at, lanes] += mm(inner, qn[head, :, 0:depth])
                part = slice(head * HD, head * HD + HD)
                dqt[part, :] += mm(kt[part, at], inner)

        @pl.loop(0, block // SUB)
        def _(step):
            first_key = turn * block + step * SUB
            inner = (first_key + SUB - 1 <= first_query) & (first_key >= begin_high)
            touched = first_key + SUB - 1 >= begin_low

            @pl.when(inner)
            def _():
                one(step, False)

            @pl.when(jnp.logical_not(inner) & touched)
            def _():
                one(step, True)

        rows = rows_ref[...]
        low_k = dk[...].astype(BF)
        low_v = dv[...].astype(BF)
        grad_out[192:384, :] += mm(low_k.astype(F32).T.astype(BF), rows)
        grad_out[384:576, :] += mm(low_v.astype(F32).T.astype(BF), rows)
        sums_out[1:2, :] += jnp.sum(low_v.astype(F32), axis=0, keepdims=True)
        through = mm_nt(low_k, wk_ref[...]) + mm_nt(low_v, wv_ref[...])

        @pl.when(turn < mine)
        def _():
            dn_out[...] = through.astype(BF)

        @pl.when(turn == mine)
        def _():
            flipped = dqt[...] * SCALE
            low_q = flipped.T.astype(BF)
            grad_out[0:192, :] += mm(flipped.astype(BF), own_ref[...])
            sums_out[0:1, :] += jnp.sum(low_q.astype(F32), axis=0, keepdims=True)
            dn_out[...] = (through + mm_nt(low_q, wq_ref[...])).astype(BF)


def attend_backward(where, rows_all, k, v, own, q, o, lse, g, wp, wq, wk, wv, begins):
    block = own.shape[0]
    count = rows_all.shape[0] // block

    def seen(turn, where_ref):
        return (jnp.minimum(turn, where_ref[0]), 0)

    def each(turn, where_ref):
        return (turn, 0)

    def fixed(turn, where_ref):
        return (0, 0)

    return pl.pallas_call(
        attend_backward_kernel,
        grid_spec=pltpu.PrefetchScalarGridSpec(
            num_scalar_prefetch=1,
            grid=(count,),
            in_specs=[
                pl.BlockSpec((block, D), seen),
                pl.BlockSpec((block, 192), seen),
                pl.BlockSpec((block, 192), seen),
                pl.BlockSpec((block, D), fixed),
                pl.BlockSpec((block, 192), fixed),
                pl.BlockSpec((192, block), fixed),
                pl.BlockSpec((8, block), fixed),
                pl.BlockSpec((block, D), fixed),
                pl.BlockSpec((192, D), fixed),
                pl.BlockSpec((D, 192), fixed),
                pl.BlockSpec((D, 192), fixed),
                pl.BlockSpec((D, 192), fixed),
                pl.BlockSpec((1, block), fixed),
            ],
            out_specs=[
                pl.BlockSpec((block, D), each),
                pl.BlockSpec((576, D), fixed),
                pl.BlockSpec((192, D), fixed),
                pl.BlockSpec((8, 192), fixed),
            ],
            scratch_shapes=[
                pltpu.VMEM((3, 128, block), BF),
                pltpu.VMEM((3, 128, block), BF),
                pltpu.VMEM((3, block, 128), BF),
                pltpu.VMEM((3, block, 128), BF),
                pltpu.VMEM((8, block), F32),
                pltpu.VMEM((192, block), F32),
                pltpu.VMEM((192, block), BF),
                pltpu.VMEM((block, 192), F32),
                pltpu.VMEM((block, 192), F32),
            ],
        ),
        out_shape=[
            jax.ShapeDtypeStruct((block * count, D), BF),
            jax.ShapeDtypeStruct((576, D), F32),
            jax.ShapeDtypeStruct((192, D), F32),
            jax.ShapeDtypeStruct((8, 192), F32),
        ],
        compiler_params=pltpu.CompilerParams(vmem_limit_bytes=48 << 20),
        name="attend_backward",
    )(where, rows_all, k, v, own, q, o, lse, g, wp, wq, wk, wv, begins)


MESH = pl.DeviceIdType.MESH


class Place:
    def __init__(self):
        ctx = lax.axis_index("ctx")
        part = lax.axis_index("fsdp")
        self.levels = lax.axis_size("ctx") // 2
        self.ctx, self.part = ctx, part
        self.level, self.side = ctx // 2, ctx % 2
        self.half, self.core = part // 2, part % 2

    def at(self, level=None, side=None, half=None, core=None):
        level = self.level if level is None else level
        side = self.side if side is None else side
        half = self.half if half is None else half
        core = self.core if core is None else core
        return (level * 2 + side, half * 2 + core)

    @property
    def twin(self):
        return self.at(core=1 - self.core)

    @property
    def across(self):
        return self.at(half=1 - self.half)

    @property
    def corner(self):
        return self.at(half=1 - self.half, core=1 - self.core)

    @property
    def beside(self):
        return self.at(side=1 - self.side)


def remote(source, target, send, recv, device):
    return pltpu.make_async_remote_copy(
        src_ref=source, dst_ref=target, send_sem=send, recv_sem=recv, device_id=device, device_id_type=MESH
    )


def signal(sem, device):
    pl.semaphore_signal(sem, inc=1, device_id=device, device_id_type=MESH)


def piece(ref, ctx, part):
    rows = 192
    return ref.at[pl.ds(pl.multiple_of((ctx * 4 + part) * rows, rows), rows)]


def rows_of(ref, part):
    return ref.at[pl.ds(pl.multiple_of(part * 192, 192), 192)]


def layer_norm(rows_in, gain, shift):
    mean = jnp.mean(rows_in, axis=1, keepdims=True)
    centered = rows_in - mean
    inverse = lax.rsqrt(jnp.mean(centered * centered, axis=1, keepdims=True) + EPS)
    unit = centered * inverse
    return unit * gain + shift, unit, inverse


def gather_kernel(
    levels, tok_ref, vec_ref, acol_ref, ecol_ref, cot_ref,
    all_ref, attend_ref, expand_ref, gtwo_ref, vec_out,
    normed, gtwo, vec_in,
    vec_send, vec_recv, att_send, att_recv, exp_send, exp_recv, two_send, two_recv,
    x_send, x_recv, z_send, z_recv, y_send, y_recv, core_send, core_recv, local_sem,
):
    me = Place()
    mine = me.part
    barrier = pltpu.get_barrier_semaphore()
    for device in (me.twin, me.across, me.corner, me.beside):
        signal(barrier, device)

    @pl.when(me.level > 0)
    def _():
        signal(barrier, me.at(level=me.level - 1))

    @pl.when(me.level < levels - 1)
    def _():
        signal(barrier, me.at(level=me.level + 1))

    ends = (me.level == 0).astype(jnp.int32) + (me.level == levels - 1).astype(jnp.int32)
    pl.semaphore_wait(barrier, 6 - ends)

    peers = (
        (me.twin, me.half * 2 + 1 - me.core),
        (me.across, (1 - me.half) * 2 + me.core),
        (me.corner, (1 - me.half) * 2 + 1 - me.core),
    )
    vecs = [remote(vec_ref, vec_in.at[i], vec_send.at[i], vec_recv.at[i], d) for i, (d, p) in enumerate(peers)]
    for copy in vecs:
        copy.start()
    atts = [
        remote(acol_ref.at[p], rows_of(attend_ref, mine), att_send.at[i], att_recv.at[i], d)
        for i, (d, p) in enumerate(peers)
    ]
    for copy in atts:
        copy.start()
    local = [
        pltpu.make_async_copy(acol_ref.at[mine], rows_of(attend_ref, mine), local_sem.at[0]),
        pltpu.make_async_copy(ecol_ref.at[:, pl.ds(pl.multiple_of(mine * D, D), D)], rows_of(expand_ref, mine), local_sem.at[1]),
    ]
    for copy in local:
        copy.start()
    gtwo[...] = (BRANCH * cot_ref[...].astype(F32)).astype(BF)
    for copy in vecs:
        copy.wait_recv()
    vec_out[...] = vec_ref[...] + vec_in[0] + vec_in[1] + vec_in[2]
    out, unit, inverse = layer_norm(tok_ref[...].astype(F32), vec_out[4:5, :], vec_out[5:6, :])
    normed[...] = out.astype(BF)

    def go(copy):
        copy.start()
        return copy

    ctx = me.ctx
    across = go(remote(normed, piece(all_ref, ctx, mine), x_send.at[0], x_recv.at[0], me.across))
    keep = go(pltpu.make_async_copy(normed, piece(all_ref, ctx, mine), local_sem.at[2]))
    keep_two = go(pltpu.make_async_copy(gtwo, rows_of(gtwo_ref, mine), local_sem.at[3]))
    local += [keep, keep_two]

    def spread_static(source, distance, slot):
        level = me.level - distance
        where = level * 2 + me.side
        half = me.half if slot == 0 else 1 - me.half
        part = half * 2 + me.core

        @pl.when(me.level < levels - 1)
        def _():
            remote(source, piece(all_ref, where, part), z_send.at[distance, slot], z_recv.at[distance + 1, slot], me.at(level=me.level + 1)).start()

        remote(source, piece(all_ref, where, part), y_send.at[distance, slot], y_recv.at[distance, slot], me.beside).start()
        remote(source, piece(all_ref, where, part), core_send.at[distance, 0, slot], core_recv.at[distance, 0, slot], me.twin).start()

    spread_static(normed, 0, 0)
    exps = [
        go(remote(ecol_ref.at[:, pl.ds(pl.multiple_of(p * D, D), D)], rows_of(expand_ref, mine), exp_send.at[i], exp_recv.at[i], d))
        for i, (d, p) in enumerate(peers)
    ]
    two_x = go(remote(gtwo, rows_of(gtwo_ref, mine), two_send.at[0], two_recv.at[0], me.across))
    two_c = go(remote(gtwo, rows_of(gtwo_ref, mine), two_send.at[1], two_recv.at[1], me.twin))

    other = (1 - me.half) * 2 + me.core

    def held(distance, slot, side):
        half = me.half if slot == 0 else 1 - me.half
        return piece(all_ref, (me.level - distance) * 2 + side, half * 2 + me.core)

    def take_y(distance):
        for slot in range(2):
            got = held(distance, slot, 1 - me.side)
            remote(got, got, y_send.at[distance, slot], y_recv.at[distance, slot], me.beside).wait_recv()
            remote(got, got, core_send.at[distance, 1, slot], core_recv.at[distance, 1, slot], me.twin).start()

    got = piece(all_ref, ctx, other)
    remote(normed, got, x_send.at[0], x_recv.at[0], me.across).wait_recv()
    spread_static(got, 0, 1)
    for distance in range(1, levels):

        @pl.when(me.level >= distance)
        def _():
            for slot in range(2):
                got = held(distance, slot, me.side)
                remote(got, got, z_send.at[distance, slot], z_recv.at[distance, slot], me.twin).wait_recv()
                spread_static(got, distance, slot)

        if distance == 1:
            take_y(0)
        else:

            @pl.when(me.level >= distance - 1)
            def _():
                take_y(distance - 1)

    @pl.when(me.level >= levels - 1)
    def _():
        take_y(levels - 1)

    got = rows_of(gtwo_ref, other)
    remote(gtwo, got, two_send.at[0], two_recv.at[0], me.across).wait_recv()
    two_f = go(remote(got, got, two_send.at[2], two_recv.at[2], me.twin))
    for copy in local:
        copy.wait()
    for copy in vecs:
        copy.wait_send()
    for copy in atts + exps + [two_c, two_f]:
        copy.wait()
    two_x.wait_send()
    across.wait_send()
    for distance in range(levels):

        @pl.when(me.level >= distance)
        def _():
            for slot in range(2):
                got = held(distance, slot, me.side)

                @pl.when(me.level < levels - 1)
                def _():
                    remote(got, got, z_send.at[distance, slot], z_recv.at[distance, slot], me.twin).wait_send()

                remote(got, got, y_send.at[distance, slot], y_recv.at[distance, slot], me.beside).wait_send()
                for side in range(2):
                    remote(got, got, core_send.at[distance, side, slot], core_recv.at[distance, side, slot], me.twin).wait()


def gather_inputs(tokens, vectors, attend_cols, expand_weight, cotangent):
    levels = lax.axis_size("ctx") // 2
    rows = tokens.shape[0]
    block = rows * 4
    vmem = pl.BlockSpec(memory_space=pltpu.VMEM)
    anywhere = pl.BlockSpec(memory_space=pl.ANY)
    dma = pltpu.SemaphoreType.DMA
    return pl.pallas_call(
        functools.partial(gather_kernel, levels),
        in_specs=[vmem, vmem, anywhere, anywhere, vmem],
        out_specs=[anywhere, anywhere, anywhere, anywhere, vmem],
        out_shape=[
            jax.ShapeDtypeStruct((block * levels * 2, D), BF),
            jax.ShapeDtypeStruct((D, 576), BF),
            jax.ShapeDtypeStruct((D, D), BF),
            jax.ShapeDtypeStruct((block, D), BF),
            jax.ShapeDtypeStruct((8, D), F32),
        ],
        scratch_shapes=[
            pltpu.VMEM((rows, D), BF),
            pltpu.VMEM((rows, D), BF),
            pltpu.VMEM((3, 8, D), F32),
            dma((3,)), dma((3,)), dma((3,)), dma((3,)), dma((3,)), dma((3,)), dma((3,)), dma((3,)),
            dma((1,)), dma((1,)),
            dma((levels, 2)), dma((levels + 1, 2)),
            dma((levels, 2)), dma((levels, 2)),
            dma((levels, 2, 2)), dma((levels, 2, 2)),
            dma((4,)),
        ],
        compiler_params=pltpu.CompilerParams(collective_id=1, has_side_effects=True, vmem_limit_bytes=16 << 20),
        name="gather_inputs",
    )(tokens, vectors, attend_cols, expand_weight, cotangent)


def gelu_pair(t):
    slope = 0.7978845608028654
    square = t * t
    bend = jnp.tanh(slope * t * (1.0 + 0.044715 * square))
    half = 0.5 * (1.0 + bend)
    return t * half, half + 0.5 * t * (1.0 - bend * bend) * (slope * (1.0 + 0.134145 * square))


def mlp_kernel(
    o_ref, wp_ref, expand_ref, contract_ref, ebias_ref, tok_ref, cot_ref, gtwo_ref, vec_ref,
    block_out, gmid_out, gone_out, cpart_out, epart_out, sums_out,
    o_rows, gact, n2, act, gexp, held, unit,
    c_send_buf, c_recv_buf, x_send_buf, x_recv_buf,
    c_send, c_recv, x_send, x_recv, ag_send, ag_recv,
):
    me = Place()
    mine = me.part
    barrier = pltpu.get_barrier_semaphore()
    signal(barrier, me.twin)
    signal(barrier, me.across)
    pl.semaphore_wait(barrier, 2)
    p_across = (1 - me.half) * 2 + me.core
    p_twin = me.half * 2 + 1 - me.core
    p_corner = (1 - me.half) * 2 + 1 - me.core

    def part(ref, p):
        return ref[pl.ds(pl.multiple_of(p * 192, 192), 192), :]

    def to_twin(i, slot, value):
        c_send_buf[i, slot] = value.astype(BF)
        remote(c_send_buf.at[i, slot], c_recv_buf.at[i, slot], c_send.at[i, slot], c_recv.at[i, slot], me.twin).start()

    def from_twin(i, slot):
        remote(c_send_buf.at[i, slot], c_recv_buf.at[i, slot], c_send.at[i, slot], c_recv.at[i, slot], me.twin).wait_recv()
        return c_recv_buf[i, slot].astype(F32)

    def to_across(i, value):
        x_send_buf[i] = value.astype(BF)
        remote(x_send_buf.at[i], x_recv_buf.at[i], x_send.at[i], x_recv.at[i], me.across).start()

    def from_across(i):
        remote(x_send_buf.at[i], x_recv_buf.at[i], x_send.at[i], x_recv.at[i], me.across).wait_recv()
        return x_recv_buf[i].astype(F32)

    def share(i, ref):
        own = rows_of(ref, mine)
        remote(own, own, ag_send.at[i, 0], ag_recv.at[i, 0], me.across).start()
        remote(own, own, ag_send.at[i, 1], ag_recv.at[i, 1], me.twin).start()

    def share_across(i, ref):
        got = rows_of(ref, p_across)
        remote(got, got, ag_send.at[i, 0], ag_recv.at[i, 0], me.across).wait_recv()
        remote(got, got, ag_send.at[i, 2], ag_recv.at[i, 2], me.twin).start()

    def share_twin(i, ref):
        got = rows_of(ref, p_twin)
        remote(got, got, ag_send.at[i, 1], ag_recv.at[i, 1], me.twin).wait_recv()

    def share_corner(i, ref):
        got = rows_of(ref, p_corner)
        remote(got, got, ag_send.at[i, 2], ag_recv.at[i, 2], me.twin).wait_recv()

    o_rows[...] = o_ref[...].T.astype(BF)
    to_twin(0, 0, mm(part(o_rows, p_corner), wp_ref[...]))
    to_twin(0, 1, mm(part(o_rows, p_twin), wp_ref[...]))
    value = mm(part(o_rows, p_across), wp_ref[...])
    to_across(0, value + from_twin(0, 0))
    for p in range(4):
        gact[p * 192 : p * 192 + 192, :] = mm_nt(gtwo_ref[p * 192 : p * 192 + 192, :], contract_ref[...])
    value = mm(part(o_rows, mine), wp_ref[...]) + from_twin(0, 1)
    value = value + from_across(0)
    middle = tok_ref[...].astype(F32) + BRANCH * (value + vec_ref[2:3, :])
    out, unit_two, inverse = layer_norm(middle, vec_ref[6:7, :], vec_ref[7:8, :])
    n2[pl.ds(pl.multiple_of(mine * 192, 192), 192), :] = out.astype(BF)
    share(0, n2)
    unit[...] = unit_two
    held[...] = middle

    def through(p):
        at = pl.ds(pl.multiple_of(p * 192, 192), 192)
        expanded = mm(n2[at, :], expand_ref[...]) + ebias_ref[...]
        activation, slope = gelu_pair(expanded)
        act[at, :] = activation.astype(BF)
        low = (gact[at, :] * slope).astype(BF)
        gexp[at, :] = low
        return mm_nt(low, expand_ref[...])

    own_value = through(mine)
    share_twin(0, n2)
    to_twin(1, 1, through(p_twin))
    share_across(0, n2)
    across_value = through(p_across)
    share_corner(0, n2)
    to_twin(1, 0, through(p_corner))
    to_across(1, across_value + from_twin(1, 0))
    own_value = own_value + from_twin(1, 1)
    to_twin(2, 0, mm(part(act, p_corner), contract_ref[...]))
    to_twin(2, 1, mm(part(act, p_twin), contract_ref[...]))
    to_across(2, mm(part(act, p_across), contract_ref[...]) + from_twin(2, 0))
    cpart_out[...] = mm_tn(act[...], gtwo_ref[...]).astype(BF)
    grad = own_value + from_across(1)
    unit_two = unit[...]
    scaled = grad * vec_ref[6:7, :]
    spread = (
        scaled
        - jnp.mean(scaled, axis=1, keepdims=True)
        - unit_two * jnp.mean(scaled * unit_two, axis=1, keepdims=True)
    )
    grad_middle = cot_ref[...].astype(F32) + inverse * spread
    gmid_out[...] = grad_middle
    low = (BRANCH * grad_middle).astype(BF)
    gone_out[pl.ds(pl.multiple_of(mine * 192, 192), 192), :] = low
    share(1, gone_out)
    sums_out[0:1, :] = jnp.sum(low.astype(F32), axis=0, keepdims=True)
    sums_out[1:2, :] = jnp.sum(part(gtwo_ref, mine).astype(F32), axis=0, keepdims=True)
    sums_out[2:3, :] = jnp.sum(grad * unit_two, axis=0, keepdims=True)
    sums_out[3:4, :] = jnp.sum(grad, axis=0, keepdims=True)
    sums_out[4:5, :] = jnp.sum(gexp[...].astype(F32), axis=0, keepdims=True)
    sums_out[5:8, :] = jnp.zeros((3, D), F32)
    epart_out[...] = mm_tn(n2[...], gexp[...]).astype(BF)
    value = mm(part(act, mine), contract_ref[...]) + from_twin(2, 1)
    value = value + from_across(2)
    block_out[...] = (held[...] + BRANCH * (value + vec_ref[3:4, :])).astype(BF)
    share_across(1, gone_out)
    share_twin(1, gone_out)
    share_corner(1, gone_out)
    for i in range(3):
        for slot in range(2):
            remote(c_send_buf.at[i, slot], c_recv_buf.at[i, slot], c_send.at[i, slot], c_recv.at[i, slot], me.twin).wait_send()
        remote(x_send_buf.at[i], x_recv_buf.at[i], x_send.at[i], x_recv.at[i], me.across).wait_send()
    for i, ref in ((0, n2), (1, gone_out)):
        own = rows_of(ref, mine)
        for j in range(3):
            remote(own, own, ag_send.at[i, j], ag_recv.at[i, j], me.twin).wait_send()


def feed_forward(o, wp, expand, contract, ebias, tokens, cotangent, gtwo, vectors):
    rows = tokens.shape[0]
    block = rows * 4
    vmem = pl.BlockSpec(memory_space=pltpu.VMEM)
    dma = pltpu.SemaphoreType.DMA
    return pl.pallas_call(
        mlp_kernel,
        in_specs=[vmem] * 9,
        out_specs=[vmem] * 6,
        out_shape=[
            jax.ShapeDtypeStruct((rows, D), BF),
            jax.ShapeDtypeStruct((rows, D), F32),
            jax.ShapeDtypeStruct((block, D), BF),
            jax.ShapeDtypeStruct((D, D), BF),
            jax.ShapeDtypeStruct((D, D), BF),
            jax.ShapeDtypeStruct((8, D), F32),
        ],
        scratch_shapes=[
            pltpu.VMEM((block, 192), BF),
            pltpu.VMEM((block, D), F32),
            pltpu.VMEM((block, D), BF),
            pltpu.VMEM((block, D), BF),
            pltpu.VMEM((block, D), BF),
            pltpu.VMEM((rows, D), F32),
            pltpu.VMEM((rows, D), F32),
            pltpu.VMEM((3, 2, rows, D), BF),
            pltpu.VMEM((3, 2, rows, D), BF),
            pltpu.VMEM((3, rows, D), BF),
            pltpu.VMEM((3, rows, D), BF),
            dma((3, 2)), dma((3, 2)), dma((3,)), dma((3,)), dma((2, 3)), dma((2, 3)),
        ],
        compiler_params=pltpu.CompilerParams(collective_id=2, has_side_effects=True, vmem_limit_bytes=48 << 20),
        name="feed_forward",
    )(o, wp, expand, contract, ebias, tokens, cotangent, gtwo, vectors)


def reduce_kernel(
    levels, dn_ref, c_ref, e_ref, a_ref, p_ref, tok_ref, gmid_ref, vec_ref, sums_ref,
    tg_out, cg_out, eg_out, ag_out, pg_out, vec_out,
    far, near, keep, x_out, x_in, y_out, y_in, d_out, d_in,
    yc, ye, ya, yp, zc_out, ze_out, za_out, zp_out, zc_in, ze_in, za_in, zp_in, v_out, v_in, e_move, a_move,
    far_send, far_recv, near_sem, x_send, x_recv, y_send, y_recv, d_send, d_recv,
    gy_send, gy_recv, gz_send, gz_recv, m_send, m_recv, u_send, u_recv, w_send, w_recv, b_send, b_recv, t_send, t_recv,
    v_send, v_recv,
):
    me = Place()
    z, side, mine = me.level, me.side, me.part
    top = levels - 1
    barrier = pltpu.get_barrier_semaphore()
    for device in (me.twin, me.across, me.corner, me.beside):
        signal(barrier, device)
    for step in range(1, levels):
        signal(barrier, me.at(level=(z + step) % levels))
    pl.semaphore_wait(barrier, levels + 3)
    below, above = me.at(level=z - 1), me.at(level=z + 1)

    def corner_of(ref, level, across):
        return ref.at[pl.ds(pl.multiple_of(level * 48, 48), 48), pl.ds(pl.multiple_of(across * 384, 128), 384)]

    grads_y = ((c_ref, yc), (e_ref, ye), (a_ref, ya))

    def grad_y(level, act):
        for i, (own, got) in enumerate(grads_y):
            act(remote(own.at[level * 2 + 1 - side], got.at[level], gy_send.at[level, i], gy_recv.at[level, i], me.beside))
        act(remote(corner_of(p_ref, level, 1 - side), yp.at[level], gy_send.at[level, 3], gy_recv.at[level, 3], me.beside))

    start = lambda copy: copy.start()
    wait_recv = lambda copy: copy.wait_recv()
    wait_send = lambda copy: copy.wait_send()

    def each_step(step, act):
        down = step - (top - z)
        up = top - (step - z)

        @pl.when((down >= 0) & (down < z))
        def _():
            act(down, 0)

        @pl.when((up <= top) & (up > z))
        def _():
            act(up, 1)

    for step in range(levels - 1):
        each_step(step, lambda level, way: grad_y(level, start))
    grad_y(z, start)

    def dn_piece(level, across, half, core):
        return dn_ref.at[(level * 2 + across) * 4 + half * 2 + core]

    for level in range(levels):

        @pl.when(level <= z)
        def _():
            for across in range(2):
                for half in range(2):
                    remote(
                        dn_piece(level, across, half, 1 - me.core), far.at[level, across, half],
                        far_send.at[level, across, half], far_recv.at[level, across, half], me.twin,
                    ).start()
                    pltpu.make_async_copy(
                        dn_piece(level, across, half, me.core), near.at[level, across, half], near_sem.at[level, across, half]
                    ).start()

    for level in range(levels):

        @pl.when(level <= z)
        def _():
            for across in range(2):
                for half in range(2):
                    remote(
                        dn_piece(level, across, half, me.core), far.at[level, across, half],
                        far_send.at[level, across, half], far_recv.at[level, across, half], me.twin,
                    ).wait_recv()
                    pltpu.make_async_copy(
                        dn_piece(level, across, half, me.core), near.at[level, across, half], near_sem.at[level, across, half]
                    ).wait()
                other = 1 - me.half
                x_out[level, across] = (
                    near[level, across, other].astype(F32) + far[level, across, other].astype(F32)
                ).astype(BF)
                remote(
                    x_out.at[level, across], x_in.at[level, across], x_send.at[level, across], x_recv.at[level, across], me.across
                ).start()
                keep[level, across] = near[level, across, me.half].astype(F32) + far[level, across, me.half].astype(F32)

    def dn_across(level):
        def take(across):
            remote(
                x_out.at[level, across], x_in.at[level, across], x_send.at[level, across], x_recv.at[level, across], me.across
            ).wait_recv()
            return keep[level, across] + x_in[level, across].astype(F32)

        y_out[level] = take(1 - side).astype(BF)
        remote(y_out.at[level], y_in.at[level], y_send.at[level], y_recv.at[level], me.beside).start()
        keep[level, side] = take(side)

    def dn_sum(level):
        remote(y_out.at[level], y_in.at[level], y_send.at[level], y_recv.at[level], me.beside).wait_recv()
        return keep[level, side] + y_in[level].astype(F32)

    def dn_down(level):
        return remote(d_out.at[level], d_in.at[level], d_send.at[level], d_recv.at[level], below)

    def dn_step(step):
        level = step - (top - z)

        @pl.when((level >= 0) & (level < z))
        def _():
            keep[level, side] = dn_sum(level)

            @pl.when(z < top)
            def _():
                dn_down(level).wait_recv()
                keep[level, side] += d_in[level].astype(F32)

            d_out[level] = keep[level, side].astype(BF)
            dn_down(level).start()

    grads_z = ((c_ref, yc, zc_out, zc_in), (e_ref, ye, ze_out, ze_in), (a_ref, ya, za_out, za_in))

    def grad_z(level, way, act):
        device = below if way == 0 else above
        for i, (own, got, out, come) in enumerate(grads_z):
            act(remote(out.at[level], come.at[way, level], gz_send.at[level, i], gz_recv.at[way, level, i], device))
        act(remote(zp_out.at[level], zp_in.at[way, level], gz_send.at[level, 3], gz_recv.at[way, level, 3], device))

    def own_corner(level):
        return p_ref[pl.ds(pl.multiple_of(level * 48, 48), 48), pl.ds(pl.multiple_of(side * 384, 128), 384)]

    def grad_step(step):
        def act(level, way):
            grad_y(level, wait_recv)
            inner = (z < top) if way == 0 else (z > 0)

            @pl.when(inner)
            def _():
                grad_z(level, way, wait_recv)
                for own, got, out, come in grads_z:
                    out[level] = (
                        own[level * 2 + side].astype(F32) + got[level].astype(F32) + come[way, level].astype(F32)
                    ).astype(BF)
                zp_out[level] = (own_corner(level).astype(F32) + yp[level].astype(F32) + zp_in[way, level].astype(F32)).astype(BF)

            @pl.when(jnp.logical_not(inner))
            def _():
                for own, got, out, come in grads_z:
                    out[level] = (own[level * 2 + side].astype(F32) + got[level].astype(F32)).astype(BF)
                zp_out[level] = (own_corner(level).astype(F32) + yp[level].astype(F32)).astype(BF)

            grad_z(level, way, start)

        each_step(step, act)

    def done_c(level, across):
        return cg_out.at[level * 2 + across]

    def done_p(level, across):
        return corner_of(pg_out, level, across)

    def up_copies(distance):
        level = z - distance
        return (
            remote(done_c(level, side), done_c(level, side), u_send.at[0, distance, 0], u_recv.at[0, distance, 0], above),
            remote(done_p(level, side), done_p(level, side), u_send.at[0, distance, 1], u_recv.at[0, distance, 1], above),
        )

    def down_copies(distance):
        level = z + distance
        return (
            remote(done_c(level, side), done_c(level, side), u_send.at[1, distance, 0], u_recv.at[1, distance, 0], below),
            remote(done_p(level, side), done_p(level, side), u_send.at[1, distance, 1], u_recv.at[1, distance, 1], below),
        )

    def side_copies(level):
        return (
            remote(done_c(level, side), done_c(level, side), w_send.at[level, 0], w_recv.at[level, 0], me.beside),
            remote(done_p(level, side), done_p(level, side), w_send.at[level, 1], w_recv.at[level, 1], me.beside),
        )

    def side_takes(level):
        other = 1 - side
        return (
            remote(done_c(level, other), done_c(level, other), w_send.at[level, 0], w_recv.at[level, 0], me.beside),
            remote(done_p(level, other), done_p(level, other), w_send.at[level, 1], w_recv.at[level, 1], me.beside),
        )

    keeper = (z // 2, z % 2)

    def move_copies():
        device = me.at(half=z // 2, core=z % 2)
        return (
            remote(e_move, eg_out.at[side, mine], m_send.at[0], m_recv.at[mine, 0], device),
            remote(a_move, ag_out.at[side, mine], m_send.at[1], m_recv.at[mine, 1], device),
        )

    def move_takes(origin):
        return (
            remote(eg_out.at[side, origin], eg_out.at[side, origin], m_send.at[0], m_recv.at[origin, 0], me.twin),
            remote(ag_out.at[side, origin], ag_out.at[side, origin], m_send.at[1], m_recv.at[origin, 1], me.twin),
        )

    def row_copies(way):
        device = below if way == 0 else above
        return (
            remote(eg_out.at[side], eg_out.at[side], b_send.at[way, 0], b_recv.at[way, 0], device),
            remote(ag_out.at[side], ag_out.at[side], b_send.at[way, 1], b_recv.at[way, 1], device),
        )

    def row_side(across):
        return (
            remote(eg_out.at[across], eg_out.at[across], t_send.at[0], t_recv.at[0], me.beside),
            remote(ag_out.at[across], ag_out.at[across], t_send.at[1], t_recv.at[1], me.beside),
        )

    def all_of(copies, act):
        for copy in copies:
            act(copy)

    def grad_final():
        grad_y(z, wait_recv)
        kept = (cg_out.at[z * 2 + side], e_move, a_move)

        def add(ways):
            for (own, got, out, come), target in zip(grads_z, kept):
                total = own[z * 2 + side].astype(F32) + got[z].astype(F32)
                for way in ways:
                    total = total + come[way, z].astype(F32)
                target[...] = total.astype(BF)
            total = own_corner(z).astype(F32) + yp[z].astype(F32)
            for way in ways:
                total = total + zp_in[way, z].astype(F32)
            done_p(z, side)[...] = total.astype(BF)

        @pl.when(z < top)
        def _():
            grad_z(z, 0, wait_recv)

        @pl.when(z > 0)
        def _():
            grad_z(z, 1, wait_recv)

        @pl.when(z == 0)
        def _():
            add((0,))

        @pl.when(z == top)
        def _():
            add((1,))

        @pl.when((z > 0) & (z < top))
        def _():
            add((0, 1))

        @pl.when(mine != z)
        def _():
            all_of(move_copies(), start)

        @pl.when(mine == z)
        def _():
            eg_out[side, mine] = e_move[...]
            ag_out[side, mine] = a_move[...]

        pass_on(0, 0)

    def pass_on(distance, way):
        if way in (0, 1):

            @pl.when(z < top)
            def _():
                all_of(up_copies(distance), start)

        if way in (0, 2):

            @pl.when(z > 0)
            def _():
                all_of(down_copies(distance), start)

        all_of(side_copies(z if way == 0 else z - distance if way == 1 else z + distance), start)

    def spread_rows():
        @pl.when(mine == z)
        def _():
            for origin in range(4):

                @pl.when(origin != mine)
                def _():
                    all_of(move_takes(origin), wait_recv)

        @pl.when(mine > z)
        def _():
            all_of(row_copies(0), wait_recv)

        @pl.when(mine < z)
        def _():
            all_of(row_copies(1), wait_recv)

        @pl.when((mine >= z) & (z > 0))
        def _():
            all_of(row_copies(0), start)

        @pl.when((mine <= z) & (z < top))
        def _():
            all_of(row_copies(1), start)

        all_of(row_side(side), start)

    for step in range(levels + 1):
        if step < levels - 1:
            grad_step(step)
        elif step == levels - 1:
            grad_final()
        if step < levels:

            @pl.when(step <= z)
            def _():
                dn_across(step)

        if step >= 1:
            dn_step(step - 1)

    spread_rows()

    def arrivals(distance):
        @pl.when(z - distance >= 0)
        def _():
            level = z - distance
            all_of(
                (
                    remote(done_c(level, side), done_c(level, side), u_send.at[0, distance - 1, 0], u_recv.at[0, distance - 1, 0], me.twin),
                    remote(done_p(level, side), done_p(level, side), u_send.at[0, distance - 1, 1], u_recv.at[0, distance - 1, 1], me.twin),
                ),
                wait_recv,
            )
            pass_on(distance, 1)

        @pl.when(z + distance <= top)
        def _():
            level = z + distance
            all_of(
                (
                    remote(done_c(level, side), done_c(level, side), u_send.at[1, distance - 1, 0], u_recv.at[1, distance - 1, 0], me.twin),
                    remote(done_p(level, side), done_p(level, side), u_send.at[1, distance - 1, 1], u_recv.at[1, distance - 1, 1], me.twin),
                ),
                wait_recv,
            )
            pass_on(distance, 2)

    arrivals(1)

    grad = dn_sum(z)

    @pl.when(z < top)
    def _():
        dn_down(z).wait_recv()

    keep[0, 0] = grad

    @pl.when(z < top)
    def _():
        keep[0, 0] += d_in[z].astype(F32)

    grad = keep[0, 0]
    gain = vec_ref[4:5, :]
    out, unit, inverse = layer_norm(tok_ref[...].astype(F32), gain, vec_ref[5:6, :])
    scaled = grad * gain
    spread = (
        scaled - jnp.mean(scaled, axis=1, keepdims=True) - unit * jnp.mean(scaled * unit, axis=1, keepdims=True)
    )
    tg_out[...] = (gmid_ref[...] + inverse * spread).astype(BF)
    v_out[0] = sums_ref[...]
    v_out[0, 4:5, :] = jnp.sum(grad * unit, axis=0, keepdims=True)
    v_out[0, 5:6, :] = jnp.sum(grad, axis=0, keepdims=True)

    for i, device in enumerate((me.twin, me.across, me.beside)):
        copy = remote(v_out.at[i], v_in.at[i], v_send.at[i], v_recv.at[i], device)
        copy.start()
        copy.wait_recv()
        v_out[i + 1] = v_out[i] + v_in[i]
    v_in[3 + z] = v_out[3]
    for step in range(1, levels):
        remote(v_out.at[3], v_in.at[3 + z], v_send.at[2 + step], v_recv.at[3 + z], me.at(level=(z + step) % levels)).start()

    for distance in range(2, levels):
        arrivals(distance)
    for step in range(1, levels):
        level = (z + step) % levels
        remote(v_out.at[3], v_in.at[3 + level], v_send.at[2 + step], v_recv.at[3 + level], me.twin).wait_recv()
    total = v_in[3]
    for level in range(1, levels):
        total = total + v_in[3 + level]
    vec_out[...] = total

    for level in range(levels):
        all_of(side_takes(level), wait_recv)
    all_of(row_side(1 - side), wait_recv)
    for level in range(levels):
        grad_y(level, wait_send)

        @pl.when(level != z)
        def _():
            for i, (own, got, out, come) in enumerate(grads_z):
                remote(out.at[level], come.at[0, level], gz_send.at[level, i], gz_recv.at[0, level, i], me.twin).wait_send()
            remote(zp_out.at[level], zp_in.at[0, level], gz_send.at[level, 3], gz_recv.at[0, level, 3], me.twin).wait_send()

        all_of(side_copies(level), wait_send)

        @pl.when(level <= z)
        def _():
            for across in range(2):
                for half in range(2):
                    remote(
                        dn_piece(level, across, half, me.core), far.at[level, across, half],
                        far_send.at[level, across, half], far_recv.at[level, across, half], me.twin,
                    ).wait_send()
                remote(
                    x_out.at[level, across], x_in.at[level, across], x_send.at[level, across], x_recv.at[level, across], me.across
                ).wait_send()
            remote(y_out.at[level], y_in.at[level], y_send.at[level], y_recv.at[level], me.beside).wait_send()

        @pl.when(level < z)
        def _():
            dn_down(level).wait_send()

    for distance in range(levels):

        @pl.when((z - distance >= 0) & (z < top))
        def _():
            all_of(up_copies(distance), wait_send)

        @pl.when((z + distance <= top) & (z > 0))
        def _():
            all_of(down_copies(distance), wait_send)

    @pl.when(mine != z)
    def _():
        all_of(move_copies(), wait_send)

    @pl.when((mine >= z) & (z > 0))
    def _():
        all_of(row_copies(0), wait_send)

    @pl.when((mine <= z) & (z < top))
    def _():
        all_of(row_copies(1), wait_send)

    all_of(row_side(side), wait_send)
    for i in range(2 + levels):
        remote(v_out.at[0], v_in.at[0], v_send.at[i], v_recv.at[0], me.twin).wait_send()


def reduce_all(dn, contract, expand, attend, project, tokens, grad_middle, vectors, sums):
    levels = lax.axis_size("ctx") // 2
    rows = tokens.shape[0]
    vmem = pl.BlockSpec(memory_space=pltpu.VMEM)
    anywhere = pl.BlockSpec(memory_space=pl.ANY)
    dma = pltpu.SemaphoreType.DMA
    n = levels

    def buf(*shape):
        return pltpu.VMEM(shape, BF)

    return pl.pallas_call(
        functools.partial(reduce_kernel, levels),
        in_specs=[anywhere] + [vmem] * 8,
        out_specs=[vmem] * 6,
        out_shape=[
            jax.ShapeDtypeStruct((rows, D), BF),
            jax.ShapeDtypeStruct((2 * n, 96, D), BF),
            jax.ShapeDtypeStruct((2, 4, 96, D), BF),
            jax.ShapeDtypeStruct((2, 4, 96, 576), BF),
            jax.ShapeDtypeStruct((192, D), BF),
            jax.ShapeDtypeStruct((16, D), F32),
        ],
        scratch_shapes=[
            buf(n, 2, 2, rows, D), buf(n, 2, 2, rows, D), pltpu.VMEM((n, 2, rows, D), F32),
            buf(n, 2, rows, D), buf(n, 2, rows, D), buf(n, rows, D), buf(n, rows, D), buf(n, rows, D), buf(n, rows, D),
            buf(n, 96, D), buf(n, 96, D), buf(n, 96, 576), buf(n, 48, 384),
            buf(n, 96, D), buf(n, 96, D), buf(n, 96, 576), buf(n, 48, 384),
            buf(2, n, 96, D), buf(2, n, 96, D), buf(2, n, 96, 576), buf(2, n, 48, 384),
            pltpu.VMEM((4, 16, D), F32), pltpu.VMEM((3 + n, 16, D), F32), buf(96, D), buf(96, 576),
            dma((n, 2, 2)), dma((n, 2, 2)), dma((n, 2, 2)), dma((n, 2)), dma((n, 2)), dma((n,)), dma((n,)), dma((n,)), dma((n,)),
            dma((n, 4)), dma((n, 4)), dma((n, 4)), dma((2, n, 4)),
            dma((2,)), dma((4, 2)), dma((2, n, 2)), dma((2, n, 2)), dma((n, 2)), dma((n, 2)),
            dma((2, 2)), dma((2, 2)), dma((2,)), dma((2,)),
            dma((2 + n,)), dma((3 + n,)),
        ],
        compiler_params=pltpu.CompilerParams(collective_id=3, has_side_effects=True, vmem_limit_bytes=56 << 20),
        name="reduce_all",
    )(dn, contract, expand, attend, project, tokens, grad_middle, vectors, sums)


def normalize(rows_in, gain, shift):
    mean = jnp.mean(rows_in, axis=1, keepdims=True)
    centered = rows_in - mean
    inverse = lax.rsqrt(jnp.mean(centered * centered, axis=1, keepdims=True) + EPS)
    unit = centered * inverse
    return (unit * gain + shift, unit, inverse)


def normalize_back(incoming, unit, inverse, gain):
    scaled = incoming * gain
    spread = (
        scaled
        - jnp.mean(scaled, axis=1, keepdims=True)
        - unit * jnp.mean(scaled * unit, axis=1, keepdims=True)
    )
    return (inverse * spread, jnp.sum(incoming * unit, axis=0), jnp.sum(incoming, axis=0))


def first_position(places, starts):
    below = starts[None, :] <= places[:, None]
    return jnp.max(jnp.where(below, starts[None, :], 0), axis=1)


def combine_plain(dn, contract_part, expand_part, attend_part, project_part, tokens, grad_middle, gain_one, mlp_sums, sums):
    both = ("ctx", "fsdp")
    rows = tokens.shape[0]
    ways = lax.axis_size("fsdp")
    part = lax.axis_index("fsdp")
    grad_normed = lax.psum_scatter(dn.astype(F32), both, scatter_dimension=0, tiled=True)
    shift = jnp.zeros_like(gain_one)
    normed, unit_one, inverse_one = normalize(tokens.astype(F32), gain_one, shift)
    first_part, gainone_grad, shiftone_grad = normalize_back(grad_normed, unit_one, inverse_one, gain_one)
    tokens_grad = (grad_middle + first_part).astype(BF)

    def summed(array_in):
        return lax.psum(array_in.astype(BF), "ctx").astype(F32)

    contract_grad = summed(contract_part)
    project_grad = summed(project_part)
    expand_grad = lax.all_to_all(summed(expand_part).reshape(ways, rows, D), "fsdp", 0, 0)
    expand_grad = expand_grad.transpose(1, 0, 2).reshape(rows, ways * D)
    attend_grad = lax.all_to_all(summed(attend_part).reshape(ways, rows, 576), "fsdp", 0, 0)
    attend_grad = attend_grad.reshape(ways, rows, 3, 192).transpose(1, 2, 0, 3).reshape(rows, 3 * D)
    spread = lax.dynamic_update_slice(jnp.zeros((2, D), F32), sums[:2], (0, part * 192))
    hidden = lax.dynamic_update_slice(jnp.zeros((4, D), F32), mlp_sums[4:5], (part, 0))
    vectors = jnp.concatenate([
        spread, mlp_sums[0:2], gainone_grad[None], shiftone_grad[None], mlp_sums[2:4], hidden, jnp.zeros((4, D), F32)
    ])
    return tokens_grad, contract_grad, expand_grad, attend_grad, project_grad, lax.psum(vectors, both)


def combine(dn, contract_part, expand_part, attend_part, project_part, tokens, grad_middle, vectors, mlp_sums, sums):
    rows = tokens.shape[0]
    ways = lax.axis_size("fsdp")
    part = lax.axis_index("fsdp")
    if lax.axis_size("ctx") != 8:
        return combine_plain(
            dn, contract_part, expand_part, attend_part, project_part, tokens, grad_middle, vectors[4], mlp_sums, sums
        )
    spread = lax.dynamic_update_slice(jnp.zeros((2, D), F32), sums[:2], (0, part * 192))
    hidden = lax.dynamic_update_slice(jnp.zeros((4, D), F32), mlp_sums[4:5], (part, 0))
    local = jnp.concatenate([spread, mlp_sums[0:2], jnp.zeros((2, D), F32), mlp_sums[2:4], hidden, jnp.zeros((4, D), F32)])
    tokens_grad, c, e, a, p, totals = reduce_all(
        dn.reshape(-1, rows, D), contract_part.reshape(8, 96, D), expand_part.reshape(8, 96, D),
        attend_part.astype(BF).reshape(8, 96, 576), project_part.astype(BF), tokens, grad_middle, vectors, local,
    )
    expand_grad = e.transpose(0, 2, 1, 3).reshape(rows, ways * D).astype(F32)
    attend_grad = a.reshape(2, ways, 96, 3, 192).transpose(0, 2, 3, 1, 4).reshape(rows, 3 * D).astype(F32)
    return tokens_grad, c.reshape(D, D).astype(F32), expand_grad, attend_grad, p.astype(F32), totals


def per_device(
    tokens, document_starts, attend_weight, attend_bias, project_weight, project_bias,
    expand_weight, expand_bias, contract_weight, contract_bias,
    gain_first, shift_first, gain_second, shift_second, cotangent,
):
    both = ("ctx", "fsdp")
    rows = tokens.shape[0]
    ways = lax.axis_size("fsdp")
    block = rows * ways
    ctx = lax.axis_index("ctx")
    part = lax.axis_index("fsdp")

    def whole(array_in):
        return lax.all_gather(array_in, "fsdp", axis=0, tiled=True)

    own_vectors = jnp.stack([project_bias, contract_bias, gain_first, shift_first, gain_second, shift_second])
    vectors = lax.dynamic_update_slice(jnp.zeros((6, D), F32), own_vectors.astype(F32), (0, part * rows))
    biases = lax.dynamic_update_slice(jnp.zeros((2 * D,), F32), attend_bias.astype(F32), (part * 2 * rows,))
    vectors = jnp.concatenate([biases.reshape(2, D), vectors])
    attend_cols = attend_weight.reshape(rows, 3, ways, 192).transpose(2, 0, 1, 3).reshape(ways, rows, 576)
    normed_all, attend_cols, expand_cols, g2, vectors = gather_inputs(
        tokens, vectors, attend_cols, expand_weight, cotangent
    )
    project_b, contract_b, gain_one, shift_one, gain_two, shift_two = [vectors[i] for i in range(2, 8)]
    wq, wk, wv = attend_cols[:, :192], attend_cols[:, 192:384], attend_cols[:, 384:]
    bias = lax.dynamic_slice(vectors, (0, part * 192), (2, 192))

    own = lax.dynamic_slice(normed_all, (ctx * block, 0), (block, D))
    places = ctx * block + jnp.arange(block, dtype=jnp.int32)
    begins = first_position(places, document_starts)
    where = jnp.stack([ctx, begins[0], begins[-1]]).astype(jnp.int32)
    begins_row = begins.reshape(1, block)
    q, k, v, o, lse = attend_forward(where, normed_all, own, wq, wk, wv, bias, begins_row)
    block_output, grad_middle, g1, contract_part, expand_part, mlp_sums = feed_forward(
        o, project_weight, expand_cols, contract_weight, expand_bias.astype(F32).reshape(1, D), tokens, cotangent, g2, vectors
    )
    dn, attend_t, project_part, sums = attend_backward(
        where, normed_all, k, v, own, q, o, lse, g1, project_weight, wq, wk, wv, begins_row
    )
    tokens_grad, contract_grad, expand_grad, attend_grad, project_grad, totals = combine(
        dn, contract_part, expand_part, attend_t.T, project_part, tokens, grad_middle, vectors, mlp_sums, sums
    )
    attbias = lax.dynamic_slice(totals[:2].reshape(-1), (part * 2 * rows,), (2 * rows,))
    mine = lax.dynamic_slice(totals, (2, part * rows), (6, rows))
    expbias = lax.dynamic_slice(totals, (8 + part, 0), (1, D)).reshape(D)
    return (
        block_output, tokens_grad, attend_grad, attbias, project_grad, mine[0], expand_grad, expbias,
        contract_grad, mine[1], mine[2], mine[3], mine[4], mine[5],
    )


def solution(mesh):
    tok, row, vec = P(("ctx", "fsdp"), None), P("fsdp", None), P("fsdp")
    in_specs = (tok, P(), row, vec, row, vec, row, vec, row, vec, vec, vec, vec, vec, tok)
    out_specs = (tok, tok, row, vec, row, vec, row, vec, row, vec, vec, vec, vec, vec)
    return jax.shard_map(per_device, mesh=mesh, in_specs=in_specs, out_specs=out_specs, check_vma=False)
```

```python
import functools
import jax
import jax.numpy as jnp
from jax import lax
from jax.experimental import pallas as pl
from jax.experimental.pallas import tpu as pltpu
from jax.sharding import PartitionSpec as P

D = 768
H = 12
HD = 64
EPS = 1e-05
SCALE = 0.125
BRANCH = 48.0 ** (-0.5)
NEG = -1e30
SUB = 768
STRIP = 256
QS = STRIP
LEAD = 4
BACK_LEAD = 2
BF = jnp.bfloat16
F32 = jnp.float32


def mm(a, b):
    return jnp.dot(a, b, preferred_element_type=F32)


def mm_nt(a, b):
    return lax.dot_general(a, b, (((1,), (1,)), ((), ())), preferred_element_type=F32)


def mm_tn(a, b):
    return lax.dot_general(a, b, (((0,), (0,)), ((), ())), preferred_element_type=F32)


def head_lanes(head):
    return slice(0, 128) if head < 2 else slice(128, 192)


def fill_masked_columns(target, flipped):
    zero = jnp.zeros((HD, flipped.shape[1]), BF)
    target[0, 0:HD, :] = flipped[0:HD]
    target[0, HD : 2 * HD, :] = zero
    target[1, 0:HD, :] = zero
    target[1, HD : 2 * HD, :] = flipped[HD : 2 * HD]
    target[2, 0:HD, :] = flipped[2 * HD : 3 * HD]


def masked_rows(array_in, head):
    if head == 2:
        return array_in[:, 128:192]
    pair = array_in[:, 0:128]
    lane = lax.broadcasted_iota(jnp.int32, pair.shape, 1)
    return jnp.where((lane < HD) if head == 0 else (lane >= HD), pair, jnp.zeros_like(pair))


def allowed_pairs(first_key, first_query, begins, shape):
    key_places = first_key + lax.broadcasted_iota(jnp.int32, shape, 0)
    query_places = first_query + lax.broadcasted_iota(jnp.int32, shape, 1)
    return (key_places <= query_places) & (key_places >= begins)


def attend_forward_kernel(
    where_ref, rows_ref, own_ref, wq_ref, wk_ref, wv_ref, bias_ref, begins_ref,
    q_out, k_out, v_out, o_out, lse_out,
    qm, vt, peak, total, acc,
):
    turn = pl.program_id(0)
    block = own_ref.shape[0]
    mine, begin_low, begin_high = where_ref[0], where_ref[1], where_ref[2]
    first_query = mine * block
    needed = (turn <= mine) & ((turn + 1) * block - 1 >= begin_low)

    @pl.when(turn == 0)
    def _():
        query = (mm(own_ref[...], wq_ref[...]) + bias_ref[0:1, :]).astype(BF)
        q_out[...] = query
        fill_masked_columns(qm, (query.astype(F32) * SCALE).T.astype(BF))
        peak[...] = jnp.full(peak.shape, NEG, F32)
        total[...] = jnp.zeros(total.shape, F32)
        acc[...] = jnp.zeros(acc.shape, F32)

    @pl.when(needed)
    def _():
        rows = rows_ref[...]
        k_out[...] = mm(rows, wk_ref[...]).astype(BF)
        value = (mm(rows, wv_ref[...]) + bias_ref[1:2, :]).astype(BF)
        v_out[...] = value
        vt[...] = value.astype(F32).T.astype(BF)

        def one(step, masked):
            at = pl.ds(pl.multiple_of(step * SUB, SUB), SUB)
            first_key = turn * block + step * SUB
            if masked:
                allowed = allowed_pairs(first_key, first_query, begins_ref[...], (SUB, block))
            strips = [(head, strip) for head in range(3) for strip in range(block // QS)]

            def scored(head, strip):
                depth = 128 if head < 2 else HD
                return mm(k_out[at, head_lanes(head)], qm[head, 0:depth, strip * QS : strip * QS + QS])

            ahead = [scored(*strips[i]) for i in range(LEAD)]
            for i, (head, strip) in enumerate(strips):
                scores = ahead.pop(0)
                if i + LEAD < len(strips):
                    ahead.append(scored(*strips[i + LEAD]))
                lanes = slice(strip * QS, strip * QS + QS)
                if masked:
                    scores = jnp.where(allowed[:, lanes], scores, NEG)
                old = peak[head : head + 1, lanes]
                new = jnp.maximum(old, jnp.max(scores, axis=0, keepdims=True))
                weights = jnp.exp(scores - new)
                if masked:
                    weights = jnp.where(allowed[:, lanes], weights, 0.0)
                factor = jnp.exp(old - new)
                peak[head : head + 1, lanes] = new
                total[head : head + 1, lanes] = total[head : head + 1, lanes] * factor + jnp.sum(
                    weights, axis=0, keepdims=True
                )
                part = slice(head * HD, head * HD + HD)
                acc[part, lanes] = acc[part, lanes] * factor + mm(vt[part, at], weights.astype(BF))

        @pl.loop(0, block // SUB)
        def _(step):
            first_key = turn * block + step * SUB
            inner = (first_key + SUB - 1 <= first_query) & (first_key >= begin_high)
            touched = first_key + SUB - 1 >= begin_low

            @pl.when(inner)
            def _():
                one(step, False)

            @pl.when(jnp.logical_not(inner) & touched)
            def _():
                one(step, True)

    @pl.when(turn == mine)
    def _():
        for head in range(3):
            part = slice(head * HD, head * HD + HD)
            o_out[part, :] = acc[part, :] / total[head : head + 1, :]
        lse_out[...] = peak[...] + jnp.log(jnp.maximum(total[...], 1e-30))


def attend_forward(where, rows_all, own, wq, wk, wv, bias, begins):
    block = own.shape[0]
    count = rows_all.shape[0] // block

    def seen(turn, where_ref):
        return (jnp.minimum(turn, where_ref[0]), 0)

    def fixed(turn, where_ref):
        return (0, 0)

    return pl.pallas_call(
        attend_forward_kernel,
        grid_spec=pltpu.PrefetchScalarGridSpec(
            num_scalar_prefetch=1,
            grid=(count,),
            in_specs=[
                pl.BlockSpec((block, D), seen),
                pl.BlockSpec((block, D), fixed),
                pl.BlockSpec((D, 192), fixed),
                pl.BlockSpec((D, 192), fixed),
                pl.BlockSpec((D, 192), fixed),
                pl.BlockSpec((2, 192), fixed),
                pl.BlockSpec((1, block), fixed),
            ],
            out_specs=[
                pl.BlockSpec((block, 192), fixed),
                pl.BlockSpec((block, 192), seen),
                pl.BlockSpec((block, 192), seen),
                pl.BlockSpec((192, block), fixed),
                pl.BlockSpec((8, block), fixed),
            ],
            scratch_shapes=[
                pltpu.VMEM((3, 128, block), BF),
                pltpu.VMEM((192, block), BF),
                pltpu.VMEM((8, block), F32),
                pltpu.VMEM((8, block), F32),
                pltpu.VMEM((192, block), F32),
            ],
        ),
        out_shape=[
            jax.ShapeDtypeStruct((block, 192), BF),
            jax.ShapeDtypeStruct((block * count, 192), BF),
            jax.ShapeDtypeStruct((block * count, 192), BF),
            jax.ShapeDtypeStruct((192, block), F32),
            jax.ShapeDtypeStruct((8, block), F32),
        ],
        compiler_params=pltpu.CompilerParams(vmem_limit_bytes=48 << 20),
        name="attend_forward",
    )(where, rows_all, own, wq, wk, wv, bias, begins)


def attend_backward_kernel(
    where_ref, rows_ref, k_ref, v_ref, own_ref, q_ref, o_ref, lse_ref, g_ref, wp_ref,
    wq_ref, wk_ref, wv_ref, begins_ref,
    dn_out, grad_out, proj_out, sums_out,
    qm, dm, qn, dn, delta, dqt, kt, dk, dv,
):
    turn = pl.program_id(0)
    block = own_ref.shape[0]
    mine, begin_low, begin_high = where_ref[0], where_ref[1], where_ref[2]
    first_query = mine * block
    needed = (turn <= mine) & ((turn + 1) * block - 1 >= begin_low)

    @pl.when(turn == 0)
    def _():
        grads = g_ref[...]
        exact = o_ref[...]
        proj_out[...] = mm(exact.astype(BF), grads)
        outer = mm_nt(grads, wp_ref[...]).astype(BF)
        flipped = outer.astype(F32).T
        product = flipped * exact
        for head in range(3):
            delta[head : head + 1, :] = jnp.sum(
                product[head * HD : head * HD + HD], axis=0, keepdims=True
            )
        fill_masked_columns(dm, flipped.astype(BF))
        scaled = (q_ref[...].astype(F32) * SCALE)
        fill_masked_columns(qm, scaled.T.astype(BF))
        scaled = scaled.astype(BF)
        for head in range(3):
            depth = 128 if head < 2 else HD
            qn[head, :, 0:depth] = masked_rows(scaled, head)
            dn[head, :, 0:depth] = masked_rows(outer, head)
        dqt[...] = jnp.zeros(dqt.shape, F32)
        grad_out[...] = jnp.zeros(grad_out.shape, F32)
        sums_out[...] = jnp.zeros(sums_out.shape, F32)

    @pl.when(jnp.logical_not(needed))
    def _():
        dn_out[...] = jnp.zeros(dn_out.shape, BF)

    @pl.when(needed)
    def _():
        kt[...] = k_ref[...].astype(F32).T.astype(BF)
        dk[...] = jnp.zeros(dk.shape, F32)
        dv[...] = jnp.zeros(dv.shape, F32)

        def one(step, masked):
            at = pl.ds(pl.multiple_of(step * SUB, SUB), SUB)
            first_key = turn * block + step * SUB
            if masked:
                allowed = allowed_pairs(first_key, first_query, begins_ref[...], (SUB, block))
            for head in range(3):
                depth = 128 if head < 2 else HD
                lanes = head_lanes(head)
                scores = mm(k_ref[at, lanes], qm[head, 0:depth, :])
                probs = jnp.exp(scores - lse_ref[head : head + 1, :])
                if masked:
                    probs = jnp.where(allowed, probs, 0.0)
                outer = mm(v_ref[at, lanes], dm[head, 0:depth, :])
                inner = (probs * (outer - delta[head : head + 1, :])).astype(BF)
                dv[at, lanes] += mm(probs.astype(BF), dn[head, :, 0:depth])
                dk[at, lanes] += mm(inner, qn[head, :, 0:depth])
                part = slice(head * HD, head * HD + HD)
                dqt[part, :] += mm(kt[part, at], inner)

        @pl.loop(0, block // SUB)
        def _(step):
            first_key = turn * block + step * SUB
            inner = (first_key + SUB - 1 <= first_query) & (first_key >= begin_high)
            touched = first_key + SUB - 1 >= begin_low

            @pl.when(inner)
            def _():
                one(step, False)

            @pl.when(jnp.logical_not(inner) & touched)
            def _():
                one(step, True)

        rows = rows_ref[...]
        low_k = dk[...].astype(BF)
        low_v = dv[...].astype(BF)
        grad_out[192:384, :] += mm(low_k.astype(F32).T.astype(BF), rows)
        grad_out[384:576, :] += mm(low_v.astype(F32).T.astype(BF), rows)
        sums_out[1:2, :] += jnp.sum(low_v.astype(F32), axis=0, keepdims=True)
        through = mm_nt(low_k, wk_ref[...]) + mm_nt(low_v, wv_ref[...])

        @pl.when(turn < mine)
        def _():
            dn_out[...] = through.astype(BF)

        @pl.when(turn == mine)
        def _():
            flipped = dqt[...] * SCALE
            low_q = flipped.T.astype(BF)
            grad_out[0:192, :] += mm(flipped.astype(BF), own_ref[...])
            sums_out[0:1, :] += jnp.sum(low_q.astype(F32), axis=0, keepdims=True)
            dn_out[...] = (through + mm_nt(low_q, wq_ref[...])).astype(BF)


def attend_backward(where, rows_all, k, v, own, q, o, lse, g, wp, wq, wk, wv, begins):
    block = own.shape[0]
    count = rows_all.shape[0] // block

    def seen(turn, where_ref):
        return (jnp.minimum(turn, where_ref[0]), 0)

    def each(turn, where_ref):
        return (turn, 0)

    def fixed(turn, where_ref):
        return (0, 0)

    return pl.pallas_call(
        attend_backward_kernel,
        grid_spec=pltpu.PrefetchScalarGridSpec(
            num_scalar_prefetch=1,
            grid=(count,),
            in_specs=[
                pl.BlockSpec((block, D), seen),
                pl.BlockSpec((block, 192), seen),
                pl.BlockSpec((block, 192), seen),
                pl.BlockSpec((block, D), fixed),
                pl.BlockSpec((block, 192), fixed),
                pl.BlockSpec((192, block), fixed),
                pl.BlockSpec((8, block), fixed),
                pl.BlockSpec((block, D), fixed),
                pl.BlockSpec((192, D), fixed),
                pl.BlockSpec((D, 192), fixed),
                pl.BlockSpec((D, 192), fixed),
                pl.BlockSpec((D, 192), fixed),
                pl.BlockSpec((1, block), fixed),
            ],
            out_specs=[
                pl.BlockSpec((block, D), each),
                pl.BlockSpec((576, D), fixed),
                pl.BlockSpec((192, D), fixed),
                pl.BlockSpec((8, 192), fixed),
            ],
            scratch_shapes=[
                pltpu.VMEM((3, 128, block), BF),
                pltpu.VMEM((3, 128, block), BF),
                pltpu.VMEM((3, block, 128), BF),
                pltpu.VMEM((3, block, 128), BF),
                pltpu.VMEM((8, block), F32),
                pltpu.VMEM((192, block), F32),
                pltpu.VMEM((192, block), BF),
                pltpu.VMEM((block, 192), F32),
                pltpu.VMEM((block, 192), F32),
            ],
        ),
        out_shape=[
            jax.ShapeDtypeStruct((block * count, D), BF),
            jax.ShapeDtypeStruct((576, D), F32),
            jax.ShapeDtypeStruct((192, D), F32),
            jax.ShapeDtypeStruct((8, 192), F32),
        ],
        compiler_params=pltpu.CompilerParams(vmem_limit_bytes=48 << 20),
        name="attend_backward",
    )(where, rows_all, k, v, own, q, o, lse, g, wp, wq, wk, wv, begins)


MESH = pl.DeviceIdType.MESH


class Place:
    def __init__(self):
        ctx = lax.axis_index("ctx")
        part = lax.axis_index("fsdp")
        self.levels = lax.axis_size("ctx") // 2
        self.ctx, self.part = ctx, part
        self.level, self.side = ctx // 2, ctx % 2
        self.half, self.core = part // 2, part % 2

    def at(self, level=None, side=None, half=None, core=None):
        level = self.level if level is None else level
        side = self.side if side is None else side
        half = self.half if half is None else half
        core = self.core if core is None else core
        return (level * 2 + side, half * 2 + core)

    @property
    def twin(self):
        return self.at(core=1 - self.core)

    @property
    def across(self):
        return self.at(half=1 - self.half)

    @property
    def corner(self):
        return self.at(half=1 - self.half, core=1 - self.core)

    @property
    def beside(self):
        return self.at(side=1 - self.side)


def remote(source, target, send, recv, device):
    return pltpu.make_async_remote_copy(
        src_ref=source, dst_ref=target, send_sem=send, recv_sem=recv, device_id=device, device_id_type=MESH
    )


def signal(sem, device):
    pl.semaphore_signal(sem, inc=1, device_id=device, device_id_type=MESH)


def piece(ref, ctx, part):
    rows = 192
    return ref.at[pl.ds(pl.multiple_of((ctx * 4 + part) * rows, rows), rows)]


def rows_of(ref, part):
    return ref.at[pl.ds(pl.multiple_of(part * 192, 192), 192)]


def layer_norm(rows_in, gain, shift):
    mean = jnp.mean(rows_in, axis=1, keepdims=True)
    centered = rows_in - mean
    inverse = lax.rsqrt(jnp.mean(centered * centered, axis=1, keepdims=True) + EPS)
    unit = centered * inverse
    return unit * gain + shift, unit, inverse


def gather_kernel(
    levels, tok_ref, vec_ref, acol_ref, ecol_ref, cot_ref,
    all_ref, attend_ref, expand_ref, gtwo_ref, vec_out,
    normed, gtwo, vec_in,
    vec_send, vec_recv, att_send, att_recv, exp_send, exp_recv, two_send, two_recv,
    x_send, x_recv, z_send, z_recv, y_send, y_recv, core_send, core_recv, local_sem,
):
    me = Place()
    mine = me.part
    barrier = pltpu.get_barrier_semaphore()
    for device in (me.twin, me.across, me.corner, me.beside):
        signal(barrier, device)

    @pl.when(me.level > 0)
    def _():
        signal(barrier, me.at(level=me.level - 1))

    @pl.when(me.level < levels - 1)
    def _():
        signal(barrier, me.at(level=me.level + 1))

    ends = (me.level == 0).astype(jnp.int32) + (me.level == levels - 1).astype(jnp.int32)
    pl.semaphore_wait(barrier, 6 - ends)

    peers = (
        (me.twin, me.half * 2 + 1 - me.core),
        (me.across, (1 - me.half) * 2 + me.core),
        (me.corner, (1 - me.half) * 2 + 1 - me.core),
    )
    vecs = [remote(vec_ref, vec_in.at[i], vec_send.at[i], vec_recv.at[i], d) for i, (d, p) in enumerate(peers)]
    for copy in vecs:
        copy.start()
    atts = [
        remote(acol_ref.at[p], rows_of(attend_ref, mine), att_send.at[i], att_recv.at[i], d)
        for i, (d, p) in enumerate(peers)
    ]
    for copy in atts:
        copy.start()
    local = [
        pltpu.make_async_copy(acol_ref.at[mine], rows_of(attend_ref, mine), local_sem.at[0]),
        pltpu.make_async_copy(ecol_ref.at[:, pl.ds(pl.multiple_of(mine * D, D), D)], rows_of(expand_ref, mine), local_sem.at[1]),
    ]
    for copy in local:
        copy.start()
    gtwo[...] = (BRANCH * cot_ref[...].astype(F32)).astype(BF)
    for copy in vecs:
        copy.wait_recv()
    vec_out[...] = vec_ref[...] + vec_in[0] + vec_in[1] + vec_in[2]
    out, unit, inverse = layer_norm(tok_ref[...].astype(F32), vec_out[4:5, :], vec_out[5:6, :])
    normed[...] = out.astype(BF)

    def go(copy):
        copy.start()
        return copy

    ctx = me.ctx
    across = go(remote(normed, piece(all_ref, ctx, mine), x_send.at[0], x_recv.at[0], me.across))
    keep = go(pltpu.make_async_copy(normed, piece(all_ref, ctx, mine), local_sem.at[2]))
    keep_two = go(pltpu.make_async_copy(gtwo, rows_of(gtwo_ref, mine), local_sem.at[3]))
    local += [keep, keep_two]

    def spread_static(source, distance, slot):
        level = me.level - distance
        where = level * 2 + me.side
        half = me.half if slot == 0 else 1 - me.half
        part = half * 2 + me.core

        @pl.when(me.level < levels - 1)
        def _():
            remote(source, piece(all_ref, where, part), z_send.at[distance, slot], z_recv.at[distance + 1, slot], me.at(level=me.level + 1)).start()

        remote(source, piece(all_ref, where, part), y_send.at[distance, slot], y_recv.at[distance, slot], me.beside).start()
        remote(source, piece(all_ref, where, part), core_send.at[distance, 0, slot], core_recv.at[distance, 0, slot], me.twin).start()

    spread_static(normed, 0, 0)
    exps = [
        go(remote(ecol_ref.at[:, pl.ds(pl.multiple_of(p * D, D), D)], rows_of(expand_ref, mine), exp_send.at[i], exp_recv.at[i], d))
        for i, (d, p) in enumerate(peers)
    ]
    two_x = go(remote(gtwo, rows_of(gtwo_ref, mine), two_send.at[0], two_recv.at[0], me.across))
    two_c = go(remote(gtwo, rows_of(gtwo_ref, mine), two_send.at[1], two_recv.at[1], me.twin))

    other = (1 - me.half) * 2 + me.core

    def held(distance, slot, side):
        half = me.half if slot == 0 else 1 - me.half
        return piece(all_ref, (me.level - distance) * 2 + side, half * 2 + me.core)

    def take_y(distance):
        for slot in range(2):
            got = held(distance, slot, 1 - me.side)
            remote(got, got, y_send.at[distance, slot], y_recv.at[distance, slot], me.beside).wait_recv()
            remote(got, got, core_send.at[distance, 1, slot], core_recv.at[distance, 1, slot], me.twin).start()

    got = piece(all_ref, ctx, other)
    remote(normed, got, x_send.at[0], x_recv.at[0], me.across).wait_recv()
    spread_static(got, 0, 1)
    for distance in range(1, levels):

        @pl.when(me.level >= distance)
        def _():
            for slot in range(2):
                got = held(distance, slot, me.side)
                remote(got, got, z_send.at[distance, slot], z_recv.at[distance, slot], me.twin).wait_recv()
                spread_static(got, distance, slot)

        if distance == 1:
            take_y(0)
        else:

            @pl.when(me.level >= distance - 1)
            def _():
                take_y(distance - 1)

    @pl.when(me.level >= levels - 1)
    def _():
        take_y(levels - 1)

    got = rows_of(gtwo_ref, other)
    remote(gtwo, got, two_send.at[0], two_recv.at[0], me.across).wait_recv()
    two_f = go(remote(got, got, two_send.at[2], two_recv.at[2], me.twin))
    for copy in local:
        copy.wait()
    for copy in vecs:
        copy.wait_send()
    for copy in atts + exps + [two_c, two_f]:
        copy.wait()
    two_x.wait_send()
    across.wait_send()
    for distance in range(levels):

        @pl.when(me.level >= distance)
        def _():
            for slot in range(2):
                got = held(distance, slot, me.side)

                @pl.when(me.level < levels - 1)
                def _():
                    remote(got, got, z_send.at[distance, slot], z_recv.at[distance, slot], me.twin).wait_send()

                remote(got, got, y_send.at[distance, slot], y_recv.at[distance, slot], me.beside).wait_send()
                for side in range(2):
                    remote(got, got, core_send.at[distance, side, slot], core_recv.at[distance, side, slot], me.twin).wait()


def gather_inputs(tokens, vectors, attend_cols, expand_weight, cotangent):
    levels = lax.axis_size("ctx") // 2
    rows = tokens.shape[0]
    block = rows * 4
    vmem = pl.BlockSpec(memory_space=pltpu.VMEM)
    anywhere = pl.BlockSpec(memory_space=pl.ANY)
    dma = pltpu.SemaphoreType.DMA
    return pl.pallas_call(
        functools.partial(gather_kernel, levels),
        in_specs=[vmem, vmem, anywhere, anywhere, vmem],
        out_specs=[anywhere, anywhere, anywhere, anywhere, vmem],
        out_shape=[
            jax.ShapeDtypeStruct((block * levels * 2, D), BF),
            jax.ShapeDtypeStruct((D, 576), BF),
            jax.ShapeDtypeStruct((D, D), BF),
            jax.ShapeDtypeStruct((block, D), BF),
            jax.ShapeDtypeStruct((8, D), F32),
        ],
        scratch_shapes=[
            pltpu.VMEM((rows, D), BF),
            pltpu.VMEM((rows, D), BF),
            pltpu.VMEM((3, 8, D), F32),
            dma((3,)), dma((3,)), dma((3,)), dma((3,)), dma((3,)), dma((3,)), dma((3,)), dma((3,)),
            dma((1,)), dma((1,)),
            dma((levels, 2)), dma((levels + 1, 2)),
            dma((levels, 2)), dma((levels, 2)),
            dma((levels, 2, 2)), dma((levels, 2, 2)),
            dma((4,)),
        ],
        compiler_params=pltpu.CompilerParams(collective_id=1, has_side_effects=True, vmem_limit_bytes=16 << 20),
        name="gather_inputs",
    )(tokens, vectors, attend_cols, expand_weight, cotangent)


def begins_of(starts_ref, first, count):
    places = first + lax.broadcasted_iota(jnp.int32, (1, count), 1)
    begins = jnp.zeros((1, count), jnp.int32)
    for document in range(8):
        start = starts_ref[document]
        begins = jnp.where(places >= start, jnp.maximum(begins, start), begins)
    return begins


def gather_attend_kernel(
    levels, starts_ref, tok_ref, vec_ref, aw_ref, ew_ref, cot_ref,
    all_ref, attend_ref, expand_ref, gtwo_ref, vec_out, q_out, k_out, v_out, o_out, lse_out,
    staged, vec_in, begins, qm, vt, acc, peak, total,
    vec_send, vec_recv, att_send, att_recv, exp_send, exp_recv, two_send, two_recv,
    x_send, x_recv, z_send, z_recv, y_send, y_recv, core_send, core_recv, local_sem,
):
    me = Place()
    mine, z, side = me.part, me.level, me.side
    top = levels - 1
    block = gtwo_ref.shape[0]
    barrier = pltpu.get_barrier_semaphore()
    for device in (me.twin, me.across, me.corner, me.beside):
        signal(barrier, device)

    @pl.when(z > 0)
    def _():
        signal(barrier, me.at(level=z - 1))

    @pl.when(z < top)
    def _():
        signal(barrier, me.at(level=z + 1))

    for part in range(4):
        for kind in range(3):
            staged[part, :, kind * 192 : kind * 192 + 192] = aw_ref[:, kind * D + part * 192 : kind * D + part * 192 + 192]
    ends = (z == 0).astype(jnp.int32) + (z == top).astype(jnp.int32)
    pl.semaphore_wait(barrier, 6 - ends)

    peers = (
        (me.twin, me.half * 2 + 1 - me.core),
        (me.across, (1 - me.half) * 2 + me.core),
        (me.corner, (1 - me.half) * 2 + 1 - me.core),
    )

    def go(copy):
        copy.start()
        return copy

    vecs = [go(remote(vec_ref, vec_in.at[mine], vec_send.at[i], vec_recv.at[i], d)) for i, (d, p) in enumerate(peers)]
    atts = [
        go(remote(staged.at[p], rows_of(attend_ref, mine), att_send.at[i], att_recv.at[i], d))
        for i, (d, p) in enumerate(peers)
    ]
    vec_in[mine] = vec_ref[...]
    rows_of(attend_ref, mine)[...] = staged[mine]
    local = [
        go(pltpu.make_async_copy(
            ew_ref.at[:, pl.ds(pl.multiple_of(mine * D, D), D)], rows_of(expand_ref, mine), local_sem.at[0]
        ))
    ]
    own_two = rows_of(gtwo_ref, mine)
    own_two[...] = (BRANCH * cot_ref[...].astype(F32)).astype(BF)
    for i, (d, p) in enumerate(peers):
        remote(vec_ref, vec_in.at[p], vec_send.at[i], vec_recv.at[i], d).wait_recv()
    for part in range(4):
        vec_out[:, part * 192 : part * 192 + 192] = vec_in[part]
    out, unit, inverse = layer_norm(tok_ref[...].astype(F32), vec_out[4:5, :], vec_out[5:6, :])
    own_rows = piece(all_ref, me.ctx, mine)
    own_rows[...] = out.astype(BF)
    across = go(remote(own_rows, own_rows, x_send.at[0], x_recv.at[0], me.across))

    def spread(distance, slot):
        half = me.half if slot == 0 else 1 - me.half
        got = piece(all_ref, (z - distance) * 2 + side, half * 2 + me.core)

        @pl.when(z < top)
        def _():
            remote(got, got, z_send.at[distance, slot], z_recv.at[distance + 1, slot], me.at(level=z + 1)).start()

        remote(got, got, y_send.at[distance, slot], y_recv.at[distance, slot], me.beside).start()
        remote(got, got, core_send.at[distance, 0, slot], core_recv.at[distance, 0, slot], me.twin).start()

    def held(distance, slot, where):
        half = me.half if slot == 0 else 1 - me.half
        return piece(all_ref, (z - distance) * 2 + where, half * 2 + me.core)

    def from_twin(distance, which, where):
        for slot in range(2):
            half = me.half if slot == 0 else 1 - me.half
            got = piece(all_ref, (z - distance) * 2 + where, half * 2 + 1 - me.core)
            remote(got, got, core_send.at[distance, which, slot], core_recv.at[distance, which, slot], me.twin).wait_recv()

    spread(0, 0)
    two_x = go(remote(own_two, own_two, two_send.at[0], two_recv.at[0], me.across))
    two_c = go(remote(own_two, own_two, two_send.at[1], two_recv.at[1], me.twin))
    exps = [
        go(remote(ew_ref.at[:, pl.ds(pl.multiple_of(p * D, D), D)], rows_of(expand_ref, mine), exp_send.at[i], exp_recv.at[i], d))
        for i, (d, p) in enumerate(peers)
    ]
    begins[...] = begins_of(starts_ref, me.ctx * block, block)
    got = held(0, 1, side)
    remote(got, got, x_send.at[0], x_recv.at[0], me.across).wait_recv()
    spread(0, 1)
    for copy in atts:
        copy.wait_recv()
    from_twin(0, 0, side)

    first_query = me.ctx * block
    bias_q = vec_in[mine // 2, pl.ds(mine % 2, 1), :]
    query = (mm(all_ref[pl.ds(pl.multiple_of(first_query, block), block), :], attend_ref[:, 0:192]) + bias_q).astype(BF)
    q_out[...] = query
    fill_masked_columns(qm, (query.astype(F32) * SCALE).T.astype(BF))
    peak[...] = jnp.full(peak.shape, NEG, F32)
    total[...] = jnp.zeros(total.shape, F32)
    acc[...] = jnp.zeros(acc.shape, F32)

    def attend(ctx, diagonal):
        first_key = ctx * block
        at = pl.ds(pl.multiple_of(first_key, block), block)
        rows = all_ref[at, :]
        key = mm(rows, attend_ref[:, 192:384]).astype(BF)
        k_out[at, :] = key
        value = (mm(rows, attend_ref[:, 384:576]) + vec_in[2 + mine // 2, pl.ds(mine % 2, 1), :]).astype(BF)
        v_out[at, :] = value
        vt[...] = value.astype(F32).T.astype(BF)
        strips = [(head, strip) for head in range(3) for strip in range(block // STRIP)]

        def keys_of(strip):
            return strip * STRIP + STRIP if diagonal else block

        def scored(head, strip):
            depth = 128 if head < 2 else HD
            return mm(key[0 : keys_of(strip), head_lanes(head)], qm[head, 0:depth, strip * STRIP : strip * STRIP + STRIP])

        ahead = [scored(*strips[i]) for i in range(LEAD)]
        for i, (head, strip) in enumerate(strips):
            scores = ahead.pop(0)
            if i + LEAD < len(strips):
                ahead.append(scored(*strips[i + LEAD]))
            lanes = slice(strip * STRIP, strip * STRIP + STRIP)
            count = keys_of(strip)
            places = first_key + lax.broadcasted_iota(jnp.int32, (count, STRIP), 0)
            allowed = places >= begins[:, lanes]
            if diagonal:
                queries = first_query + strip * STRIP + lax.broadcasted_iota(jnp.int32, (count, STRIP), 1)
                allowed = allowed & (places <= queries)
            scores = jnp.where(allowed, scores, NEG)
            old = peak[head : head + 1, lanes]
            new = jnp.maximum(old, jnp.max(scores, axis=0, keepdims=True))
            weights = jnp.exp(scores - new)
            factor = jnp.exp(old - new)
            peak[head : head + 1, lanes] = new
            total[head : head + 1, lanes] = total[head : head + 1, lanes] * factor + jnp.sum(
                weights, axis=0, keepdims=True
            )
            part = slice(head * HD, head * HD + HD)
            acc[part, lanes] = acc[part, lanes] * factor + mm(vt[part, 0:count], weights.astype(BF))

    attend(me.ctx, True)

    @pl.loop(0, levels)
    def _(step):
        @pl.when(step + 1 <= z)
        def _():
            for slot in range(2):
                got = held(step + 1, slot, side)
                remote(got, got, z_send.at[step, slot], z_recv.at[step + 1, slot], me.twin).wait_recv()
                spread(step + 1, slot)

        @pl.when(step <= z)
        def _():
            for slot in range(2):
                got = held(step, slot, 1 - side)
                remote(got, got, y_send.at[step, slot], y_recv.at[step, slot], me.beside).wait_recv()
                remote(got, got, core_send.at[step, 1, slot], core_recv.at[step, 1, slot], me.twin).start()

        @pl.loop(0, 2)
        def _(turn):
            ctx = me.ctx - 2 * step + (1 - turn) * (1 - 2 * side) - 2 * turn

            @pl.when((turn == 0) & (step <= z))
            def _():
                from_twin(step, 1, 1 - side)

            @pl.when((turn == 1) & (step + 1 <= z))
            def _():
                from_twin(step + 1, 0, side)

            @pl.when((ctx >= 0) & (ctx < me.ctx))
            def _():
                attend(ctx, False)

    for head in range(3):
        part = slice(head * HD, head * HD + HD)
        o_out[part, :] = acc[part, :] / total[head : head + 1, :]
    lse_out[...] = peak[...] + jnp.log(jnp.maximum(total[...], 1e-30))

    other = (1 - me.half) * 2 + me.core
    got = rows_of(gtwo_ref, other)
    remote(got, got, two_send.at[0], two_recv.at[0], me.across).wait_recv()
    two_f = go(remote(got, got, two_send.at[2], two_recv.at[2], me.twin))
    for copy in local:
        copy.wait()
    for copy in vecs + atts + [two_x, across]:
        copy.wait_send()
    for copy in exps + [two_c, two_f]:
        copy.wait()

    @pl.loop(0, levels)
    def _(step):
        @pl.when(step <= z)
        def _():
            for slot in range(2):
                got = held(step, slot, side)

                @pl.when(z < top)
                def _():
                    remote(got, got, z_send.at[step, slot], z_recv.at[step, slot], me.twin).wait_send()

                remote(got, got, y_send.at[step, slot], y_recv.at[step, slot], me.beside).wait_send()
                for which in range(2):
                    remote(got, got, core_send.at[step, which, slot], core_recv.at[step, which, slot], me.twin).wait_send()


def gather_attend(starts, tokens, vectors, attend_weight, expand_weight, cotangent):
    levels = lax.axis_size("ctx") // 2
    rows = tokens.shape[0]
    block = rows * 4
    length = block * levels * 2
    vmem = pl.BlockSpec(memory_space=pltpu.VMEM)
    dma = pltpu.SemaphoreType.DMA
    return pl.pallas_call(
        functools.partial(gather_attend_kernel, levels),
        in_specs=[pl.BlockSpec(memory_space=pltpu.SMEM), vmem, vmem, vmem, pl.BlockSpec(memory_space=pl.ANY), vmem],
        out_specs=[vmem] * 10,
        out_shape=[
            jax.ShapeDtypeStruct((length, D), BF),
            jax.ShapeDtypeStruct((D, 576), BF),
            jax.ShapeDtypeStruct((D, D), BF),
            jax.ShapeDtypeStruct((block, D), BF),
            jax.ShapeDtypeStruct((8, D), F32),
            jax.ShapeDtypeStruct((block, 192), BF),
            jax.ShapeDtypeStruct((length, 192), BF),
            jax.ShapeDtypeStruct((length, 192), BF),
            jax.ShapeDtypeStruct((192, block), F32),
            jax.ShapeDtypeStruct((8, block), F32),
        ],
        scratch_shapes=[
            pltpu.VMEM((4, rows, 576), BF),
            pltpu.VMEM((4, 8, 192), F32),
            pltpu.VMEM((1, block), jnp.int32),
            pltpu.VMEM((3, 128, block), BF),
            pltpu.VMEM((192, block), BF),
            pltpu.VMEM((192, block), F32),
            pltpu.VMEM((8, block), F32),
            pltpu.VMEM((8, block), F32),
            dma((3,)), dma((3,)), dma((3,)), dma((3,)), dma((3,)), dma((3,)), dma((3,)), dma((3,)),
            dma((1,)), dma((1,)),
            dma((levels, 2)), dma((levels + 1, 2)),
            dma((levels, 2)), dma((levels, 2)),
            dma((levels, 2, 2)), dma((levels, 2, 2)),
            dma((1,)),
        ],
        compiler_params=pltpu.CompilerParams(collective_id=4, has_side_effects=True, vmem_limit_bytes=48 << 20),
        name="gather_attend",
    )(starts, tokens, vectors, attend_weight, expand_weight, cotangent)


def gelu_pair(t):
    slope = 0.7978845608028654
    square = t * t
    bend = jnp.tanh(slope * t * (1.0 + 0.044715 * square))
    half = 0.5 * (1.0 + bend)
    return t * half, half + 0.5 * t * (1.0 - bend * bend) * (slope * (1.0 + 0.134145 * square))


def mlp_kernel(
    o_ref, wp_ref, expand_ref, contract_ref, ebias_ref, tok_ref, cot_ref, gtwo_ref, vec_ref,
    block_out, gmid_out, gone_out, cpart_out, epart_out, sums_out,
    o_rows, gact, n2, act, gexp, held, unit,
    c_send_buf, c_recv_buf, x_send_buf, x_recv_buf,
    c_send, c_recv, x_send, x_recv, ag_send, ag_recv,
):
    me = Place()
    mine = me.part
    barrier = pltpu.get_barrier_semaphore()
    signal(barrier, me.twin)
    signal(barrier, me.across)
    pl.semaphore_wait(barrier, 2)
    p_across = (1 - me.half) * 2 + me.core
    p_twin = me.half * 2 + 1 - me.core
    p_corner = (1 - me.half) * 2 + 1 - me.core

    def part(ref, p):
        return ref[pl.ds(pl.multiple_of(p * 192, 192), 192), :]

    def to_twin(i, slot, value):
        c_send_buf[i, slot] = value.astype(BF)
        remote(c_send_buf.at[i, slot], c_recv_buf.at[i, slot], c_send.at[i, slot], c_recv.at[i, slot], me.twin).start()

    def from_twin(i, slot):
        remote(c_send_buf.at[i, slot], c_recv_buf.at[i, slot], c_send.at[i, slot], c_recv.at[i, slot], me.twin).wait_recv()
        return c_recv_buf[i, slot].astype(F32)

    def to_across(i, value):
        x_send_buf[i] = value.astype(BF)
        remote(x_send_buf.at[i], x_recv_buf.at[i], x_send.at[i], x_recv.at[i], me.across).start()

    def from_across(i):
        remote(x_send_buf.at[i], x_recv_buf.at[i], x_send.at[i], x_recv.at[i], me.across).wait_recv()
        return x_recv_buf[i].astype(F32)

    def share(i, ref):
        own = rows_of(ref, mine)
        remote(own, own, ag_send.at[i, 0], ag_recv.at[i, 0], me.across).start()
        remote(own, own, ag_send.at[i, 1], ag_recv.at[i, 1], me.twin).start()

    def share_across(i, ref):
        got = rows_of(ref, p_across)
        remote(got, got, ag_send.at[i, 0], ag_recv.at[i, 0], me.across).wait_recv()
        remote(got, got, ag_send.at[i, 2], ag_recv.at[i, 2], me.twin).start()

    def share_twin(i, ref):
        got = rows_of(ref, p_twin)
        remote(got, got, ag_send.at[i, 1], ag_recv.at[i, 1], me.twin).wait_recv()

    def share_corner(i, ref):
        got = rows_of(ref, p_corner)
        remote(got, got, ag_send.at[i, 2], ag_recv.at[i, 2], me.twin).wait_recv()

    o_rows[...] = o_ref[...].T.astype(BF)
    to_twin(0, 0, mm(part(o_rows, p_corner), wp_ref[...]))
    to_twin(0, 1, mm(part(o_rows, p_twin), wp_ref[...]))
    value = mm(part(o_rows, p_across), wp_ref[...])
    to_across(0, value + from_twin(0, 0))
    for p in range(4):
        gact[p * 192 : p * 192 + 192, :] = mm_nt(gtwo_ref[p * 192 : p * 192 + 192, :], contract_ref[...])
    value = mm(part(o_rows, mine), wp_ref[...]) + from_twin(0, 1)
    value = value + from_across(0)
    middle = tok_ref[...].astype(F32) + BRANCH * (value + vec_ref[2:3, :])
    out, unit_two, inverse = layer_norm(middle, vec_ref[6:7, :], vec_ref[7:8, :])
    n2[pl.ds(pl.multiple_of(mine * 192, 192), 192), :] = out.astype(BF)
    share(0, n2)
    unit[...] = unit_two
    held[...] = middle

    def through(p):
        at = pl.ds(pl.multiple_of(p * 192, 192), 192)
        expanded = mm(n2[at, :], expand_ref[...]) + ebias_ref[...]
        activation, slope = gelu_pair(expanded)
        act[at, :] = activation.astype(BF)
        low = (gact[at, :] * slope).astype(BF)
        gexp[at, :] = low
        return mm_nt(low, expand_ref[...])

    own_value = through(mine)
    share_twin(0, n2)
    to_twin(1, 1, through(p_twin))
    share_across(0, n2)
    across_value = through(p_across)
    share_corner(0, n2)
    to_twin(1, 0, through(p_corner))
    to_across(1, across_value + from_twin(1, 0))
    own_value = own_value + from_twin(1, 1)
    to_twin(2, 0, mm(part(act, p_corner), contract_ref[...]))
    to_twin(2, 1, mm(part(act, p_twin), contract_ref[...]))
    to_across(2, mm(part(act, p_across), contract_ref[...]) + from_twin(2, 0))
    cpart_out[...] = mm_tn(act[...], gtwo_ref[...]).astype(BF)
    grad = own_value + from_across(1)
    unit_two = unit[...]
    scaled = grad * vec_ref[6:7, :]
    spread = (
        scaled
        - jnp.mean(scaled, axis=1, keepdims=True)
        - unit_two * jnp.mean(scaled * unit_two, axis=1, keepdims=True)
    )
    grad_middle = cot_ref[...].astype(F32) + inverse * spread
    gmid_out[...] = grad_middle
    low = (BRANCH * grad_middle).astype(BF)
    gone_out[pl.ds(pl.multiple_of(mine * 192, 192), 192), :] = low
    share(1, gone_out)
    sums_out[0:1, :] = jnp.sum(low.astype(F32), axis=0, keepdims=True)
    sums_out[1:2, :] = jnp.sum(part(gtwo_ref, mine).astype(F32), axis=0, keepdims=True)
    sums_out[2:3, :] = jnp.sum(grad * unit_two, axis=0, keepdims=True)
    sums_out[3:4, :] = jnp.sum(grad, axis=0, keepdims=True)
    sums_out[4:5, :] = jnp.sum(gexp[...].astype(F32), axis=0, keepdims=True)
    sums_out[5:8, :] = jnp.zeros((3, D), F32)
    epart_out[...] = mm_tn(n2[...], gexp[...]).astype(BF)
    value = mm(part(act, mine), contract_ref[...]) + from_twin(2, 1)
    value = value + from_across(2)
    block_out[...] = (held[...] + BRANCH * (value + vec_ref[3:4, :])).astype(BF)
    share_across(1, gone_out)
    share_twin(1, gone_out)
    share_corner(1, gone_out)
    for i in range(3):
        for slot in range(2):
            remote(c_send_buf.at[i, slot], c_recv_buf.at[i, slot], c_send.at[i, slot], c_recv.at[i, slot], me.twin).wait_send()
        remote(x_send_buf.at[i], x_recv_buf.at[i], x_send.at[i], x_recv.at[i], me.across).wait_send()
    for i, ref in ((0, n2), (1, gone_out)):
        own = rows_of(ref, mine)
        for j in range(3):
            remote(own, own, ag_send.at[i, j], ag_recv.at[i, j], me.twin).wait_send()


def feed_forward(o, wp, expand, contract, ebias, tokens, cotangent, gtwo, vectors):
    rows = tokens.shape[0]
    block = rows * 4
    vmem = pl.BlockSpec(memory_space=pltpu.VMEM)
    dma = pltpu.SemaphoreType.DMA
    return pl.pallas_call(
        mlp_kernel,
        in_specs=[vmem] * 9,
        out_specs=[vmem] * 6,
        out_shape=[
            jax.ShapeDtypeStruct((rows, D), BF),
            jax.ShapeDtypeStruct((rows, D), F32),
            jax.ShapeDtypeStruct((block, D), BF),
            jax.ShapeDtypeStruct((D, D), BF),
            jax.ShapeDtypeStruct((D, D), BF),
            jax.ShapeDtypeStruct((8, D), F32),
        ],
        scratch_shapes=[
            pltpu.VMEM((block, 192), BF),
            pltpu.VMEM((block, D), F32),
            pltpu.VMEM((block, D), BF),
            pltpu.VMEM((block, D), BF),
            pltpu.VMEM((block, D), BF),
            pltpu.VMEM((rows, D), F32),
            pltpu.VMEM((rows, D), F32),
            pltpu.VMEM((3, 2, rows, D), BF),
            pltpu.VMEM((3, 2, rows, D), BF),
            pltpu.VMEM((3, rows, D), BF),
            pltpu.VMEM((3, rows, D), BF),
            dma((3, 2)), dma((3, 2)), dma((3,)), dma((3,)), dma((2, 3)), dma((2, 3)),
        ],
        compiler_params=pltpu.CompilerParams(collective_id=2, has_side_effects=True, vmem_limit_bytes=48 << 20),
        name="feed_forward",
    )(o, wp, expand, contract, ebias, tokens, cotangent, gtwo, vectors)


class Exchange:
    def __init__(self, me, levels, items, y_send, y_recv, z_send, z_recv):
        self.me, self.top, self.items = me, levels - 1, items
        self.y_send, self.y_recv, self.z_send, self.z_recv = y_send, y_recv, z_send, z_recv

    def beside(self, level, act, only=None):
        for i, (chunk, y_in, z_out, z_in) in enumerate(self.items):
            if only is None or i in only:
                act(remote(chunk(level, 1 - self.me.side), y_in.at[level], self.y_send.at[level, i], self.y_recv.at[level, i], self.me.beside))

    def steps(self, step, act):
        z, top = self.me.level, self.top
        down = step - (top - z)
        up = top - (step - z)

        @pl.when((down >= 0) & (down < z))
        def _():
            act(down, 0)

        @pl.when((up <= top) & (up > z))
        def _():
            act(up, 1)

    def along(self, level, way, act):
        device = self.me.at(level=self.me.level - 1) if way == 0 else self.me.at(level=self.me.level + 1)
        last = level == (self.me.level - 1 if way == 0 else self.me.level + 1)
        spot = level if way == 0 else jnp.where(last, self.top + 1, level)
        for i, (chunk, y_in, z_out, z_in) in enumerate(self.items):
            act(remote(z_out.at[level], z_in.at[spot], self.z_send.at[level, i], self.z_recv.at[spot, i], device))

    def arrived(self, level, way):
        spot = level if way == 0 else jnp.where(level == self.me.level, self.top + 1, level)
        for i, (chunk, y_in, z_out, z_in) in enumerate(self.items):
            remote(z_out.at[level], z_in.at[spot], self.z_send.at[level, i], self.z_recv.at[spot, i], self.me.twin).wait_recv()
        return spot

    def step(self, step):
        z, top, side = self.me.level, self.top, self.me.side

        def act(level, way):
            self.beside(level, lambda copy: copy.wait_recv())
            inner = (z < top) if way == 0 else (z > 0)

            @pl.when(inner)
            def _():
                spot = self.arrived(level, way)
                for chunk, y_in, z_out, z_in in self.items:
                    z_out[level] = (
                        chunk(level, side)[...].astype(F32) + y_in[level].astype(F32) + z_in[spot].astype(F32)
                    ).astype(BF)

            @pl.when(jnp.logical_not(inner))
            def _():
                for chunk, y_in, z_out, z_in in self.items:
                    z_out[level] = (chunk(level, side)[...].astype(F32) + y_in[level].astype(F32)).astype(BF)

            self.along(level, way, lambda copy: copy.start())

        self.steps(step, act)

    def final(self, targets):
        z, top, side = self.me.level, self.top, self.me.side
        self.beside(z, lambda copy: copy.wait_recv())

        def add(spots):
            for (chunk, y_in, z_out, z_in), target in zip(self.items, targets):
                sum_of = chunk(z, side)[...].astype(F32) + y_in[z].astype(F32)
                for spot in spots:
                    sum_of = sum_of + z_in[spot].astype(F32)
                target[...] = sum_of.astype(BF)

        @pl.when(z < top)
        def _():
            self.arrived(z, 0)

        @pl.when(z > 0)
        def _():
            self.arrived(z, 1)

        @pl.when(z == 0)
        def _():
            add((z,))

        @pl.when(z == top)
        def _():
            add((top + 1,))

        @pl.when((z > 0) & (z < top))
        def _():
            add((z, top + 1))

    def drain(self):
        for level in range(self.top + 1):
            self.beside(level, lambda copy: copy.wait_send())

            @pl.when(level != self.me.level)
            def _():
                for i, (chunk, y_in, z_out, z_in) in enumerate(self.items):
                    remote(z_out.at[level], z_in.at[level], self.z_send.at[level, i], self.z_recv.at[level, i], self.me.twin).wait_send()


def attend_reduce_kernel(
    levels, starts_ref, all_ref, k_ref, v_ref, q_ref, o_ref, lse_ref, g_ref, wp_ref, aw_ref,
    c_ref, e_ref, tok_ref, gmid_ref, vec_ref, sums_ref,
    tg_out, cg_out, eg_out, ag_out, pg_out, vec_out, hid_out,
    rows_in, keys_in, values_in, begins, qm, dm, qn, dn, delta, dqt, kt, dk, dv, gt, a_part, p_part,
    dnb, far, keep, x_out, x_in, y_out, y_in, d_out, d_in,
    yc, ye, ya, yp, zc_out, ze_out, za_out, zp_out, zc_in, ze_in, za_in, zp_in, v_out, v_in, e_move, a_move, a_rows,
    pre_sem, far_send, far_recv, x_send, x_recv, y_send, y_recv, d_send, d_recv,
    gy_send, gy_recv, gz_send, gz_recv, ay_send, ay_recv, az_send, az_recv,
    me_send, me_recv, ma_send, ma_recv, u_send, u_recv, w_send, w_recv,
    be_send, be_recv, ba_send, ba_recv, te_send, te_recv, ta_send, ta_recv, v_send, v_recv,
):
    me = Place()
    z, side, mine, ctx = me.level, me.side, me.part, me.ctx
    top = levels - 1
    block = g_ref.shape[0]
    barrier = pltpu.get_barrier_semaphore()
    for device in (me.twin, me.across, me.corner, me.beside):
        signal(barrier, device)
    for step in range(1, levels):
        signal(barrier, me.at(level=(z + step) % levels))
    below, above = me.at(level=z - 1), me.at(level=z + 1)
    start = lambda copy: copy.start()
    wait_recv = lambda copy: copy.wait_recv()
    wait_send = lambda copy: copy.wait_send()

    def prefetch(index):
        slot = index % 2
        at = pl.ds(pl.multiple_of(index * block, block), block)
        return (
            pltpu.make_async_copy(all_ref.at[at], rows_in.at[slot], pre_sem.at[slot, 0]),
            pltpu.make_async_copy(k_ref.at[at], keys_in.at[slot], pre_sem.at[slot, 1]),
            pltpu.make_async_copy(v_ref.at[at], values_in.at[slot], pre_sem.at[slot, 2]),
        )

    def all_of(copies, act):
        for copy in copies:
            act(copy)

    all_of(prefetch(0), start)

    def corner_of(ref, level, where):
        return ref.at[pl.ds(pl.multiple_of(level * 48, 48), 48), pl.ds(pl.multiple_of(where * 384, 128), 384)]

    grads = Exchange(
        me, levels,
        (
            (lambda level, where: c_ref.at[level * 2 + where], yc, zc_out, zc_in),
            (lambda level, where: e_ref.at[level * 2 + where], ye, ze_out, ze_in),
            (lambda level, where: corner_of(p_part, level, where), yp, zp_out, zp_in),
        ),
        gy_send, gy_recv, gz_send, gz_recv,
    )
    attends = Exchange(
        me, levels, ((lambda level, where: a_part.at[level * 2 + where], ya, za_out, za_in),), ay_send, ay_recv, az_send, az_recv
    )
    grads_in = g_ref[...]
    exact = o_ref[...]
    p_part[...] = mm(exact.astype(BF), grads_in).astype(BF)
    outer = mm_nt(grads_in, wp_ref[...]).astype(BF)
    pl.semaphore_wait(barrier, levels + 3)
    for step in range(levels - 1):
        grads.steps(step, lambda level, way: grads.beside(level, start))
    grads.beside(z, start)
    flipped = outer.astype(F32).T
    product = flipped * exact
    for head in range(3):
        delta[head : head + 1, :] = jnp.sum(product[head * HD : head * HD + HD], axis=0, keepdims=True)
    fill_masked_columns(dm, flipped.astype(BF))
    scaled = q_ref[...].astype(F32) * SCALE
    fill_masked_columns(qm, scaled.T.astype(BF))
    scaled = scaled.astype(BF)
    for head in range(3):
        depth = 128 if head < 2 else HD
        qn[head, :, 0:depth] = masked_rows(scaled, head)
        dn[head, :, 0:depth] = masked_rows(outer, head)
    dqt[...] = jnp.zeros(dqt.shape, F32)
    gt[...] = jnp.zeros(gt.shape, F32)
    first_query = ctx * block
    begins[...] = begins_of(starts_ref, first_query, block)
    v_out[0] = jnp.zeros(v_out.shape[1:], F32)

    def attend(index, diagonal):
        slot = index % 2
        first_key = index * block
        kt[...] = keys_in[slot].astype(F32).T.astype(BF)
        dk[...] = jnp.zeros(dk.shape, F32)
        dv[...] = jnp.zeros(dv.shape, F32)
        strips = [(head, strip) for head in range(3) for strip in range(block // STRIP)]

        def keys_of(strip):
            return strip * STRIP + STRIP if diagonal else block

        def scored(head, strip):
            depth = 128 if head < 2 else HD
            lanes = head_lanes(head)
            cols = slice(strip * STRIP, strip * STRIP + STRIP)
            count = keys_of(strip)
            return (
                mm(keys_in[slot, 0:count, lanes], qm[head, 0:depth, cols]),
                mm(values_in[slot, 0:count, lanes], dm[head, 0:depth, cols]),
            )

        ahead = [scored(*strips[i]) for i in range(BACK_LEAD)]
        for i, (head, strip) in enumerate(strips):
            scores, outer = ahead.pop(0)
            if i + BACK_LEAD < len(strips):
                ahead.append(scored(*strips[i + BACK_LEAD]))
            depth = 128 if head < 2 else HD
            lanes = head_lanes(head)
            cols = slice(strip * STRIP, strip * STRIP + STRIP)
            count = keys_of(strip)
            places = first_key + lax.broadcasted_iota(jnp.int32, (count, STRIP), 0)
            allowed = places >= begins[:, cols]
            if diagonal:
                queries = first_query + strip * STRIP + lax.broadcasted_iota(jnp.int32, (count, STRIP), 1)
                allowed = allowed & (places <= queries)
            probs = jnp.where(allowed, jnp.exp(scores - lse_ref[head : head + 1, cols]), 0.0)
            inner = (probs * (outer - delta[head : head + 1, cols])).astype(BF)
            dv[0:count, lanes] += mm(probs.astype(BF), dn[head, cols, 0:depth])
            dk[0:count, lanes] += mm(inner, qn[head, cols, 0:depth])
            part = slice(head * HD, head * HD + HD)
            dqt[part, cols] += mm(kt[part, 0:count], inner)
        rows = rows_in[slot]
        low_k = dk[...].astype(BF)
        low_v = dv[...].astype(BF)
        gt[192:384, :] += mm(low_k.astype(F32).T.astype(BF), rows)
        gt[384:576, :] += mm(low_v.astype(F32).T.astype(BF), rows)
        v_out[0, 12:13, 0:192] += jnp.sum(low_v.astype(F32), axis=0, keepdims=True)
        through = mm_nt(low_k, aw_ref[:, 192:384]) + mm_nt(low_v, aw_ref[:, 384:576])
        if diagonal:
            flipped = dqt[...] * SCALE
            low_q = flipped.T.astype(BF)
            gt[0:192, :] = mm(flipped.astype(BF), rows)
            v_out[0, 13:14, 0:192] = jnp.sum(low_q.astype(F32), axis=0, keepdims=True)
            through = through + mm_nt(low_q, aw_ref[:, 0:192])
        dnb[index % 3] = through.astype(BF)

    def to_twin(index):
        slot = index % 3
        return tuple(
            remote(
                rows_of(dnb.at[slot], half * 2 + 1 - me.core), far.at[index, half],
                far_send.at[index, half], far_recv.at[index, half], me.twin,
            )
            for half in range(2)
        )

    def x_copy(index):
        return remote(x_out.at[index], x_in.at[index], x_send.at[index], x_recv.at[index], me.across)

    def y_copy(level):
        return remote(y_out.at[level], y_in.at[level], y_send.at[level], y_recv.at[level], me.beside)

    def down_copy(level):
        return remote(d_out.at[level], d_in.at[level], d_send.at[level], d_recv.at[level], below)

    def with_twin(index):
        slot = index % 3
        all_of(to_twin(index), lambda copy: copy.wait())

        def rows(half):
            own = dnb[slot, pl.ds(pl.multiple_of((half * 2 + me.core) * 192, 192), 192), :]
            return own.astype(F32) + far[index, half].astype(F32)

        x_out[index] = rows(1 - me.half).astype(BF)
        x_copy(index).start()
        keep[index] = rows(me.half)

    def with_across(index):
        x_copy(index).wait_recv()
        keep[index] += x_in[index].astype(F32)
        level = index // 2

        @pl.when((index % 2 != side))
        def _():
            y_out[level] = keep[index].astype(BF)
            y_copy(level).start()

    def with_beside(level):
        y_copy(level).wait_recv()
        keep[level * 2 + side] += y_in[level].astype(F32)

    def dn_step(step):
        level = step - (top - z)

        @pl.when((level >= 0) & (level < z))
        def _():
            with_beside(level)
            index = level * 2 + side

            @pl.when(z < top)
            def _():
                down_copy(level).wait_recv()
                keep[index] += d_in[level].astype(F32)

            d_out[level] = keep[index].astype(BF)
            down_copy(level).start()

    def done(level, where):
        return (cg_out.at[level * 2 + where], corner_of(pg_out, level, where))

    def along_copies(way, distance):
        level = z - distance if way == 0 else z + distance
        device = above if way == 0 else below
        return tuple(
            remote(ref, ref, u_send.at[way, distance, i], u_recv.at[way, distance, i], device)
            for i, ref in enumerate(done(level, side))
        )

    def side_copies(level, where):
        return tuple(
            remote(ref, ref, w_send.at[level, i], w_recv.at[level, i], me.beside) for i, ref in enumerate(done(level, where))
        )

    def pass_on(distance, way):
        if way != 1:

            @pl.when(z < top)
            def _():
                all_of(along_copies(0, distance), start)

        if way != 0:

            @pl.when(z > 0)
            def _():
                all_of(along_copies(1, distance), start)

        all_of(side_copies(z - distance if way == 0 else z + distance, side), start)

    def arrivals(distance):
        for way in range(2):
            level = z - distance if way == 0 else z + distance

            @pl.when((level >= 0) & (level <= top))
            def _():
                for i, ref in enumerate(done(level, side)):
                    remote(ref, ref, u_send.at[way, distance - 1, i], u_recv.at[way, distance - 1, i], me.twin).wait_recv()
                pass_on(distance, way)

    def e_chunk(where, origin):
        return eg_out.at[pl.ds(pl.multiple_of(where * 96, 96), 96), pl.ds(pl.multiple_of(origin * D, D), D)]

    def a_chunk(where, origin):
        return a_rows.at[where, origin]

    class Rows:
        def __init__(self, moved, chunk, m_send, m_recv, b_send, b_recv, t_send, t_recv):
            self.moved, self.chunk = moved, chunk
            self.m_send, self.m_recv, self.b_send, self.b_recv = m_send, m_recv, b_send, b_recv
            self.t_send, self.t_recv = t_send, t_recv

        def move(self):
            return remote(self.moved, self.chunk(side, mine), self.m_send.at[0], self.m_recv.at[mine], me.at(half=z // 2, core=z % 2))

        def begin(self):
            @pl.when(mine != z)
            def _():
                self.move().start()

            @pl.when(mine == z)
            def _():
                self.chunk(side, mine)[...] = self.moved[...]

        def line(self, way, origin):
            ref = self.chunk(side, origin)
            return remote(ref, ref, self.b_send.at[way, origin], self.b_recv.at[way, origin], below if way == 0 else above)

        def turn(self, origin, where):
            ref = self.chunk(where, origin)
            return remote(ref, ref, self.t_send.at[origin], self.t_recv.at[origin], me.beside)

        def spread(self, origin):
            @pl.when((mine == z) & (mine != origin))
            def _():
                remote(self.moved, self.chunk(side, origin), self.m_send.at[0], self.m_recv.at[origin], me.twin).wait_recv()

            @pl.when(mine > z)
            def _():
                self.line(0, origin).wait_recv()

            @pl.when(mine < z)
            def _():
                self.line(1, origin).wait_recv()

            @pl.when((mine >= z) & (z > 0))
            def _():
                self.line(0, origin).start()

            @pl.when((mine <= z) & (z < top))
            def _():
                self.line(1, origin).start()

            self.turn(origin, side).start()

        def drain(self):
            @pl.when(mine != z)
            def _():
                self.move().wait_send()

            for origin in range(4):

                @pl.when((mine >= z) & (z > 0))
                def _():
                    self.line(0, origin).wait_send()

                @pl.when((mine <= z) & (z < top))
                def _():
                    self.line(1, origin).wait_send()

                self.turn(origin, side).wait_send()

    e_flow = Rows(e_move, e_chunk, me_send, me_recv, be_send, be_recv, te_send, te_recv)
    a_flow = Rows(a_move, a_chunk, ma_send, ma_recv, ba_send, ba_recv, ta_send, ta_recv)

    @pl.loop(0, 2 * levels + 3)
    def _(turn):
        @pl.when(turn <= ctx)
        def _():
            all_of(prefetch(turn), lambda copy: copy.wait())

        @pl.when(turn + 1 <= ctx)
        def _():
            all_of(prefetch(turn + 1), start)

        @pl.when(turn < ctx)
        def _():
            attend(turn, False)

        @pl.when(turn == ctx)
        def _():
            attend(turn, True)
            flipped = gt[...].T.astype(BF)
            for chunk in range(8):
                a_part[chunk] = flipped[chunk * 96 : chunk * 96 + 96]
            for step in range(levels - 1):
                attends.steps(step, lambda level, way: attends.beside(level, start))
            attends.beside(z, start)

        @pl.when(turn <= ctx)
        def _():
            all_of(to_twin(turn), start)

        @pl.when((turn >= 1) & (turn - 1 <= ctx))
        def _():
            with_twin(turn - 1)

        @pl.when((turn % 2 == 1) & (turn < 2 * levels - 1))
        def _():
            grads.step(turn // 2)

        @pl.when(turn == 2 * levels - 1)
        def _():
            grads.final((cg_out.at[ctx], e_move, corner_of(pg_out, z, side)))
            e_flow.begin()
            pass_on(0, 2)

        @pl.when((turn >= 3) & (turn - 3 <= ctx))
        def _():
            with_across(turn - 3)

        @pl.when((turn >= 6) & (turn % 2 == 0))
        def _():
            dn_step((turn - 6) // 2)

    attends.step(0)
    arrivals(1)
    attends.step(1)
    for origin in range(4):
        e_flow.spread(origin)
    attends.step(2)
    arrivals(2)
    attends.final((a_move,))
    a_flow.begin()

    @pl.when(side == 0)
    def _():
        with_beside(z)

    @pl.when(z < top)
    def _():
        down_copy(z).wait_recv()
        keep[ctx] += d_in[z].astype(F32)

    grad = keep[ctx]
    gain = vec_ref[4:5, :]
    normed, unit, inverse = layer_norm(tok_ref[...].astype(F32), gain, vec_ref[5:6, :])
    scaled = grad * gain
    spread = (
        scaled - jnp.mean(scaled, axis=1, keepdims=True) - unit * jnp.mean(scaled * unit, axis=1, keepdims=True)
    )
    tg_out[...] = (gmid_ref[...] + inverse * spread).astype(BF)
    for part in range(4):

        @pl.when(mine == part)
        def _():
            v_out[0, 0:1, part * 192 : part * 192 + 192] = v_out[0, 13:14, 0:192]
            v_out[0, 1:2, part * 192 : part * 192 + 192] = v_out[0, 12:13, 0:192]
            v_out[0, 8 + part : 9 + part, :] = sums_ref[4:5, :]

    v_out[0, 12:16, :] = jnp.zeros((4, D), F32)
    v_out[0, 2:4, :] = sums_ref[0:2, :]
    v_out[0, 4:5, :] = jnp.sum(grad * unit, axis=0, keepdims=True)
    v_out[0, 5:6, :] = jnp.sum(grad, axis=0, keepdims=True)
    v_out[0, 6:8, :] = sums_ref[2:4, :]
    for origin in range(4):
        a_flow.spread(origin)
    for i, device in enumerate((me.twin, me.across, me.beside)):
        copy = remote(v_out.at[i], v_in.at[i], v_send.at[i], v_recv.at[i], device)
        copy.start()
        copy.wait_recv()
        v_out[i + 1] = v_out[i] + v_in[i]
    v_in[3 + z] = v_out[3]
    for step in range(1, levels):
        remote(v_out.at[3], v_in.at[3 + z], v_send.at[2 + step], v_recv.at[3 + z], me.at(level=(z + step) % levels)).start()
    arrivals(3)
    for step in range(1, levels):
        level = (z + step) % levels
        remote(v_out.at[3], v_in.at[3 + level], v_send.at[2 + step], v_recv.at[3 + level], me.twin).wait_recv()
    total = v_in[3]
    for level in range(1, levels):
        total = total + v_in[3 + level]
    v_out[4] = total
    hid_out[...] = v_out[4, pl.ds(8 + mine, 1), :]
    for part in range(4):

        @pl.when(mine == part)
        def _():
            source, lane = part // 2, (part % 2) * 384
            vec_out[0:1, :] = total[source : source + 1, lane : lane + 192]
            vec_out[1:2, :] = total[source : source + 1, lane + 192 : lane + 384]
            vec_out[2:8, :] = total[2:8, part * 192 : part * 192 + 192]

    for level in range(levels):
        all_of(side_copies(level, 1 - side), wait_recv)
    for flow in (e_flow, a_flow):
        for origin in range(4):
            flow.turn(origin, 1 - side).wait_recv()
    for where in range(2):
        for part in range(4):
            for kind in range(3):
                lane = kind * D + part * 192
                ag_out[where * 96 : where * 96 + 96, lane : lane + 192] = a_rows[
                    where, part, :, kind * 192 : kind * 192 + 192
                ].astype(F32)
    grads.drain()
    attends.drain()
    e_flow.drain()
    a_flow.drain()
    for level in range(levels):
        all_of(side_copies(level, side), wait_send)

        @pl.when((level < z) | ((level == z) & (side == 1)))
        def _():
            y_copy(level).wait_send()

        @pl.when(level < z)
        def _():
            down_copy(level).wait_send()

    @pl.loop(0, 2 * levels)
    def _(index):
        @pl.when(index <= ctx)
        def _():
            x_copy(index).wait_send()

    for distance in range(levels):

        @pl.when((z - distance >= 0) & (z < top))
        def _():
            all_of(along_copies(0, distance), wait_send)

        @pl.when((z + distance <= top) & (z > 0))
        def _():
            all_of(along_copies(1, distance), wait_send)

    for i in range(2 + levels):
        remote(v_out.at[0], v_in.at[0], v_send.at[i], v_recv.at[0], me.twin).wait_send()


def attend_reduce(starts, rows_all, k, v, q, o, lse, g, wp, aw, contract, expand, tokens, grad_middle, vectors, sums):
    levels = lax.axis_size("ctx") // 2
    rows = tokens.shape[0]
    block = rows * 4
    vmem = pl.BlockSpec(memory_space=pltpu.VMEM)
    anywhere = pl.BlockSpec(memory_space=pl.ANY)
    dma = pltpu.SemaphoreType.DMA
    n = levels

    def buf(*shape):
        return pltpu.VMEM(shape, BF)

    def wide(*shape):
        return pltpu.VMEM(shape, F32)

    return pl.pallas_call(
        functools.partial(attend_reduce_kernel, levels),
        in_specs=[pl.BlockSpec(memory_space=pltpu.SMEM)] + [anywhere] * 3 + [vmem] * 12,
        out_specs=[vmem] * 7,
        out_shape=[
            jax.ShapeDtypeStruct((rows, D), BF),
            jax.ShapeDtypeStruct((2 * n, 96, D), BF),
            jax.ShapeDtypeStruct((192, 4 * D), BF),
            jax.ShapeDtypeStruct((192, 3 * D), F32),
            jax.ShapeDtypeStruct((192, D), BF),
            jax.ShapeDtypeStruct((8, 192), F32),
            jax.ShapeDtypeStruct((1, D), F32),
        ],
        scratch_shapes=[
            buf(2, block, D), buf(2, block, 192), buf(2, block, 192), pltpu.VMEM((1, block), jnp.int32),
            buf(3, 128, block), buf(3, 128, block), buf(3, block, 128), buf(3, block, 128),
            wide(8, block), wide(192, block), buf(192, block), wide(block, 192), wide(block, 192), wide(576, D),
            buf(2 * n, 96, 576), buf(192, D),
            buf(3, block, D), buf(2 * n, 2, rows, D), wide(2 * n, rows, D), buf(2 * n, rows, D), buf(2 * n, rows, D),
            buf(n, rows, D), buf(n, rows, D), buf(n, rows, D), buf(n, rows, D),
            buf(n, 96, D), buf(n, 96, D), buf(n, 96, 576), buf(n, 48, 384),
            buf(n, 96, D), buf(n, 96, D), buf(n, 96, 576), buf(n, 48, 384),
            buf(n + 1, 96, D), buf(n + 1, 96, D), buf(n + 1, 96, 576), buf(n + 1, 48, 384),
            wide(5, 16, D), wide(3 + n, 16, D), buf(96, D), buf(96, 576), buf(2, 4, 96, 576),
            dma((2, 3)), dma((2 * n, 2)), dma((2 * n, 2)), dma((2 * n,)), dma((2 * n,)),
            dma((n,)), dma((n,)), dma((n,)), dma((n,)),
            dma((n, 3)), dma((n, 3)), dma((n, 3)), dma((n + 1, 3)),
            dma((n, 1)), dma((n, 1)), dma((n, 1)), dma((n + 1, 1)),
            dma((1,)), dma((4,)), dma((1,)), dma((4,)),
            dma((2, n, 2)), dma((2, n, 2)), dma((n, 2)), dma((n, 2)),
            dma((2, 4)), dma((2, 4)), dma((2, 4)), dma((2, 4)), dma((4,)), dma((4,)), dma((4,)), dma((4,)),
            dma((2 + n,)), dma((3 + n,)),
        ],
        compiler_params=pltpu.CompilerParams(collective_id=5, has_side_effects=True, vmem_limit_bytes=60 << 20),
        name="attend_reduce",
    )(starts, rows_all, k, v, q, o, lse, g, wp, aw, contract, expand, tokens, grad_middle, vectors, sums)


def normalize(rows_in, gain, shift):
    mean = jnp.mean(rows_in, axis=1, keepdims=True)
    centered = rows_in - mean
    inverse = lax.rsqrt(jnp.mean(centered * centered, axis=1, keepdims=True) + EPS)
    unit = centered * inverse
    return (unit * gain + shift, unit, inverse)


def normalize_back(incoming, unit, inverse, gain):
    scaled = incoming * gain
    spread = (
        scaled
        - jnp.mean(scaled, axis=1, keepdims=True)
        - unit * jnp.mean(scaled * unit, axis=1, keepdims=True)
    )
    return (inverse * spread, jnp.sum(incoming * unit, axis=0), jnp.sum(incoming, axis=0))


def first_position(places, starts):
    below = starts[None, :] <= places[:, None]
    return jnp.max(jnp.where(below, starts[None, :], 0), axis=1)


def forward_plain(
    tokens, document_starts, attend_weight, attend_bias, expand_weight, cotangent, own_vectors
):
    rows = tokens.shape[0]
    ways = lax.axis_size("fsdp")
    block = rows * ways
    ctx = lax.axis_index("ctx")
    part = lax.axis_index("fsdp")
    vectors = lax.dynamic_update_slice(jnp.zeros((6, D), F32), jnp.stack(own_vectors).astype(F32), (0, part * rows))
    biases = lax.dynamic_update_slice(jnp.zeros((2 * D,), F32), attend_bias.astype(F32), (part * 2 * rows,))
    vectors = jnp.concatenate([biases.reshape(2, D), vectors])
    attend_cols = attend_weight.reshape(rows, 3, ways, 192).transpose(2, 0, 1, 3).reshape(ways, rows, 576)
    normed_all, attend_cols, expand_cols, g2, vectors = gather_inputs(
        tokens, vectors, attend_cols, expand_weight, cotangent
    )
    wq, wk, wv = attend_cols[:, :192], attend_cols[:, 192:384], attend_cols[:, 384:]
    bias = lax.dynamic_slice(vectors, (0, part * 192), (2, 192))
    own = lax.dynamic_slice(normed_all, (ctx * block, 0), (block, D))
    where, begins_row = places_of(document_starts, block)
    q, k, v, o, lse = attend_forward(where, normed_all, own, wq, wk, wv, bias, begins_row)
    return normed_all, attend_cols, expand_cols, g2, vectors, q, k, v, o, lse


def places_of(document_starts, block):
    ctx = lax.axis_index("ctx")
    places = ctx * block + jnp.arange(block, dtype=jnp.int32)
    begins = first_position(places, document_starts)
    where = jnp.stack([ctx, begins[0], begins[-1]]).astype(jnp.int32)
    return where, begins.reshape(1, block)


def forward(tokens, document_starts, attend_weight, attend_bias, expand_weight, cotangent, own_vectors):
    rows = tokens.shape[0]
    if lax.axis_size("ctx") != 8:
        return forward_plain(
            tokens, document_starts, attend_weight, attend_bias, expand_weight, cotangent, own_vectors
        )
    listed = [attend_bias[:rows], attend_bias[rows:]] + list(own_vectors)
    line = lax.broadcasted_iota(jnp.int32, (8, rows), 0)
    vectors = jnp.zeros((8, rows), F32)
    for i, vector in enumerate(listed):
        vectors = jnp.where(line == i, vector.astype(F32)[None, :], vectors)
    return gather_attend(document_starts, tokens, vectors, attend_weight, expand_weight, cotangent)


def backward_plain(
    document_starts, normed_all, k, v, q, o, lse, g1, project_weight, attend_cols,
    contract_part, expand_part, tokens, grad_middle, vectors, mlp_sums,
):
    both = ("ctx", "fsdp")
    rows = tokens.shape[0]
    ways = lax.axis_size("fsdp")
    block = rows * ways
    ctx = lax.axis_index("ctx")
    part = lax.axis_index("fsdp")
    gain_one = vectors[4]
    wq, wk, wv = attend_cols[:, :192], attend_cols[:, 192:384], attend_cols[:, 384:]
    where, begins_row = places_of(document_starts, block)
    own = lax.dynamic_slice(normed_all, (ctx * block, 0), (block, D))
    dn, attend_t, project_part, sums = attend_backward(
        where, normed_all, k, v, own, q, o, lse, g1, project_weight, wq, wk, wv, begins_row
    )
    grad_normed = lax.psum_scatter(dn.astype(F32), both, scatter_dimension=0, tiled=True)
    normed, unit_one, inverse_one = normalize(tokens.astype(F32), gain_one, jnp.zeros_like(gain_one))
    first_part, gainone_grad, shiftone_grad = normalize_back(grad_normed, unit_one, inverse_one, gain_one)
    tokens_grad = (grad_middle + first_part).astype(BF)

    def summed(array_in):
        return lax.psum(array_in.astype(BF), "ctx").astype(F32)

    contract_grad = summed(contract_part)
    project_grad = summed(project_part)
    expand_grad = lax.all_to_all(summed(expand_part).reshape(ways, rows, D), "fsdp", 0, 0)
    expand_grad = expand_grad.transpose(1, 0, 2).reshape(rows, ways * D)
    attend_grad = lax.all_to_all(summed(attend_t.T).reshape(ways, rows, 576), "fsdp", 0, 0)
    attend_grad = attend_grad.reshape(ways, rows, 3, 192).transpose(1, 2, 0, 3).reshape(rows, 3 * D)
    spread = lax.dynamic_update_slice(jnp.zeros((2, D), F32), sums[:2], (0, part * 192))
    hidden = lax.dynamic_update_slice(jnp.zeros((4, D), F32), mlp_sums[4:5], (part, 0))
    totals = jnp.concatenate([
        spread, mlp_sums[0:2], gainone_grad[None], shiftone_grad[None], mlp_sums[2:4], hidden
    ])
    totals = lax.psum(totals, both)
    attbias = lax.dynamic_slice(totals[:2].reshape(-1), (part * 2 * rows,), (2 * rows,))
    mine = lax.dynamic_slice(totals, (2, part * rows), (6, rows))
    expbias = lax.dynamic_slice(totals, (8 + part, 0), (1, D)).reshape(D)
    return (
        tokens_grad, attend_grad, attbias, project_grad, mine[0], expand_grad, expbias,
        contract_grad, mine[1], mine[2], mine[3], mine[4], mine[5],
    )


def per_device(
    tokens, document_starts, attend_weight, attend_bias, project_weight, project_bias,
    expand_weight, expand_bias, contract_weight, contract_bias,
    gain_first, shift_first, gain_second, shift_second, cotangent,
):
    both = ("ctx", "fsdp")
    rows = tokens.shape[0]
    ways = lax.axis_size("fsdp")
    block = rows * ways
    ctx = lax.axis_index("ctx")
    part = lax.axis_index("fsdp")

    def whole(array_in):
        return lax.all_gather(array_in, "fsdp", axis=0, tiled=True)

    normed_all, attend_cols, expand_cols, g2, vectors, q, k, v, o, lse = forward(
        tokens, document_starts, attend_weight, attend_bias, expand_weight, cotangent,
        (project_bias, contract_bias, gain_first, shift_first, gain_second, shift_second),
    )
    block_output, grad_middle, g1, contract_part, expand_part, mlp_sums = feed_forward(
        o, project_weight, expand_cols, contract_weight, expand_bias.astype(F32).reshape(1, D), tokens, cotangent, g2, vectors
    )
    if lax.axis_size("ctx") != 8:
        return (block_output,) + backward_plain(
            document_starts, normed_all, k, v, q, o, lse, g1, project_weight, attend_cols,
            contract_part, expand_part, tokens, grad_middle, vectors, mlp_sums,
        )
    tokens_grad, contract_grad, expand_grad, attend_grad, project_grad, small, hidden = attend_reduce(
        document_starts, normed_all, k, v, q, o, lse, g1, project_weight, attend_cols,
        contract_part.reshape(8, 96, D), expand_part.reshape(8, 96, D), tokens, grad_middle, vectors, mlp_sums,
    )
    return (
        block_output, tokens_grad, attend_grad, small[:2].reshape(-1), project_grad.astype(F32), small[2],
        expand_grad.astype(F32), hidden.reshape(-1), contract_grad.reshape(D, D).astype(F32),
        small[3], small[4], small[5], small[6], small[7],
    )


def solution(mesh):
    tok, row, vec = P(("ctx", "fsdp"), None), P("fsdp", None), P("fsdp")
    in_specs = (tok, P(), row, vec, row, vec, row, vec, row, vec, vec, vec, vec, vec, tok)
    out_specs = (tok, tok, row, vec, row, vec, row, vec, row, vec, vec, vec, vec, vec)
    return jax.shard_map(per_device, mesh=mesh, in_specs=in_specs, out_specs=out_specs, check_vma=False)
```

```python
import functools
import jax
import jax.numpy as jnp
from jax import lax
from jax.experimental import pallas as pl
from jax.experimental.pallas import tpu as pltpu
from jax.sharding import PartitionSpec as P

D = 768
H = 12
HD = 64
EPS = 1e-05
SCALE = 0.125
BRANCH = 48.0 ** (-0.5)
NEG = -1e30
SUB = 768
STRIP = 256
QS = STRIP
LEAD = 4
BACK_LEAD = 2
BF = jnp.bfloat16
F32 = jnp.float32


def mm(a, b):
    return jnp.dot(a, b, preferred_element_type=F32)


def mm_nt(a, b):
    return lax.dot_general(a, b, (((1,), (1,)), ((), ())), preferred_element_type=F32)


def mm_tn(a, b):
    return lax.dot_general(a, b, (((0,), (0,)), ((), ())), preferred_element_type=F32)


def head_lanes(head):
    return slice(0, 128) if head < 2 else slice(128, 192)


def fill_masked_columns(target, flipped):
    zero = jnp.zeros((HD, flipped.shape[1]), BF)
    target[0, 0:HD, :] = flipped[0:HD]
    target[0, HD : 2 * HD, :] = zero
    target[1, 0:HD, :] = zero
    target[1, HD : 2 * HD, :] = flipped[HD : 2 * HD]
    target[2, 0:HD, :] = flipped[2 * HD : 3 * HD]


def masked_rows(array_in, head):
    if head == 2:
        return array_in[:, 128:192]
    pair = array_in[:, 0:128]
    lane = lax.broadcasted_iota(jnp.int32, pair.shape, 1)
    return jnp.where((lane < HD) if head == 0 else (lane >= HD), pair, jnp.zeros_like(pair))


def allowed_pairs(first_key, first_query, begins, shape):
    key_places = first_key + lax.broadcasted_iota(jnp.int32, shape, 0)
    query_places = first_query + lax.broadcasted_iota(jnp.int32, shape, 1)
    return (key_places <= query_places) & (key_places >= begins)


def attend_forward_kernel(
    where_ref, rows_ref, own_ref, wq_ref, wk_ref, wv_ref, bias_ref, begins_ref,
    q_out, k_out, v_out, o_out, lse_out,
    qm, vt, peak, total, acc,
):
    turn = pl.program_id(0)
    block = own_ref.shape[0]
    mine, begin_low, begin_high = where_ref[0], where_ref[1], where_ref[2]
    first_query = mine * block
    needed = (turn <= mine) & ((turn + 1) * block - 1 >= begin_low)

    @pl.when(turn == 0)
    def _():
        query = (mm(own_ref[...], wq_ref[...]) + bias_ref[0:1, :]).astype(BF)
        q_out[...] = query
        fill_masked_columns(qm, (query.astype(F32) * SCALE).T.astype(BF))
        peak[...] = jnp.full(peak.shape, NEG, F32)
        total[...] = jnp.zeros(total.shape, F32)
        acc[...] = jnp.zeros(acc.shape, F32)

    @pl.when(needed)
    def _():
        rows = rows_ref[...]
        k_out[...] = mm(rows, wk_ref[...]).astype(BF)
        value = (mm(rows, wv_ref[...]) + bias_ref[1:2, :]).astype(BF)
        v_out[...] = value
        vt[...] = value.astype(F32).T.astype(BF)

        def one(step, masked):
            at = pl.ds(pl.multiple_of(step * SUB, SUB), SUB)
            first_key = turn * block + step * SUB
            if masked:
                allowed = allowed_pairs(first_key, first_query, begins_ref[...], (SUB, block))
            strips = [(head, strip) for head in range(3) for strip in range(block // QS)]

            def scored(head, strip):
                depth = 128 if head < 2 else HD
                return mm(k_out[at, head_lanes(head)], qm[head, 0:depth, strip * QS : strip * QS + QS])

            ahead = [scored(*strips[i]) for i in range(LEAD)]
            for i, (head, strip) in enumerate(strips):
                scores = ahead.pop(0)
                if i + LEAD < len(strips):
                    ahead.append(scored(*strips[i + LEAD]))
                lanes = slice(strip * QS, strip * QS + QS)
                if masked:
                    scores = jnp.where(allowed[:, lanes], scores, NEG)
                old = peak[head : head + 1, lanes]
                new = jnp.maximum(old, jnp.max(scores, axis=0, keepdims=True))
                weights = jnp.exp(scores - new)
                if masked:
                    weights = jnp.where(allowed[:, lanes], weights, 0.0)
                factor = jnp.exp(old - new)
                peak[head : head + 1, lanes] = new
                total[head : head + 1, lanes] = total[head : head + 1, lanes] * factor + jnp.sum(
                    weights, axis=0, keepdims=True
                )
                part = slice(head * HD, head * HD + HD)
                acc[part, lanes] = acc[part, lanes] * factor + mm(vt[part, at], weights.astype(BF))

        @pl.loop(0, block // SUB)
        def _(step):
            first_key = turn * block + step * SUB
            inner = (first_key + SUB - 1 <= first_query) & (first_key >= begin_high)
            touched = first_key + SUB - 1 >= begin_low

            @pl.when(inner)
            def _():
                one(step, False)

            @pl.when(jnp.logical_not(inner) & touched)
            def _():
                one(step, True)

    @pl.when(turn == mine)
    def _():
        for head in range(3):
            part = slice(head * HD, head * HD + HD)
            o_out[part, :] = acc[part, :] / total[head : head + 1, :]
        lse_out[...] = peak[...] + jnp.log(jnp.maximum(total[...], 1e-30))


def attend_forward(where, rows_all, own, wq, wk, wv, bias, begins):
    block = own.shape[0]
    count = rows_all.shape[0] // block

    def seen(turn, where_ref):
        return (jnp.minimum(turn, where_ref[0]), 0)

    def fixed(turn, where_ref):
        return (0, 0)

    return pl.pallas_call(
        attend_forward_kernel,
        grid_spec=pltpu.PrefetchScalarGridSpec(
            num_scalar_prefetch=1,
            grid=(count,),
            in_specs=[
                pl.BlockSpec((block, D), seen),
                pl.BlockSpec((block, D), fixed),
                pl.BlockSpec((D, 192), fixed),
                pl.BlockSpec((D, 192), fixed),
                pl.BlockSpec((D, 192), fixed),
                pl.BlockSpec((2, 192), fixed),
                pl.BlockSpec((1, block), fixed),
            ],
            out_specs=[
                pl.BlockSpec((block, 192), fixed),
                pl.BlockSpec((block, 192), seen),
                pl.BlockSpec((block, 192), seen),
                pl.BlockSpec((192, block), fixed),
                pl.BlockSpec((8, block), fixed),
            ],
            scratch_shapes=[
                pltpu.VMEM((3, 128, block), BF),
                pltpu.VMEM((192, block), BF),
                pltpu.VMEM((8, block), F32),
                pltpu.VMEM((8, block), F32),
                pltpu.VMEM((192, block), F32),
            ],
        ),
        out_shape=[
            jax.ShapeDtypeStruct((block, 192), BF),
            jax.ShapeDtypeStruct((block * count, 192), BF),
            jax.ShapeDtypeStruct((block * count, 192), BF),
            jax.ShapeDtypeStruct((192, block), F32),
            jax.ShapeDtypeStruct((8, block), F32),
        ],
        compiler_params=pltpu.CompilerParams(vmem_limit_bytes=48 << 20),
        name="attend_forward",
    )(where, rows_all, own, wq, wk, wv, bias, begins)


def attend_backward_kernel(
    where_ref, rows_ref, k_ref, v_ref, own_ref, q_ref, o_ref, lse_ref, g_ref, wp_ref,
    wq_ref, wk_ref, wv_ref, begins_ref,
    dn_out, grad_out, proj_out, sums_out,
    qm, dm, qn, dn, delta, dqt, kt, dk, dv,
):
    turn = pl.program_id(0)
    block = own_ref.shape[0]
    mine, begin_low, begin_high = where_ref[0], where_ref[1], where_ref[2]
    first_query = mine * block
    needed = (turn <= mine) & ((turn + 1) * block - 1 >= begin_low)

    @pl.when(turn == 0)
    def _():
        grads = g_ref[...]
        exact = o_ref[...]
        proj_out[...] = mm(exact.astype(BF), grads)
        outer = mm_nt(grads, wp_ref[...]).astype(BF)
        flipped = outer.astype(F32).T
        product = flipped * exact
        for head in range(3):
            delta[head : head + 1, :] = jnp.sum(
                product[head * HD : head * HD + HD], axis=0, keepdims=True
            )
        fill_masked_columns(dm, flipped.astype(BF))
        scaled = (q_ref[...].astype(F32) * SCALE)
        fill_masked_columns(qm, scaled.T.astype(BF))
        scaled = scaled.astype(BF)
        for head in range(3):
            depth = 128 if head < 2 else HD
            qn[head, :, 0:depth] = masked_rows(scaled, head)
            dn[head, :, 0:depth] = masked_rows(outer, head)
        dqt[...] = jnp.zeros(dqt.shape, F32)
        grad_out[...] = jnp.zeros(grad_out.shape, F32)
        sums_out[...] = jnp.zeros(sums_out.shape, F32)

    @pl.when(jnp.logical_not(needed))
    def _():
        dn_out[...] = jnp.zeros(dn_out.shape, BF)

    @pl.when(needed)
    def _():
        kt[...] = k_ref[...].astype(F32).T.astype(BF)
        dk[...] = jnp.zeros(dk.shape, F32)
        dv[...] = jnp.zeros(dv.shape, F32)

        def one(step, masked):
            at = pl.ds(pl.multiple_of(step * SUB, SUB), SUB)
            first_key = turn * block + step * SUB
            if masked:
                allowed = allowed_pairs(first_key, first_query, begins_ref[...], (SUB, block))
            for head in range(3):
                depth = 128 if head < 2 else HD
                lanes = head_lanes(head)
                scores = mm(k_ref[at, lanes], qm[head, 0:depth, :])
                probs = jnp.exp(scores - lse_ref[head : head + 1, :])
                if masked:
                    probs = jnp.where(allowed, probs, 0.0)
                outer = mm(v_ref[at, lanes], dm[head, 0:depth, :])
                inner = (probs * (outer - delta[head : head + 1, :])).astype(BF)
                dv[at, lanes] += mm(probs.astype(BF), dn[head, :, 0:depth])
                dk[at, lanes] += mm(inner, qn[head, :, 0:depth])
                part = slice(head * HD, head * HD + HD)
                dqt[part, :] += mm(kt[part, at], inner)

        @pl.loop(0, block // SUB)
        def _(step):
            first_key = turn * block + step * SUB
            inner = (first_key + SUB - 1 <= first_query) & (first_key >= begin_high)
            touched = first_key + SUB - 1 >= begin_low

            @pl.when(inner)
            def _():
                one(step, False)

            @pl.when(jnp.logical_not(inner) & touched)
            def _():
                one(step, True)

        rows = rows_ref[...]
        low_k = dk[...].astype(BF)
        low_v = dv[...].astype(BF)
        grad_out[192:384, :] += mm(low_k.astype(F32).T.astype(BF), rows)
        grad_out[384:576, :] += mm(low_v.astype(F32).T.astype(BF), rows)
        sums_out[1:2, :] += jnp.sum(low_v.astype(F32), axis=0, keepdims=True)
        through = mm_nt(low_k, wk_ref[...]) + mm_nt(low_v, wv_ref[...])

        @pl.when(turn < mine)
        def _():
            dn_out[...] = through.astype(BF)

        @pl.when(turn == mine)
        def _():
            flipped = dqt[...] * SCALE
            low_q = flipped.T.astype(BF)
            grad_out[0:192, :] += mm(flipped.astype(BF), own_ref[...])
            sums_out[0:1, :] += jnp.sum(low_q.astype(F32), axis=0, keepdims=True)
            dn_out[...] = (through + mm_nt(low_q, wq_ref[...])).astype(BF)


def attend_backward(where, rows_all, k, v, own, q, o, lse, g, wp, wq, wk, wv, begins):
    block = own.shape[0]
    count = rows_all.shape[0] // block

    def seen(turn, where_ref):
        return (jnp.minimum(turn, where_ref[0]), 0)

    def each(turn, where_ref):
        return (turn, 0)

    def fixed(turn, where_ref):
        return (0, 0)

    return pl.pallas_call(
        attend_backward_kernel,
        grid_spec=pltpu.PrefetchScalarGridSpec(
            num_scalar_prefetch=1,
            grid=(count,),
            in_specs=[
                pl.BlockSpec((block, D), seen),
                pl.BlockSpec((block, 192), seen),
                pl.BlockSpec((block, 192), seen),
                pl.BlockSpec((block, D), fixed),
                pl.BlockSpec((block, 192), fixed),
                pl.BlockSpec((192, block), fixed),
                pl.BlockSpec((8, block), fixed),
                pl.BlockSpec((block, D), fixed),
                pl.BlockSpec((192, D), fixed),
                pl.BlockSpec((D, 192), fixed),
                pl.BlockSpec((D, 192), fixed),
                pl.BlockSpec((D, 192), fixed),
                pl.BlockSpec((1, block), fixed),
            ],
            out_specs=[
                pl.BlockSpec((block, D), each),
                pl.BlockSpec((576, D), fixed),
                pl.BlockSpec((192, D), fixed),
                pl.BlockSpec((8, 192), fixed),
            ],
            scratch_shapes=[
                pltpu.VMEM((3, 128, block), BF),
                pltpu.VMEM((3, 128, block), BF),
                pltpu.VMEM((3, block, 128), BF),
                pltpu.VMEM((3, block, 128), BF),
                pltpu.VMEM((8, block), F32),
                pltpu.VMEM((192, block), F32),
                pltpu.VMEM((192, block), BF),
                pltpu.VMEM((block, 192), F32),
                pltpu.VMEM((block, 192), F32),
            ],
        ),
        out_shape=[
            jax.ShapeDtypeStruct((block * count, D), BF),
            jax.ShapeDtypeStruct((576, D), F32),
            jax.ShapeDtypeStruct((192, D), F32),
            jax.ShapeDtypeStruct((8, 192), F32),
        ],
        compiler_params=pltpu.CompilerParams(vmem_limit_bytes=48 << 20),
        name="attend_backward",
    )(where, rows_all, k, v, own, q, o, lse, g, wp, wq, wk, wv, begins)


MESH = pl.DeviceIdType.MESH


class Place:
    def __init__(self):
        ctx = lax.axis_index("ctx")
        part = lax.axis_index("fsdp")
        self.levels = lax.axis_size("ctx") // 2
        self.ctx, self.part = ctx, part
        self.level, self.side = ctx // 2, ctx % 2
        self.half, self.core = part // 2, part % 2

    def at(self, level=None, side=None, half=None, core=None):
        level = self.level if level is None else level
        side = self.side if side is None else side
        half = self.half if half is None else half
        core = self.core if core is None else core
        return (level * 2 + side, half * 2 + core)

    @property
    def twin(self):
        return self.at(core=1 - self.core)

    @property
    def across(self):
        return self.at(half=1 - self.half)

    @property
    def corner(self):
        return self.at(half=1 - self.half, core=1 - self.core)

    @property
    def beside(self):
        return self.at(side=1 - self.side)


def remote(source, target, send, recv, device):
    return pltpu.make_async_remote_copy(
        src_ref=source, dst_ref=target, send_sem=send, recv_sem=recv, device_id=device, device_id_type=MESH
    )


def signal(sem, device):
    pl.semaphore_signal(sem, inc=1, device_id=device, device_id_type=MESH)


def piece(ref, ctx, part):
    rows = 192
    return ref.at[pl.ds(pl.multiple_of((ctx * 4 + part) * rows, rows), rows)]


def rows_of(ref, part):
    return ref.at[pl.ds(pl.multiple_of(part * 192, 192), 192)]


def layer_norm(rows_in, gain, shift):
    mean = jnp.mean(rows_in, axis=1, keepdims=True)
    centered = rows_in - mean
    inverse = lax.rsqrt(jnp.mean(centered * centered, axis=1, keepdims=True) + EPS)
    unit = centered * inverse
    return unit * gain + shift, unit, inverse


def gather_kernel(
    levels, tok_ref, vec_ref, acol_ref, ecol_ref, cot_ref,
    all_ref, attend_ref, expand_ref, gtwo_ref, vec_out,
    normed, gtwo, vec_in,
    vec_send, vec_recv, att_send, att_recv, exp_send, exp_recv, two_send, two_recv,
    x_send, x_recv, z_send, z_recv, y_send, y_recv, core_send, core_recv, local_sem,
):
    me = Place()
    mine = me.part
    barrier = pltpu.get_barrier_semaphore()
    for device in (me.twin, me.across, me.corner, me.beside):
        signal(barrier, device)

    @pl.when(me.level > 0)
    def _():
        signal(barrier, me.at(level=me.level - 1))

    @pl.when(me.level < levels - 1)
    def _():
        signal(barrier, me.at(level=me.level + 1))

    ends = (me.level == 0).astype(jnp.int32) + (me.level == levels - 1).astype(jnp.int32)
    pl.semaphore_wait(barrier, 6 - ends)

    peers = (
        (me.twin, me.half * 2 + 1 - me.core),
        (me.across, (1 - me.half) * 2 + me.core),
        (me.corner, (1 - me.half) * 2 + 1 - me.core),
    )
    vecs = [remote(vec_ref, vec_in.at[i], vec_send.at[i], vec_recv.at[i], d) for i, (d, p) in enumerate(peers)]
    for copy in vecs:
        copy.start()
    atts = [
        remote(acol_ref.at[p], rows_of(attend_ref, mine), att_send.at[i], att_recv.at[i], d)
        for i, (d, p) in enumerate(peers)
    ]
    for copy in atts:
        copy.start()
    local = [
        pltpu.make_async_copy(acol_ref.at[mine], rows_of(attend_ref, mine), local_sem.at[0]),
        pltpu.make_async_copy(ecol_ref.at[:, pl.ds(pl.multiple_of(mine * D, D), D)], rows_of(expand_ref, mine), local_sem.at[1]),
    ]
    for copy in local:
        copy.start()
    gtwo[...] = (BRANCH * cot_ref[...].astype(F32)).astype(BF)
    for copy in vecs:
        copy.wait_recv()
    vec_out[...] = vec_ref[...] + vec_in[0] + vec_in[1] + vec_in[2]
    out, unit, inverse = layer_norm(tok_ref[...].astype(F32), vec_out[4:5, :], vec_out[5:6, :])
    normed[...] = out.astype(BF)

    def go(copy):
        copy.start()
        return copy

    ctx = me.ctx
    across = go(remote(normed, piece(all_ref, ctx, mine), x_send.at[0], x_recv.at[0], me.across))
    keep = go(pltpu.make_async_copy(normed, piece(all_ref, ctx, mine), local_sem.at[2]))
    keep_two = go(pltpu.make_async_copy(gtwo, rows_of(gtwo_ref, mine), local_sem.at[3]))
    local += [keep, keep_two]

    def spread_static(source, distance, slot):
        level = me.level - distance
        where = level * 2 + me.side
        half = me.half if slot == 0 else 1 - me.half
        part = half * 2 + me.core

        @pl.when(me.level < levels - 1)
        def _():
            remote(source, piece(all_ref, where, part), z_send.at[distance, slot], z_recv.at[distance + 1, slot], me.at(level=me.level + 1)).start()

        remote(source, piece(all_ref, where, part), y_send.at[distance, slot], y_recv.at[distance, slot], me.beside).start()
        remote(source, piece(all_ref, where, part), core_send.at[distance, 0, slot], core_recv.at[distance, 0, slot], me.twin).start()

    spread_static(normed, 0, 0)
    exps = [
        go(remote(ecol_ref.at[:, pl.ds(pl.multiple_of(p * D, D), D)], rows_of(expand_ref, mine), exp_send.at[i], exp_recv.at[i], d))
        for i, (d, p) in enumerate(peers)
    ]
    two_x = go(remote(gtwo, rows_of(gtwo_ref, mine), two_send.at[0], two_recv.at[0], me.across))
    two_c = go(remote(gtwo, rows_of(gtwo_ref, mine), two_send.at[1], two_recv.at[1], me.twin))

    other = (1 - me.half) * 2 + me.core

    def held(distance, slot, side):
        half = me.half if slot == 0 else 1 - me.half
        return piece(all_ref, (me.level - distance) * 2 + side, half * 2 + me.core)

    def take_y(distance):
        for slot in range(2):
            got = held(distance, slot, 1 - me.side)
            remote(got, got, y_send.at[distance, slot], y_recv.at[distance, slot], me.beside).wait_recv()
            remote(got, got, core_send.at[distance, 1, slot], core_recv.at[distance, 1, slot], me.twin).start()

    got = piece(all_ref, ctx, other)
    remote(normed, got, x_send.at[0], x_recv.at[0], me.across).wait_recv()
    spread_static(got, 0, 1)
    for distance in range(1, levels):

        @pl.when(me.level >= distance)
        def _():
            for slot in range(2):
                got = held(distance, slot, me.side)
                remote(got, got, z_send.at[distance, slot], z_recv.at[distance, slot], me.twin).wait_recv()
                spread_static(got, distance, slot)

        if distance == 1:
            take_y(0)
        else:

            @pl.when(me.level >= distance - 1)
            def _():
                take_y(distance - 1)

    @pl.when(me.level >= levels - 1)
    def _():
        take_y(levels - 1)

    got = rows_of(gtwo_ref, other)
    remote(gtwo, got, two_send.at[0], two_recv.at[0], me.across).wait_recv()
    two_f = go(remote(got, got, two_send.at[2], two_recv.at[2], me.twin))
    for copy in local:
        copy.wait()
    for copy in vecs:
        copy.wait_send()
    for copy in atts + exps + [two_c, two_f]:
        copy.wait()
    two_x.wait_send()
    across.wait_send()
    for distance in range(levels):

        @pl.when(me.level >= distance)
        def _():
            for slot in range(2):
                got = held(distance, slot, me.side)

                @pl.when(me.level < levels - 1)
                def _():
                    remote(got, got, z_send.at[distance, slot], z_recv.at[distance, slot], me.twin).wait_send()

                remote(got, got, y_send.at[distance, slot], y_recv.at[distance, slot], me.beside).wait_send()
                for side in range(2):
                    remote(got, got, core_send.at[distance, side, slot], core_recv.at[distance, side, slot], me.twin).wait()


def gather_inputs(tokens, vectors, attend_cols, expand_weight, cotangent):
    levels = lax.axis_size("ctx") // 2
    rows = tokens.shape[0]
    block = rows * 4
    vmem = pl.BlockSpec(memory_space=pltpu.VMEM)
    anywhere = pl.BlockSpec(memory_space=pl.ANY)
    dma = pltpu.SemaphoreType.DMA
    return pl.pallas_call(
        functools.partial(gather_kernel, levels),
        in_specs=[vmem, vmem, anywhere, anywhere, vmem],
        out_specs=[anywhere, anywhere, anywhere, anywhere, vmem],
        out_shape=[
            jax.ShapeDtypeStruct((block * levels * 2, D), BF),
            jax.ShapeDtypeStruct((D, 576), BF),
            jax.ShapeDtypeStruct((D, D), BF),
            jax.ShapeDtypeStruct((block, D), BF),
            jax.ShapeDtypeStruct((8, D), F32),
        ],
        scratch_shapes=[
            pltpu.VMEM((rows, D), BF),
            pltpu.VMEM((rows, D), BF),
            pltpu.VMEM((3, 8, D), F32),
            dma((3,)), dma((3,)), dma((3,)), dma((3,)), dma((3,)), dma((3,)), dma((3,)), dma((3,)),
            dma((1,)), dma((1,)),
            dma((levels, 2)), dma((levels + 1, 2)),
            dma((levels, 2)), dma((levels, 2)),
            dma((levels, 2, 2)), dma((levels, 2, 2)),
            dma((4,)),
        ],
        compiler_params=pltpu.CompilerParams(collective_id=1, has_side_effects=True, vmem_limit_bytes=16 << 20),
        name="gather_inputs",
    )(tokens, vectors, attend_cols, expand_weight, cotangent)


SHARE = 160


def begins_of(starts_ref, first, count):
    places = first + lax.broadcasted_iota(jnp.int32, (1, count), 1)
    begins = jnp.zeros((1, count), jnp.int32)
    for document in range(8):
        start = starts_ref[document]
        begins = jnp.where(places >= start, jnp.maximum(begins, start), begins)
    return begins


def gather_attend_kernel(
    levels, starts_ref, tok_hbm, aw_hbm, ew_ref, cot_hbm, *rest_refs,
):
    vector_hbm, vector_refs = rest_refs[:7], rest_refs[-7:]
    (
        all_ref, attend_ref, expand_ref, gtwo_ref, vec_out, q_out, k_out, v_out, o_out, lse_out,
        tok_ref, aw_ref, cot_ref, vec_ref, staged, vec_in, begins, qm, vt, acc, peak, total,
        vec_send, vec_recv, att_send, att_recv, exp_send, exp_recv, two_send, two_recv,
        x_send, x_recv, z_send, z_recv, y_send, y_recv, core_send, core_recv, r_send, r_recv, rc_send, rc_recv, local_sem,
    ) = rest_refs[7:-7]
    me = Place()
    mine, z, side = me.part, me.level, me.side
    top = levels - 1
    block = gtwo_ref.shape[0]
    fetched = (
        pltpu.make_async_copy(tok_hbm, tok_ref, local_sem.at[1]),
        pltpu.make_async_copy(aw_hbm, aw_ref, local_sem.at[2]),
        pltpu.make_async_copy(cot_hbm, cot_ref, local_sem.at[3]),
    ) + tuple(
        pltpu.make_async_copy(source, target, local_sem.at[4 + i])
        for i, (source, target) in enumerate(zip(vector_hbm, vector_refs))
    )
    for copy in fetched:
        copy.start()
    barrier = pltpu.get_barrier_semaphore()
    for device in (me.twin, me.across, me.corner, me.beside):
        signal(barrier, device)

    @pl.when(z > 0)
    def _():
        signal(barrier, me.at(level=z - 1))

    @pl.when(z < top)
    def _():
        signal(barrier, me.at(level=z + 1))

    for copy in fetched:
        copy.wait()
    both = vector_refs[0][...].astype(F32).reshape(1, 384)
    vec_ref[0:1, :] = both[:, 0:192]
    vec_ref[1:2, :] = both[:, 192:384]
    for i, ref in enumerate(vector_refs[1:]):
        vec_ref[2 + i : 3 + i, :] = ref[...].astype(F32).reshape(1, 192)
    for part in range(4):
        for kind in range(3):
            staged[part, :, kind * 192 : kind * 192 + 192] = aw_ref[:, kind * D + part * 192 : kind * D + part * 192 + 192]
    ends = (z == 0).astype(jnp.int32) + (z == top).astype(jnp.int32)
    pl.semaphore_wait(barrier, 6 - ends)

    peers = (
        (me.twin, me.half * 2 + 1 - me.core),
        (me.across, (1 - me.half) * 2 + me.core),
        (me.corner, (1 - me.half) * 2 + 1 - me.core),
    )

    def go(copy):
        copy.start()
        return copy

    vecs = [go(remote(vec_ref, vec_in.at[mine], vec_send.at[i], vec_recv.at[i], d)) for i, (d, p) in enumerate(peers)]
    atts = [
        remote(staged.at[p], rows_of(attend_ref, mine), att_send.at[i], att_recv.at[i], d) for i, (d, p) in enumerate(peers)
    ]
    atts[0].start()
    atts[1].start()
    vec_in[mine] = vec_ref[...]
    rows_of(attend_ref, mine)[...] = staged[mine]
    local = [
        go(pltpu.make_async_copy(
            ew_ref.at[:, pl.ds(pl.multiple_of(mine * D, D), D)], rows_of(expand_ref, mine), local_sem.at[0]
        ))
    ]
    own_two = rows_of(gtwo_ref, mine)
    own_two[...] = (BRANCH * cot_ref[...].astype(F32)).astype(BF)
    for i, (d, p) in enumerate(peers):
        remote(vec_ref, vec_in.at[p], vec_send.at[i], vec_recv.at[i], d).wait_recv()
    for part in range(4):
        vec_out[:, part * 192 : part * 192 + 192] = vec_in[part]
    out, unit, inverse = layer_norm(tok_ref[...].astype(F32), vec_out[4:5, :], vec_out[5:6, :])
    own_rows = piece(all_ref, me.ctx, mine)
    own_rows[...] = out.astype(BF)
    across = go(remote(own_rows, own_rows, x_send.at[0], x_recv.at[0], me.across))
    atts[2].start()

    def most(ref):
        return ref.at[pl.ds(0, SHARE)]

    def rest(ref):
        return ref.at[pl.ds(SHARE, 192 - SHARE)]

    def held(distance, slot, where):
        half = me.half + slot * (1 - 2 * me.half)
        return piece(all_ref, (z - distance) * 2 + where, half * 2 + me.core)

    def y_copy(distance, slot, where, whole):
        got = held(distance, slot, where)
        if not whole:
            got = most(got)
        return remote(got, got, y_send.at[distance, slot], y_recv.at[distance, slot], me.beside)

    def rest_up(distance, slot):
        got = rest(held(distance, slot, 1 - side))
        return remote(got, got, r_send.at[distance, slot], r_recv.at[distance + 1, slot], me.at(level=z + 1))

    def rest_twin(distance, slot):
        got = rest(held(distance, slot, 1 - side))
        return remote(got, got, rc_send.at[distance, slot], rc_recv.at[distance, slot], me.twin)

    def spread(distance, slot, first):
        half = me.half + slot * (1 - 2 * me.half)
        got = piece(all_ref, (z - distance) * 2 + side, half * 2 + me.core)

        @pl.when(z < top)
        def _():
            remote(got, got, z_send.at[distance, slot], z_recv.at[distance + 1, slot], me.at(level=z + 1)).start()

        y_copy(distance, slot, side, first).start()
        remote(got, got, core_send.at[distance, 0, slot], core_recv.at[distance, 0, slot], me.twin).start()

    def from_twin(distance, which, where, whole):
        for slot in range(2):
            half = me.half + slot * (1 - 2 * me.half)
            got = piece(all_ref, (z - distance) * 2 + where, half * 2 + 1 - me.core)
            if not whole:
                last = rest(got)
                remote(last, last, rc_send.at[distance, slot], rc_recv.at[distance, slot], me.twin).wait_recv()
                got = most(got)
            remote(got, got, core_send.at[distance, which, slot], core_recv.at[distance, which, slot], me.twin).wait_recv()

    spread(0, 0, True)
    two_x = go(remote(own_two, own_two, two_send.at[0], two_recv.at[0], me.across))
    two_c = go(remote(own_two, own_two, two_send.at[1], two_recv.at[1], me.twin))
    exps = [
        go(remote(ew_ref.at[:, pl.ds(pl.multiple_of(p * D, D), D)], rows_of(expand_ref, mine), exp_send.at[i], exp_recv.at[i], d))
        for i, (d, p) in enumerate(peers)
    ]
    begins[...] = begins_of(starts_ref, me.ctx * block, block)
    got = held(0, 1, side)
    remote(got, got, x_send.at[0], x_recv.at[0], me.across).wait_recv()
    spread(0, 1, True)
    def from_below(distance, slot):
        @pl.when(distance <= z)
        def _():
            got = held(distance, slot, side)
            remote(got, got, z_send.at[distance - 1, slot], z_recv.at[distance, slot], me.twin).wait_recv()
            spread(distance, slot, False)

    from_below(1, 0)
    for copy in atts:
        copy.wait_recv()
    from_twin(0, 0, side, True)

    first_query = me.ctx * block
    bias_q = vec_in[mine // 2, pl.ds(mine % 2, 1), :]
    query = (mm(all_ref[pl.ds(pl.multiple_of(first_query, block), block), :], attend_ref[:, 0:192]) + bias_q).astype(BF)
    q_out[...] = query
    fill_masked_columns(qm, (query.astype(F32) * SCALE).T.astype(BF))
    peak[...] = jnp.full(peak.shape, NEG, F32)
    total[...] = jnp.zeros(total.shape, F32)
    acc[...] = jnp.zeros(acc.shape, F32)

    def attend(ctx, diagonal):
        first_key = ctx * block
        at = pl.ds(pl.multiple_of(first_key, block), block)
        rows = all_ref[at, :]
        key = mm(rows, attend_ref[:, 192:384]).astype(BF)
        k_out[at, :] = key
        value = (mm(rows, attend_ref[:, 384:576]) + vec_in[2 + mine // 2, pl.ds(mine % 2, 1), :]).astype(BF)
        v_out[at, :] = value
        vt[...] = value.astype(F32).T.astype(BF)
        strips = [(head, strip) for head in range(3) for strip in range(block // STRIP)]

        def keys_of(strip):
            return strip * STRIP + STRIP if diagonal else block

        def scored(head, strip):
            depth = 128 if head < 2 else HD
            return mm(key[0 : keys_of(strip), head_lanes(head)], qm[head, 0:depth, strip * STRIP : strip * STRIP + STRIP])

        ahead = [scored(*strips[i]) for i in range(LEAD)]
        for i, (head, strip) in enumerate(strips):
            scores = ahead.pop(0)
            if i + LEAD < len(strips):
                ahead.append(scored(*strips[i + LEAD]))
            lanes = slice(strip * STRIP, strip * STRIP + STRIP)
            count = keys_of(strip)
            places = first_key + lax.broadcasted_iota(jnp.int32, (count, STRIP), 0)
            allowed = places >= begins[:, lanes]
            if diagonal:
                queries = first_query + strip * STRIP + lax.broadcasted_iota(jnp.int32, (count, STRIP), 1)
                allowed = allowed & (places <= queries)
            scores = jnp.where(allowed, scores, NEG)
            old = peak[head : head + 1, lanes]
            new = jnp.maximum(old, jnp.max(scores, axis=0, keepdims=True))
            weights = jnp.exp(scores - new)
            factor = jnp.exp(old - new)
            peak[head : head + 1, lanes] = new
            total[head : head + 1, lanes] = total[head : head + 1, lanes] * factor + jnp.sum(
                weights, axis=0, keepdims=True
            )
            part = slice(head * HD, head * HD + HD)
            acc[part, lanes] = acc[part, lanes] * factor + mm(vt[part, 0:count], weights.astype(BF))

    attend(me.ctx, True)

    def take_side(distance, whole):
        for slot in range(2):
            y_copy(distance, slot, 1 - side, whole).wait_recv()
            got = held(distance, slot, 1 - side)
            if not whole:
                got = most(got)
            remote(got, got, core_send.at[distance, 1, slot], core_recv.at[distance, 1, slot], me.twin).start()

    @pl.loop(1, 2 * levels)
    def _(turn):
        @pl.when(turn < 2 * levels - 2)
        def _():
            from_below(turn // 2 + 1, turn % 2)

        distance = turn // 2

        @pl.when(turn == 1)
        def _():
            take_side(0, True)

            @pl.when(z < top)
            def _():
                for slot in range(2):
                    rest_up(0, slot).start()

            from_twin(0, 1, 1 - side, True)

        @pl.when((turn > 1) & (turn % 2 == 1) & (distance <= z))
        def _():
            take_side(distance, False)
            for slot in range(2):
                got = rest(held(distance, slot, 1 - side))
                remote(got, got, r_send.at[distance - 1, slot], r_recv.at[distance, slot], me.twin).wait_recv()
                rest_twin(distance, slot).start()

                @pl.when(z < top)
                def _():
                    rest_up(distance, slot).start()

            from_twin(distance, 1, 1 - side, False)

        @pl.when((turn % 2 == 0) & (distance <= z))
        def _():
            from_twin(distance, 0, side, True)

        ctx = me.ctx - 2 * distance + (turn % 2) * (1 - 2 * side)

        @pl.when((ctx >= 0) & (ctx < me.ctx))
        def _():
            attend(ctx, False)

    for head in range(3):
        part = slice(head * HD, head * HD + HD)
        o_out[part, :] = acc[part, :] / total[head : head + 1, :]
    lse_out[...] = peak[...] + jnp.log(jnp.maximum(total[...], 1e-30))

    other = (1 - me.half) * 2 + me.core
    got = rows_of(gtwo_ref, other)
    remote(got, got, two_send.at[0], two_recv.at[0], me.across).wait_recv()
    two_f = go(remote(got, got, two_send.at[2], two_recv.at[2], me.twin))
    for copy in local:
        copy.wait()
    for copy in vecs + atts + [two_x, across]:
        copy.wait_send()
    for copy in exps + [two_c, two_f]:
        copy.wait()

    def left(distance, whole):
        for slot in range(2):
            got = held(distance, slot, side)

            @pl.when(z < top)
            def _():
                remote(got, got, z_send.at[distance, slot], z_recv.at[distance, slot], me.twin).wait_send()
                rest_up(distance, slot).wait_send()

            y_copy(distance, slot, side, whole).wait_send()
            remote(got, got, core_send.at[distance, 0, slot], core_recv.at[distance, 0, slot], me.twin).wait_send()
            if not whole:
                rest_twin(distance, slot).wait_send()
                got = most(got)
            remote(got, got, core_send.at[distance, 1, slot], core_recv.at[distance, 1, slot], me.twin).wait_send()

    left(0, True)

    @pl.loop(1, levels)
    def _(step):
        @pl.when(step <= z)
        def _():
            left(step, False)


def gather_attend(starts, tokens, attend_weight, expand_weight, cotangent, vectors):
    levels = lax.axis_size("ctx") // 2
    rows = tokens.shape[0]
    block = rows * 4
    length = block * levels * 2
    vmem = pl.BlockSpec(memory_space=pltpu.VMEM)
    dma = pltpu.SemaphoreType.DMA
    return pl.pallas_call(
        functools.partial(gather_attend_kernel, levels),
        in_specs=[pl.BlockSpec(memory_space=pltpu.SMEM)] + [pl.BlockSpec(memory_space=pl.ANY)] * 11,
        out_specs=[vmem] * 10,
        out_shape=[
            jax.ShapeDtypeStruct((length, D), BF),
            jax.ShapeDtypeStruct((D, 576), BF),
            jax.ShapeDtypeStruct((D, D), BF),
            jax.ShapeDtypeStruct((block, D), BF),
            jax.ShapeDtypeStruct((8, D), F32),
            jax.ShapeDtypeStruct((block, 192), BF),
            jax.ShapeDtypeStruct((length, 192), BF),
            jax.ShapeDtypeStruct((length, 192), BF),
            jax.ShapeDtypeStruct((192, block), F32),
            jax.ShapeDtypeStruct((8, block), F32),
        ],
        scratch_shapes=[
            pltpu.VMEM((rows, D), BF),
            pltpu.VMEM((rows, 3 * D), BF),
            pltpu.VMEM((rows, D), BF),
            pltpu.VMEM((8, 192), F32),
            pltpu.VMEM((4, rows, 576), BF),
            pltpu.VMEM((4, 8, 192), F32),
            pltpu.VMEM((1, block), jnp.int32),
            pltpu.VMEM((3, 128, block), BF),
            pltpu.VMEM((192, block), BF),
            pltpu.VMEM((192, block), F32),
            pltpu.VMEM((8, block), F32),
            pltpu.VMEM((8, block), F32),
            dma((3,)), dma((3,)), dma((3,)), dma((3,)), dma((3,)), dma((3,)), dma((3,)), dma((3,)),
            dma((1,)), dma((1,)),
            dma((levels, 2)), dma((levels + 1, 2)),
            dma((levels, 2)), dma((levels, 2)),
            dma((levels, 2, 2)), dma((levels, 2, 2)),
            dma((levels, 2)), dma((levels + 1, 2)), dma((levels, 2)), dma((levels, 2)),
            dma((11,)),
            pltpu.VMEM((2 * rows,), BF),
        ]
        + [pltpu.VMEM((rows,), BF)] * 6,
        compiler_params=pltpu.CompilerParams(collective_id=4, has_side_effects=True, vmem_limit_bytes=60 << 20),
        name="gather_attend",
    )(starts, tokens, attend_weight, expand_weight, cotangent, *vectors)


def gelu_pair(t):
    slope = 0.7978845608028654
    square = t * t
    bend = jnp.tanh(slope * t * (1.0 + 0.044715 * square))
    half = 0.5 * (1.0 + bend)
    return t * half, half + 0.5 * t * (1.0 - bend * bend) * (slope * (1.0 + 0.134145 * square))


def mlp_kernel(
    o_ref, wp_hbm, expand_ref, contract_hbm, ebias_hbm, tok_hbm, cot_hbm, gtwo_ref, vec_ref,
    block_out, gmid_out, gone_out, cpart_out, epart_out, sums_out,
    wp_ref, contract_ref, tok_ref, cot_ref, ebias_ref, bias_row, o_rows, gact, n2, act, gexp, held, unit,
    c_send_buf, c_recv_buf, x_send_buf, x_recv_buf,
    c_send, c_recv, x_send, x_recv, ag_send, ag_recv, local_sem,
):
    me = Place()
    mine = me.part
    fetched = [
        pltpu.make_async_copy(source, target, local_sem.at[i])
        for i, (source, target) in enumerate(
            ((wp_hbm, wp_ref), (contract_hbm, contract_ref), (tok_hbm, tok_ref), (cot_hbm, cot_ref), (ebias_hbm, ebias_ref))
        )
    ]
    for copy in fetched:
        copy.start()
    o_rows[...] = o_ref[...].T.astype(BF)
    barrier = pltpu.get_barrier_semaphore()
    signal(barrier, me.twin)
    signal(barrier, me.across)
    pl.semaphore_wait(barrier, 2)
    p_across = (1 - me.half) * 2 + me.core
    p_twin = me.half * 2 + 1 - me.core
    p_corner = (1 - me.half) * 2 + 1 - me.core

    def part(ref, p):
        return ref[pl.ds(pl.multiple_of(p * 192, 192), 192), :]

    def to_twin(i, slot, value):
        c_send_buf[i, slot] = value.astype(BF)
        remote(c_send_buf.at[i, slot], c_recv_buf.at[i, slot], c_send.at[i, slot], c_recv.at[i, slot], me.twin).start()

    def from_twin(i, slot):
        remote(c_send_buf.at[i, slot], c_recv_buf.at[i, slot], c_send.at[i, slot], c_recv.at[i, slot], me.twin).wait_recv()
        return c_recv_buf[i, slot].astype(F32)

    def to_across(i, value):
        x_send_buf[i] = value.astype(BF)
        remote(x_send_buf.at[i], x_recv_buf.at[i], x_send.at[i], x_recv.at[i], me.across).start()

    def from_across(i):
        remote(x_send_buf.at[i], x_recv_buf.at[i], x_send.at[i], x_recv.at[i], me.across).wait_recv()
        return x_recv_buf[i].astype(F32)

    def share(i, ref):
        own = rows_of(ref, mine)
        remote(own, own, ag_send.at[i, 0], ag_recv.at[i, 0], me.across).start()
        remote(own, own, ag_send.at[i, 1], ag_recv.at[i, 1], me.twin).start()

    def share_across(i, ref):
        got = rows_of(ref, p_across)
        remote(got, got, ag_send.at[i, 0], ag_recv.at[i, 0], me.across).wait_recv()
        remote(got, got, ag_send.at[i, 2], ag_recv.at[i, 2], me.twin).start()

    def share_twin(i, ref):
        got = rows_of(ref, p_twin)
        remote(got, got, ag_send.at[i, 1], ag_recv.at[i, 1], me.twin).wait_recv()

    def share_corner(i, ref):
        got = rows_of(ref, p_corner)
        remote(got, got, ag_send.at[i, 2], ag_recv.at[i, 2], me.twin).wait_recv()

    fetched[0].wait()
    to_twin(0, 0, mm(part(o_rows, p_corner), wp_ref[...]))
    to_twin(0, 1, mm(part(o_rows, p_twin), wp_ref[...]))
    value = mm(part(o_rows, p_across), wp_ref[...])
    to_across(0, value + from_twin(0, 0))
    for copy in fetched[1:]:
        copy.wait()
    bias_row[...] = ebias_ref[...].astype(F32).reshape(1, D)
    for p in range(4):
        gact[p * 192 : p * 192 + 192, :] = mm_nt(gtwo_ref[p * 192 : p * 192 + 192, :], contract_ref[...])
    value = mm(part(o_rows, mine), wp_ref[...]) + from_twin(0, 1)
    value = value + from_across(0)
    middle = tok_ref[...].astype(F32) + BRANCH * (value + vec_ref[2:3, :])
    out, unit_two, inverse = layer_norm(middle, vec_ref[6:7, :], vec_ref[7:8, :])
    n2[pl.ds(pl.multiple_of(mine * 192, 192), 192), :] = out.astype(BF)
    share(0, n2)
    unit[...] = unit_two
    held[...] = middle

    def through(p):
        at = pl.ds(pl.multiple_of(p * 192, 192), 192)
        expanded = mm(n2[at, :], expand_ref[...]) + bias_row[...]
        activation, slope = gelu_pair(expanded)
        act[at, :] = activation.astype(BF)
        low = (gact[at, :] * slope).astype(BF)
        gexp[at, :] = low
        return mm_nt(low, expand_ref[...])

    own_value = through(mine)
    share_twin(0, n2)
    to_twin(1, 1, through(p_twin))
    share_across(0, n2)
    across_value = through(p_across)
    share_corner(0, n2)
    to_twin(1, 0, through(p_corner))
    to_across(1, across_value + from_twin(1, 0))
    own_value = own_value + from_twin(1, 1)
    to_twin(2, 0, mm(part(act, p_corner), contract_ref[...]))
    to_twin(2, 1, mm(part(act, p_twin), contract_ref[...]))
    to_across(2, mm(part(act, p_across), contract_ref[...]) + from_twin(2, 0))
    cpart_out[...] = mm_tn(act[...], gtwo_ref[...]).astype(BF)
    grad = own_value + from_across(1)
    unit_two = unit[...]
    scaled = grad * vec_ref[6:7, :]
    spread = (
        scaled
        - jnp.mean(scaled, axis=1, keepdims=True)
        - unit_two * jnp.mean(scaled * unit_two, axis=1, keepdims=True)
    )
    grad_middle = cot_ref[...].astype(F32) + inverse * spread
    gmid_out[...] = grad_middle
    low = (BRANCH * grad_middle).astype(BF)
    gone_out[pl.ds(pl.multiple_of(mine * 192, 192), 192), :] = low
    share(1, gone_out)
    sums_out[0:1, :] = jnp.sum(low.astype(F32), axis=0, keepdims=True)
    sums_out[1:2, :] = jnp.sum(part(gtwo_ref, mine).astype(F32), axis=0, keepdims=True)
    sums_out[2:3, :] = jnp.sum(grad * unit_two, axis=0, keepdims=True)
    sums_out[3:4, :] = jnp.sum(grad, axis=0, keepdims=True)
    sums_out[4:5, :] = jnp.sum(gexp[...].astype(F32), axis=0, keepdims=True)
    sums_out[5:8, :] = jnp.zeros((3, D), F32)
    epart_out[...] = mm_tn(n2[...], gexp[...]).astype(BF)
    value = mm(part(act, mine), contract_ref[...]) + from_twin(2, 1)
    value = value + from_across(2)
    block_out[...] = (held[...] + BRANCH * (value + vec_ref[3:4, :])).astype(BF)
    share_across(1, gone_out)
    share_twin(1, gone_out)
    share_corner(1, gone_out)
    for i in range(3):
        for slot in range(2):
            remote(c_send_buf.at[i, slot], c_recv_buf.at[i, slot], c_send.at[i, slot], c_recv.at[i, slot], me.twin).wait_send()
        remote(x_send_buf.at[i], x_recv_buf.at[i], x_send.at[i], x_recv.at[i], me.across).wait_send()
    for i, ref in ((0, n2), (1, gone_out)):
        own = rows_of(ref, mine)
        for j in range(3):
            remote(own, own, ag_send.at[i, j], ag_recv.at[i, j], me.twin).wait_send()


def feed_forward(o, wp, expand, contract, ebias, tokens, cotangent, gtwo, vectors):
    rows = tokens.shape[0]
    block = rows * 4
    vmem = pl.BlockSpec(memory_space=pltpu.VMEM)
    anywhere = pl.BlockSpec(memory_space=pl.ANY)
    dma = pltpu.SemaphoreType.DMA
    return pl.pallas_call(
        mlp_kernel,
        in_specs=[vmem, anywhere, vmem, anywhere, anywhere, anywhere, anywhere, vmem, vmem],
        out_specs=[vmem] * 6,
        out_shape=[
            jax.ShapeDtypeStruct((rows, D), BF),
            jax.ShapeDtypeStruct((rows, D), F32),
            jax.ShapeDtypeStruct((block, D), BF),
            jax.ShapeDtypeStruct((D, D), BF),
            jax.ShapeDtypeStruct((D, D), BF),
            jax.ShapeDtypeStruct((8, D), F32),
        ],
        scratch_shapes=[
            pltpu.VMEM((192, D), BF),
            pltpu.VMEM((D, D), BF),
            pltpu.VMEM((rows, D), BF),
            pltpu.VMEM((rows, D), BF),
            pltpu.VMEM((D,), BF),
            pltpu.VMEM((1, D), F32),
            pltpu.VMEM((block, 192), BF),
            pltpu.VMEM((block, D), F32),
            pltpu.VMEM((block, D), BF),
            pltpu.VMEM((block, D), BF),
            pltpu.VMEM((block, D), BF),
            pltpu.VMEM((rows, D), F32),
            pltpu.VMEM((rows, D), F32),
            pltpu.VMEM((3, 2, rows, D), BF),
            pltpu.VMEM((3, 2, rows, D), BF),
            pltpu.VMEM((3, rows, D), BF),
            pltpu.VMEM((3, rows, D), BF),
            dma((3, 2)), dma((3, 2)), dma((3,)), dma((3,)), dma((2, 3)), dma((2, 3)), dma((5,)),
        ],
        compiler_params=pltpu.CompilerParams(collective_id=2, has_side_effects=True, vmem_limit_bytes=58 << 20),
        name="feed_forward",
    )(o, wp, expand, contract, ebias, tokens, cotangent, gtwo, vectors)


class Exchange:
    def __init__(self, me, levels, items, y_send, y_recv, z_send, z_recv):
        self.me, self.top, self.items = me, levels - 1, items
        self.y_send, self.y_recv, self.z_send, self.z_recv = y_send, y_recv, z_send, z_recv

    def beside(self, level, act, only=None):
        for i, (chunk, y_in, z_out, z_in) in enumerate(self.items):
            if only is None or i in only:
                act(remote(chunk(level, 1 - self.me.side), y_in.at[level], self.y_send.at[level, i], self.y_recv.at[level, i], self.me.beside))

    def steps(self, step, act):
        z, top = self.me.level, self.top
        down = step - (top - z)
        up = top - (step - z)

        @pl.when((down >= 0) & (down < z))
        def _():
            act(down, 0)

        @pl.when((up <= top) & (up > z))
        def _():
            act(up, 1)

    def along(self, level, way, act):
        device = self.me.at(level=self.me.level - 1) if way == 0 else self.me.at(level=self.me.level + 1)
        last = level == (self.me.level - 1 if way == 0 else self.me.level + 1)
        spot = level if way == 0 else jnp.where(last, self.top + 1, level)
        for i, (chunk, y_in, z_out, z_in) in enumerate(self.items):
            act(remote(z_out.at[level], z_in.at[spot], self.z_send.at[level, i], self.z_recv.at[spot, i], device))

    def arrived(self, level, way):
        spot = level if way == 0 else jnp.where(level == self.me.level, self.top + 1, level)
        for i, (chunk, y_in, z_out, z_in) in enumerate(self.items):
            remote(z_out.at[level], z_in.at[spot], self.z_send.at[level, i], self.z_recv.at[spot, i], self.me.twin).wait_recv()
        return spot

    def step(self, step):
        z, top, side = self.me.level, self.top, self.me.side

        def act(level, way):
            self.beside(level, lambda copy: copy.wait_recv())
            inner = (z < top) if way == 0 else (z > 0)

            @pl.when(inner)
            def _():
                spot = self.arrived(level, way)
                for chunk, y_in, z_out, z_in in self.items:
                    z_out[level] = (
                        chunk(level, side)[...].astype(F32) + y_in[level].astype(F32) + z_in[spot].astype(F32)
                    ).astype(BF)

            @pl.when(jnp.logical_not(inner))
            def _():
                for chunk, y_in, z_out, z_in in self.items:
                    z_out[level] = (chunk(level, side)[...].astype(F32) + y_in[level].astype(F32)).astype(BF)

            self.along(level, way, lambda copy: copy.start())

        self.steps(step, act)

    def final(self, targets):
        z, top, side = self.me.level, self.top, self.me.side
        self.beside(z, lambda copy: copy.wait_recv())

        def add(spots):
            for (chunk, y_in, z_out, z_in), target in zip(self.items, targets):
                sum_of = chunk(z, side)[...].astype(F32) + y_in[z].astype(F32)
                for spot in spots:
                    sum_of = sum_of + z_in[spot].astype(F32)
                target[...] = sum_of.astype(BF)

        @pl.when(z < top)
        def _():
            self.arrived(z, 0)

        @pl.when(z > 0)
        def _():
            self.arrived(z, 1)

        @pl.when(z == 0)
        def _():
            add((z,))

        @pl.when(z == top)
        def _():
            add((top + 1,))

        @pl.when((z > 0) & (z < top))
        def _():
            add((z, top + 1))

    def drain(self):
        for level in range(self.top + 1):
            self.beside(level, lambda copy: copy.wait_send())

            @pl.when(level != self.me.level)
            def _():
                for i, (chunk, y_in, z_out, z_in) in enumerate(self.items):
                    remote(z_out.at[level], z_in.at[level], self.z_send.at[level, i], self.z_recv.at[level, i], self.me.twin).wait_send()


def attend_reduce_kernel(
    levels, starts_ref, all_ref, k_ref, v_ref, q_ref, o_ref, lse_ref, g_ref, wp_hbm, aw_ref,
    c_ref, e_ref, tok_hbm, gmid_ref, vec_ref, sums_ref,
    tg_out, cg_out, eg_out, a_rows, pg_out, vec_out,
    wp_ref, tok_ref, rows_in, keys_in, values_in, begins, qm, dm, qn, dn, delta, dqt, kt, dk, dv, gt, a_part, p_part,
    dnb, far, keep, x_in, y_out, y_in, d_out, d_in,
    yc, ye, ya, yp, zc_out, ze_out, za_out, zp_out, zc_in, ze_in, za_in, zp_in, v_out, v_in, e_move, a_move,
    pre_sem, far_send, far_recv, x_send, x_recv, y_send, y_recv, d_send, d_recv,
    gy_send, gy_recv, gz_send, gz_recv, ay_send, ay_recv, az_send, az_recv,
    me_send, me_recv, ma_send, ma_recv, u_send, u_recv, w_send, w_recv,
    be_send, be_recv, ba_send, ba_recv, te_send, te_recv, ta_send, ta_recv, v_send, v_recv, local_sem,
):
    me = Place()
    z, side, mine, ctx = me.level, me.side, me.part, me.ctx
    top = levels - 1
    block = g_ref.shape[0]
    barrier = pltpu.get_barrier_semaphore()
    for device in (me.twin, me.across, me.corner, me.beside):
        signal(barrier, device)
    for step in range(1, levels):
        signal(barrier, me.at(level=(z + step) % levels))
    below, above = me.at(level=z - 1), me.at(level=z + 1)
    start = lambda copy: copy.start()
    wait_recv = lambda copy: copy.wait_recv()
    wait_send = lambda copy: copy.wait_send()

    def prefetch(index):
        slot = index % 2
        at = pl.ds(pl.multiple_of(index * block, block), block)
        return (
            pltpu.make_async_copy(all_ref.at[at], rows_in.at[slot], pre_sem.at[slot, 0]),
            pltpu.make_async_copy(k_ref.at[at], keys_in.at[slot], pre_sem.at[slot, 1]),
            pltpu.make_async_copy(v_ref.at[at], values_in.at[slot], pre_sem.at[slot, 2]),
        )

    def all_of(copies, act):
        for copy in copies:
            act(copy)

    all_of(prefetch(0), start)
    fetched = (
        pltpu.make_async_copy(wp_hbm, wp_ref, local_sem.at[0]),
        pltpu.make_async_copy(tok_hbm, tok_ref, local_sem.at[1]),
    )
    all_of(fetched, start)

    def corner_of(ref, level, where):
        return ref.at[pl.ds(pl.multiple_of(level * 48, 48), 48), pl.ds(pl.multiple_of(where * 384, 128), 384)]

    grads = Exchange(
        me, levels,
        (
            (lambda level, where: c_ref.at[level * 2 + where], yc, zc_out, zc_in),
            (lambda level, where: e_ref.at[level * 2 + where], ye, ze_out, ze_in),
            (lambda level, where: corner_of(p_part, level, where), yp, zp_out, zp_in),
        ),
        gy_send, gy_recv, gz_send, gz_recv,
    )
    attends = Exchange(
        me, levels, ((lambda level, where: a_part.at[level * 2 + where], ya, za_out, za_in),), ay_send, ay_recv, az_send, az_recv
    )
    grads_in = g_ref[...]
    exact = o_ref[...]
    p_part[...] = mm(exact.astype(BF), grads_in).astype(BF)
    all_of(fetched, lambda copy: copy.wait())
    outer = mm_nt(grads_in, wp_ref[...]).astype(BF)
    pl.semaphore_wait(barrier, levels + 3)
    for step in range(levels - 1):
        grads.steps(step, lambda level, way: grads.beside(level, start))
    grads.beside(z, start)
    flipped = outer.astype(F32).T
    product = flipped * exact
    for head in range(3):
        delta[head : head + 1, :] = jnp.sum(product[head * HD : head * HD + HD], axis=0, keepdims=True)
    fill_masked_columns(dm, flipped.astype(BF))
    scaled = q_ref[...].astype(F32) * SCALE
    fill_masked_columns(qm, scaled.T.astype(BF))
    scaled = scaled.astype(BF)
    for head in range(3):
        depth = 128 if head < 2 else HD
        qn[head, :, 0:depth] = masked_rows(scaled, head)
        dn[head, :, 0:depth] = masked_rows(outer, head)
    dqt[...] = jnp.zeros(dqt.shape, F32)
    gt[...] = jnp.zeros(gt.shape, F32)
    first_query = ctx * block
    begins[...] = begins_of(starts_ref, first_query, block)
    v_out[0] = jnp.zeros(v_out.shape[1:], F32)

    def attend(index, diagonal):
        slot = index % 2
        first_key = index * block
        kt[...] = keys_in[slot].astype(F32).T.astype(BF)
        dk[...] = jnp.zeros(dk.shape, F32)
        dv[...] = jnp.zeros(dv.shape, F32)
        strips = [(head, strip) for head in range(3) for strip in range(block // STRIP)]

        def keys_of(strip):
            return strip * STRIP + STRIP if diagonal else block

        def scored(head, strip):
            depth = 128 if head < 2 else HD
            lanes = head_lanes(head)
            cols = slice(strip * STRIP, strip * STRIP + STRIP)
            count = keys_of(strip)
            return (
                mm(keys_in[slot, 0:count, lanes], qm[head, 0:depth, cols]),
                mm(values_in[slot, 0:count, lanes], dm[head, 0:depth, cols]),
            )

        ahead = [scored(*strips[i]) for i in range(BACK_LEAD)]
        for i, (head, strip) in enumerate(strips):
            scores, outer = ahead.pop(0)
            if i + BACK_LEAD < len(strips):
                ahead.append(scored(*strips[i + BACK_LEAD]))
            depth = 128 if head < 2 else HD
            lanes = head_lanes(head)
            cols = slice(strip * STRIP, strip * STRIP + STRIP)
            count = keys_of(strip)
            places = first_key + lax.broadcasted_iota(jnp.int32, (count, STRIP), 0)
            allowed = places >= begins[:, cols]
            if diagonal:
                queries = first_query + strip * STRIP + lax.broadcasted_iota(jnp.int32, (count, STRIP), 1)
                allowed = allowed & (places <= queries)
            probs = jnp.where(allowed, jnp.exp(scores - lse_ref[head : head + 1, cols]), 0.0)
            inner = (probs * (outer - delta[head : head + 1, cols])).astype(BF)
            dv[0:count, lanes] += mm(probs.astype(BF), dn[head, cols, 0:depth])
            dk[0:count, lanes] += mm(inner, qn[head, cols, 0:depth])
            part = slice(head * HD, head * HD + HD)
            dqt[part, cols] += mm(kt[part, 0:count], inner)
        rows = rows_in[slot]
        low_k = dk[...].astype(BF)
        low_v = dv[...].astype(BF)
        gt[192:384, :] += mm(low_k.astype(F32).T.astype(BF), rows)
        gt[384:576, :] += mm(low_v.astype(F32).T.astype(BF), rows)
        v_out[0, 12:13, 0:192] += jnp.sum(low_v.astype(F32), axis=0, keepdims=True)
        through = mm_nt(low_k, aw_ref[:, 192:384]) + mm_nt(low_v, aw_ref[:, 384:576])
        if diagonal:
            flipped = dqt[...] * SCALE
            low_q = flipped.T.astype(BF)
            gt[0:192, :] = mm(flipped.astype(BF), rows)
            v_out[0, 13:14, 0:192] = jnp.sum(low_q.astype(F32), axis=0, keepdims=True)
            through = through + mm_nt(low_q, aw_ref[:, 0:192])
        dnb[index % 3] = through.astype(BF)

    def to_twin(index):
        slot = index % 3
        return tuple(
            remote(
                rows_of(dnb.at[slot], half * 2 + 1 - me.core), far.at[index, half],
                far_send.at[index, half], far_recv.at[index, half], me.twin,
            )
            for half in range(2)
        )

    def x_copy(index):
        return remote(far.at[index, 0], x_in.at[index], x_send.at[index], x_recv.at[index], me.across)

    def y_copy(level):
        return remote(y_out.at[level], y_in.at[level], y_send.at[level], y_recv.at[level], me.beside)

    def down_copy(level):
        return remote(d_out.at[level], d_in.at[level], d_send.at[level], d_recv.at[level], below)

    def with_twin(index):
        slot = index % 3
        all_of(to_twin(index), lambda copy: copy.wait())

        def rows(half):
            own = dnb[slot, pl.ds(pl.multiple_of((half * 2 + me.core) * 192, 192), 192), :]
            return own.astype(F32) + far[index, half].astype(F32)

        keep[index] = rows(me.half)
        far[index, 0] = rows(1 - me.half).astype(BF)
        x_copy(index).start()

    def with_across(index):
        x_copy(index).wait_recv()
        keep[index] += x_in[index].astype(F32)
        level = index // 2

        @pl.when((index % 2 != side))
        def _():
            y_out[level] = keep[index].astype(BF)
            y_copy(level).start()

    def with_beside(level):
        y_copy(level).wait_recv()
        keep[level * 2 + side] += y_in[level].astype(F32)

    def dn_step(step):
        level = step - (top - z)

        @pl.when((level >= 0) & (level < z))
        def _():
            with_beside(level)
            index = level * 2 + side

            @pl.when(z < top)
            def _():
                down_copy(level).wait_recv()
                keep[index] += d_in[level].astype(F32)

            d_out[level] = keep[index].astype(BF)
            down_copy(level).start()

    def done(level, where):
        return (cg_out.at[level * 2 + where], corner_of(pg_out, level, where))

    def along_copies(way, distance):
        level = z - distance if way == 0 else z + distance
        device = above if way == 0 else below
        return tuple(
            remote(ref, ref, u_send.at[way, distance, i], u_recv.at[way, distance, i], device)
            for i, ref in enumerate(done(level, side))
        )

    def side_copies(level, where):
        return tuple(
            remote(ref, ref, w_send.at[level, i], w_recv.at[level, i], me.beside) for i, ref in enumerate(done(level, where))
        )

    def pass_on(distance, way):
        if way != 1:

            @pl.when(z < top)
            def _():
                all_of(along_copies(0, distance), start)

        if way != 0:

            @pl.when(z > 0)
            def _():
                all_of(along_copies(1, distance), start)

        all_of(side_copies(z - distance if way == 0 else z + distance, side), start)

    def arrivals(distance):
        for way in range(2):
            level = z - distance if way == 0 else z + distance

            @pl.when((level >= 0) & (level <= top))
            def _():
                for i, ref in enumerate(done(level, side)):
                    remote(ref, ref, u_send.at[way, distance - 1, i], u_recv.at[way, distance - 1, i], me.twin).wait_recv()
                pass_on(distance, way)

    def e_chunk(where, origin):
        return eg_out.at[pl.ds(pl.multiple_of(where * 96, 96), 96), pl.ds(pl.multiple_of(origin * D, D), D)]

    def a_chunk(where, origin):
        return a_rows.at[where, origin]

    class Rows:
        def __init__(self, moved, chunk, m_send, m_recv, b_send, b_recv, t_send, t_recv):
            self.moved, self.chunk = moved, chunk
            self.m_send, self.m_recv, self.b_send, self.b_recv = m_send, m_recv, b_send, b_recv
            self.t_send, self.t_recv = t_send, t_recv

        def move(self):
            return remote(self.moved, self.chunk(side, mine), self.m_send.at[0], self.m_recv.at[mine], me.at(half=z // 2, core=z % 2))

        def begin(self):
            @pl.when(mine != z)
            def _():
                self.move().start()

            @pl.when(mine == z)
            def _():
                self.chunk(side, mine)[...] = self.moved[...]

        def line(self, way, origin):
            ref = self.chunk(side, origin)
            return remote(ref, ref, self.b_send.at[way, origin], self.b_recv.at[way, origin], below if way == 0 else above)

        def turn(self, origin, where):
            ref = self.chunk(where, origin)
            return remote(ref, ref, self.t_send.at[origin], self.t_recv.at[origin], me.beside)

        def spread(self, origin):
            @pl.when((mine == z) & (mine != origin))
            def _():
                remote(self.moved, self.chunk(side, origin), self.m_send.at[0], self.m_recv.at[origin], me.twin).wait_recv()

            @pl.when(mine > z)
            def _():
                self.line(0, origin).wait_recv()

            @pl.when(mine < z)
            def _():
                self.line(1, origin).wait_recv()

            @pl.when((mine >= z) & (z > 0))
            def _():
                self.line(0, origin).start()

            @pl.when((mine <= z) & (z < top))
            def _():
                self.line(1, origin).start()

            self.turn(origin, side).start()

        def drain(self):
            @pl.when(mine != z)
            def _():
                self.move().wait_send()

            for origin in range(4):

                @pl.when((mine >= z) & (z > 0))
                def _():
                    self.line(0, origin).wait_send()

                @pl.when((mine <= z) & (z < top))
                def _():
                    self.line(1, origin).wait_send()

                self.turn(origin, side).wait_send()

    e_flow = Rows(e_move, e_chunk, me_send, me_recv, be_send, be_recv, te_send, te_recv)
    a_flow = Rows(a_move, a_chunk, ma_send, ma_recv, ba_send, ba_recv, ta_send, ta_recv)

    @pl.loop(0, 2 * levels + 3)
    def _(turn):
        @pl.when(turn <= ctx)
        def _():
            all_of(prefetch(turn), lambda copy: copy.wait())

        @pl.when(turn + 1 <= ctx)
        def _():
            all_of(prefetch(turn + 1), start)

        @pl.when(turn < ctx)
        def _():
            attend(turn, False)

        @pl.when(turn == ctx)
        def _():
            attend(turn, True)
            flipped = gt[...].T.astype(BF)
            for chunk in range(8):
                a_part[chunk] = flipped[chunk * 96 : chunk * 96 + 96]
            for step in range(levels - 1):
                attends.steps(step, lambda level, way: attends.beside(level, start))
            attends.beside(z, start)

        @pl.when(turn <= ctx)
        def _():
            all_of(to_twin(turn), start)

        @pl.when((turn >= 1) & (turn - 1 <= ctx))
        def _():
            with_twin(turn - 1)

        @pl.when((turn % 2 == 1) & (turn < 2 * levels - 1))
        def _():
            grads.step(turn // 2)

        @pl.when(turn == 2 * levels - 1)
        def _():
            grads.final((cg_out.at[ctx], e_move, corner_of(pg_out, z, side)))
            e_flow.begin()
            pass_on(0, 2)

        @pl.when((turn >= 3) & (turn - 3 <= ctx))
        def _():
            with_across(turn - 3)

        @pl.when((turn >= 6) & (turn % 2 == 0))
        def _():
            dn_step((turn - 6) // 2)

    attends.step(0)
    arrivals(1)
    attends.step(1)
    for origin in range(4):
        e_flow.spread(origin)
    attends.step(2)
    arrivals(2)
    attends.final((a_move,))
    a_flow.begin()

    @pl.when(side == 0)
    def _():
        with_beside(z)

    @pl.when(z < top)
    def _():
        down_copy(z).wait_recv()
        keep[ctx] += d_in[z].astype(F32)

    grad = keep[ctx]
    gain = vec_ref[4:5, :]
    normed, unit, inverse = layer_norm(tok_ref[...].astype(F32), gain, vec_ref[5:6, :])
    scaled = grad * gain
    spread = (
        scaled - jnp.mean(scaled, axis=1, keepdims=True) - unit * jnp.mean(scaled * unit, axis=1, keepdims=True)
    )
    tg_out[...] = (gmid_ref[...] + inverse * spread).astype(BF)
    for part in range(4):

        @pl.when(mine == part)
        def _():
            v_out[0, 0:1, part * 192 : part * 192 + 192] = v_out[0, 13:14, 0:192]
            v_out[0, 1:2, part * 192 : part * 192 + 192] = v_out[0, 12:13, 0:192]
            v_out[0, 8 + part : 9 + part, :] = sums_ref[4:5, :]

    v_out[0, 12:16, :] = jnp.zeros((4, D), F32)
    v_out[0, 2:4, :] = sums_ref[0:2, :]
    v_out[0, 4:5, :] = jnp.sum(grad * unit, axis=0, keepdims=True)
    v_out[0, 5:6, :] = jnp.sum(grad, axis=0, keepdims=True)
    v_out[0, 6:8, :] = sums_ref[2:4, :]
    for origin in range(4):
        a_flow.spread(origin)
    for i, device in enumerate((me.twin, me.across, me.beside)):
        copy = remote(v_out.at[i], v_in.at[i], v_send.at[i], v_recv.at[i], device)
        copy.start()
        copy.wait_recv()
        v_out[i + 1] = v_out[i] + v_in[i]
    v_in[3 + z] = v_out[3]
    for step in range(1, levels):
        remote(v_out.at[3], v_in.at[3 + z], v_send.at[2 + step], v_recv.at[3 + z], me.at(level=(z + step) % levels)).start()
    arrivals(3)
    for step in range(1, levels):
        level = (z + step) % levels
        remote(v_out.at[3], v_in.at[3 + level], v_send.at[2 + step], v_recv.at[3 + level], me.twin).wait_recv()
    total = v_in[3]
    for level in range(1, levels):
        total = total + v_in[3 + level]
    vec_out[...] = total

    for level in range(levels):
        all_of(side_copies(level, 1 - side), wait_recv)
    for flow in (e_flow, a_flow):
        for origin in range(4):
            flow.turn(origin, 1 - side).wait_recv()
    grads.drain()
    attends.drain()
    e_flow.drain()
    a_flow.drain()
    for level in range(levels):
        all_of(side_copies(level, side), wait_send)

        @pl.when((level < z) | ((level == z) & (side == 1)))
        def _():
            y_copy(level).wait_send()

        @pl.when(level < z)
        def _():
            down_copy(level).wait_send()

    @pl.loop(0, 2 * levels)
    def _(index):
        @pl.when(index <= ctx)
        def _():
            x_copy(index).wait_send()

    for distance in range(levels):

        @pl.when((z - distance >= 0) & (z < top))
        def _():
            all_of(along_copies(0, distance), wait_send)

        @pl.when((z + distance <= top) & (z > 0))
        def _():
            all_of(along_copies(1, distance), wait_send)

    for i in range(2 + levels):
        remote(v_out.at[0], v_in.at[0], v_send.at[i], v_recv.at[0], me.twin).wait_send()


def attend_reduce(starts, rows_all, k, v, q, o, lse, g, wp, aw, contract, expand, tokens, grad_middle, vectors, sums):
    levels = lax.axis_size("ctx") // 2
    rows = tokens.shape[0]
    block = rows * 4
    vmem = pl.BlockSpec(memory_space=pltpu.VMEM)
    anywhere = pl.BlockSpec(memory_space=pl.ANY)
    dma = pltpu.SemaphoreType.DMA
    n = levels

    def buf(*shape):
        return pltpu.VMEM(shape, BF)

    def wide(*shape):
        return pltpu.VMEM(shape, F32)

    return pl.pallas_call(
        functools.partial(attend_reduce_kernel, levels),
        in_specs=[pl.BlockSpec(memory_space=pltpu.SMEM)] + [anywhere] * 3 + [vmem] * 4 + [anywhere] + [vmem] * 3 + [anywhere] + [vmem] * 3,
        out_specs=[vmem] * 6,
        out_shape=[
            jax.ShapeDtypeStruct((rows, D), BF),
            jax.ShapeDtypeStruct((2 * n, 96, D), BF),
            jax.ShapeDtypeStruct((192, 4 * D), BF),
            jax.ShapeDtypeStruct((2, 4, 96, 576), BF),
            jax.ShapeDtypeStruct((192, D), BF),
            jax.ShapeDtypeStruct((16, D), F32),
        ],
        scratch_shapes=[
            buf(192, D), buf(rows, D),
            buf(2, block, D), buf(2, block, 192), buf(2, block, 192), pltpu.VMEM((1, block), jnp.int32),
            buf(3, 128, block), buf(3, 128, block), buf(3, block, 128), buf(3, block, 128),
            wide(8, block), wide(192, block), buf(192, block), wide(block, 192), wide(block, 192), wide(576, D),
            buf(2 * n, 96, 576), buf(192, D),
            buf(3, block, D), buf(2 * n, 2, rows, D), wide(2 * n, rows, D), buf(2 * n, rows, D),
            buf(n, rows, D), buf(n, rows, D), buf(n, rows, D), buf(n, rows, D),
            buf(n, 96, D), buf(n, 96, D), buf(n, 96, 576), buf(n, 48, 384),
            buf(n, 96, D), buf(n, 96, D), buf(n, 96, 576), buf(n, 48, 384),
            buf(n + 1, 96, D), buf(n + 1, 96, D), buf(n + 1, 96, 576), buf(n + 1, 48, 384),
            wide(4, 16, D), wide(3 + n, 16, D), buf(96, D), buf(96, 576),
            dma((2, 3)), dma((2 * n, 2)), dma((2 * n, 2)), dma((2 * n,)), dma((2 * n,)),
            dma((n,)), dma((n,)), dma((n,)), dma((n,)),
            dma((n, 3)), dma((n, 3)), dma((n, 3)), dma((n + 1, 3)),
            dma((n, 1)), dma((n, 1)), dma((n, 1)), dma((n + 1, 1)),
            dma((1,)), dma((4,)), dma((1,)), dma((4,)),
            dma((2, n, 2)), dma((2, n, 2)), dma((n, 2)), dma((n, 2)),
            dma((2, 4)), dma((2, 4)), dma((2, 4)), dma((2, 4)), dma((4,)), dma((4,)), dma((4,)), dma((4,)),
            dma((2 + n,)), dma((3 + n,)), dma((2,)),
        ],
        compiler_params=pltpu.CompilerParams(collective_id=5, has_side_effects=True, vmem_limit_bytes=60 << 20),
        name="attend_reduce",
    )(starts, rows_all, k, v, q, o, lse, g, wp, aw, contract, expand, tokens, grad_middle, vectors, sums)


def finish_kernel(
    tg_ref, c_ref, e_ref, a_ref, p_ref, vec_ref, block_ref,
    block_out, tg_out, a_out, ab_out, p_out, pb_out, e_out, hid_out, c_out, cb_out, gf_out, sf_out, gs_out, ss_out,
):
    mine = lax.axis_index("fsdp")
    block_out[...] = block_ref[...]
    tg_out[...] = tg_ref[...]
    p_out[...] = p_ref[...].astype(F32)
    e_out[...] = e_ref[...].astype(F32)
    for chunk in range(8):
        c_out[chunk * 96 : chunk * 96 + 96, :] = c_ref[chunk].astype(F32)
    for where in range(2):
        for part in range(4):
            for kind in range(3):
                lane = kind * D + part * 192
                a_out[where * 96 : where * 96 + 96, lane : lane + 192] = a_ref[
                    where, part, :, kind * 192 : kind * 192 + 192
                ].astype(F32)
    hid_out[...] = vec_ref[pl.ds(8 + mine, 1), :].reshape(D)
    for part in range(4):

        @pl.when(mine == part)
        def _():
            source, lane = part // 2, (part % 2) * 384
            ab_out[...] = vec_ref[source : source + 1, lane : lane + 384].reshape(384)
            for i, ref in enumerate((pb_out, cb_out, gf_out, sf_out, gs_out, ss_out)):
                ref[...] = vec_ref[2 + i : 3 + i, part * 192 : part * 192 + 192].reshape(192)


def finish(tokens_grad, contract, expand, attend, project, vectors, block_output):
    rows = tokens_grad.shape[0]
    one = jax.ShapeDtypeStruct((192,), F32)
    return pl.pallas_call(
        finish_kernel,
        in_specs=[pl.BlockSpec(memory_space=pltpu.VMEM)] * 7,
        out_shape=[
            jax.ShapeDtypeStruct((rows, D), BF),
            jax.ShapeDtypeStruct((rows, D), BF),
            jax.ShapeDtypeStruct((192, 3 * D), F32),
            jax.ShapeDtypeStruct((384,), F32),
            jax.ShapeDtypeStruct((192, D), F32),
            one,
            jax.ShapeDtypeStruct((192, 4 * D), F32),
            jax.ShapeDtypeStruct((D,), F32),
            jax.ShapeDtypeStruct((D, D), F32),
            one, one, one, one, one,
        ],
        compiler_params=pltpu.CompilerParams(vmem_limit_bytes=32 << 20),
        name="finish",
    )(tokens_grad, contract, expand, attend, project, vectors, block_output)


def normalize(rows_in, gain, shift):
    mean = jnp.mean(rows_in, axis=1, keepdims=True)
    centered = rows_in - mean
    inverse = lax.rsqrt(jnp.mean(centered * centered, axis=1, keepdims=True) + EPS)
    unit = centered * inverse
    return (unit * gain + shift, unit, inverse)


def normalize_back(incoming, unit, inverse, gain):
    scaled = incoming * gain
    spread = (
        scaled
        - jnp.mean(scaled, axis=1, keepdims=True)
        - unit * jnp.mean(scaled * unit, axis=1, keepdims=True)
    )
    return (inverse * spread, jnp.sum(incoming * unit, axis=0), jnp.sum(incoming, axis=0))


def first_position(places, starts):
    below = starts[None, :] <= places[:, None]
    return jnp.max(jnp.where(below, starts[None, :], 0), axis=1)


def forward_plain(
    tokens, document_starts, attend_weight, attend_bias, expand_weight, cotangent, own_vectors
):
    rows = tokens.shape[0]
    ways = lax.axis_size("fsdp")
    block = rows * ways
    ctx = lax.axis_index("ctx")
    part = lax.axis_index("fsdp")
    vectors = lax.dynamic_update_slice(jnp.zeros((6, D), F32), jnp.stack(own_vectors).astype(F32), (0, part * rows))
    biases = lax.dynamic_update_slice(jnp.zeros((2 * D,), F32), attend_bias.astype(F32), (part * 2 * rows,))
    vectors = jnp.concatenate([biases.reshape(2, D), vectors])
    attend_cols = attend_weight.reshape(rows, 3, ways, 192).transpose(2, 0, 1, 3).reshape(ways, rows, 576)
    normed_all, attend_cols, expand_cols, g2, vectors = gather_inputs(
        tokens, vectors, attend_cols, expand_weight, cotangent
    )
    wq, wk, wv = attend_cols[:, :192], attend_cols[:, 192:384], attend_cols[:, 384:]
    bias = lax.dynamic_slice(vectors, (0, part * 192), (2, 192))
    own = lax.dynamic_slice(normed_all, (ctx * block, 0), (block, D))
    where, begins_row = places_of(document_starts, block)
    q, k, v, o, lse = attend_forward(where, normed_all, own, wq, wk, wv, bias, begins_row)
    return normed_all, attend_cols, expand_cols, g2, vectors, q, k, v, o, lse


def places_of(document_starts, block):
    ctx = lax.axis_index("ctx")
    places = ctx * block + jnp.arange(block, dtype=jnp.int32)
    begins = first_position(places, document_starts)
    where = jnp.stack([ctx, begins[0], begins[-1]]).astype(jnp.int32)
    return where, begins.reshape(1, block)


def forward(tokens, document_starts, attend_weight, attend_bias, expand_weight, cotangent, own_vectors):
    rows = tokens.shape[0]
    if lax.axis_size("ctx") != 8:
        return forward_plain(
            tokens, document_starts, attend_weight, attend_bias, expand_weight, cotangent, own_vectors
        )
    return gather_attend(
        document_starts, tokens, attend_weight, expand_weight, cotangent, (attend_bias,) + tuple(own_vectors)
    )


def backward_plain(
    document_starts, normed_all, k, v, q, o, lse, g1, project_weight, attend_cols,
    contract_part, expand_part, tokens, grad_middle, vectors, mlp_sums,
):
    both = ("ctx", "fsdp")
    rows = tokens.shape[0]
    ways = lax.axis_size("fsdp")
    block = rows * ways
    ctx = lax.axis_index("ctx")
    part = lax.axis_index("fsdp")
    gain_one = vectors[4]
    wq, wk, wv = attend_cols[:, :192], attend_cols[:, 192:384], attend_cols[:, 384:]
    where, begins_row = places_of(document_starts, block)
    own = lax.dynamic_slice(normed_all, (ctx * block, 0), (block, D))
    dn, attend_t, project_part, sums = attend_backward(
        where, normed_all, k, v, own, q, o, lse, g1, project_weight, wq, wk, wv, begins_row
    )
    grad_normed = lax.psum_scatter(dn.astype(F32), both, scatter_dimension=0, tiled=True)
    normed, unit_one, inverse_one = normalize(tokens.astype(F32), gain_one, jnp.zeros_like(gain_one))
    first_part, gainone_grad, shiftone_grad = normalize_back(grad_normed, unit_one, inverse_one, gain_one)
    tokens_grad = (grad_middle + first_part).astype(BF)

    def summed(array_in):
        return lax.psum(array_in.astype(BF), "ctx").astype(F32)

    contract_grad = summed(contract_part)
    project_grad = summed(project_part)
    expand_grad = lax.all_to_all(summed(expand_part).reshape(ways, rows, D), "fsdp", 0, 0)
    expand_grad = expand_grad.transpose(1, 0, 2).reshape(rows, ways * D)
    attend_grad = lax.all_to_all(summed(attend_t.T).reshape(ways, rows, 576), "fsdp", 0, 0)
    attend_grad = attend_grad.reshape(ways, rows, 3, 192).transpose(1, 2, 0, 3).reshape(rows, 3 * D)
    spread = lax.dynamic_update_slice(jnp.zeros((2, D), F32), sums[:2], (0, part * 192))
    hidden = lax.dynamic_update_slice(jnp.zeros((4, D), F32), mlp_sums[4:5], (part, 0))
    totals = jnp.concatenate([
        spread, mlp_sums[0:2], gainone_grad[None], shiftone_grad[None], mlp_sums[2:4], hidden
    ])
    totals = lax.psum(totals, both)
    attbias = lax.dynamic_slice(totals[:2].reshape(-1), (part * 2 * rows,), (2 * rows,))
    mine = lax.dynamic_slice(totals, (2, part * rows), (6, rows))
    expbias = lax.dynamic_slice(totals, (8 + part, 0), (1, D)).reshape(D)
    return (
        tokens_grad, attend_grad, attbias, project_grad, mine[0], expand_grad, expbias,
        contract_grad, mine[1], mine[2], mine[3], mine[4], mine[5],
    )


def per_device(
    tokens, document_starts, attend_weight, attend_bias, project_weight, project_bias,
    expand_weight, expand_bias, contract_weight, contract_bias,
    gain_first, shift_first, gain_second, shift_second, cotangent,
):
    both = ("ctx", "fsdp")
    rows = tokens.shape[0]
    ways = lax.axis_size("fsdp")
    block = rows * ways
    ctx = lax.axis_index("ctx")
    part = lax.axis_index("fsdp")

    def whole(array_in):
        return lax.all_gather(array_in, "fsdp", axis=0, tiled=True)

    normed_all, attend_cols, expand_cols, g2, vectors, q, k, v, o, lse = forward(
        tokens, document_starts, attend_weight, attend_bias, expand_weight, cotangent,
        (project_bias, contract_bias, gain_first, shift_first, gain_second, shift_second),
    )
    block_output, grad_middle, g1, contract_part, expand_part, mlp_sums = feed_forward(
        o, project_weight, expand_cols, contract_weight, expand_bias, tokens, cotangent, g2, vectors
    )
    if lax.axis_size("ctx") != 8:
        return (block_output,) + backward_plain(
            document_starts, normed_all, k, v, q, o, lse, g1, project_weight, attend_cols,
            contract_part, expand_part, tokens, grad_middle, vectors, mlp_sums,
        )
    reduced = attend_reduce(
        document_starts, normed_all, k, v, q, o, lse, g1, project_weight, attend_cols,
        contract_part.reshape(8, 96, D), expand_part.reshape(8, 96, D), tokens, grad_middle, vectors, mlp_sums,
    )
    return tuple(finish(*reduced, block_output))


def solution(mesh):
    tok, row, vec = P(("ctx", "fsdp"), None), P("fsdp", None), P("fsdp")
    in_specs = (tok, P(), row, vec, row, vec, row, vec, row, vec, vec, vec, vec, vec, tok)
    out_specs = (tok, tok, row, vec, row, vec, row, vec, row, vec, vec, vec, vec, vec)
    return jax.shard_map(per_device, mesh=mesh, in_specs=in_specs, out_specs=out_specs, check_vma=False)
```

```python
import functools
import jax
import jax.numpy as jnp
from jax import lax
from jax.experimental import pallas as pl
from jax.experimental.pallas import tpu as pltpu
from jax.sharding import PartitionSpec as P

D = 768
H = 12
HD = 64
EPS = 1e-05
SCALE = 0.125
BRANCH = 48.0 ** (-0.5)
NEG = -1e30
SUB = 768
STRIP = 256
QS = STRIP
LEAD = 4
BACK_LEAD = 2
BF = jnp.bfloat16
F32 = jnp.float32


def mm(a, b):
    return jnp.dot(a, b, preferred_element_type=F32)


def mm_nt(a, b):
    return lax.dot_general(a, b, (((1,), (1,)), ((), ())), preferred_element_type=F32)


def mm_tn(a, b):
    return lax.dot_general(a, b, (((0,), (0,)), ((), ())), preferred_element_type=F32)


def head_lanes(head):
    return slice(0, 128) if head < 2 else slice(128, 192)


def fill_masked_columns(target, flipped):
    zero = jnp.zeros((HD, flipped.shape[1]), BF)
    target[0, 0:HD, :] = flipped[0:HD]
    target[0, HD : 2 * HD, :] = zero
    target[1, 0:HD, :] = zero
    target[1, HD : 2 * HD, :] = flipped[HD : 2 * HD]
    target[2, 0:HD, :] = flipped[2 * HD : 3 * HD]


def masked_rows(array_in, head):
    if head == 2:
        return array_in[:, 128:192]
    pair = array_in[:, 0:128]
    lane = lax.broadcasted_iota(jnp.int32, pair.shape, 1)
    return jnp.where((lane < HD) if head == 0 else (lane >= HD), pair, jnp.zeros_like(pair))


def allowed_pairs(first_key, first_query, begins, shape):
    key_places = first_key + lax.broadcasted_iota(jnp.int32, shape, 0)
    query_places = first_query + lax.broadcasted_iota(jnp.int32, shape, 1)
    return (key_places <= query_places) & (key_places >= begins)


def attend_forward_kernel(
    where_ref, rows_ref, own_ref, wq_ref, wk_ref, wv_ref, bias_ref, begins_ref,
    q_out, k_out, v_out, o_out, lse_out,
    qm, vt, peak, total, acc,
):
    turn = pl.program_id(0)
    block = own_ref.shape[0]
    mine, begin_low, begin_high = where_ref[0], where_ref[1], where_ref[2]
    first_query = mine * block
    needed = (turn <= mine) & ((turn + 1) * block - 1 >= begin_low)

    @pl.when(turn == 0)
    def _():
        query = (mm(own_ref[...], wq_ref[...]) + bias_ref[0:1, :]).astype(BF)
        q_out[...] = query
        fill_masked_columns(qm, (query.astype(F32) * SCALE).T.astype(BF))
        peak[...] = jnp.full(peak.shape, NEG, F32)
        total[...] = jnp.zeros(total.shape, F32)
        acc[...] = jnp.zeros(acc.shape, F32)

    @pl.when(needed)
    def _():
        rows = rows_ref[...]
        k_out[...] = mm(rows, wk_ref[...]).astype(BF)
        value = (mm(rows, wv_ref[...]) + bias_ref[1:2, :]).astype(BF)
        v_out[...] = value
        vt[...] = value.astype(F32).T.astype(BF)

        def one(step, masked):
            at = pl.ds(pl.multiple_of(step * SUB, SUB), SUB)
            first_key = turn * block + step * SUB
            if masked:
                allowed = allowed_pairs(first_key, first_query, begins_ref[...], (SUB, block))
            strips = [(head, strip) for head in range(3) for strip in range(block // QS)]

            def scored(head, strip):
                depth = 128 if head < 2 else HD
                return mm(k_out[at, head_lanes(head)], qm[head, 0:depth, strip * QS : strip * QS + QS])

            ahead = [scored(*strips[i]) for i in range(LEAD)]
            for i, (head, strip) in enumerate(strips):
                scores = ahead.pop(0)
                if i + LEAD < len(strips):
                    ahead.append(scored(*strips[i + LEAD]))
                lanes = slice(strip * QS, strip * QS + QS)
                if masked:
                    scores = jnp.where(allowed[:, lanes], scores, NEG)
                old = peak[head : head + 1, lanes]
                new = jnp.maximum(old, jnp.max(scores, axis=0, keepdims=True))
                weights = jnp.exp(scores - new)
                if masked:
                    weights = jnp.where(allowed[:, lanes], weights, 0.0)
                factor = jnp.exp(old - new)
                peak[head : head + 1, lanes] = new
                total[head : head + 1, lanes] = total[head : head + 1, lanes] * factor + jnp.sum(
                    weights, axis=0, keepdims=True
                )
                part = slice(head * HD, head * HD + HD)
                acc[part, lanes] = acc[part, lanes] * factor + mm(vt[part, at], weights.astype(BF))

        @pl.loop(0, block // SUB)
        def _(step):
            first_key = turn * block + step * SUB
            inner = (first_key + SUB - 1 <= first_query) & (first_key >= begin_high)
            touched = first_key + SUB - 1 >= begin_low

            @pl.when(inner)
            def _():
                one(step, False)

            @pl.when(jnp.logical_not(inner) & touched)
            def _():
                one(step, True)

    @pl.when(turn == mine)
    def _():
        for head in range(3):
            part = slice(head * HD, head * HD + HD)
            o_out[part, :] = acc[part, :] / total[head : head + 1, :]
        lse_out[...] = peak[...] + jnp.log(jnp.maximum(total[...], 1e-30))


def attend_forward(where, rows_all, own, wq, wk, wv, bias, begins):
    block = own.shape[0]
    count = rows_all.shape[0] // block

    def seen(turn, where_ref):
        return (jnp.minimum(turn, where_ref[0]), 0)

    def fixed(turn, where_ref):
        return (0, 0)

    return pl.pallas_call(
        attend_forward_kernel,
        grid_spec=pltpu.PrefetchScalarGridSpec(
            num_scalar_prefetch=1,
            grid=(count,),
            in_specs=[
                pl.BlockSpec((block, D), seen),
                pl.BlockSpec((block, D), fixed),
                pl.BlockSpec((D, 192), fixed),
                pl.BlockSpec((D, 192), fixed),
                pl.BlockSpec((D, 192), fixed),
                pl.BlockSpec((2, 192), fixed),
                pl.BlockSpec((1, block), fixed),
            ],
            out_specs=[
                pl.BlockSpec((block, 192), fixed),
                pl.BlockSpec((block, 192), seen),
                pl.BlockSpec((block, 192), seen),
                pl.BlockSpec((192, block), fixed),
                pl.BlockSpec((8, block), fixed),
            ],
            scratch_shapes=[
                pltpu.VMEM((3, 128, block), BF),
                pltpu.VMEM((192, block), BF),
                pltpu.VMEM((8, block), F32),
                pltpu.VMEM((8, block), F32),
                pltpu.VMEM((192, block), F32),
            ],
        ),
        out_shape=[
            jax.ShapeDtypeStruct((block, 192), BF),
            jax.ShapeDtypeStruct((block * count, 192), BF),
            jax.ShapeDtypeStruct((block * count, 192), BF),
            jax.ShapeDtypeStruct((192, block), F32),
            jax.ShapeDtypeStruct((8, block), F32),
        ],
        compiler_params=pltpu.CompilerParams(vmem_limit_bytes=48 << 20),
        name="attend_forward",
    )(where, rows_all, own, wq, wk, wv, bias, begins)


def attend_backward_kernel(
    where_ref, rows_ref, k_ref, v_ref, own_ref, q_ref, o_ref, lse_ref, g_ref, wp_ref,
    wq_ref, wk_ref, wv_ref, begins_ref,
    dn_out, grad_out, proj_out, sums_out,
    qm, dm, qn, dn, delta, dqt, kt, dk, dv,
):
    turn = pl.program_id(0)
    block = own_ref.shape[0]
    mine, begin_low, begin_high = where_ref[0], where_ref[1], where_ref[2]
    first_query = mine * block
    needed = (turn <= mine) & ((turn + 1) * block - 1 >= begin_low)

    @pl.when(turn == 0)
    def _():
        grads = g_ref[...]
        exact = o_ref[...]
        proj_out[...] = mm(exact.astype(BF), grads)
        outer = mm_nt(grads, wp_ref[...]).astype(BF)
        flipped = outer.astype(F32).T
        product = flipped * exact
        for head in range(3):
            delta[head : head + 1, :] = jnp.sum(
                product[head * HD : head * HD + HD], axis=0, keepdims=True
            )
        fill_masked_columns(dm, flipped.astype(BF))
        scaled = (q_ref[...].astype(F32) * SCALE)
        fill_masked_columns(qm, scaled.T.astype(BF))
        scaled = scaled.astype(BF)
        for head in range(3):
            depth = 128 if head < 2 else HD
            qn[head, :, 0:depth] = masked_rows(scaled, head)
            dn[head, :, 0:depth] = masked_rows(outer, head)
        dqt[...] = jnp.zeros(dqt.shape, F32)
        grad_out[...] = jnp.zeros(grad_out.shape, F32)
        sums_out[...] = jnp.zeros(sums_out.shape, F32)

    @pl.when(jnp.logical_not(needed))
    def _():
        dn_out[...] = jnp.zeros(dn_out.shape, BF)

    @pl.when(needed)
    def _():
        kt[...] = k_ref[...].astype(F32).T.astype(BF)
        dk[...] = jnp.zeros(dk.shape, F32)
        dv[...] = jnp.zeros(dv.shape, F32)

        def one(step, masked):
            at = pl.ds(pl.multiple_of(step * SUB, SUB), SUB)
            first_key = turn * block + step * SUB
            if masked:
                allowed = allowed_pairs(first_key, first_query, begins_ref[...], (SUB, block))
            for head in range(3):
                depth = 128 if head < 2 else HD
                lanes = head_lanes(head)
                scores = mm(k_ref[at, lanes], qm[head, 0:depth, :])
                probs = jnp.exp(scores - lse_ref[head : head + 1, :])
                if masked:
                    probs = jnp.where(allowed, probs, 0.0)
                outer = mm(v_ref[at, lanes], dm[head, 0:depth, :])
                inner = (probs * (outer - delta[head : head + 1, :])).astype(BF)
                dv[at, lanes] += mm(probs.astype(BF), dn[head, :, 0:depth])
                dk[at, lanes] += mm(inner, qn[head, :, 0:depth])
                part = slice(head * HD, head * HD + HD)
                dqt[part, :] += mm(kt[part, at], inner)

        @pl.loop(0, block // SUB)
        def _(step):
            first_key = turn * block + step * SUB
            inner = (first_key + SUB - 1 <= first_query) & (first_key >= begin_high)
            touched = first_key + SUB - 1 >= begin_low

            @pl.when(inner)
            def _():
                one(step, False)

            @pl.when(jnp.logical_not(inner) & touched)
            def _():
                one(step, True)

        rows = rows_ref[...]
        low_k = dk[...].astype(BF)
        low_v = dv[...].astype(BF)
        grad_out[192:384, :] += mm(low_k.astype(F32).T.astype(BF), rows)
        grad_out[384:576, :] += mm(low_v.astype(F32).T.astype(BF), rows)
        sums_out[1:2, :] += jnp.sum(low_v.astype(F32), axis=0, keepdims=True)
        through = mm_nt(low_k, wk_ref[...]) + mm_nt(low_v, wv_ref[...])

        @pl.when(turn < mine)
        def _():
            dn_out[...] = through.astype(BF)

        @pl.when(turn == mine)
        def _():
            flipped = dqt[...] * SCALE
            low_q = flipped.T.astype(BF)
            grad_out[0:192, :] += mm(flipped.astype(BF), own_ref[...])
            sums_out[0:1, :] += jnp.sum(low_q.astype(F32), axis=0, keepdims=True)
            dn_out[...] = (through + mm_nt(low_q, wq_ref[...])).astype(BF)


def attend_backward(where, rows_all, k, v, own, q, o, lse, g, wp, wq, wk, wv, begins):
    block = own.shape[0]
    count = rows_all.shape[0] // block

    def seen(turn, where_ref):
        return (jnp.minimum(turn, where_ref[0]), 0)

    def each(turn, where_ref):
        return (turn, 0)

    def fixed(turn, where_ref):
        return (0, 0)

    return pl.pallas_call(
        attend_backward_kernel,
        grid_spec=pltpu.PrefetchScalarGridSpec(
            num_scalar_prefetch=1,
            grid=(count,),
            in_specs=[
                pl.BlockSpec((block, D), seen),
                pl.BlockSpec((block, 192), seen),
                pl.BlockSpec((block, 192), seen),
                pl.BlockSpec((block, D), fixed),
                pl.BlockSpec((block, 192), fixed),
                pl.BlockSpec((192, block), fixed),
                pl.BlockSpec((8, block), fixed),
                pl.BlockSpec((block, D), fixed),
                pl.BlockSpec((192, D), fixed),
                pl.BlockSpec((D, 192), fixed),
                pl.BlockSpec((D, 192), fixed),
                pl.BlockSpec((D, 192), fixed),
                pl.BlockSpec((1, block), fixed),
            ],
            out_specs=[
                pl.BlockSpec((block, D), each),
                pl.BlockSpec((576, D), fixed),
                pl.BlockSpec((192, D), fixed),
                pl.BlockSpec((8, 192), fixed),
            ],
            scratch_shapes=[
                pltpu.VMEM((3, 128, block), BF),
                pltpu.VMEM((3, 128, block), BF),
                pltpu.VMEM((3, block, 128), BF),
                pltpu.VMEM((3, block, 128), BF),
                pltpu.VMEM((8, block), F32),
                pltpu.VMEM((192, block), F32),
                pltpu.VMEM((192, block), BF),
                pltpu.VMEM((block, 192), F32),
                pltpu.VMEM((block, 192), F32),
            ],
        ),
        out_shape=[
            jax.ShapeDtypeStruct((block * count, D), BF),
            jax.ShapeDtypeStruct((576, D), F32),
            jax.ShapeDtypeStruct((192, D), F32),
            jax.ShapeDtypeStruct((8, 192), F32),
        ],
        compiler_params=pltpu.CompilerParams(vmem_limit_bytes=48 << 20),
        name="attend_backward",
    )(where, rows_all, k, v, own, q, o, lse, g, wp, wq, wk, wv, begins)


MESH = pl.DeviceIdType.MESH


class Place:
    def __init__(self):
        ctx = lax.axis_index("ctx")
        part = lax.axis_index("fsdp")
        self.levels = lax.axis_size("ctx") // 2
        self.ctx, self.part = ctx, part
        self.level, self.side = ctx // 2, ctx % 2
        self.half, self.core = part // 2, part % 2

    def at(self, level=None, side=None, half=None, core=None):
        level = self.level if level is None else level
        side = self.side if side is None else side
        half = self.half if half is None else half
        core = self.core if core is None else core
        return (level * 2 + side, half * 2 + core)

    @property
    def twin(self):
        return self.at(core=1 - self.core)

    @property
    def across(self):
        return self.at(half=1 - self.half)

    @property
    def corner(self):
        return self.at(half=1 - self.half, core=1 - self.core)

    @property
    def beside(self):
        return self.at(side=1 - self.side)


def remote(source, target, send, recv, device):
    return pltpu.make_async_remote_copy(
        src_ref=source, dst_ref=target, send_sem=send, recv_sem=recv, device_id=device, device_id_type=MESH
    )


def signal(sem, device):
    pl.semaphore_signal(sem, inc=1, device_id=device, device_id_type=MESH)


def piece(ref, ctx, part):
    rows = 192
    return ref.at[pl.ds(pl.multiple_of((ctx * 4 + part) * rows, rows), rows)]


def rows_of(ref, part):
    return ref.at[pl.ds(pl.multiple_of(part * 192, 192), 192)]


def layer_norm(rows_in, gain, shift):
    mean = jnp.mean(rows_in, axis=1, keepdims=True)
    centered = rows_in - mean
    inverse = lax.rsqrt(jnp.mean(centered * centered, axis=1, keepdims=True) + EPS)
    unit = centered * inverse
    return unit * gain + shift, unit, inverse


def gather_kernel(
    levels, tok_ref, vec_ref, acol_ref, ecol_ref, cot_ref,
    all_ref, attend_ref, expand_ref, gtwo_ref, vec_out,
    normed, gtwo, vec_in,
    vec_send, vec_recv, att_send, att_recv, exp_send, exp_recv, two_send, two_recv,
    x_send, x_recv, z_send, z_recv, y_send, y_recv, core_send, core_recv, local_sem,
):
    me = Place()
    mine = me.part
    barrier = pltpu.get_barrier_semaphore()
    for device in (me.twin, me.across, me.corner, me.beside):
        signal(barrier, device)

    @pl.when(me.level > 0)
    def _():
        signal(barrier, me.at(level=me.level - 1))

    @pl.when(me.level < levels - 1)
    def _():
        signal(barrier, me.at(level=me.level + 1))

    ends = (me.level == 0).astype(jnp.int32) + (me.level == levels - 1).astype(jnp.int32)
    pl.semaphore_wait(barrier, 6 - ends)

    peers = (
        (me.twin, me.half * 2 + 1 - me.core),
        (me.across, (1 - me.half) * 2 + me.core),
        (me.corner, (1 - me.half) * 2 + 1 - me.core),
    )
    vecs = [remote(vec_ref, vec_in.at[i], vec_send.at[i], vec_recv.at[i], d) for i, (d, p) in enumerate(peers)]
    for copy in vecs:
        copy.start()
    atts = [
        remote(acol_ref.at[p], rows_of(attend_ref, mine), att_send.at[i], att_recv.at[i], d)
        for i, (d, p) in enumerate(peers)
    ]
    for copy in atts:
        copy.start()
    local = [
        pltpu.make_async_copy(acol_ref.at[mine], rows_of(attend_ref, mine), local_sem.at[0]),
        pltpu.make_async_copy(ecol_ref.at[:, pl.ds(pl.multiple_of(mine * D, D), D)], rows_of(expand_ref, mine), local_sem.at[1]),
    ]
    for copy in local:
        copy.start()
    gtwo[...] = (BRANCH * cot_ref[...].astype(F32)).astype(BF)
    for copy in vecs:
        copy.wait_recv()
    vec_out[...] = vec_ref[...] + vec_in[0] + vec_in[1] + vec_in[2]
    out, unit, inverse = layer_norm(tok_ref[...].astype(F32), vec_out[4:5, :], vec_out[5:6, :])
    normed[...] = out.astype(BF)

    def go(copy):
        copy.start()
        return copy

    ctx = me.ctx
    across = go(remote(normed, piece(all_ref, ctx, mine), x_send.at[0], x_recv.at[0], me.across))
    keep = go(pltpu.make_async_copy(normed, piece(all_ref, ctx, mine), local_sem.at[2]))
    keep_two = go(pltpu.make_async_copy(gtwo, rows_of(gtwo_ref, mine), local_sem.at[3]))
    local += [keep, keep_two]

    def spread_static(source, distance, slot):
        level = me.level - distance
        where = level * 2 + me.side
        half = me.half if slot == 0 else 1 - me.half
        part = half * 2 + me.core

        @pl.when(me.level < levels - 1)
        def _():
            remote(source, piece(all_ref, where, part), z_send.at[distance, slot], z_recv.at[distance + 1, slot], me.at(level=me.level + 1)).start()

        remote(source, piece(all_ref, where, part), y_send.at[distance, slot], y_recv.at[distance, slot], me.beside).start()
        remote(source, piece(all_ref, where, part), core_send.at[distance, 0, slot], core_recv.at[distance, 0, slot], me.twin).start()

    spread_static(normed, 0, 0)
    exps = [
        go(remote(ecol_ref.at[:, pl.ds(pl.multiple_of(p * D, D), D)], rows_of(expand_ref, mine), exp_send.at[i], exp_recv.at[i], d))
        for i, (d, p) in enumerate(peers)
    ]
    two_x = go(remote(gtwo, rows_of(gtwo_ref, mine), two_send.at[0], two_recv.at[0], me.across))
    two_c = go(remote(gtwo, rows_of(gtwo_ref, mine), two_send.at[1], two_recv.at[1], me.twin))

    other = (1 - me.half) * 2 + me.core

    def held(distance, slot, side):
        half = me.half if slot == 0 else 1 - me.half
        return piece(all_ref, (me.level - distance) * 2 + side, half * 2 + me.core)

    def take_y(distance):
        for slot in range(2):
            got = held(distance, slot, 1 - me.side)
            remote(got, got, y_send.at[distance, slot], y_recv.at[distance, slot], me.beside).wait_recv()
            remote(got, got, core_send.at[distance, 1, slot], core_recv.at[distance, 1, slot], me.twin).start()

    got = piece(all_ref, ctx, other)
    remote(normed, got, x_send.at[0], x_recv.at[0], me.across).wait_recv()
    spread_static(got, 0, 1)
    for distance in range(1, levels):

        @pl.when(me.level >= distance)
        def _():
            for slot in range(2):
                got = held(distance, slot, me.side)
                remote(got, got, z_send.at[distance, slot], z_recv.at[distance, slot], me.twin).wait_recv()
                spread_static(got, distance, slot)

        if distance == 1:
            take_y(0)
        else:

            @pl.when(me.level >= distance - 1)
            def _():
                take_y(distance - 1)

    @pl.when(me.level >= levels - 1)
    def _():
        take_y(levels - 1)

    got = rows_of(gtwo_ref, other)
    remote(gtwo, got, two_send.at[0], two_recv.at[0], me.across).wait_recv()
    two_f = go(remote(got, got, two_send.at[2], two_recv.at[2], me.twin))
    for copy in local:
        copy.wait()
    for copy in vecs:
        copy.wait_send()
    for copy in atts + exps + [two_c, two_f]:
        copy.wait()
    two_x.wait_send()
    across.wait_send()
    for distance in range(levels):

        @pl.when(me.level >= distance)
        def _():
            for slot in range(2):
                got = held(distance, slot, me.side)

                @pl.when(me.level < levels - 1)
                def _():
                    remote(got, got, z_send.at[distance, slot], z_recv.at[distance, slot], me.twin).wait_send()

                remote(got, got, y_send.at[distance, slot], y_recv.at[distance, slot], me.beside).wait_send()
                for side in range(2):
                    remote(got, got, core_send.at[distance, side, slot], core_recv.at[distance, side, slot], me.twin).wait()


def gather_inputs(tokens, vectors, attend_cols, expand_weight, cotangent):
    levels = lax.axis_size("ctx") // 2
    rows = tokens.shape[0]
    block = rows * 4
    vmem = pl.BlockSpec(memory_space=pltpu.VMEM)
    anywhere = pl.BlockSpec(memory_space=pl.ANY)
    dma = pltpu.SemaphoreType.DMA
    return pl.pallas_call(
        functools.partial(gather_kernel, levels),
        in_specs=[vmem, vmem, anywhere, anywhere, vmem],
        out_specs=[anywhere, anywhere, anywhere, anywhere, vmem],
        out_shape=[
            jax.ShapeDtypeStruct((block * levels * 2, D), BF),
            jax.ShapeDtypeStruct((D, 576), BF),
            jax.ShapeDtypeStruct((D, D), BF),
            jax.ShapeDtypeStruct((block, D), BF),
            jax.ShapeDtypeStruct((8, D), F32),
        ],
        scratch_shapes=[
            pltpu.VMEM((rows, D), BF),
            pltpu.VMEM((rows, D), BF),
            pltpu.VMEM((3, 8, D), F32),
            dma((3,)), dma((3,)), dma((3,)), dma((3,)), dma((3,)), dma((3,)), dma((3,)), dma((3,)),
            dma((1,)), dma((1,)),
            dma((levels, 2)), dma((levels + 1, 2)),
            dma((levels, 2)), dma((levels, 2)),
            dma((levels, 2, 2)), dma((levels, 2, 2)),
            dma((4,)),
        ],
        compiler_params=pltpu.CompilerParams(collective_id=1, has_side_effects=True, vmem_limit_bytes=16 << 20),
        name="gather_inputs",
    )(tokens, vectors, attend_cols, expand_weight, cotangent)


SHARE = 160


def begins_of(starts_ref, first, count):
    places = first + lax.broadcasted_iota(jnp.int32, (1, count), 1)
    begins = jnp.zeros((1, count), jnp.int32)
    for document in range(8):
        start = starts_ref[document]
        begins = jnp.where(places >= start, jnp.maximum(begins, start), begins)
    return begins


def gather_attend_kernel(
    levels, starts_ref, tok_hbm, aw_hbm, ew_ref, cot_hbm, *rest_refs,
):
    vector_hbm, vector_refs = rest_refs[:7], rest_refs[-7:]
    (
        all_ref, attend_ref, expand_ref, gtwo_ref, vec_out, q_out, k_out, v_out, o_out, lse_out,
        tok_ref, aw_ref, cot_ref, vec_ref, staged, vec_in, begins, qm, vt, acc, peak, total,
        vec_send, vec_recv, att_send, att_recv, exp_send, exp_recv, two_send, two_recv,
        x_send, x_recv, z_send, z_recv, y_send, y_recv, core_send, core_recv, r_send, r_recv, rc_send, rc_recv, local_sem,
    ) = rest_refs[7:-7]
    me = Place()
    mine, z, side = me.part, me.level, me.side
    top = levels - 1
    block = gtwo_ref.shape[0]
    fetched = (
        pltpu.make_async_copy(tok_hbm, tok_ref, local_sem.at[1]),
        pltpu.make_async_copy(aw_hbm, aw_ref, local_sem.at[2]),
        pltpu.make_async_copy(cot_hbm, cot_ref, local_sem.at[3]),
    ) + tuple(
        pltpu.make_async_copy(source, target, local_sem.at[4 + i])
        for i, (source, target) in enumerate(zip(vector_hbm, vector_refs))
    )
    for copy in fetched:
        copy.start()
    barrier = pltpu.get_barrier_semaphore()
    for device in (me.twin, me.across, me.corner, me.beside):
        signal(barrier, device)

    @pl.when(z > 0)
    def _():
        signal(barrier, me.at(level=z - 1))

    @pl.when(z < top)
    def _():
        signal(barrier, me.at(level=z + 1))

    for copy in fetched:
        copy.wait()
    both = vector_refs[0][...].astype(F32).reshape(1, 384)
    vec_ref[0:1, :] = both[:, 0:192]
    vec_ref[1:2, :] = both[:, 192:384]
    for i, ref in enumerate(vector_refs[1:]):
        vec_ref[2 + i : 3 + i, :] = ref[...].astype(F32).reshape(1, 192)
    for part in range(4):
        for kind in range(3):
            staged[part, :, kind * 192 : kind * 192 + 192] = aw_ref[:, kind * D + part * 192 : kind * D + part * 192 + 192]
    ends = (z == 0).astype(jnp.int32) + (z == top).astype(jnp.int32)
    pl.semaphore_wait(barrier, 6 - ends)

    peers = (
        (me.twin, me.half * 2 + 1 - me.core),
        (me.across, (1 - me.half) * 2 + me.core),
        (me.corner, (1 - me.half) * 2 + 1 - me.core),
    )

    def go(copy):
        copy.start()
        return copy

    vecs = [go(remote(vec_ref, vec_in.at[mine], vec_send.at[i], vec_recv.at[i], d)) for i, (d, p) in enumerate(peers)]
    atts = [
        remote(staged.at[p], rows_of(attend_ref, mine), att_send.at[i], att_recv.at[i], d) for i, (d, p) in enumerate(peers)
    ]
    atts[0].start()
    atts[1].start()
    vec_in[mine] = vec_ref[...]
    rows_of(attend_ref, mine)[...] = staged[mine]
    local = [
        go(pltpu.make_async_copy(
            ew_ref.at[:, pl.ds(pl.multiple_of(mine * D, D), D)], rows_of(expand_ref, mine), local_sem.at[0]
        ))
    ]
    own_two = rows_of(gtwo_ref, mine)
    own_two[...] = (BRANCH * cot_ref[...].astype(F32)).astype(BF)
    for i, (d, p) in enumerate(peers):
        remote(vec_ref, vec_in.at[p], vec_send.at[i], vec_recv.at[i], d).wait_recv()
    for part in range(4):
        vec_out[:, part * 192 : part * 192 + 192] = vec_in[part]
    out, unit, inverse = layer_norm(tok_ref[...].astype(F32), vec_out[4:5, :], vec_out[5:6, :])
    own_rows = piece(all_ref, me.ctx, mine)
    own_rows[...] = out.astype(BF)
    across = go(remote(own_rows, own_rows, x_send.at[0], x_recv.at[0], me.across))
    atts[2].start()

    def most(ref):
        return ref.at[pl.ds(0, SHARE)]

    def rest(ref):
        return ref.at[pl.ds(SHARE, 192 - SHARE)]

    def held(distance, slot, where):
        half = me.half + slot * (1 - 2 * me.half)
        return piece(all_ref, (z - distance) * 2 + where, half * 2 + me.core)

    def y_copy(distance, slot, where, whole):
        got = held(distance, slot, where)
        if not whole:
            got = most(got)
        return remote(got, got, y_send.at[distance, slot], y_recv.at[distance, slot], me.beside)

    def rest_up(distance, slot):
        got = rest(held(distance, slot, 1 - side))
        return remote(got, got, r_send.at[distance, slot], r_recv.at[distance + 1, slot], me.at(level=z + 1))

    def rest_twin(distance, slot):
        got = rest(held(distance, slot, 1 - side))
        return remote(got, got, rc_send.at[distance, slot], rc_recv.at[distance, slot], me.twin)

    def spread(distance, slot, first):
        half = me.half + slot * (1 - 2 * me.half)
        got = piece(all_ref, (z - distance) * 2 + side, half * 2 + me.core)

        @pl.when(z < top)
        def _():
            remote(got, got, z_send.at[distance, slot], z_recv.at[distance + 1, slot], me.at(level=z + 1)).start()

        y_copy(distance, slot, side, first).start()
        remote(got, got, core_send.at[distance, 0, slot], core_recv.at[distance, 0, slot], me.twin).start()

    def from_twin(distance, which, where, whole):
        for slot in range(2):
            half = me.half + slot * (1 - 2 * me.half)
            got = piece(all_ref, (z - distance) * 2 + where, half * 2 + 1 - me.core)
            if not whole:
                last = rest(got)
                remote(last, last, rc_send.at[distance, slot], rc_recv.at[distance, slot], me.twin).wait_recv()
                got = most(got)
            remote(got, got, core_send.at[distance, which, slot], core_recv.at[distance, which, slot], me.twin).wait_recv()

    spread(0, 0, True)
    two_x = go(remote(own_two, own_two, two_send.at[0], two_recv.at[0], me.across))
    two_c = go(remote(own_two, own_two, two_send.at[1], two_recv.at[1], me.twin))
    exps = [
        go(remote(ew_ref.at[:, pl.ds(pl.multiple_of(p * D, D), D)], rows_of(expand_ref, mine), exp_send.at[i], exp_recv.at[i], d))
        for i, (d, p) in enumerate(peers)
    ]
    begins[...] = begins_of(starts_ref, me.ctx * block, block)
    got = held(0, 1, side)
    remote(got, got, x_send.at[0], x_recv.at[0], me.across).wait_recv()
    spread(0, 1, True)
    def from_below(distance, slot):
        @pl.when(distance <= z)
        def _():
            got = held(distance, slot, side)
            remote(got, got, z_send.at[distance - 1, slot], z_recv.at[distance, slot], me.twin).wait_recv()
            spread(distance, slot, False)

    from_below(1, 0)
    for copy in atts:
        copy.wait_recv()
    from_twin(0, 0, side, True)

    first_query = me.ctx * block
    bias_q = vec_in[mine // 2, pl.ds(mine % 2, 1), :]
    query = (mm(all_ref[pl.ds(pl.multiple_of(first_query, block), block), :], attend_ref[:, 0:192]) + bias_q).astype(BF)
    q_out[...] = query
    fill_masked_columns(qm, (query.astype(F32) * SCALE).T.astype(BF))
    peak[...] = jnp.full(peak.shape, NEG, F32)
    total[...] = jnp.zeros(total.shape, F32)
    acc[...] = jnp.zeros(acc.shape, F32)

    def attend(ctx, diagonal):
        first_key = ctx * block
        at = pl.ds(pl.multiple_of(first_key, block), block)
        rows = all_ref[at, :]
        key = mm(rows, attend_ref[:, 192:384]).astype(BF)
        k_out[at, :] = key
        value = (mm(rows, attend_ref[:, 384:576]) + vec_in[2 + mine // 2, pl.ds(mine % 2, 1), :]).astype(BF)
        v_out[at, :] = value
        vt[...] = value.astype(F32).T.astype(BF)
        strips = [(head, strip) for head in range(3) for strip in range(block // STRIP)]

        def keys_of(strip):
            return strip * STRIP + STRIP if diagonal else block

        def scored(head, strip):
            depth = 128 if head < 2 else HD
            return mm(key[0 : keys_of(strip), head_lanes(head)], qm[head, 0:depth, strip * STRIP : strip * STRIP + STRIP])

        ahead = [scored(*strips[i]) for i in range(LEAD)]
        for i, (head, strip) in enumerate(strips):
            scores = ahead.pop(0)
            if i + LEAD < len(strips):
                ahead.append(scored(*strips[i + LEAD]))
            lanes = slice(strip * STRIP, strip * STRIP + STRIP)
            count = keys_of(strip)
            places = first_key + lax.broadcasted_iota(jnp.int32, (count, STRIP), 0)
            allowed = places >= begins[:, lanes]
            if diagonal:
                queries = first_query + strip * STRIP + lax.broadcasted_iota(jnp.int32, (count, STRIP), 1)
                allowed = allowed & (places <= queries)
            scores = jnp.where(allowed, scores, NEG)
            old = peak[head : head + 1, lanes]
            new = jnp.maximum(old, jnp.max(scores, axis=0, keepdims=True))
            weights = jnp.exp(scores - new)
            factor = jnp.exp(old - new)
            peak[head : head + 1, lanes] = new
            total[head : head + 1, lanes] = total[head : head + 1, lanes] * factor + jnp.sum(
                weights, axis=0, keepdims=True
            )
            part = slice(head * HD, head * HD + HD)
            acc[part, lanes] = acc[part, lanes] * factor + mm(vt[part, 0:count], weights.astype(BF))

    attend(me.ctx, True)

    def take_side(distance, whole):
        for slot in range(2):
            y_copy(distance, slot, 1 - side, whole).wait_recv()
            got = held(distance, slot, 1 - side)
            if not whole:
                got = most(got)
            remote(got, got, core_send.at[distance, 1, slot], core_recv.at[distance, 1, slot], me.twin).start()

    @pl.loop(1, 2 * levels)
    def _(turn):
        @pl.when(turn < 2 * levels - 2)
        def _():
            from_below(turn // 2 + 1, turn % 2)

        distance = turn // 2

        @pl.when(turn == 1)
        def _():
            take_side(0, True)

            @pl.when(z < top)
            def _():
                for slot in range(2):
                    rest_up(0, slot).start()

            from_twin(0, 1, 1 - side, True)

        @pl.when((turn > 1) & (turn % 2 == 1) & (distance <= z))
        def _():
            take_side(distance, False)
            for slot in range(2):
                got = rest(held(distance, slot, 1 - side))
                remote(got, got, r_send.at[distance - 1, slot], r_recv.at[distance, slot], me.twin).wait_recv()
                rest_twin(distance, slot).start()

                @pl.when(z < top)
                def _():
                    rest_up(distance, slot).start()

            from_twin(distance, 1, 1 - side, False)

        @pl.when((turn % 2 == 0) & (distance <= z))
        def _():
            from_twin(distance, 0, side, True)

        ctx = me.ctx - 2 * distance + (turn % 2) * (1 - 2 * side)

        @pl.when((ctx >= 0) & (ctx < me.ctx))
        def _():
            attend(ctx, False)

    for head in range(3):
        part = slice(head * HD, head * HD + HD)
        o_out[part, :] = acc[part, :] / total[head : head + 1, :]
    lse_out[...] = peak[...] + jnp.log(jnp.maximum(total[...], 1e-30))

    other = (1 - me.half) * 2 + me.core
    got = rows_of(gtwo_ref, other)
    remote(got, got, two_send.at[0], two_recv.at[0], me.across).wait_recv()
    two_f = go(remote(got, got, two_send.at[2], two_recv.at[2], me.twin))
    for copy in local:
        copy.wait()
    for copy in vecs + atts + [two_x, across]:
        copy.wait_send()
    for copy in exps + [two_c, two_f]:
        copy.wait()

    def left(distance, whole):
        for slot in range(2):
            got = held(distance, slot, side)

            @pl.when(z < top)
            def _():
                remote(got, got, z_send.at[distance, slot], z_recv.at[distance, slot], me.twin).wait_send()
                rest_up(distance, slot).wait_send()

            y_copy(distance, slot, side, whole).wait_send()
            remote(got, got, core_send.at[distance, 0, slot], core_recv.at[distance, 0, slot], me.twin).wait_send()
            if not whole:
                rest_twin(distance, slot).wait_send()
                got = most(got)
            remote(got, got, core_send.at[distance, 1, slot], core_recv.at[distance, 1, slot], me.twin).wait_send()

    left(0, True)

    @pl.loop(1, levels)
    def _(step):
        @pl.when(step <= z)
        def _():
            left(step, False)


def gather_attend(starts, tokens, attend_weight, expand_weight, cotangent, vectors):
    levels = lax.axis_size("ctx") // 2
    rows = tokens.shape[0]
    block = rows * 4
    length = block * levels * 2
    vmem = pl.BlockSpec(memory_space=pltpu.VMEM)
    dma = pltpu.SemaphoreType.DMA
    return pl.pallas_call(
        functools.partial(gather_attend_kernel, levels),
        in_specs=[pl.BlockSpec(memory_space=pltpu.SMEM)] + [pl.BlockSpec(memory_space=pl.ANY)] * 11,
        out_specs=[vmem] * 10,
        out_shape=[
            jax.ShapeDtypeStruct((length, D), BF),
            jax.ShapeDtypeStruct((D, 576), BF),
            jax.ShapeDtypeStruct((D, D), BF),
            jax.ShapeDtypeStruct((block, D), BF),
            jax.ShapeDtypeStruct((8, D), F32),
            jax.ShapeDtypeStruct((block, 192), BF),
            jax.ShapeDtypeStruct((length, 192), BF),
            jax.ShapeDtypeStruct((length, 192), BF),
            jax.ShapeDtypeStruct((192, block), F32),
            jax.ShapeDtypeStruct((8, block), F32),
        ],
        scratch_shapes=[
            pltpu.VMEM((rows, D), BF),
            pltpu.VMEM((rows, 3 * D), BF),
            pltpu.VMEM((rows, D), BF),
            pltpu.VMEM((8, 192), F32),
            pltpu.VMEM((4, rows, 576), BF),
            pltpu.VMEM((4, 8, 192), F32),
            pltpu.VMEM((1, block), jnp.int32),
            pltpu.VMEM((3, 128, block), BF),
            pltpu.VMEM((192, block), BF),
            pltpu.VMEM((192, block), F32),
            pltpu.VMEM((8, block), F32),
            pltpu.VMEM((8, block), F32),
            dma((3,)), dma((3,)), dma((3,)), dma((3,)), dma((3,)), dma((3,)), dma((3,)), dma((3,)),
            dma((1,)), dma((1,)),
            dma((levels, 2)), dma((levels + 1, 2)),
            dma((levels, 2)), dma((levels, 2)),
            dma((levels, 2, 2)), dma((levels, 2, 2)),
            dma((levels, 2)), dma((levels + 1, 2)), dma((levels, 2)), dma((levels, 2)),
            dma((11,)),
            pltpu.VMEM((2 * rows,), BF),
        ]
        + [pltpu.VMEM((rows,), BF)] * 6,
        compiler_params=pltpu.CompilerParams(collective_id=4, has_side_effects=True, vmem_limit_bytes=60 << 20),
        name="gather_attend",
    )(starts, tokens, attend_weight, expand_weight, cotangent, *vectors)


def gelu_pair(t):
    slope = 0.7978845608028654
    square = t * t
    bend = jnp.tanh(slope * t * (1.0 + 0.044715 * square))
    half = 0.5 * (1.0 + bend)
    return t * half, half + 0.5 * t * (1.0 - bend * bend) * (slope * (1.0 + 0.134145 * square))


def mlp_kernel(
    o_ref, wp_hbm, expand_ref, contract_hbm, ebias_hbm, tok_hbm, cot_hbm, gtwo_ref, vec_ref,
    block_out, gmid_out, gone_out, cpart_out, epart_out, sums_out,
    wp_ref, contract_ref, tok_ref, cot_ref, ebias_ref, bias_row, o_rows, gact, n2, act, gexp, held, unit,
    c_send_buf, c_recv_buf, x_send_buf, x_recv_buf,
    c_send, c_recv, x_send, x_recv, ag_send, ag_recv, local_sem,
):
    me = Place()
    mine = me.part
    fetched = [
        pltpu.make_async_copy(source, target, local_sem.at[i])
        for i, (source, target) in enumerate(
            ((wp_hbm, wp_ref), (contract_hbm, contract_ref), (tok_hbm, tok_ref), (cot_hbm, cot_ref), (ebias_hbm, ebias_ref))
        )
    ]
    for copy in fetched:
        copy.start()
    o_rows[...] = o_ref[...].T.astype(BF)
    barrier = pltpu.get_barrier_semaphore()
    signal(barrier, me.twin)
    signal(barrier, me.across)
    pl.semaphore_wait(barrier, 2)
    p_across = (1 - me.half) * 2 + me.core
    p_twin = me.half * 2 + 1 - me.core
    p_corner = (1 - me.half) * 2 + 1 - me.core

    def part(ref, p):
        return ref[pl.ds(pl.multiple_of(p * 192, 192), 192), :]

    def to_twin(i, slot, value):
        c_send_buf[i, slot] = value.astype(BF)
        remote(c_send_buf.at[i, slot], c_recv_buf.at[i, slot], c_send.at[i, slot], c_recv.at[i, slot], me.twin).start()

    def from_twin(i, slot):
        remote(c_send_buf.at[i, slot], c_recv_buf.at[i, slot], c_send.at[i, slot], c_recv.at[i, slot], me.twin).wait_recv()
        return c_recv_buf[i, slot].astype(F32)

    def to_across(i, value):
        x_send_buf[i] = value.astype(BF)
        remote(x_send_buf.at[i], x_recv_buf.at[i], x_send.at[i], x_recv.at[i], me.across).start()

    def from_across(i):
        remote(x_send_buf.at[i], x_recv_buf.at[i], x_send.at[i], x_recv.at[i], me.across).wait_recv()
        return x_recv_buf[i].astype(F32)

    def share(i, ref):
        own = rows_of(ref, mine)
        remote(own, own, ag_send.at[i, 0], ag_recv.at[i, 0], me.across).start()
        remote(own, own, ag_send.at[i, 1], ag_recv.at[i, 1], me.twin).start()

    def share_across(i, ref):
        got = rows_of(ref, p_across)
        remote(got, got, ag_send.at[i, 0], ag_recv.at[i, 0], me.across).wait_recv()
        remote(got, got, ag_send.at[i, 2], ag_recv.at[i, 2], me.twin).start()

    def share_twin(i, ref):
        got = rows_of(ref, p_twin)
        remote(got, got, ag_send.at[i, 1], ag_recv.at[i, 1], me.twin).wait_recv()

    def share_corner(i, ref):
        got = rows_of(ref, p_corner)
        remote(got, got, ag_send.at[i, 2], ag_recv.at[i, 2], me.twin).wait_recv()

    fetched[0].wait()
    to_twin(0, 0, mm(part(o_rows, p_corner), wp_ref[...]))
    to_twin(0, 1, mm(part(o_rows, p_twin), wp_ref[...]))
    value = mm(part(o_rows, p_across), wp_ref[...])
    to_across(0, value + from_twin(0, 0))
    for copy in fetched[1:]:
        copy.wait()
    bias_row[...] = ebias_ref[...].astype(F32).reshape(1, D)
    for p in range(4):
        gact[p * 192 : p * 192 + 192, :] = mm_nt(gtwo_ref[p * 192 : p * 192 + 192, :], contract_ref[...])
    value = mm(part(o_rows, mine), wp_ref[...]) + from_twin(0, 1)
    value = value + from_across(0)
    middle = tok_ref[...].astype(F32) + BRANCH * (value + vec_ref[2:3, :])
    out, unit_two, inverse = layer_norm(middle, vec_ref[6:7, :], vec_ref[7:8, :])
    n2[pl.ds(pl.multiple_of(mine * 192, 192), 192), :] = out.astype(BF)
    share(0, n2)
    unit[...] = unit_two
    held[...] = middle

    def through(p):
        at = pl.ds(pl.multiple_of(p * 192, 192), 192)
        expanded = mm(n2[at, :], expand_ref[...]) + bias_row[...]
        activation, slope = gelu_pair(expanded)
        act[at, :] = activation.astype(BF)
        low = (gact[at, :] * slope).astype(BF)
        gexp[at, :] = low
        return mm_nt(low, expand_ref[...])

    own_value = through(mine)
    share_twin(0, n2)
    to_twin(1, 1, through(p_twin))
    share_across(0, n2)
    across_value = through(p_across)
    share_corner(0, n2)
    to_twin(1, 0, through(p_corner))
    to_across(1, across_value + from_twin(1, 0))
    own_value = own_value + from_twin(1, 1)
    to_twin(2, 0, mm(part(act, p_corner), contract_ref[...]))
    to_twin(2, 1, mm(part(act, p_twin), contract_ref[...]))
    to_across(2, mm(part(act, p_across), contract_ref[...]) + from_twin(2, 0))
    cpart_out[...] = mm_tn(act[...], gtwo_ref[...]).astype(BF)
    grad = own_value + from_across(1)
    unit_two = unit[...]
    scaled = grad * vec_ref[6:7, :]
    spread = (
        scaled
        - jnp.mean(scaled, axis=1, keepdims=True)
        - unit_two * jnp.mean(scaled * unit_two, axis=1, keepdims=True)
    )
    grad_middle = cot_ref[...].astype(F32) + inverse * spread
    gmid_out[...] = grad_middle
    low = (BRANCH * grad_middle).astype(BF)
    gone_out[pl.ds(pl.multiple_of(mine * 192, 192), 192), :] = low
    share(1, gone_out)
    sums_out[0:1, :] = jnp.sum(low.astype(F32), axis=0, keepdims=True)
    sums_out[1:2, :] = jnp.sum(part(gtwo_ref, mine).astype(F32), axis=0, keepdims=True)
    sums_out[2:3, :] = jnp.sum(grad * unit_two, axis=0, keepdims=True)
    sums_out[3:4, :] = jnp.sum(grad, axis=0, keepdims=True)
    sums_out[4:5, :] = jnp.sum(gexp[...].astype(F32), axis=0, keepdims=True)
    sums_out[5:8, :] = jnp.zeros((3, D), F32)
    epart_out[...] = mm_tn(n2[...], gexp[...]).astype(BF)
    value = mm(part(act, mine), contract_ref[...]) + from_twin(2, 1)
    value = value + from_across(2)
    block_out[...] = (held[...] + BRANCH * (value + vec_ref[3:4, :])).astype(BF)
    share_across(1, gone_out)
    share_twin(1, gone_out)
    share_corner(1, gone_out)
    for i in range(3):
        for slot in range(2):
            remote(c_send_buf.at[i, slot], c_recv_buf.at[i, slot], c_send.at[i, slot], c_recv.at[i, slot], me.twin).wait_send()
        remote(x_send_buf.at[i], x_recv_buf.at[i], x_send.at[i], x_recv.at[i], me.across).wait_send()
    for i, ref in ((0, n2), (1, gone_out)):
        own = rows_of(ref, mine)
        for j in range(3):
            remote(own, own, ag_send.at[i, j], ag_recv.at[i, j], me.twin).wait_send()


def feed_forward(o, wp, expand, contract, ebias, tokens, cotangent, gtwo, vectors):
    rows = tokens.shape[0]
    block = rows * 4
    vmem = pl.BlockSpec(memory_space=pltpu.VMEM)
    anywhere = pl.BlockSpec(memory_space=pl.ANY)
    dma = pltpu.SemaphoreType.DMA
    return pl.pallas_call(
        mlp_kernel,
        in_specs=[vmem, anywhere, vmem, anywhere, anywhere, anywhere, anywhere, vmem, vmem],
        out_specs=[vmem] * 6,
        out_shape=[
            jax.ShapeDtypeStruct((rows, D), BF),
            jax.ShapeDtypeStruct((rows, D), F32),
            jax.ShapeDtypeStruct((block, D), BF),
            jax.ShapeDtypeStruct((D, D), BF),
            jax.ShapeDtypeStruct((D, D), BF),
            jax.ShapeDtypeStruct((8, D), F32),
        ],
        scratch_shapes=[
            pltpu.VMEM((192, D), BF),
            pltpu.VMEM((D, D), BF),
            pltpu.VMEM((rows, D), BF),
            pltpu.VMEM((rows, D), BF),
            pltpu.VMEM((D,), BF),
            pltpu.VMEM((1, D), F32),
            pltpu.VMEM((block, 192), BF),
            pltpu.VMEM((block, D), F32),
            pltpu.VMEM((block, D), BF),
            pltpu.VMEM((block, D), BF),
            pltpu.VMEM((block, D), BF),
            pltpu.VMEM((rows, D), F32),
            pltpu.VMEM((rows, D), F32),
            pltpu.VMEM((3, 2, rows, D), BF),
            pltpu.VMEM((3, 2, rows, D), BF),
            pltpu.VMEM((3, rows, D), BF),
            pltpu.VMEM((3, rows, D), BF),
            dma((3, 2)), dma((3, 2)), dma((3,)), dma((3,)), dma((2, 3)), dma((2, 3)), dma((5,)),
        ],
        compiler_params=pltpu.CompilerParams(collective_id=2, has_side_effects=True, vmem_limit_bytes=58 << 20),
        name="feed_forward",
    )(o, wp, expand, contract, ebias, tokens, cotangent, gtwo, vectors)


ORDERS = (
    (
        "g0", "A0", "A1", "g1", "g2", "W0", "d0", "X0", "d1", "s0", "s1", "W1",
        "gf", "X1", "E", "d2", "dn", "s2", "v0", "r1", "v1", "af", "r2", "v2",
        "r3", "a", "v3",
    ),
    (
        "A0", "g0", "d0", "A1", "W0", "d1", "A2", "W1", "A3", "g1", "W2", "X0",
        "g2", "X1", "gf", "s0", "r1", "X2", "W3", "X3", "d2", "s1", "E", "s2",
        "r2", "dn", "af", "a", "v0", "v1", "v2", "r3", "v3",
    ),
    (
        "A0", "A1", "W0", "W1", "A2", "g0", "W2", "A3", "X0", "g1", "X1", "W3",
        "X2", "d0", "g2", "A4", "gf", "A5", "s0", "d1", "r1", "W4", "X3", "X4",
        "W5", "E", "d2", "r2", "r3", "s1", "s2", "X5", "af", "dn", "v0", "a",
        "v1", "v2", "v3",
    ),
    (
        "A0", "A1", "W0", "g0", "A2", "X0", "W1", "A3", "X1", "g1", "W2", "A4",
        "W3", "g2", "d0", "X2", "A5", "W4", "X3", "gf", "A6", "W5", "X4", "A7",
        "W6", "d1", "W7", "s0", "X5", "X6", "E", "s1", "d2", "X7", "s2", "dn",
        "v0", "r1", "r2", "af", "v1", "r3", "v2", "a", "v3",
    ),
)


class Exchange:
    def __init__(self, me, levels, items, y_send, y_recv, z_send, z_recv):
        self.me, self.top, self.items = me, levels - 1, items
        self.y_send, self.y_recv, self.z_send, self.z_recv = y_send, y_recv, z_send, z_recv

    def beside(self, level, act, only=None):
        for i, (chunk, y_in, z_out, z_in) in enumerate(self.items):
            if only is None or i in only:
                act(remote(chunk(level, 1 - self.me.side), y_in.at[level], self.y_send.at[level, i], self.y_recv.at[level, i], self.me.beside))

    def steps(self, step, act):
        z, top = self.me.level, self.top
        down = step - (top - z)
        up = top - (step - z)

        @pl.when((down >= 0) & (down < z))
        def _():
            act(down, 0)

        @pl.when((up <= top) & (up > z))
        def _():
            act(up, 1)

    def along(self, level, way, act):
        device = self.me.at(level=self.me.level - 1) if way == 0 else self.me.at(level=self.me.level + 1)
        last = level == (self.me.level - 1 if way == 0 else self.me.level + 1)
        spot = level if way == 0 else jnp.where(last, self.top + 1, level)
        for i, (chunk, y_in, z_out, z_in) in enumerate(self.items):
            act(remote(z_out.at[level], z_in.at[spot], self.z_send.at[level, i], self.z_recv.at[spot, i], device))

    def arrived(self, level, way):
        spot = level if way == 0 else jnp.where(level == self.me.level, self.top + 1, level)
        for i, (chunk, y_in, z_out, z_in) in enumerate(self.items):
            remote(z_out.at[level], z_in.at[spot], self.z_send.at[level, i], self.z_recv.at[spot, i], self.me.twin).wait_recv()
        return spot

    def step(self, step):
        z, top, side = self.me.level, self.top, self.me.side

        def act(level, way):
            self.beside(level, lambda copy: copy.wait_recv())
            inner = (z < top) if way == 0 else (z > 0)

            @pl.when(inner)
            def _():
                spot = self.arrived(level, way)
                for chunk, y_in, z_out, z_in in self.items:
                    z_out[level] = (
                        chunk(level, side)[...].astype(F32) + y_in[level].astype(F32) + z_in[spot].astype(F32)
                    ).astype(BF)

            @pl.when(jnp.logical_not(inner))
            def _():
                for chunk, y_in, z_out, z_in in self.items:
                    z_out[level] = (chunk(level, side)[...].astype(F32) + y_in[level].astype(F32)).astype(BF)

            self.along(level, way, lambda copy: copy.start())

        self.steps(step, act)

    def final(self, targets):
        z, top, side = self.me.level, self.top, self.me.side
        self.beside(z, lambda copy: copy.wait_recv())

        def add(spots):
            for (chunk, y_in, z_out, z_in), target in zip(self.items, targets):
                sum_of = chunk(z, side)[...].astype(F32) + y_in[z].astype(F32)
                for spot in spots:
                    sum_of = sum_of + z_in[spot].astype(F32)
                target[...] = sum_of.astype(BF)

        @pl.when(z < top)
        def _():
            self.arrived(z, 0)

        @pl.when(z > 0)
        def _():
            self.arrived(z, 1)

        @pl.when(z == 0)
        def _():
            add((z,))

        @pl.when(z == top)
        def _():
            add((top + 1,))

        @pl.when((z > 0) & (z < top))
        def _():
            add((z, top + 1))

    def drain(self):
        for level in range(self.top + 1):
            self.beside(level, lambda copy: copy.wait_send())

            @pl.when(level != self.me.level)
            def _():
                for i, (chunk, y_in, z_out, z_in) in enumerate(self.items):
                    remote(z_out.at[level], z_in.at[level], self.z_send.at[level, i], self.z_recv.at[level, i], self.me.twin).wait_send()


def attend_reduce_kernel(
    levels, starts_ref, all_ref, k_ref, v_ref, q_ref, o_ref, lse_ref, g_ref, wp_hbm, aw_ref,
    c_ref, e_ref, tok_hbm, gmid_ref, vec_ref, sums_ref,
    tg_out, cg_out, eg_out, a_rows, pg_out, vec_out,
    wp_ref, tok_ref, rows_in, keys_in, values_in, begins, qm, dm, qn, dn, delta, dqt, kt, dk, dv, gt, a_part, p_part,
    dnb, far, keep, x_in, y_out, y_in, d_out, d_in,
    yc, ye, ya, yp, zc_out, ze_out, za_out, zp_out, zc_in, ze_in, za_in, zp_in, v_out, v_in, e_move, a_move,
    pre_sem, far_send, far_recv, x_send, x_recv, y_send, y_recv, d_send, d_recv,
    gy_send, gy_recv, gz_send, gz_recv, ay_send, ay_recv, az_send, az_recv,
    me_send, me_recv, ma_send, ma_recv, u_send, u_recv, w_send, w_recv,
    be_send, be_recv, ba_send, ba_recv, te_send, te_recv, ta_send, ta_recv, v_send, v_recv, local_sem,
):
    me = Place()
    z, side, mine, ctx = me.level, me.side, me.part, me.ctx
    top = levels - 1
    block = g_ref.shape[0]
    barrier = pltpu.get_barrier_semaphore()
    for device in (me.twin, me.across, me.corner, me.beside):
        signal(barrier, device)
    for step in range(1, levels):
        signal(barrier, me.at(level=(z + step) % levels))
    below, above = me.at(level=z - 1), me.at(level=z + 1)
    start = lambda copy: copy.start()
    wait_recv = lambda copy: copy.wait_recv()
    wait_send = lambda copy: copy.wait_send()

    def prefetch(index):
        slot = index % 2
        at = pl.ds(pl.multiple_of(index * block, block), block)
        return (
            pltpu.make_async_copy(all_ref.at[at], rows_in.at[slot], pre_sem.at[slot, 0]),
            pltpu.make_async_copy(k_ref.at[at], keys_in.at[slot], pre_sem.at[slot, 1]),
            pltpu.make_async_copy(v_ref.at[at], values_in.at[slot], pre_sem.at[slot, 2]),
        )

    def all_of(copies, act):
        for copy in copies:
            act(copy)

    all_of(prefetch(0), start)
    fetched = (
        pltpu.make_async_copy(wp_hbm, wp_ref, local_sem.at[0]),
        pltpu.make_async_copy(tok_hbm, tok_ref, local_sem.at[1]),
    )
    all_of(fetched, start)

    def corner_of(ref, level, where):
        return ref.at[pl.ds(pl.multiple_of(level * 48, 48), 48), pl.ds(pl.multiple_of(where * 384, 128), 384)]

    grads = Exchange(
        me, levels,
        (
            (lambda level, where: c_ref.at[level * 2 + where], yc, zc_out, zc_in),
            (lambda level, where: e_ref.at[level * 2 + where], ye, ze_out, ze_in),
            (lambda level, where: corner_of(p_part, level, where), yp, zp_out, zp_in),
        ),
        gy_send, gy_recv, gz_send, gz_recv,
    )
    attends = Exchange(
        me, levels, ((lambda level, where: a_part.at[level * 2 + where], ya, za_out, za_in),), ay_send, ay_recv, az_send, az_recv
    )
    grads_in = g_ref[...]
    exact = o_ref[...]
    p_part[...] = mm(exact.astype(BF), grads_in).astype(BF)
    all_of(fetched, lambda copy: copy.wait())
    outer = mm_nt(grads_in, wp_ref[...]).astype(BF)
    pl.semaphore_wait(barrier, levels + 3)
    for step in range(levels - 1):
        grads.steps(step, lambda level, way: grads.beside(level, start))
    grads.beside(z, start)
    flipped = outer.astype(F32).T
    product = flipped * exact
    for head in range(3):
        delta[head : head + 1, :] = jnp.sum(product[head * HD : head * HD + HD], axis=0, keepdims=True)
    fill_masked_columns(dm, flipped.astype(BF))
    scaled = q_ref[...].astype(F32) * SCALE
    fill_masked_columns(qm, scaled.T.astype(BF))
    scaled = scaled.astype(BF)
    for head in range(3):
        depth = 128 if head < 2 else HD
        qn[head, :, 0:depth] = masked_rows(scaled, head)
        dn[head, :, 0:depth] = masked_rows(outer, head)
    dqt[...] = jnp.zeros(dqt.shape, F32)
    gt[...] = jnp.zeros(gt.shape, F32)
    first_query = ctx * block
    begins[...] = begins_of(starts_ref, first_query, block)
    v_out[0] = jnp.zeros(v_out.shape[1:], F32)

    def attend(index, diagonal):
        slot = index % 2
        first_key = index * block
        kt[...] = keys_in[slot].astype(F32).T.astype(BF)
        dk[...] = jnp.zeros(dk.shape, F32)
        dv[...] = jnp.zeros(dv.shape, F32)
        strips = [(head, strip) for head in range(3) for strip in range(block // STRIP)]

        def keys_of(strip):
            return strip * STRIP + STRIP if diagonal else block

        def scored(head, strip):
            depth = 128 if head < 2 else HD
            lanes = head_lanes(head)
            cols = slice(strip * STRIP, strip * STRIP + STRIP)
            count = keys_of(strip)
            return (
                mm(keys_in[slot, 0:count, lanes], qm[head, 0:depth, cols]),
                mm(values_in[slot, 0:count, lanes], dm[head, 0:depth, cols]),
            )

        ahead = [scored(*strips[i]) for i in range(BACK_LEAD)]
        for i, (head, strip) in enumerate(strips):
            scores, outer = ahead.pop(0)
            if i + BACK_LEAD < len(strips):
                ahead.append(scored(*strips[i + BACK_LEAD]))
            depth = 128 if head < 2 else HD
            lanes = head_lanes(head)
            cols = slice(strip * STRIP, strip * STRIP + STRIP)
            count = keys_of(strip)
            places = first_key + lax.broadcasted_iota(jnp.int32, (count, STRIP), 0)
            allowed = places >= begins[:, cols]
            if diagonal:
                queries = first_query + strip * STRIP + lax.broadcasted_iota(jnp.int32, (count, STRIP), 1)
                allowed = allowed & (places <= queries)
            probs = jnp.where(allowed, jnp.exp(scores - lse_ref[head : head + 1, cols]), 0.0)
            inner = (probs * (outer - delta[head : head + 1, cols])).astype(BF)
            dv[0:count, lanes] += mm(probs.astype(BF), dn[head, cols, 0:depth])
            dk[0:count, lanes] += mm(inner, qn[head, cols, 0:depth])
            part = slice(head * HD, head * HD + HD)
            dqt[part, cols] += mm(kt[part, 0:count], inner)
        rows = rows_in[slot]
        low_k = dk[...].astype(BF)
        low_v = dv[...].astype(BF)
        gt[192:384, :] += mm(low_k.astype(F32).T.astype(BF), rows)
        gt[384:576, :] += mm(low_v.astype(F32).T.astype(BF), rows)
        v_out[0, 12:13, 0:192] += jnp.sum(low_v.astype(F32), axis=0, keepdims=True)
        through = mm_nt(low_k, aw_ref[:, 192:384]) + mm_nt(low_v, aw_ref[:, 384:576])
        if diagonal:
            flipped = dqt[...] * SCALE
            low_q = flipped.T.astype(BF)
            gt[0:192, :] = mm(flipped.astype(BF), rows)
            v_out[0, 13:14, 0:192] = jnp.sum(low_q.astype(F32), axis=0, keepdims=True)
            through = through + mm_nt(low_q, aw_ref[:, 0:192])
        dnb[index % 3] = through.astype(BF)

    def to_twin(index):
        slot = index % 3
        return tuple(
            remote(
                rows_of(dnb.at[slot], half * 2 + 1 - me.core), far.at[index, half],
                far_send.at[index, half], far_recv.at[index, half], me.twin,
            )
            for half in range(2)
        )

    def x_copy(index):
        return remote(far.at[index, 0], x_in.at[index], x_send.at[index], x_recv.at[index], me.across)

    def y_copy(level):
        return remote(y_out.at[level], y_in.at[level], y_send.at[level], y_recv.at[level], me.beside)

    def down_copy(level):
        return remote(d_out.at[level], d_in.at[level], d_send.at[level], d_recv.at[level], below)

    def with_twin(index):
        slot = index % 3
        all_of(to_twin(index), lambda copy: copy.wait())

        def rows(half):
            own = dnb[slot, pl.ds(pl.multiple_of((half * 2 + me.core) * 192, 192), 192), :]
            return own.astype(F32) + far[index, half].astype(F32)

        keep[index] = rows(me.half)
        far[index, 0] = rows(1 - me.half).astype(BF)
        x_copy(index).start()

    def with_across(index):
        x_copy(index).wait_recv()
        keep[index] += x_in[index].astype(F32)
        level = index // 2

        @pl.when((index % 2 != side))
        def _():
            y_out[level] = keep[index].astype(BF)
            y_copy(level).start()

    def with_beside(level):
        y_copy(level).wait_recv()
        keep[level * 2 + side] += y_in[level].astype(F32)

    def dn_step(step):
        level = step - (top - z)

        @pl.when((level >= 0) & (level < z))
        def _():
            with_beside(level)
            index = level * 2 + side

            @pl.when(z < top)
            def _():
                down_copy(level).wait_recv()
                keep[index] += d_in[level].astype(F32)

            d_out[level] = keep[index].astype(BF)
            down_copy(level).start()

    def done(level, where):
        return (cg_out.at[level * 2 + where], corner_of(pg_out, level, where))

    def along_copies(way, distance):
        level = z - distance if way == 0 else z + distance
        device = above if way == 0 else below
        return tuple(
            remote(ref, ref, u_send.at[way, distance, i], u_recv.at[way, distance, i], device)
            for i, ref in enumerate(done(level, side))
        )

    def side_copies(level, where):
        return tuple(
            remote(ref, ref, w_send.at[level, i], w_recv.at[level, i], me.beside) for i, ref in enumerate(done(level, where))
        )

    def pass_on(distance, way):
        if way != 1:

            @pl.when(z < top)
            def _():
                all_of(along_copies(0, distance), start)

        if way != 0:

            @pl.when(z > 0)
            def _():
                all_of(along_copies(1, distance), start)

        all_of(side_copies(z - distance if way == 0 else z + distance, side), start)

    def arrivals(distance):
        for way in range(2):
            level = z - distance if way == 0 else z + distance

            @pl.when((level >= 0) & (level <= top))
            def _():
                for i, ref in enumerate(done(level, side)):
                    remote(ref, ref, u_send.at[way, distance - 1, i], u_recv.at[way, distance - 1, i], me.twin).wait_recv()
                pass_on(distance, way)

    def e_chunk(where, origin):
        return eg_out.at[pl.ds(pl.multiple_of(where * 96, 96), 96), pl.ds(pl.multiple_of(origin * D, D), D)]

    def a_chunk(where, origin):
        return a_rows.at[where, origin]

    class Rows:
        def __init__(self, moved, chunk, m_send, m_recv, b_send, b_recv, t_send, t_recv):
            self.moved, self.chunk = moved, chunk
            self.m_send, self.m_recv, self.b_send, self.b_recv = m_send, m_recv, b_send, b_recv
            self.t_send, self.t_recv = t_send, t_recv

        def move(self):
            return remote(self.moved, self.chunk(side, mine), self.m_send.at[0], self.m_recv.at[mine], me.at(half=z // 2, core=z % 2))

        def begin(self):
            @pl.when(mine != z)
            def _():
                self.move().start()

            @pl.when(mine == z)
            def _():
                self.chunk(side, mine)[...] = self.moved[...]

        def line(self, way, origin):
            ref = self.chunk(side, origin)
            return remote(ref, ref, self.b_send.at[way, origin], self.b_recv.at[way, origin], below if way == 0 else above)

        def turn(self, origin, where):
            ref = self.chunk(where, origin)
            return remote(ref, ref, self.t_send.at[origin], self.t_recv.at[origin], me.beside)

        def spread(self, origin):
            @pl.when((mine == z) & (mine != origin))
            def _():
                remote(self.moved, self.chunk(side, origin), self.m_send.at[0], self.m_recv.at[origin], me.twin).wait_recv()

            @pl.when(mine > z)
            def _():
                self.line(0, origin).wait_recv()

            @pl.when(mine < z)
            def _():
                self.line(1, origin).wait_recv()

            @pl.when((mine >= z) & (z > 0))
            def _():
                self.line(0, origin).start()

            @pl.when((mine <= z) & (z < top))
            def _():
                self.line(1, origin).start()

            self.turn(origin, side).start()

        def drain(self):
            @pl.when(mine != z)
            def _():
                self.move().wait_send()

            for origin in range(4):

                @pl.when((mine >= z) & (z > 0))
                def _():
                    self.line(0, origin).wait_send()

                @pl.when((mine <= z) & (z < top))
                def _():
                    self.line(1, origin).wait_send()

                self.turn(origin, side).wait_send()

    e_flow = Rows(e_move, e_chunk, me_send, me_recv, be_send, be_recv, te_send, te_recv)
    a_flow = Rows(a_move, a_chunk, ma_send, ma_recv, ba_send, ba_recv, ta_send, ta_recv)

    def finish_rows():
        @pl.when(side == 0)
        def _():
            with_beside(z)

        @pl.when(z < top)
        def _():
            down_copy(z).wait_recv()
            keep[ctx] += d_in[z].astype(F32)

        grad = keep[ctx]
        gain = vec_ref[4:5, :]
        normed, unit, inverse = layer_norm(tok_ref[...].astype(F32), gain, vec_ref[5:6, :])
        scaled = grad * gain
        spread = (
            scaled - jnp.mean(scaled, axis=1, keepdims=True) - unit * jnp.mean(scaled * unit, axis=1, keepdims=True)
        )
        tg_out[...] = (gmid_ref[...] + inverse * spread).astype(BF)
        for part in range(4):

            @pl.when(mine == part)
            def _():
                v_out[0, 0:1, part * 192 : part * 192 + 192] = v_out[0, 13:14, 0:192]
                v_out[0, 1:2, part * 192 : part * 192 + 192] = v_out[0, 12:13, 0:192]
                v_out[0, 8 + part : 9 + part, :] = sums_ref[4:5, :]

        v_out[0, 12:16, :] = jnp.zeros((4, D), F32)
        v_out[0, 2:4, :] = sums_ref[0:2, :]
        v_out[0, 4:5, :] = jnp.sum(grad * unit, axis=0, keepdims=True)
        v_out[0, 5:6, :] = jnp.sum(grad, axis=0, keepdims=True)
        v_out[0, 6:8, :] = sums_ref[2:4, :]

    def v_copy(i):
        return remote(v_out.at[i], v_in.at[i], v_send.at[i], v_recv.at[i], (me.twin, me.across, me.beside)[i])

    def vectors_on(i):
        if i > 0:
            v_copy(i - 1).wait_recv()
            v_out[i] = v_out[i - 1] + v_in[i - 1]
        if i < 3:
            v_copy(i).start()
        else:
            v_in[3 + z] = v_out[3]
            for step in range(1, levels):
                remote(
                    v_out.at[3], v_in.at[3 + z], v_send.at[2 + step], v_recv.at[3 + z], me.at(level=(z + step) % levels)
                ).start()


    def slot_of(name):
        spots = [order.index(name) if name in order else -1 for order in ORDERS]
        spot = jnp.int32(spots[0])
        for level in range(1, levels):
            spot = jnp.where(z == level, jnp.int32(spots[level]), spot)
        return spot

    def spots_of(kind, count):
        return [slot_of(kind + str(i)) for i in range(count)]

    spots = {kind: spots_of(kind, count) for kind, count in (("A", 8), ("W", 8), ("X", 8), ("g", 3), ("d", 3), ("s", 3), ("v", 4))}
    spots["r"] = [slot_of("r" + str(i + 1)) for i in range(3)]
    single = {name: slot_of(name) for name in ("gf", "af", "dn", "E", "a")}

    @pl.loop(0, max(len(order) for order in ORDERS))
    def _(slot):
        def number(kind):
            found = jnp.int32(-1)
            for i, spot in enumerate(spots[kind]):
                found = jnp.where(slot == spot, jnp.int32(i), found)
            return found

        turn = number("A")

        @pl.when((turn >= 0) & (turn <= ctx))
        def _():
            all_of(prefetch(turn), lambda copy: copy.wait())

            @pl.when(turn + 1 <= ctx)
            def _():
                all_of(prefetch(turn + 1), start)

            @pl.when(turn < ctx)
            def _():
                attend(turn, False)

            @pl.when(turn == ctx)
            def _():
                attend(turn, True)
                flipped = gt[...].T.astype(BF)
                for chunk in range(8):
                    a_part[chunk] = flipped[chunk * 96 : chunk * 96 + 96]
                for step in range(levels - 1):
                    attends.steps(step, lambda level, way: attends.beside(level, start))
                attends.beside(z, start)

            all_of(to_twin(turn), start)

        after = number("W")

        @pl.when((after >= 0) & (after <= ctx))
        def _():
            with_twin(after)

        last = number("X")

        @pl.when((last >= 0) & (last <= ctx))
        def _():
            with_across(last)

        for kind, act in (("g", grads.step), ("d", dn_step), ("s", attends.step)):
            step = number(kind)

            @pl.when(step >= 0)
            def _():
                act(step)

        distance = number("r")

        @pl.when(distance >= 0)
        def _():
            arrivals(distance + 1)

        @pl.when(slot == single["gf"])
        def _():
            grads.final((cg_out.at[ctx], e_move, corner_of(pg_out, z, side)))
            e_flow.begin()
            pass_on(0, 2)

        @pl.when(slot == single["af"])
        def _():
            attends.final((a_move,))
            a_flow.begin()

        for name, flow in (("E", e_flow), ("a", a_flow)):

            @pl.when(slot == single[name])
            def _():
                for origin in range(4):
                    flow.spread(origin)

        @pl.when(slot == single["dn"])
        def _():
            finish_rows()

        for i in range(4):

            @pl.when(slot == spots["v"][i])
            def _():
                vectors_on(i)

    for step in range(1, levels):
        level = (z + step) % levels
        remote(v_out.at[3], v_in.at[3 + level], v_send.at[2 + step], v_recv.at[3 + level], me.twin).wait_recv()
    total = v_in[3]
    for level in range(1, levels):
        total = total + v_in[3 + level]
    vec_out[...] = total

    for level in range(levels):
        all_of(side_copies(level, 1 - side), wait_recv)
    for flow in (e_flow, a_flow):
        for origin in range(4):
            flow.turn(origin, 1 - side).wait_recv()
    grads.drain()
    attends.drain()
    e_flow.drain()
    a_flow.drain()
    for level in range(levels):
        all_of(side_copies(level, side), wait_send)

        @pl.when((level < z) | ((level == z) & (side == 1)))
        def _():
            y_copy(level).wait_send()

        @pl.when(level < z)
        def _():
            down_copy(level).wait_send()

    @pl.loop(0, 2 * levels)
    def _(index):
        @pl.when(index <= ctx)
        def _():
            x_copy(index).wait_send()

    for distance in range(levels):

        @pl.when((z - distance >= 0) & (z < top))
        def _():
            all_of(along_copies(0, distance), wait_send)

        @pl.when((z + distance <= top) & (z > 0))
        def _():
            all_of(along_copies(1, distance), wait_send)

    for i in range(2 + levels):
        remote(v_out.at[0], v_in.at[0], v_send.at[i], v_recv.at[0], me.twin).wait_send()


def attend_reduce(starts, rows_all, k, v, q, o, lse, g, wp, aw, contract, expand, tokens, grad_middle, vectors, sums):
    levels = lax.axis_size("ctx") // 2
    rows = tokens.shape[0]
    block = rows * 4
    vmem = pl.BlockSpec(memory_space=pltpu.VMEM)
    anywhere = pl.BlockSpec(memory_space=pl.ANY)
    dma = pltpu.SemaphoreType.DMA
    n = levels

    def buf(*shape):
        return pltpu.VMEM(shape, BF)

    def wide(*shape):
        return pltpu.VMEM(shape, F32)

    return pl.pallas_call(
        functools.partial(attend_reduce_kernel, levels),
        in_specs=[pl.BlockSpec(memory_space=pltpu.SMEM)] + [anywhere] * 3 + [vmem] * 4 + [anywhere] + [vmem] * 3 + [anywhere] + [vmem] * 3,
        out_specs=[vmem] * 6,
        out_shape=[
            jax.ShapeDtypeStruct((rows, D), BF),
            jax.ShapeDtypeStruct((2 * n, 96, D), BF),
            jax.ShapeDtypeStruct((192, 4 * D), BF),
            jax.ShapeDtypeStruct((2, 4, 96, 576), BF),
            jax.ShapeDtypeStruct((192, D), BF),
            jax.ShapeDtypeStruct((16, D), F32),
        ],
        scratch_shapes=[
            buf(192, D), buf(rows, D),
            buf(2, block, D), buf(2, block, 192), buf(2, block, 192), pltpu.VMEM((1, block), jnp.int32),
            buf(3, 128, block), buf(3, 128, block), buf(3, block, 128), buf(3, block, 128),
            wide(8, block), wide(192, block), buf(192, block), wide(block, 192), wide(block, 192), wide(576, D),
            buf(2 * n, 96, 576), buf(192, D),
            buf(3, block, D), buf(2 * n, 2, rows, D), wide(2 * n, rows, D), buf(2 * n, rows, D),
            buf(n, rows, D), buf(n, rows, D), buf(n, rows, D), buf(n, rows, D),
            buf(n, 96, D), buf(n, 96, D), buf(n, 96, 576), buf(n, 48, 384),
            buf(n, 96, D), buf(n, 96, D), buf(n, 96, 576), buf(n, 48, 384),
            buf(n + 1, 96, D), buf(n + 1, 96, D), buf(n + 1, 96, 576), buf(n + 1, 48, 384),
            wide(4, 16, D), wide(3 + n, 16, D), buf(96, D), buf(96, 576),
            dma((2, 3)), dma((2 * n, 2)), dma((2 * n, 2)), dma((2 * n,)), dma((2 * n,)),
            dma((n,)), dma((n,)), dma((n,)), dma((n,)),
            dma((n, 3)), dma((n, 3)), dma((n, 3)), dma((n + 1, 3)),
            dma((n, 1)), dma((n, 1)), dma((n, 1)), dma((n + 1, 1)),
            dma((1,)), dma((4,)), dma((1,)), dma((4,)),
            dma((2, n, 2)), dma((2, n, 2)), dma((n, 2)), dma((n, 2)),
            dma((2, 4)), dma((2, 4)), dma((2, 4)), dma((2, 4)), dma((4,)), dma((4,)), dma((4,)), dma((4,)),
            dma((2 + n,)), dma((3 + n,)), dma((2,)),
        ],
        compiler_params=pltpu.CompilerParams(collective_id=5, has_side_effects=True, vmem_limit_bytes=60 << 20),
        name="attend_reduce",
    )(starts, rows_all, k, v, q, o, lse, g, wp, aw, contract, expand, tokens, grad_middle, vectors, sums)


def finish_kernel(
    tg_ref, c_ref, e_ref, a_ref, p_ref, vec_ref, block_ref,
    block_out, tg_out, a_out, ab_out, p_out, pb_out, e_out, hid_out, c_out, cb_out, gf_out, sf_out, gs_out, ss_out,
):
    mine = lax.axis_index("fsdp")
    block_out[...] = block_ref[...]
    tg_out[...] = tg_ref[...]
    p_out[...] = p_ref[...].astype(F32)
    e_out[...] = e_ref[...].astype(F32)
    for chunk in range(8):
        c_out[chunk * 96 : chunk * 96 + 96, :] = c_ref[chunk].astype(F32)
    for where in range(2):
        for part in range(4):
            for kind in range(3):
                lane = kind * D + part * 192
                a_out[where * 96 : where * 96 + 96, lane : lane + 192] = a_ref[
                    where, part, :, kind * 192 : kind * 192 + 192
                ].astype(F32)
    hid_out[...] = vec_ref[pl.ds(8 + mine, 1), :].reshape(D)
    for part in range(4):

        @pl.when(mine == part)
        def _():
            source, lane = part // 2, (part % 2) * 384
            ab_out[...] = vec_ref[source : source + 1, lane : lane + 384].reshape(384)
            for i, ref in enumerate((pb_out, cb_out, gf_out, sf_out, gs_out, ss_out)):
                ref[...] = vec_ref[2 + i : 3 + i, part * 192 : part * 192 + 192].reshape(192)


def finish(tokens_grad, contract, expand, attend, project, vectors, block_output):
    rows = tokens_grad.shape[0]
    one = jax.ShapeDtypeStruct((192,), F32)
    return pl.pallas_call(
        finish_kernel,
        in_specs=[pl.BlockSpec(memory_space=pltpu.VMEM)] * 7,
        out_shape=[
            jax.ShapeDtypeStruct((rows, D), BF),
            jax.ShapeDtypeStruct((rows, D), BF),
            jax.ShapeDtypeStruct((192, 3 * D), F32),
            jax.ShapeDtypeStruct((384,), F32),
            jax.ShapeDtypeStruct((192, D), F32),
            one,
            jax.ShapeDtypeStruct((192, 4 * D), F32),
            jax.ShapeDtypeStruct((D,), F32),
            jax.ShapeDtypeStruct((D, D), F32),
            one, one, one, one, one,
        ],
        compiler_params=pltpu.CompilerParams(vmem_limit_bytes=32 << 20),
        name="finish",
    )(tokens_grad, contract, expand, attend, project, vectors, block_output)


def normalize(rows_in, gain, shift):
    mean = jnp.mean(rows_in, axis=1, keepdims=True)
    centered = rows_in - mean
    inverse = lax.rsqrt(jnp.mean(centered * centered, axis=1, keepdims=True) + EPS)
    unit = centered * inverse
    return (unit * gain + shift, unit, inverse)


def normalize_back(incoming, unit, inverse, gain):
    scaled = incoming * gain
    spread = (
        scaled
        - jnp.mean(scaled, axis=1, keepdims=True)
        - unit * jnp.mean(scaled * unit, axis=1, keepdims=True)
    )
    return (inverse * spread, jnp.sum(incoming * unit, axis=0), jnp.sum(incoming, axis=0))


def first_position(places, starts):
    below = starts[None, :] <= places[:, None]
    return jnp.max(jnp.where(below, starts[None, :], 0), axis=1)


def forward_plain(
    tokens, document_starts, attend_weight, attend_bias, expand_weight, cotangent, own_vectors
):
    rows = tokens.shape[0]
    ways = lax.axis_size("fsdp")
    block = rows * ways
    ctx = lax.axis_index("ctx")
    part = lax.axis_index("fsdp")
    vectors = lax.dynamic_update_slice(jnp.zeros((6, D), F32), jnp.stack(own_vectors).astype(F32), (0, part * rows))
    biases = lax.dynamic_update_slice(jnp.zeros((2 * D,), F32), attend_bias.astype(F32), (part * 2 * rows,))
    vectors = jnp.concatenate([biases.reshape(2, D), vectors])
    attend_cols = attend_weight.reshape(rows, 3, ways, 192).transpose(2, 0, 1, 3).reshape(ways, rows, 576)
    normed_all, attend_cols, expand_cols, g2, vectors = gather_inputs(
        tokens, vectors, attend_cols, expand_weight, cotangent
    )
    wq, wk, wv = attend_cols[:, :192], attend_cols[:, 192:384], attend_cols[:, 384:]
    bias = lax.dynamic_slice(vectors, (0, part * 192), (2, 192))
    own = lax.dynamic_slice(normed_all, (ctx * block, 0), (block, D))
    where, begins_row = places_of(document_starts, block)
    q, k, v, o, lse = attend_forward(where, normed_all, own, wq, wk, wv, bias, begins_row)
    return normed_all, attend_cols, expand_cols, g2, vectors, q, k, v, o, lse


def places_of(document_starts, block):
    ctx = lax.axis_index("ctx")
    places = ctx * block + jnp.arange(block, dtype=jnp.int32)
    begins = first_position(places, document_starts)
    where = jnp.stack([ctx, begins[0], begins[-1]]).astype(jnp.int32)
    return where, begins.reshape(1, block)


def forward(tokens, document_starts, attend_weight, attend_bias, expand_weight, cotangent, own_vectors):
    rows = tokens.shape[0]
    if lax.axis_size("ctx") != 8:
        return forward_plain(
            tokens, document_starts, attend_weight, attend_bias, expand_weight, cotangent, own_vectors
        )
    return gather_attend(
        document_starts, tokens, attend_weight, expand_weight, cotangent, (attend_bias,) + tuple(own_vectors)
    )


def backward_plain(
    document_starts, normed_all, k, v, q, o, lse, g1, project_weight, attend_cols,
    contract_part, expand_part, tokens, grad_middle, vectors, mlp_sums,
):
    both = ("ctx", "fsdp")
    rows = tokens.shape[0]
    ways = lax.axis_size("fsdp")
    block = rows * ways
    ctx = lax.axis_index("ctx")
    part = lax.axis_index("fsdp")
    gain_one = vectors[4]
    wq, wk, wv = attend_cols[:, :192], attend_cols[:, 192:384], attend_cols[:, 384:]
    where, begins_row = places_of(document_starts, block)
    own = lax.dynamic_slice(normed_all, (ctx * block, 0), (block, D))
    dn, attend_t, project_part, sums = attend_backward(
        where, normed_all, k, v, own, q, o, lse, g1, project_weight, wq, wk, wv, begins_row
    )
    grad_normed = lax.psum_scatter(dn.astype(F32), both, scatter_dimension=0, tiled=True)
    normed, unit_one, inverse_one = normalize(tokens.astype(F32), gain_one, jnp.zeros_like(gain_one))
    first_part, gainone_grad, shiftone_grad = normalize_back(grad_normed, unit_one, inverse_one, gain_one)
    tokens_grad = (grad_middle + first_part).astype(BF)

    def summed(array_in):
        return lax.psum(array_in.astype(BF), "ctx").astype(F32)

    contract_grad = summed(contract_part)
    project_grad = summed(project_part)
    expand_grad = lax.all_to_all(summed(expand_part).reshape(ways, rows, D), "fsdp", 0, 0)
    expand_grad = expand_grad.transpose(1, 0, 2).reshape(rows, ways * D)
    attend_grad = lax.all_to_all(summed(attend_t.T).reshape(ways, rows, 576), "fsdp", 0, 0)
    attend_grad = attend_grad.reshape(ways, rows, 3, 192).transpose(1, 2, 0, 3).reshape(rows, 3 * D)
    spread = lax.dynamic_update_slice(jnp.zeros((2, D), F32), sums[:2], (0, part * 192))
    hidden = lax.dynamic_update_slice(jnp.zeros((4, D), F32), mlp_sums[4:5], (part, 0))
    totals = jnp.concatenate([
        spread, mlp_sums[0:2], gainone_grad[None], shiftone_grad[None], mlp_sums[2:4], hidden
    ])
    totals = lax.psum(totals, both)
    attbias = lax.dynamic_slice(totals[:2].reshape(-1), (part * 2 * rows,), (2 * rows,))
    mine = lax.dynamic_slice(totals, (2, part * rows), (6, rows))
    expbias = lax.dynamic_slice(totals, (8 + part, 0), (1, D)).reshape(D)
    return (
        tokens_grad, attend_grad, attbias, project_grad, mine[0], expand_grad, expbias,
        contract_grad, mine[1], mine[2], mine[3], mine[4], mine[5],
    )


def per_device(
    tokens, document_starts, attend_weight, attend_bias, project_weight, project_bias,
    expand_weight, expand_bias, contract_weight, contract_bias,
    gain_first, shift_first, gain_second, shift_second, cotangent,
):
    both = ("ctx", "fsdp")
    rows = tokens.shape[0]
    ways = lax.axis_size("fsdp")
    block = rows * ways
    ctx = lax.axis_index("ctx")
    part = lax.axis_index("fsdp")

    def whole(array_in):
        return lax.all_gather(array_in, "fsdp", axis=0, tiled=True)

    normed_all, attend_cols, expand_cols, g2, vectors, q, k, v, o, lse = forward(
        tokens, document_starts, attend_weight, attend_bias, expand_weight, cotangent,
        (project_bias, contract_bias, gain_first, shift_first, gain_second, shift_second),
    )
    block_output, grad_middle, g1, contract_part, expand_part, mlp_sums = feed_forward(
        o, project_weight, expand_cols, contract_weight, expand_bias, tokens, cotangent, g2, vectors
    )
    if lax.axis_size("ctx") != 8:
        return (block_output,) + backward_plain(
            document_starts, normed_all, k, v, q, o, lse, g1, project_weight, attend_cols,
            contract_part, expand_part, tokens, grad_middle, vectors, mlp_sums,
        )
    reduced = attend_reduce(
        document_starts, normed_all, k, v, q, o, lse, g1, project_weight, attend_cols,
        contract_part.reshape(8, 96, D), expand_part.reshape(8, 96, D), tokens, grad_middle, vectors, mlp_sums,
    )
    return tuple(finish(*reduced, block_output))


def solution(mesh):
    tok, row, vec = P(("ctx", "fsdp"), None), P("fsdp", None), P("fsdp")
    in_specs = (tok, P(), row, vec, row, vec, row, vec, row, vec, vec, vec, vec, vec, tok)
    out_specs = (tok, tok, row, vec, row, vec, row, vec, row, vec, vec, vec, vec, vec)
    return jax.shard_map(per_device, mesh=mesh, in_specs=in_specs, out_specs=out_specs, check_vma=False)
```

```python
import functools
import jax
import jax.numpy as jnp
from jax import lax
from jax.experimental import pallas as pl
from jax.experimental.pallas import tpu as pltpu
from jax.sharding import PartitionSpec as P

D = 768
H = 12
HD = 64
EPS = 1e-05
SCALE = 0.125
BRANCH = 48.0 ** (-0.5)
NEG = -1e30
SUB = 768
STRIP = 256
QS = STRIP
LEAD = 4
BACK_LEAD = 2
BF = jnp.bfloat16
F32 = jnp.float32


def mm(a, b):
    return jnp.dot(a, b, preferred_element_type=F32)


def mm_nt(a, b):
    return lax.dot_general(a, b, (((1,), (1,)), ((), ())), preferred_element_type=F32)


def mm_tn(a, b):
    return lax.dot_general(a, b, (((0,), (0,)), ((), ())), preferred_element_type=F32)


def head_lanes(head):
    return slice(0, 128) if head < 2 else slice(128, 192)


def fill_masked_columns(target, flipped):
    zero = jnp.zeros((HD, flipped.shape[1]), BF)
    target[0, 0:HD, :] = flipped[0:HD]
    target[0, HD : 2 * HD, :] = zero
    target[1, 0:HD, :] = zero
    target[1, HD : 2 * HD, :] = flipped[HD : 2 * HD]
    target[2, 0:HD, :] = flipped[2 * HD : 3 * HD]


def masked_rows(array_in, head):
    if head == 2:
        return array_in[:, 128:192]
    pair = array_in[:, 0:128]
    lane = lax.broadcasted_iota(jnp.int32, pair.shape, 1)
    return jnp.where((lane < HD) if head == 0 else (lane >= HD), pair, jnp.zeros_like(pair))


def allowed_pairs(first_key, first_query, begins, shape):
    key_places = first_key + lax.broadcasted_iota(jnp.int32, shape, 0)
    query_places = first_query + lax.broadcasted_iota(jnp.int32, shape, 1)
    return (key_places <= query_places) & (key_places >= begins)


def attend_forward_kernel(
    where_ref, rows_ref, own_ref, wq_ref, wk_ref, wv_ref, bias_ref, begins_ref,
    q_out, k_out, v_out, o_out, lse_out,
    qm, vt, peak, total, acc,
):
    turn = pl.program_id(0)
    block = own_ref.shape[0]
    mine, begin_low, begin_high = where_ref[0], where_ref[1], where_ref[2]
    first_query = mine * block
    needed = (turn <= mine) & ((turn + 1) * block - 1 >= begin_low)

    @pl.when(turn == 0)
    def _():
        query = (mm(own_ref[...], wq_ref[...]) + bias_ref[0:1, :]).astype(BF)
        q_out[...] = query
        fill_masked_columns(qm, (query.astype(F32) * SCALE).T.astype(BF))
        peak[...] = jnp.full(peak.shape, NEG, F32)
        total[...] = jnp.zeros(total.shape, F32)
        acc[...] = jnp.zeros(acc.shape, F32)

    @pl.when(needed)
    def _():
        rows = rows_ref[...]
        k_out[...] = mm(rows, wk_ref[...]).astype(BF)
        value = (mm(rows, wv_ref[...]) + bias_ref[1:2, :]).astype(BF)
        v_out[...] = value
        vt[...] = value.astype(F32).T.astype(BF)

        def one(step, masked):
            at = pl.ds(pl.multiple_of(step * SUB, SUB), SUB)
            first_key = turn * block + step * SUB
            if masked:
                allowed = allowed_pairs(first_key, first_query, begins_ref[...], (SUB, block))
            strips = [(head, strip) for head in range(3) for strip in range(block // QS)]

            def scored(head, strip):
                depth = 128 if head < 2 else HD
                return mm(k_out[at, head_lanes(head)], qm[head, 0:depth, strip * QS : strip * QS + QS])

            ahead = [scored(*strips[i]) for i in range(LEAD)]
            for i, (head, strip) in enumerate(strips):
                scores = ahead.pop(0)
                if i + LEAD < len(strips):
                    ahead.append(scored(*strips[i + LEAD]))
                lanes = slice(strip * QS, strip * QS + QS)
                if masked:
                    scores = jnp.where(allowed[:, lanes], scores, NEG)
                old = peak[head : head + 1, lanes]
                new = jnp.maximum(old, jnp.max(scores, axis=0, keepdims=True))
                weights = jnp.exp(scores - new)
                if masked:
                    weights = jnp.where(allowed[:, lanes], weights, 0.0)
                factor = jnp.exp(old - new)
                peak[head : head + 1, lanes] = new
                total[head : head + 1, lanes] = total[head : head + 1, lanes] * factor + jnp.sum(
                    weights, axis=0, keepdims=True
                )
                part = slice(head * HD, head * HD + HD)
                acc[part, lanes] = acc[part, lanes] * factor + mm(vt[part, at], weights.astype(BF))

        @pl.loop(0, block // SUB)
        def _(step):
            first_key = turn * block + step * SUB
            inner = (first_key + SUB - 1 <= first_query) & (first_key >= begin_high)
            touched = first_key + SUB - 1 >= begin_low

            @pl.when(inner)
            def _():
                one(step, False)

            @pl.when(jnp.logical_not(inner) & touched)
            def _():
                one(step, True)

    @pl.when(turn == mine)
    def _():
        for head in range(3):
            part = slice(head * HD, head * HD + HD)
            o_out[part, :] = acc[part, :] / total[head : head + 1, :]
        lse_out[...] = peak[...] + jnp.log(jnp.maximum(total[...], 1e-30))


def attend_forward(where, rows_all, own, wq, wk, wv, bias, begins):
    block = own.shape[0]
    count = rows_all.shape[0] // block

    def seen(turn, where_ref):
        return (jnp.minimum(turn, where_ref[0]), 0)

    def fixed(turn, where_ref):
        return (0, 0)

    return pl.pallas_call(
        attend_forward_kernel,
        grid_spec=pltpu.PrefetchScalarGridSpec(
            num_scalar_prefetch=1,
            grid=(count,),
            in_specs=[
                pl.BlockSpec((block, D), seen),
                pl.BlockSpec((block, D), fixed),
                pl.BlockSpec((D, 192), fixed),
                pl.BlockSpec((D, 192), fixed),
                pl.BlockSpec((D, 192), fixed),
                pl.BlockSpec((2, 192), fixed),
                pl.BlockSpec((1, block), fixed),
            ],
            out_specs=[
                pl.BlockSpec((block, 192), fixed),
                pl.BlockSpec((block, 192), seen),
                pl.BlockSpec((block, 192), seen),
                pl.BlockSpec((192, block), fixed),
                pl.BlockSpec((8, block), fixed),
            ],
            scratch_shapes=[
                pltpu.VMEM((3, 128, block), BF),
                pltpu.VMEM((192, block), BF),
                pltpu.VMEM((8, block), F32),
                pltpu.VMEM((8, block), F32),
                pltpu.VMEM((192, block), F32),
            ],
        ),
        out_shape=[
            jax.ShapeDtypeStruct((block, 192), BF),
            jax.ShapeDtypeStruct((block * count, 192), BF),
            jax.ShapeDtypeStruct((block * count, 192), BF),
            jax.ShapeDtypeStruct((192, block), F32),
            jax.ShapeDtypeStruct((8, block), F32),
        ],
        compiler_params=pltpu.CompilerParams(vmem_limit_bytes=48 << 20),
        name="attend_forward",
    )(where, rows_all, own, wq, wk, wv, bias, begins)


def attend_backward_kernel(
    where_ref, rows_ref, k_ref, v_ref, own_ref, q_ref, o_ref, lse_ref, g_ref, wp_ref,
    wq_ref, wk_ref, wv_ref, begins_ref,
    dn_out, grad_out, proj_out, sums_out,
    qm, dm, qn, dn, delta, dqt, kt, dk, dv,
):
    turn = pl.program_id(0)
    block = own_ref.shape[0]
    mine, begin_low, begin_high = where_ref[0], where_ref[1], where_ref[2]
    first_query = mine * block
    needed = (turn <= mine) & ((turn + 1) * block - 1 >= begin_low)

    @pl.when(turn == 0)
    def _():
        grads = g_ref[...]
        exact = o_ref[...]
        proj_out[...] = mm(exact.astype(BF), grads)
        outer = mm_nt(grads, wp_ref[...]).astype(BF)
        flipped = outer.astype(F32).T
        product = flipped * exact
        for head in range(3):
            delta[head : head + 1, :] = jnp.sum(
                product[head * HD : head * HD + HD], axis=0, keepdims=True
            )
        fill_masked_columns(dm, flipped.astype(BF))
        scaled = (q_ref[...].astype(F32) * SCALE)
        fill_masked_columns(qm, scaled.T.astype(BF))
        scaled = scaled.astype(BF)
        for head in range(3):
            depth = 128 if head < 2 else HD
            qn[head, :, 0:depth] = masked_rows(scaled, head)
            dn[head, :, 0:depth] = masked_rows(outer, head)
        dqt[...] = jnp.zeros(dqt.shape, F32)
        grad_out[...] = jnp.zeros(grad_out.shape, F32)
        sums_out[...] = jnp.zeros(sums_out.shape, F32)

    @pl.when(jnp.logical_not(needed))
    def _():
        dn_out[...] = jnp.zeros(dn_out.shape, BF)

    @pl.when(needed)
    def _():
        kt[...] = k_ref[...].astype(F32).T.astype(BF)
        dk[...] = jnp.zeros(dk.shape, F32)
        dv[...] = jnp.zeros(dv.shape, F32)

        def one(step, masked):
            at = pl.ds(pl.multiple_of(step * SUB, SUB), SUB)
            first_key = turn * block + step * SUB
            if masked:
                allowed = allowed_pairs(first_key, first_query, begins_ref[...], (SUB, block))
            for head in range(3):
                depth = 128 if head < 2 else HD
                lanes = head_lanes(head)
                scores = mm(k_ref[at, lanes], qm[head, 0:depth, :])
                probs = jnp.exp(scores - lse_ref[head : head + 1, :])
                if masked:
                    probs = jnp.where(allowed, probs, 0.0)
                outer = mm(v_ref[at, lanes], dm[head, 0:depth, :])
                inner = (probs * (outer - delta[head : head + 1, :])).astype(BF)
                dv[at, lanes] += mm(probs.astype(BF), dn[head, :, 0:depth])
                dk[at, lanes] += mm(inner, qn[head, :, 0:depth])
                part = slice(head * HD, head * HD + HD)
                dqt[part, :] += mm(kt[part, at], inner)

        @pl.loop(0, block // SUB)
        def _(step):
            first_key = turn * block + step * SUB
            inner = (first_key + SUB - 1 <= first_query) & (first_key >= begin_high)
            touched = first_key + SUB - 1 >= begin_low

            @pl.when(inner)
            def _():
                one(step, False)

            @pl.when(jnp.logical_not(inner) & touched)
            def _():
                one(step, True)

        rows = rows_ref[...]
        low_k = dk[...].astype(BF)
        low_v = dv[...].astype(BF)
        grad_out[192:384, :] += mm(low_k.astype(F32).T.astype(BF), rows)
        grad_out[384:576, :] += mm(low_v.astype(F32).T.astype(BF), rows)
        sums_out[1:2, :] += jnp.sum(low_v.astype(F32), axis=0, keepdims=True)
        through = mm_nt(low_k, wk_ref[...]) + mm_nt(low_v, wv_ref[...])

        @pl.when(turn < mine)
        def _():
            dn_out[...] = through.astype(BF)

        @pl.when(turn == mine)
        def _():
            flipped = dqt[...] * SCALE
            low_q = flipped.T.astype(BF)
            grad_out[0:192, :] += mm(flipped.astype(BF), own_ref[...])
            sums_out[0:1, :] += jnp.sum(low_q.astype(F32), axis=0, keepdims=True)
            dn_out[...] = (through + mm_nt(low_q, wq_ref[...])).astype(BF)


def attend_backward(where, rows_all, k, v, own, q, o, lse, g, wp, wq, wk, wv, begins):
    block = own.shape[0]
    count = rows_all.shape[0] // block

    def seen(turn, where_ref):
        return (jnp.minimum(turn, where_ref[0]), 0)

    def each(turn, where_ref):
        return (turn, 0)

    def fixed(turn, where_ref):
        return (0, 0)

    return pl.pallas_call(
        attend_backward_kernel,
        grid_spec=pltpu.PrefetchScalarGridSpec(
            num_scalar_prefetch=1,
            grid=(count,),
            in_specs=[
                pl.BlockSpec((block, D), seen),
                pl.BlockSpec((block, 192), seen),
                pl.BlockSpec((block, 192), seen),
                pl.BlockSpec((block, D), fixed),
                pl.BlockSpec((block, 192), fixed),
                pl.BlockSpec((192, block), fixed),
                pl.BlockSpec((8, block), fixed),
                pl.BlockSpec((block, D), fixed),
                pl.BlockSpec((192, D), fixed),
                pl.BlockSpec((D, 192), fixed),
                pl.BlockSpec((D, 192), fixed),
                pl.BlockSpec((D, 192), fixed),
                pl.BlockSpec((1, block), fixed),
            ],
            out_specs=[
                pl.BlockSpec((block, D), each),
                pl.BlockSpec((576, D), fixed),
                pl.BlockSpec((192, D), fixed),
                pl.BlockSpec((8, 192), fixed),
            ],
            scratch_shapes=[
                pltpu.VMEM((3, 128, block), BF),
                pltpu.VMEM((3, 128, block), BF),
                pltpu.VMEM((3, block, 128), BF),
                pltpu.VMEM((3, block, 128), BF),
                pltpu.VMEM((8, block), F32),
                pltpu.VMEM((192, block), F32),
                pltpu.VMEM((192, block), BF),
                pltpu.VMEM((block, 192), F32),
                pltpu.VMEM((block, 192), F32),
            ],
        ),
        out_shape=[
            jax.ShapeDtypeStruct((block * count, D), BF),
            jax.ShapeDtypeStruct((576, D), F32),
            jax.ShapeDtypeStruct((192, D), F32),
            jax.ShapeDtypeStruct((8, 192), F32),
        ],
        compiler_params=pltpu.CompilerParams(vmem_limit_bytes=48 << 20),
        name="attend_backward",
    )(where, rows_all, k, v, own, q, o, lse, g, wp, wq, wk, wv, begins)


MESH = pl.DeviceIdType.MESH


class Place:
    def __init__(self):
        ctx = lax.axis_index("ctx")
        part = lax.axis_index("fsdp")
        self.levels = lax.axis_size("ctx") // 2
        self.ctx, self.part = ctx, part
        self.level, self.side = ctx // 2, ctx % 2
        self.half, self.core = part // 2, part % 2

    def at(self, level=None, side=None, half=None, core=None):
        level = self.level if level is None else level
        side = self.side if side is None else side
        half = self.half if half is None else half
        core = self.core if core is None else core
        return (level * 2 + side, half * 2 + core)

    @property
    def twin(self):
        return self.at(core=1 - self.core)

    @property
    def across(self):
        return self.at(half=1 - self.half)

    @property
    def corner(self):
        return self.at(half=1 - self.half, core=1 - self.core)

    @property
    def beside(self):
        return self.at(side=1 - self.side)


def remote(source, target, send, recv, device):
    return pltpu.make_async_remote_copy(
        src_ref=source, dst_ref=target, send_sem=send, recv_sem=recv, device_id=device, device_id_type=MESH
    )


def signal(sem, device):
    pl.semaphore_signal(sem, inc=1, device_id=device, device_id_type=MESH)


def piece(ref, ctx, part):
    rows = 192
    return ref.at[pl.ds(pl.multiple_of((ctx * 4 + part) * rows, rows), rows)]


def rows_of(ref, part):
    return ref.at[pl.ds(pl.multiple_of(part * 192, 192), 192)]


def layer_norm(rows_in, gain, shift):
    mean = jnp.mean(rows_in, axis=1, keepdims=True)
    centered = rows_in - mean
    inverse = lax.rsqrt(jnp.mean(centered * centered, axis=1, keepdims=True) + EPS)
    unit = centered * inverse
    return unit * gain + shift, unit, inverse


def gather_kernel(
    levels, tok_ref, vec_ref, acol_ref, ecol_ref, cot_ref,
    all_ref, attend_ref, expand_ref, gtwo_ref, vec_out,
    normed, gtwo, vec_in,
    vec_send, vec_recv, att_send, att_recv, exp_send, exp_recv, two_send, two_recv,
    x_send, x_recv, z_send, z_recv, y_send, y_recv, core_send, core_recv, local_sem,
):
    me = Place()
    mine = me.part
    barrier = pltpu.get_barrier_semaphore()
    for device in (me.twin, me.across, me.corner, me.beside):
        signal(barrier, device)

    @pl.when(me.level > 0)
    def _():
        signal(barrier, me.at(level=me.level - 1))

    @pl.when(me.level < levels - 1)
    def _():
        signal(barrier, me.at(level=me.level + 1))

    ends = (me.level == 0).astype(jnp.int32) + (me.level == levels - 1).astype(jnp.int32)
    pl.semaphore_wait(barrier, 6 - ends)

    peers = (
        (me.twin, me.half * 2 + 1 - me.core),
        (me.across, (1 - me.half) * 2 + me.core),
        (me.corner, (1 - me.half) * 2 + 1 - me.core),
    )
    vecs = [remote(vec_ref, vec_in.at[i], vec_send.at[i], vec_recv.at[i], d) for i, (d, p) in enumerate(peers)]
    for copy in vecs:
        copy.start()
    atts = [
        remote(acol_ref.at[p], rows_of(attend_ref, mine), att_send.at[i], att_recv.at[i], d)
        for i, (d, p) in enumerate(peers)
    ]
    for copy in atts:
        copy.start()
    local = [
        pltpu.make_async_copy(acol_ref.at[mine], rows_of(attend_ref, mine), local_sem.at[0]),
        pltpu.make_async_copy(ecol_ref.at[:, pl.ds(pl.multiple_of(mine * D, D), D)], rows_of(expand_ref, mine), local_sem.at[1]),
    ]
    for copy in local:
        copy.start()
    gtwo[...] = (BRANCH * cot_ref[...].astype(F32)).astype(BF)
    for copy in vecs:
        copy.wait_recv()
    vec_out[...] = vec_ref[...] + vec_in[0] + vec_in[1] + vec_in[2]
    out, unit, inverse = layer_norm(tok_ref[...].astype(F32), vec_out[4:5, :], vec_out[5:6, :])
    normed[...] = out.astype(BF)

    def go(copy):
        copy.start()
        return copy

    ctx = me.ctx
    across = go(remote(normed, piece(all_ref, ctx, mine), x_send.at[0], x_recv.at[0], me.across))
    keep = go(pltpu.make_async_copy(normed, piece(all_ref, ctx, mine), local_sem.at[2]))
    keep_two = go(pltpu.make_async_copy(gtwo, rows_of(gtwo_ref, mine), local_sem.at[3]))
    local += [keep, keep_two]

    def spread_static(source, distance, slot):
        level = me.level - distance
        where = level * 2 + me.side
        half = me.half if slot == 0 else 1 - me.half
        part = half * 2 + me.core

        @pl.when(me.level < levels - 1)
        def _():
            remote(source, piece(all_ref, where, part), z_send.at[distance, slot], z_recv.at[distance + 1, slot], me.at(level=me.level + 1)).start()

        remote(source, piece(all_ref, where, part), y_send.at[distance, slot], y_recv.at[distance, slot], me.beside).start()
        remote(source, piece(all_ref, where, part), core_send.at[distance, 0, slot], core_recv.at[distance, 0, slot], me.twin).start()

    spread_static(normed, 0, 0)
    exps = [
        go(remote(ecol_ref.at[:, pl.ds(pl.multiple_of(p * D, D), D)], rows_of(expand_ref, mine), exp_send.at[i], exp_recv.at[i], d))
        for i, (d, p) in enumerate(peers)
    ]
    two_x = go(remote(gtwo, rows_of(gtwo_ref, mine), two_send.at[0], two_recv.at[0], me.across))
    two_c = go(remote(gtwo, rows_of(gtwo_ref, mine), two_send.at[1], two_recv.at[1], me.twin))

    other = (1 - me.half) * 2 + me.core

    def held(distance, slot, side):
        half = me.half if slot == 0 else 1 - me.half
        return piece(all_ref, (me.level - distance) * 2 + side, half * 2 + me.core)

    def take_y(distance):
        for slot in range(2):
            got = held(distance, slot, 1 - me.side)
            remote(got, got, y_send.at[distance, slot], y_recv.at[distance, slot], me.beside).wait_recv()
            remote(got, got, core_send.at[distance, 1, slot], core_recv.at[distance, 1, slot], me.twin).start()

    got = piece(all_ref, ctx, other)
    remote(normed, got, x_send.at[0], x_recv.at[0], me.across).wait_recv()
    spread_static(got, 0, 1)
    for distance in range(1, levels):

        @pl.when(me.level >= distance)
        def _():
            for slot in range(2):
                got = held(distance, slot, me.side)
                remote(got, got, z_send.at[distance, slot], z_recv.at[distance, slot], me.twin).wait_recv()
                spread_static(got, distance, slot)

        if distance == 1:
            take_y(0)
        else:

            @pl.when(me.level >= distance - 1)
            def _():
                take_y(distance - 1)

    @pl.when(me.level >= levels - 1)
    def _():
        take_y(levels - 1)

    got = rows_of(gtwo_ref, other)
    remote(gtwo, got, two_send.at[0], two_recv.at[0], me.across).wait_recv()
    two_f = go(remote(got, got, two_send.at[2], two_recv.at[2], me.twin))
    for copy in local:
        copy.wait()
    for copy in vecs:
        copy.wait_send()
    for copy in atts + exps + [two_c, two_f]:
        copy.wait()
    two_x.wait_send()
    across.wait_send()
    for distance in range(levels):

        @pl.when(me.level >= distance)
        def _():
            for slot in range(2):
                got = held(distance, slot, me.side)

                @pl.when(me.level < levels - 1)
                def _():
                    remote(got, got, z_send.at[distance, slot], z_recv.at[distance, slot], me.twin).wait_send()

                remote(got, got, y_send.at[distance, slot], y_recv.at[distance, slot], me.beside).wait_send()
                for side in range(2):
                    remote(got, got, core_send.at[distance, side, slot], core_recv.at[distance, side, slot], me.twin).wait()


def gather_inputs(tokens, vectors, attend_cols, expand_weight, cotangent):
    levels = lax.axis_size("ctx") // 2
    rows = tokens.shape[0]
    block = rows * 4
    vmem = pl.BlockSpec(memory_space=pltpu.VMEM)
    anywhere = pl.BlockSpec(memory_space=pl.ANY)
    dma = pltpu.SemaphoreType.DMA
    return pl.pallas_call(
        functools.partial(gather_kernel, levels),
        in_specs=[vmem, vmem, anywhere, anywhere, vmem],
        out_specs=[anywhere, anywhere, anywhere, anywhere, vmem],
        out_shape=[
            jax.ShapeDtypeStruct((block * levels * 2, D), BF),
            jax.ShapeDtypeStruct((D, 576), BF),
            jax.ShapeDtypeStruct((D, D), BF),
            jax.ShapeDtypeStruct((block, D), BF),
            jax.ShapeDtypeStruct((8, D), F32),
        ],
        scratch_shapes=[
            pltpu.VMEM((rows, D), BF),
            pltpu.VMEM((rows, D), BF),
            pltpu.VMEM((3, 8, D), F32),
            dma((3,)), dma((3,)), dma((3,)), dma((3,)), dma((3,)), dma((3,)), dma((3,)), dma((3,)),
            dma((1,)), dma((1,)),
            dma((levels, 2)), dma((levels + 1, 2)),
            dma((levels, 2)), dma((levels, 2)),
            dma((levels, 2, 2)), dma((levels, 2, 2)),
            dma((4,)),
        ],
        compiler_params=pltpu.CompilerParams(collective_id=1, has_side_effects=True, vmem_limit_bytes=16 << 20),
        name="gather_inputs",
    )(tokens, vectors, attend_cols, expand_weight, cotangent)


SHARE = 160


def begins_of(starts_ref, first, count):
    places = first + lax.broadcasted_iota(jnp.int32, (1, count), 1)
    begins = jnp.zeros((1, count), jnp.int32)
    for document in range(8):
        start = starts_ref[document]
        begins = jnp.where(places >= start, jnp.maximum(begins, start), begins)
    return begins


def gather_attend_kernel(
    levels, starts_ref, tok_hbm, aw_hbm, ew_ref, cot_hbm, *rest_refs,
):
    vector_hbm, vector_refs = rest_refs[:7], rest_refs[-7:]
    (
        all_ref, attend_ref, expand_ref, gtwo_ref, vec_out, q_out, k_out, v_out, o_out, lse_out,
        tok_ref, aw_ref, cot_ref, vec_ref, staged, vec_in, begins, qm, vt, acc, peak, total,
        vec_send, vec_recv, att_send, att_recv, exp_send, exp_recv, two_send, two_recv,
        x_send, x_recv, z_send, z_recv, y_send, y_recv, core_send, core_recv, r_send, r_recv, rc_send, rc_recv, local_sem,
    ) = rest_refs[7:-7]
    me = Place()
    mine, z, side = me.part, me.level, me.side
    top = levels - 1
    block = gtwo_ref.shape[0]
    fetched = (
        pltpu.make_async_copy(tok_hbm, tok_ref, local_sem.at[1]),
        pltpu.make_async_copy(aw_hbm, aw_ref, local_sem.at[2]),
        pltpu.make_async_copy(cot_hbm, cot_ref, local_sem.at[3]),
    ) + tuple(
        pltpu.make_async_copy(source, target, local_sem.at[4 + i])
        for i, (source, target) in enumerate(zip(vector_hbm, vector_refs))
    )
    for copy in fetched:
        copy.start()
    barrier = pltpu.get_barrier_semaphore()
    for device in (me.twin, me.across, me.corner, me.beside):
        signal(barrier, device)

    @pl.when(z > 0)
    def _():
        signal(barrier, me.at(level=z - 1))

    @pl.when(z < top)
    def _():
        signal(barrier, me.at(level=z + 1))

    for copy in fetched:
        copy.wait()
    both = vector_refs[0][...].astype(F32).reshape(1, 384)
    vec_ref[0:1, :] = both[:, 0:192]
    vec_ref[1:2, :] = both[:, 192:384]
    for i, ref in enumerate(vector_refs[1:]):
        vec_ref[2 + i : 3 + i, :] = ref[...].astype(F32).reshape(1, 192)
    for part in range(4):
        for kind in range(3):
            staged[part, :, kind * 192 : kind * 192 + 192] = aw_ref[:, kind * D + part * 192 : kind * D + part * 192 + 192]
    ends = (z == 0).astype(jnp.int32) + (z == top).astype(jnp.int32)
    pl.semaphore_wait(barrier, 6 - ends)

    peers = (
        (me.twin, me.half * 2 + 1 - me.core),
        (me.across, (1 - me.half) * 2 + me.core),
        (me.corner, (1 - me.half) * 2 + 1 - me.core),
    )

    def go(copy):
        copy.start()
        return copy

    vecs = [go(remote(vec_ref, vec_in.at[mine], vec_send.at[i], vec_recv.at[i], d)) for i, (d, p) in enumerate(peers)]
    atts = [
        remote(staged.at[p], rows_of(attend_ref, mine), att_send.at[i], att_recv.at[i], d) for i, (d, p) in enumerate(peers)
    ]
    atts[0].start()
    atts[1].start()
    vec_in[mine] = vec_ref[...]
    rows_of(attend_ref, mine)[...] = staged[mine]
    local = [
        go(pltpu.make_async_copy(
            ew_ref.at[:, pl.ds(pl.multiple_of(mine * D, D), D)], rows_of(expand_ref, mine), local_sem.at[0]
        ))
    ]
    own_two = rows_of(gtwo_ref, mine)
    own_two[...] = (BRANCH * cot_ref[...].astype(F32)).astype(BF)
    for i, (d, p) in enumerate(peers):
        remote(vec_ref, vec_in.at[p], vec_send.at[i], vec_recv.at[i], d).wait_recv()
    for part in range(4):
        vec_out[:, part * 192 : part * 192 + 192] = vec_in[part]
    out, unit, inverse = layer_norm(tok_ref[...].astype(F32), vec_out[4:5, :], vec_out[5:6, :])
    own_rows = piece(all_ref, me.ctx, mine)
    own_rows[...] = out.astype(BF)
    across = go(remote(own_rows, own_rows, x_send.at[0], x_recv.at[0], me.across))
    atts[2].start()

    def most(ref):
        return ref.at[pl.ds(0, SHARE)]

    def rest(ref):
        return ref.at[pl.ds(SHARE, 192 - SHARE)]

    def held(distance, slot, where):
        half = me.half + slot * (1 - 2 * me.half)
        return piece(all_ref, (z - distance) * 2 + where, half * 2 + me.core)

    def y_copy(distance, slot, where, whole):
        got = held(distance, slot, where)
        if not whole:
            got = most(got)
        return remote(got, got, y_send.at[distance, slot], y_recv.at[distance, slot], me.beside)

    def rest_up(distance, slot):
        got = rest(held(distance, slot, 1 - side))
        return remote(got, got, r_send.at[distance, slot], r_recv.at[distance + 1, slot], me.at(level=z + 1))

    def rest_twin(distance, slot):
        got = rest(held(distance, slot, 1 - side))
        return remote(got, got, rc_send.at[distance, slot], rc_recv.at[distance, slot], me.twin)

    def spread(distance, slot, first):
        half = me.half + slot * (1 - 2 * me.half)
        got = piece(all_ref, (z - distance) * 2 + side, half * 2 + me.core)

        @pl.when(z < top)
        def _():
            remote(got, got, z_send.at[distance, slot], z_recv.at[distance + 1, slot], me.at(level=z + 1)).start()

        y_copy(distance, slot, side, first).start()
        remote(got, got, core_send.at[distance, 0, slot], core_recv.at[distance, 0, slot], me.twin).start()

    def from_twin(distance, which, where, whole):
        for slot in range(2):
            half = me.half + slot * (1 - 2 * me.half)
            got = piece(all_ref, (z - distance) * 2 + where, half * 2 + 1 - me.core)
            if not whole:
                last = rest(got)
                remote(last, last, rc_send.at[distance, slot], rc_recv.at[distance, slot], me.twin).wait_recv()
                got = most(got)
            remote(got, got, core_send.at[distance, which, slot], core_recv.at[distance, which, slot], me.twin).wait_recv()

    spread(0, 0, True)
    two_x = go(remote(own_two, own_two, two_send.at[0], two_recv.at[0], me.across))
    two_c = go(remote(own_two, own_two, two_send.at[1], two_recv.at[1], me.twin))
    exps = [
        go(remote(ew_ref.at[:, pl.ds(pl.multiple_of(p * D, D), D)], rows_of(expand_ref, mine), exp_send.at[i], exp_recv.at[i], d))
        for i, (d, p) in enumerate(peers)
    ]
    begins[...] = begins_of(starts_ref, me.ctx * block, block)
    got = held(0, 1, side)
    remote(got, got, x_send.at[0], x_recv.at[0], me.across).wait_recv()
    spread(0, 1, True)
    def from_below(distance, slot):
        @pl.when(distance <= z)
        def _():
            got = held(distance, slot, side)
            remote(got, got, z_send.at[distance - 1, slot], z_recv.at[distance, slot], me.twin).wait_recv()
            spread(distance, slot, False)

    from_below(1, 0)
    for copy in atts:
        copy.wait_recv()
    from_twin(0, 0, side, True)

    first_query = me.ctx * block
    bias_q = vec_in[mine // 2, pl.ds(mine % 2, 1), :]
    query = (mm(all_ref[pl.ds(pl.multiple_of(first_query, block), block), :], attend_ref[:, 0:192]) + bias_q).astype(BF)
    q_out[...] = query
    fill_masked_columns(qm, (query.astype(F32) * SCALE).T.astype(BF))
    peak[...] = jnp.full(peak.shape, NEG, F32)
    total[...] = jnp.zeros(total.shape, F32)
    acc[...] = jnp.zeros(acc.shape, F32)

    def attend(ctx, diagonal):
        first_key = ctx * block
        at = pl.ds(pl.multiple_of(first_key, block), block)
        rows = all_ref[at, :]
        key = mm(rows, attend_ref[:, 192:384]).astype(BF)
        k_out[at, :] = key
        value = (mm(rows, attend_ref[:, 384:576]) + vec_in[2 + mine // 2, pl.ds(mine % 2, 1), :]).astype(BF)
        v_out[at, :] = value
        vt[...] = value.astype(F32).T.astype(BF)
        strips = [(head, strip) for head in range(3) for strip in range(block // STRIP)]

        def keys_of(strip):
            return strip * STRIP + STRIP if diagonal else block

        def scored(head, strip):
            depth = 128 if head < 2 else HD
            return mm(key[0 : keys_of(strip), head_lanes(head)], qm[head, 0:depth, strip * STRIP : strip * STRIP + STRIP])

        ahead = [scored(*strips[i]) for i in range(LEAD)]
        for i, (head, strip) in enumerate(strips):
            scores = ahead.pop(0)
            if i + LEAD < len(strips):
                ahead.append(scored(*strips[i + LEAD]))
            lanes = slice(strip * STRIP, strip * STRIP + STRIP)
            count = keys_of(strip)
            places = first_key + lax.broadcasted_iota(jnp.int32, (count, STRIP), 0)
            allowed = places >= begins[:, lanes]
            if diagonal:
                queries = first_query + strip * STRIP + lax.broadcasted_iota(jnp.int32, (count, STRIP), 1)
                allowed = allowed & (places <= queries)
            scores = jnp.where(allowed, scores, NEG)
            old = peak[head : head + 1, lanes]
            new = jnp.maximum(old, jnp.max(scores, axis=0, keepdims=True))
            weights = jnp.exp(scores - new)
            factor = jnp.exp(old - new)
            peak[head : head + 1, lanes] = new
            total[head : head + 1, lanes] = total[head : head + 1, lanes] * factor + jnp.sum(
                weights, axis=0, keepdims=True
            )
            part = slice(head * HD, head * HD + HD)
            acc[part, lanes] = acc[part, lanes] * factor + mm(vt[part, 0:count], weights.astype(BF))

    attend(me.ctx, True)

    def take_side(distance, whole):
        for slot in range(2):
            y_copy(distance, slot, 1 - side, whole).wait_recv()
            got = held(distance, slot, 1 - side)
            if not whole:
                got = most(got)
            remote(got, got, core_send.at[distance, 1, slot], core_recv.at[distance, 1, slot], me.twin).start()

    @pl.loop(1, 2 * levels)
    def _(turn):
        @pl.when(turn < 2 * levels - 2)
        def _():
            from_below(turn // 2 + 1, turn % 2)

        distance = turn // 2

        @pl.when(turn == 1)
        def _():
            take_side(0, True)

            @pl.when(z < top)
            def _():
                for slot in range(2):
                    rest_up(0, slot).start()

            from_twin(0, 1, 1 - side, True)

        @pl.when((turn > 1) & (turn % 2 == 1) & (distance <= z))
        def _():
            take_side(distance, False)
            for slot in range(2):
                got = rest(held(distance, slot, 1 - side))
                remote(got, got, r_send.at[distance - 1, slot], r_recv.at[distance, slot], me.twin).wait_recv()
                rest_twin(distance, slot).start()

                @pl.when(z < top)
                def _():
                    rest_up(distance, slot).start()

            from_twin(distance, 1, 1 - side, False)

        @pl.when((turn % 2 == 0) & (distance <= z))
        def _():
            from_twin(distance, 0, side, True)

        ctx = me.ctx - 2 * distance + (turn % 2) * (1 - 2 * side)

        @pl.when((ctx >= 0) & (ctx < me.ctx))
        def _():
            attend(ctx, False)

    for head in range(3):
        part = slice(head * HD, head * HD + HD)
        o_out[part, :] = acc[part, :] / total[head : head + 1, :]
    lse_out[...] = peak[...] + jnp.log(jnp.maximum(total[...], 1e-30))

    other = (1 - me.half) * 2 + me.core
    got = rows_of(gtwo_ref, other)
    remote(got, got, two_send.at[0], two_recv.at[0], me.across).wait_recv()
    two_f = go(remote(got, got, two_send.at[2], two_recv.at[2], me.twin))
    for copy in local:
        copy.wait()
    for copy in vecs + atts + [two_x, across]:
        copy.wait_send()
    for copy in exps + [two_c, two_f]:
        copy.wait()

    def left(distance, whole):
        for slot in range(2):
            got = held(distance, slot, side)

            @pl.when(z < top)
            def _():
                remote(got, got, z_send.at[distance, slot], z_recv.at[distance, slot], me.twin).wait_send()
                rest_up(distance, slot).wait_send()

            y_copy(distance, slot, side, whole).wait_send()
            remote(got, got, core_send.at[distance, 0, slot], core_recv.at[distance, 0, slot], me.twin).wait_send()
            if not whole:
                rest_twin(distance, slot).wait_send()
                got = most(got)
            remote(got, got, core_send.at[distance, 1, slot], core_recv.at[distance, 1, slot], me.twin).wait_send()

    left(0, True)

    @pl.loop(1, levels)
    def _(step):
        @pl.when(step <= z)
        def _():
            left(step, False)


def gather_attend(starts, tokens, attend_weight, expand_weight, cotangent, vectors):
    levels = lax.axis_size("ctx") // 2
    rows = tokens.shape[0]
    block = rows * 4
    length = block * levels * 2
    vmem = pl.BlockSpec(memory_space=pltpu.VMEM)
    dma = pltpu.SemaphoreType.DMA
    return pl.pallas_call(
        functools.partial(gather_attend_kernel, levels),
        in_specs=[pl.BlockSpec(memory_space=pltpu.SMEM)] + [pl.BlockSpec(memory_space=pl.ANY)] * 11,
        out_specs=[vmem] * 10,
        out_shape=[
            jax.ShapeDtypeStruct((length, D), BF),
            jax.ShapeDtypeStruct((D, 576), BF),
            jax.ShapeDtypeStruct((D, D), BF),
            jax.ShapeDtypeStruct((block, D), BF),
            jax.ShapeDtypeStruct((8, D), F32),
            jax.ShapeDtypeStruct((block, 192), BF),
            jax.ShapeDtypeStruct((length, 192), BF),
            jax.ShapeDtypeStruct((length, 192), BF),
            jax.ShapeDtypeStruct((192, block), F32),
            jax.ShapeDtypeStruct((8, block), F32),
        ],
        scratch_shapes=[
            pltpu.VMEM((rows, D), BF),
            pltpu.VMEM((rows, 3 * D), BF),
            pltpu.VMEM((rows, D), BF),
            pltpu.VMEM((8, 192), F32),
            pltpu.VMEM((4, rows, 576), BF),
            pltpu.VMEM((4, 8, 192), F32),
            pltpu.VMEM((1, block), jnp.int32),
            pltpu.VMEM((3, 128, block), BF),
            pltpu.VMEM((192, block), BF),
            pltpu.VMEM((192, block), F32),
            pltpu.VMEM((8, block), F32),
            pltpu.VMEM((8, block), F32),
            dma((3,)), dma((3,)), dma((3,)), dma((3,)), dma((3,)), dma((3,)), dma((3,)), dma((3,)),
            dma((1,)), dma((1,)),
            dma((levels, 2)), dma((levels + 1, 2)),
            dma((levels, 2)), dma((levels, 2)),
            dma((levels, 2, 2)), dma((levels, 2, 2)),
            dma((levels, 2)), dma((levels + 1, 2)), dma((levels, 2)), dma((levels, 2)),
            dma((11,)),
            pltpu.VMEM((2 * rows,), BF),
        ]
        + [pltpu.VMEM((rows,), BF)] * 6,
        compiler_params=pltpu.CompilerParams(collective_id=4, has_side_effects=True, vmem_limit_bytes=60 << 20),
        name="gather_attend",
    )(starts, tokens, attend_weight, expand_weight, cotangent, *vectors)


def gelu_pair(t):
    slope = 0.7978845608028654
    square = t * t
    bend = jnp.tanh(slope * t * (1.0 + 0.044715 * square))
    half = 0.5 * (1.0 + bend)
    return t * half, half + 0.5 * t * (1.0 - bend * bend) * (slope * (1.0 + 0.134145 * square))


def mlp_kernel(
    o_ref, wp_hbm, expand_ref, contract_hbm, ebias_hbm, tok_hbm, cot_hbm, gtwo_ref, vec_ref,
    block_out, gmid_out, gone_out, cpart_out, epart_out, sums_out,
    wp_ref, contract_ref, tok_ref, cot_ref, ebias_ref, bias_row, o_rows, gact, n2, act, gexp, held, unit,
    c_send_buf, c_recv_buf, x_send_buf, x_recv_buf,
    c_send, c_recv, x_send, x_recv, ag_send, ag_recv, local_sem,
):
    me = Place()
    mine = me.part
    fetched = [
        pltpu.make_async_copy(source, target, local_sem.at[i])
        for i, (source, target) in enumerate(
            ((wp_hbm, wp_ref), (contract_hbm, contract_ref), (tok_hbm, tok_ref), (cot_hbm, cot_ref), (ebias_hbm, ebias_ref))
        )
    ]
    for copy in fetched:
        copy.start()
    o_rows[...] = o_ref[...].T.astype(BF)
    barrier = pltpu.get_barrier_semaphore()
    signal(barrier, me.twin)
    signal(barrier, me.across)
    pl.semaphore_wait(barrier, 2)
    p_across = (1 - me.half) * 2 + me.core
    p_twin = me.half * 2 + 1 - me.core
    p_corner = (1 - me.half) * 2 + 1 - me.core

    def part(ref, p):
        return ref[pl.ds(pl.multiple_of(p * 192, 192), 192), :]

    def to_twin(i, slot, value):
        c_send_buf[i, slot] = value.astype(BF)
        remote(c_send_buf.at[i, slot], c_recv_buf.at[i, slot], c_send.at[i, slot], c_recv.at[i, slot], me.twin).start()

    def from_twin(i, slot):
        remote(c_send_buf.at[i, slot], c_recv_buf.at[i, slot], c_send.at[i, slot], c_recv.at[i, slot], me.twin).wait_recv()
        return c_recv_buf[i, slot].astype(F32)

    def to_across(i, value):
        x_send_buf[i] = value.astype(BF)
        remote(x_send_buf.at[i], x_recv_buf.at[i], x_send.at[i], x_recv.at[i], me.across).start()

    def from_across(i):
        remote(x_send_buf.at[i], x_recv_buf.at[i], x_send.at[i], x_recv.at[i], me.across).wait_recv()
        return x_recv_buf[i].astype(F32)

    def share(i, ref):
        own = rows_of(ref, mine)
        remote(own, own, ag_send.at[i, 0], ag_recv.at[i, 0], me.across).start()
        remote(own, own, ag_send.at[i, 1], ag_recv.at[i, 1], me.twin).start()

    def share_across(i, ref):
        got = rows_of(ref, p_across)
        remote(got, got, ag_send.at[i, 0], ag_recv.at[i, 0], me.across).wait_recv()
        remote(got, got, ag_send.at[i, 2], ag_recv.at[i, 2], me.twin).start()

    def share_twin(i, ref):
        got = rows_of(ref, p_twin)
        remote(got, got, ag_send.at[i, 1], ag_recv.at[i, 1], me.twin).wait_recv()

    def share_corner(i, ref):
        got = rows_of(ref, p_corner)
        remote(got, got, ag_send.at[i, 2], ag_recv.at[i, 2], me.twin).wait_recv()

    fetched[0].wait()
    to_twin(0, 0, mm(part(o_rows, p_corner), wp_ref[...]))
    to_twin(0, 1, mm(part(o_rows, p_twin), wp_ref[...]))
    value = mm(part(o_rows, p_across), wp_ref[...])
    to_across(0, value + from_twin(0, 0))
    for copy in fetched[1:]:
        copy.wait()
    bias_row[...] = ebias_ref[...].astype(F32).reshape(1, D)
    for p in range(4):
        gact[p * 192 : p * 192 + 192, :] = mm_nt(gtwo_ref[p * 192 : p * 192 + 192, :], contract_ref[...])
    value = mm(part(o_rows, mine), wp_ref[...]) + from_twin(0, 1)
    value = value + from_across(0)
    middle = tok_ref[...].astype(F32) + BRANCH * (value + vec_ref[2:3, :])
    out, unit_two, inverse = layer_norm(middle, vec_ref[6:7, :], vec_ref[7:8, :])
    n2[pl.ds(pl.multiple_of(mine * 192, 192), 192), :] = out.astype(BF)
    share(0, n2)
    unit[...] = unit_two
    held[...] = middle

    def through(p):
        at = pl.ds(pl.multiple_of(p * 192, 192), 192)
        expanded = mm(n2[at, :], expand_ref[...]) + bias_row[...]
        activation, slope = gelu_pair(expanded)
        act[at, :] = activation.astype(BF)
        low = (gact[at, :] * slope).astype(BF)
        gexp[at, :] = low
        return mm_nt(low, expand_ref[...])

    own_value = through(mine)
    share_twin(0, n2)
    to_twin(1, 1, through(p_twin))
    share_across(0, n2)
    across_value = through(p_across)
    share_corner(0, n2)
    to_twin(1, 0, through(p_corner))
    to_across(1, across_value + from_twin(1, 0))
    own_value = own_value + from_twin(1, 1)
    to_twin(2, 0, mm(part(act, p_corner), contract_ref[...]))
    to_twin(2, 1, mm(part(act, p_twin), contract_ref[...]))
    to_across(2, mm(part(act, p_across), contract_ref[...]) + from_twin(2, 0))
    cpart_out[...] = mm_tn(act[...], gtwo_ref[...]).astype(BF)
    grad = own_value + from_across(1)
    unit_two = unit[...]
    scaled = grad * vec_ref[6:7, :]
    spread = (
        scaled
        - jnp.mean(scaled, axis=1, keepdims=True)
        - unit_two * jnp.mean(scaled * unit_two, axis=1, keepdims=True)
    )
    grad_middle = cot_ref[...].astype(F32) + inverse * spread
    gmid_out[...] = grad_middle
    low = (BRANCH * grad_middle).astype(BF)
    gone_out[pl.ds(pl.multiple_of(mine * 192, 192), 192), :] = low
    share(1, gone_out)
    sums_out[0:1, :] = jnp.sum(low.astype(F32), axis=0, keepdims=True)
    sums_out[1:2, :] = jnp.sum(part(gtwo_ref, mine).astype(F32), axis=0, keepdims=True)
    sums_out[2:3, :] = jnp.sum(grad * unit_two, axis=0, keepdims=True)
    sums_out[3:4, :] = jnp.sum(grad, axis=0, keepdims=True)
    sums_out[4:5, :] = jnp.sum(gexp[...].astype(F32), axis=0, keepdims=True)
    sums_out[5:8, :] = jnp.zeros((3, D), F32)
    epart_out[...] = mm_tn(n2[...], gexp[...]).astype(BF)
    value = mm(part(act, mine), contract_ref[...]) + from_twin(2, 1)
    value = value + from_across(2)
    block_out[...] = (held[...] + BRANCH * (value + vec_ref[3:4, :])).astype(BF)
    share_across(1, gone_out)
    share_twin(1, gone_out)
    share_corner(1, gone_out)
    for i in range(3):
        for slot in range(2):
            remote(c_send_buf.at[i, slot], c_recv_buf.at[i, slot], c_send.at[i, slot], c_recv.at[i, slot], me.twin).wait_send()
        remote(x_send_buf.at[i], x_recv_buf.at[i], x_send.at[i], x_recv.at[i], me.across).wait_send()
    for i, ref in ((0, n2), (1, gone_out)):
        own = rows_of(ref, mine)
        for j in range(3):
            remote(own, own, ag_send.at[i, j], ag_recv.at[i, j], me.twin).wait_send()


def feed_forward(o, wp, expand, contract, ebias, tokens, cotangent, gtwo, vectors):
    rows = tokens.shape[0]
    block = rows * 4
    vmem = pl.BlockSpec(memory_space=pltpu.VMEM)
    anywhere = pl.BlockSpec(memory_space=pl.ANY)
    dma = pltpu.SemaphoreType.DMA
    return pl.pallas_call(
        mlp_kernel,
        in_specs=[vmem, anywhere, vmem, anywhere, anywhere, anywhere, anywhere, vmem, vmem],
        out_specs=[vmem] * 6,
        out_shape=[
            jax.ShapeDtypeStruct((rows, D), BF),
            jax.ShapeDtypeStruct((rows, D), F32),
            jax.ShapeDtypeStruct((block, D), BF),
            jax.ShapeDtypeStruct((D, D), BF),
            jax.ShapeDtypeStruct((D, D), BF),
            jax.ShapeDtypeStruct((8, D), F32),
        ],
        scratch_shapes=[
            pltpu.VMEM((192, D), BF),
            pltpu.VMEM((D, D), BF),
            pltpu.VMEM((rows, D), BF),
            pltpu.VMEM((rows, D), BF),
            pltpu.VMEM((D,), BF),
            pltpu.VMEM((1, D), F32),
            pltpu.VMEM((block, 192), BF),
            pltpu.VMEM((block, D), F32),
            pltpu.VMEM((block, D), BF),
            pltpu.VMEM((block, D), BF),
            pltpu.VMEM((block, D), BF),
            pltpu.VMEM((rows, D), F32),
            pltpu.VMEM((rows, D), F32),
            pltpu.VMEM((3, 2, rows, D), BF),
            pltpu.VMEM((3, 2, rows, D), BF),
            pltpu.VMEM((3, rows, D), BF),
            pltpu.VMEM((3, rows, D), BF),
            dma((3, 2)), dma((3, 2)), dma((3,)), dma((3,)), dma((2, 3)), dma((2, 3)), dma((5,)),
        ],
        compiler_params=pltpu.CompilerParams(collective_id=2, has_side_effects=True, vmem_limit_bytes=58 << 20),
        name="feed_forward",
    )(o, wp, expand, contract, ebias, tokens, cotangent, gtwo, vectors)


def mlp_near_kernel(
    o_ref, wp_hbm, expand_ref, contract_hbm, ebias_hbm, tok_hbm, cot_hbm, gtwo_ref, vec_ref,
    block_out, over_out, gmid_out, gone_out, cpart_out, epart_out, sums_out,
    wp_ref, contract_ref, tok_ref, cot_ref, ebias_ref, bias_row, o_rows, gact, n2, act, gexp, held, unit,
    c_send_buf, c_recv_buf, x_send_buf, x_recv_buf,
    c_send, c_recv, x_send, x_recv, ag_send, ag_recv, local_sem,
):
    me = Place()
    mine = me.part
    fetched = [
        pltpu.make_async_copy(source, target, local_sem.at[i])
        for i, (source, target) in enumerate(
            ((wp_hbm, wp_ref), (contract_hbm, contract_ref), (tok_hbm, tok_ref), (cot_hbm, cot_ref), (ebias_hbm, ebias_ref))
        )
    ]
    for copy in fetched:
        copy.start()
    o_rows[...] = o_ref[...].T.astype(BF)
    barrier = pltpu.get_barrier_semaphore()
    signal(barrier, me.twin)
    signal(barrier, me.across)
    pl.semaphore_wait(barrier, 2)
    p_across = (1 - me.half) * 2 + me.core
    p_twin = me.half * 2 + 1 - me.core
    p_corner = (1 - me.half) * 2 + 1 - me.core

    def part(ref, p):
        return ref[pl.ds(pl.multiple_of(p * 192, 192), 192), :]

    def to_twin(i, slot, value):
        c_send_buf[i, slot] = value.astype(BF)
        remote(c_send_buf.at[i, slot], c_recv_buf.at[i, slot], c_send.at[i, slot], c_recv.at[i, slot], me.twin).start()

    def from_twin(i, slot):
        remote(c_send_buf.at[i, slot], c_recv_buf.at[i, slot], c_send.at[i, slot], c_recv.at[i, slot], me.twin).wait_recv()
        return c_recv_buf[i, slot].astype(F32)

    def to_across(i, value):
        x_send_buf[i] = value.astype(BF)
        remote(x_send_buf.at[i], x_recv_buf.at[i], x_send.at[i], x_recv.at[i], me.across).start()

    def from_across(i):
        remote(x_send_buf.at[i], x_recv_buf.at[i], x_send.at[i], x_recv.at[i], me.across).wait_recv()
        return x_recv_buf[i].astype(F32)

    def share(i, ref):
        own = rows_of(ref, mine)
        remote(own, own, ag_send.at[i, 0], ag_recv.at[i, 0], me.across).start()
        remote(own, own, ag_send.at[i, 1], ag_recv.at[i, 1], me.twin).start()

    def share_across(i, ref):
        got = rows_of(ref, p_across)
        remote(got, got, ag_send.at[i, 0], ag_recv.at[i, 0], me.across).wait_recv()
        remote(got, got, ag_send.at[i, 2], ag_recv.at[i, 2], me.twin).start()

    def share_twin(i, ref):
        got = rows_of(ref, p_twin)
        remote(got, got, ag_send.at[i, 1], ag_recv.at[i, 1], me.twin).wait_recv()

    def share_corner(i, ref):
        got = rows_of(ref, p_corner)
        remote(got, got, ag_send.at[i, 2], ag_recv.at[i, 2], me.twin).wait_recv()

    fetched[0].wait()
    to_twin(0, 0, mm(part(o_rows, p_corner), wp_ref[...]))
    to_twin(0, 1, mm(part(o_rows, p_twin), wp_ref[...]))
    value = mm(part(o_rows, p_across), wp_ref[...])
    to_across(0, value + from_twin(0, 0))
    for copy in fetched[1:]:
        copy.wait()
    bias_row[...] = ebias_ref[...].astype(F32).reshape(1, D)
    for p in range(4):
        gact[p * 192 : p * 192 + 192, :] = mm_nt(gtwo_ref[p * 192 : p * 192 + 192, :], contract_ref[...])
    value = mm(part(o_rows, mine), wp_ref[...]) + from_twin(0, 1)
    value = value + from_across(0)
    middle = tok_ref[...].astype(F32) + BRANCH * (value + vec_ref[2:3, :])
    out, unit_two, inverse = layer_norm(middle, vec_ref[6:7, :], vec_ref[7:8, :])
    n2[pl.ds(pl.multiple_of(mine * 192, 192), 192), :] = out.astype(BF)
    share(0, n2)
    unit[...] = unit_two
    held[...] = middle

    def through(p):
        at = pl.ds(pl.multiple_of(p * 192, 192), 192)
        expanded = mm(n2[at, :], expand_ref[...]) + bias_row[...]
        activation, slope = gelu_pair(expanded)
        act[at, :] = activation.astype(BF)
        low = (gact[at, :] * slope).astype(BF)
        gexp[at, :] = low
        return mm_nt(low, expand_ref[...])

    own_value = through(mine)
    share_twin(0, n2)
    to_twin(1, 1, through(p_twin))
    share_across(0, n2)
    across_value = through(p_across)
    share_corner(0, n2)
    to_twin(1, 0, through(p_corner))
    to_across(1, across_value + from_twin(1, 0))
    own_value = own_value + from_twin(1, 1)
    to_twin(2, 0, mm(part(act, p_corner), contract_ref[...]))
    to_twin(2, 1, mm(part(act, p_twin), contract_ref[...]))
    cpart_out[...] = mm_tn(act[...], gtwo_ref[...]).astype(BF)
    grad = own_value + from_across(1)
    unit_two = unit[...]
    scaled = grad * vec_ref[6:7, :]
    spread = (
        scaled
        - jnp.mean(scaled, axis=1, keepdims=True)
        - unit_two * jnp.mean(scaled * unit_two, axis=1, keepdims=True)
    )
    grad_middle = cot_ref[...].astype(F32) + inverse * spread
    gmid_out[...] = grad_middle
    low = (BRANCH * grad_middle).astype(BF)
    gone_out[pl.ds(pl.multiple_of(mine * 192, 192), 192), :] = low
    share(1, gone_out)
    sums_out[0:1, :] = jnp.sum(low.astype(F32), axis=0, keepdims=True)
    sums_out[1:2, :] = jnp.sum(part(gtwo_ref, mine).astype(F32), axis=0, keepdims=True)
    sums_out[2:3, :] = jnp.sum(grad * unit_two, axis=0, keepdims=True)
    sums_out[3:4, :] = jnp.sum(grad, axis=0, keepdims=True)
    sums_out[4:5, :] = jnp.sum(gexp[...].astype(F32), axis=0, keepdims=True)
    sums_out[5:8, :] = jnp.zeros((3, D), F32)
    epart_out[...] = mm_tn(n2[...], gexp[...]).astype(BF)
    value = mm(part(act, mine), contract_ref[...]) + from_twin(2, 1)
    block_out[...] = held[...] + BRANCH * (value + vec_ref[3:4, :])
    over_out[...] = (mm(part(act, p_across), contract_ref[...]) + from_twin(2, 0)).astype(BF)
    share_across(1, gone_out)
    share_twin(1, gone_out)
    share_corner(1, gone_out)
    for i in range(3):
        for slot in range(2):
            remote(c_send_buf.at[i, slot], c_recv_buf.at[i, slot], c_send.at[i, slot], c_recv.at[i, slot], me.twin).wait_send()
    for i in range(2):
        remote(x_send_buf.at[i], x_recv_buf.at[i], x_send.at[i], x_recv.at[i], me.across).wait_send()
    for i, ref in ((0, n2), (1, gone_out)):
        own = rows_of(ref, mine)
        for j in range(3):
            remote(own, own, ag_send.at[i, j], ag_recv.at[i, j], me.twin).wait_send()


def feed_forward_near(o, wp, expand, contract, ebias, tokens, cotangent, gtwo, vectors):
    rows = tokens.shape[0]
    block = rows * 4
    vmem = pl.BlockSpec(memory_space=pltpu.VMEM)
    anywhere = pl.BlockSpec(memory_space=pl.ANY)
    dma = pltpu.SemaphoreType.DMA
    return pl.pallas_call(
        mlp_near_kernel,
        in_specs=[vmem, anywhere, vmem, anywhere, anywhere, anywhere, anywhere, vmem, vmem],
        out_specs=[vmem] * 7,
        out_shape=[
            jax.ShapeDtypeStruct((rows, D), F32),
            jax.ShapeDtypeStruct((rows, D), BF),
            jax.ShapeDtypeStruct((rows, D), F32),
            jax.ShapeDtypeStruct((block, D), BF),
            jax.ShapeDtypeStruct((D, D), BF),
            jax.ShapeDtypeStruct((D, D), BF),
            jax.ShapeDtypeStruct((8, D), F32),
        ],
        scratch_shapes=[
            pltpu.VMEM((192, D), BF),
            pltpu.VMEM((D, D), BF),
            pltpu.VMEM((rows, D), BF),
            pltpu.VMEM((rows, D), BF),
            pltpu.VMEM((D,), BF),
            pltpu.VMEM((1, D), F32),
            pltpu.VMEM((block, 192), BF),
            pltpu.VMEM((block, D), F32),
            pltpu.VMEM((block, D), BF),
            pltpu.VMEM((block, D), BF),
            pltpu.VMEM((block, D), BF),
            pltpu.VMEM((rows, D), F32),
            pltpu.VMEM((rows, D), F32),
            pltpu.VMEM((3, 2, rows, D), BF),
            pltpu.VMEM((3, 2, rows, D), BF),
            pltpu.VMEM((2, rows, D), BF),
            pltpu.VMEM((2, rows, D), BF),
            dma((3, 2)), dma((3, 2)), dma((2,)), dma((2,)), dma((2, 3)), dma((2, 3)), dma((5,)),
        ],
        compiler_params=pltpu.CompilerParams(collective_id=7, has_side_effects=True, vmem_limit_bytes=58 << 20),
        name="feed_forward_near",
    )(o, wp, expand, contract, ebias, tokens, cotangent, gtwo, vectors)


ORDERS = (
    (
        "g0", "A0", "A1", "g1", "g2", "W0", "d0", "X0", "d1", "s0", "s1", "W1",
        "gf", "X1", "E", "d2", "dn", "s2", "v0", "r1", "v1", "af", "r2", "v2",
        "r3", "a", "v3",
    ),
    (
        "A0", "g0", "d0", "A1", "W0", "d1", "A2", "W1", "A3", "g1", "W2", "X0",
        "g2", "X1", "gf", "s0", "r1", "X2", "W3", "X3", "d2", "s1", "E", "s2",
        "r2", "dn", "af", "a", "v0", "v1", "v2", "r3", "v3",
    ),
    (
        "A0", "A1", "W0", "W1", "A2", "g0", "W2", "A3", "X0", "g1", "X1", "W3",
        "X2", "d0", "g2", "A4", "gf", "A5", "s0", "d1", "r1", "W4", "X3", "X4",
        "W5", "E", "d2", "r2", "r3", "s1", "s2", "X5", "af", "dn", "v0", "a",
        "v1", "v2", "v3",
    ),
    (
        "A0", "A1", "W0", "g0", "A2", "X0", "W1", "A3", "X1", "g1", "W2", "A4",
        "W3", "g2", "d0", "X2", "A5", "W4", "X3", "gf", "A6", "W5", "X4", "A7",
        "W6", "d1", "W7", "s0", "X5", "X6", "E", "s1", "d2", "X7", "s2", "dn",
        "v0", "r1", "r2", "af", "v1", "r3", "v2", "a", "v3",
    ),
)


class Exchange:
    def __init__(self, me, levels, items, y_send, y_recv, z_send, z_recv):
        self.me, self.top, self.items = me, levels - 1, items
        self.y_send, self.y_recv, self.z_send, self.z_recv = y_send, y_recv, z_send, z_recv

    def beside(self, level, act, only=None):
        for i, (chunk, y_in, z_out, z_in) in enumerate(self.items):
            if only is None or i in only:
                act(remote(chunk(level, 1 - self.me.side), y_in.at[level], self.y_send.at[level, i], self.y_recv.at[level, i], self.me.beside))

    def steps(self, step, act):
        z, top = self.me.level, self.top
        down = step - (top - z)
        up = top - (step - z)

        @pl.when((down >= 0) & (down < z))
        def _():
            act(down, 0)

        @pl.when((up <= top) & (up > z))
        def _():
            act(up, 1)

    def along(self, level, way, act):
        device = self.me.at(level=self.me.level - 1) if way == 0 else self.me.at(level=self.me.level + 1)
        last = level == (self.me.level - 1 if way == 0 else self.me.level + 1)
        spot = level if way == 0 else jnp.where(last, self.top + 1, level)
        for i, (chunk, y_in, z_out, z_in) in enumerate(self.items):
            act(remote(z_out.at[level], z_in.at[spot], self.z_send.at[level, i], self.z_recv.at[spot, i], device))

    def arrived(self, level, way):
        spot = level if way == 0 else jnp.where(level == self.me.level, self.top + 1, level)
        for i, (chunk, y_in, z_out, z_in) in enumerate(self.items):
            remote(z_out.at[level], z_in.at[spot], self.z_send.at[level, i], self.z_recv.at[spot, i], self.me.twin).wait_recv()
        return spot

    def step(self, step):
        z, top, side = self.me.level, self.top, self.me.side

        def act(level, way):
            self.beside(level, lambda copy: copy.wait_recv())
            inner = (z < top) if way == 0 else (z > 0)

            @pl.when(inner)
            def _():
                spot = self.arrived(level, way)
                for chunk, y_in, z_out, z_in in self.items:
                    z_out[level] = (
                        chunk(level, side)[...].astype(F32) + y_in[level].astype(F32) + z_in[spot].astype(F32)
                    ).astype(BF)

            @pl.when(jnp.logical_not(inner))
            def _():
                for chunk, y_in, z_out, z_in in self.items:
                    z_out[level] = (chunk(level, side)[...].astype(F32) + y_in[level].astype(F32)).astype(BF)

            self.along(level, way, lambda copy: copy.start())

        self.steps(step, act)

    def final(self, targets):
        z, top, side = self.me.level, self.top, self.me.side
        self.beside(z, lambda copy: copy.wait_recv())

        def add(spots):
            for (chunk, y_in, z_out, z_in), target in zip(self.items, targets):
                sum_of = chunk(z, side)[...].astype(F32) + y_in[z].astype(F32)
                for spot in spots:
                    sum_of = sum_of + z_in[spot].astype(F32)
                target[...] = sum_of.astype(BF)

        @pl.when(z < top)
        def _():
            self.arrived(z, 0)

        @pl.when(z > 0)
        def _():
            self.arrived(z, 1)

        @pl.when(z == 0)
        def _():
            add((z,))

        @pl.when(z == top)
        def _():
            add((top + 1,))

        @pl.when((z > 0) & (z < top))
        def _():
            add((z, top + 1))

    def drain(self):
        for level in range(self.top + 1):
            self.beside(level, lambda copy: copy.wait_send())

            @pl.when(level != self.me.level)
            def _():
                for i, (chunk, y_in, z_out, z_in) in enumerate(self.items):
                    remote(z_out.at[level], z_in.at[level], self.z_send.at[level, i], self.z_recv.at[level, i], self.me.twin).wait_send()


def attend_reduce_kernel(
    levels, starts_ref, all_ref, k_ref, v_ref, q_ref, o_ref, lse_ref, g_ref, wp_hbm, aw_ref,
    c_ref, e_ref, tok_hbm, gmid_ref, vec_ref, sums_ref, near_ref, over_ref,
    tg_out, cg_out, eg_out, a_rows, pg_out, vec_out, block_out,
    over_in, wp_ref, tok_ref, rows_in, keys_in, values_in, begins, qm, dm, qn, dn, delta, dqt, kt, dk, dv, gt, a_part, p_part,
    dnb, far, keep, x_in, y_out, y_in, d_out, d_in,
    yc, ye, ya, yp, zc_out, ze_out, za_out, zp_out, zc_in, ze_in, za_in, zp_in, v_out, v_in, e_move, a_move,
    pre_sem, far_send, far_recv, x_send, x_recv, y_send, y_recv, d_send, d_recv,
    gy_send, gy_recv, gz_send, gz_recv, ay_send, ay_recv, az_send, az_recv,
    me_send, me_recv, ma_send, ma_recv, u_send, u_recv, w_send, w_recv,
    be_send, be_recv, ba_send, ba_recv, te_send, te_recv, ta_send, ta_recv, v_send, v_recv, local_sem, o_send, o_recv,
):
    me = Place()
    z, side, mine, ctx = me.level, me.side, me.part, me.ctx
    top = levels - 1
    block = g_ref.shape[0]
    barrier = pltpu.get_barrier_semaphore()
    for device in (me.twin, me.across, me.corner, me.beside):
        signal(barrier, device)
    for step in range(1, levels):
        signal(barrier, me.at(level=(z + step) % levels))
    below, above = me.at(level=z - 1), me.at(level=z + 1)
    start = lambda copy: copy.start()
    wait_recv = lambda copy: copy.wait_recv()
    wait_send = lambda copy: copy.wait_send()

    def prefetch(index):
        slot = index % 2
        at = pl.ds(pl.multiple_of(index * block, block), block)
        return (
            pltpu.make_async_copy(all_ref.at[at], rows_in.at[slot], pre_sem.at[slot, 0]),
            pltpu.make_async_copy(k_ref.at[at], keys_in.at[slot], pre_sem.at[slot, 1]),
            pltpu.make_async_copy(v_ref.at[at], values_in.at[slot], pre_sem.at[slot, 2]),
        )

    def all_of(copies, act):
        for copy in copies:
            act(copy)

    all_of(prefetch(0), start)
    fetched = (
        pltpu.make_async_copy(wp_hbm, wp_ref, local_sem.at[0]),
        pltpu.make_async_copy(tok_hbm, tok_ref, local_sem.at[1]),
    )
    all_of(fetched, start)

    def corner_of(ref, level, where):
        return ref.at[pl.ds(pl.multiple_of(level * 48, 48), 48), pl.ds(pl.multiple_of(where * 384, 128), 384)]

    grads = Exchange(
        me, levels,
        (
            (lambda level, where: c_ref.at[level * 2 + where], yc, zc_out, zc_in),
            (lambda level, where: e_ref.at[level * 2 + where], ye, ze_out, ze_in),
            (lambda level, where: corner_of(p_part, level, where), yp, zp_out, zp_in),
        ),
        gy_send, gy_recv, gz_send, gz_recv,
    )
    attends = Exchange(
        me, levels, ((lambda level, where: a_part.at[level * 2 + where], ya, za_out, za_in),), ay_send, ay_recv, az_send, az_recv
    )
    grads_in = g_ref[...]
    exact = o_ref[...]
    p_part[...] = mm(exact.astype(BF), grads_in).astype(BF)
    all_of(fetched, lambda copy: copy.wait())
    outer = mm_nt(grads_in, wp_ref[...]).astype(BF)
    pl.semaphore_wait(barrier, levels + 3)
    over = remote(over_ref, over_in, o_send.at[0], o_recv.at[0], me.across)
    over.start()
    for step in range(levels - 1):
        grads.steps(step, lambda level, way: grads.beside(level, start))
    grads.beside(z, start)
    flipped = outer.astype(F32).T
    product = flipped * exact
    for head in range(3):
        delta[head : head + 1, :] = jnp.sum(product[head * HD : head * HD + HD], axis=0, keepdims=True)
    fill_masked_columns(dm, flipped.astype(BF))
    scaled = q_ref[...].astype(F32) * SCALE
    fill_masked_columns(qm, scaled.T.astype(BF))
    scaled = scaled.astype(BF)
    for head in range(3):
        depth = 128 if head < 2 else HD
        qn[head, :, 0:depth] = masked_rows(scaled, head)
        dn[head, :, 0:depth] = masked_rows(outer, head)
    dqt[...] = jnp.zeros(dqt.shape, F32)
    gt[...] = jnp.zeros(gt.shape, F32)
    first_query = ctx * block
    begins[...] = begins_of(starts_ref, first_query, block)
    v_out[0] = jnp.zeros(v_out.shape[1:], F32)

    def attend(index, diagonal):
        slot = index % 2
        first_key = index * block
        kt[...] = keys_in[slot].astype(F32).T.astype(BF)
        dk[...] = jnp.zeros(dk.shape, F32)
        dv[...] = jnp.zeros(dv.shape, F32)
        strips = [(head, strip) for head in range(3) for strip in range(block // STRIP)]

        def keys_of(strip):
            return strip * STRIP + STRIP if diagonal else block

        def scored(head, strip):
            depth = 128 if head < 2 else HD
            lanes = head_lanes(head)
            cols = slice(strip * STRIP, strip * STRIP + STRIP)
            count = keys_of(strip)
            return (
                mm(keys_in[slot, 0:count, lanes], qm[head, 0:depth, cols]),
                mm(values_in[slot, 0:count, lanes], dm[head, 0:depth, cols]),
            )

        ahead = [scored(*strips[i]) for i in range(BACK_LEAD)]
        for i, (head, strip) in enumerate(strips):
            scores, outer = ahead.pop(0)
            if i + BACK_LEAD < len(strips):
                ahead.append(scored(*strips[i + BACK_LEAD]))
            depth = 128 if head < 2 else HD
            lanes = head_lanes(head)
            cols = slice(strip * STRIP, strip * STRIP + STRIP)
            count = keys_of(strip)
            places = first_key + lax.broadcasted_iota(jnp.int32, (count, STRIP), 0)
            allowed = places >= begins[:, cols]
            if diagonal:
                queries = first_query + strip * STRIP + lax.broadcasted_iota(jnp.int32, (count, STRIP), 1)
                allowed = allowed & (places <= queries)
            probs = jnp.where(allowed, jnp.exp(scores - lse_ref[head : head + 1, cols]), 0.0)
            inner = (probs * (outer - delta[head : head + 1, cols])).astype(BF)
            dv[0:count, lanes] += mm(probs.astype(BF), dn[head, cols, 0:depth])
            dk[0:count, lanes] += mm(inner, qn[head, cols, 0:depth])
            part = slice(head * HD, head * HD + HD)
            dqt[part, cols] += mm(kt[part, 0:count], inner)
        rows = rows_in[slot]
        low_k = dk[...].astype(BF)
        low_v = dv[...].astype(BF)
        gt[192:384, :] += mm(low_k.astype(F32).T.astype(BF), rows)
        gt[384:576, :] += mm(low_v.astype(F32).T.astype(BF), rows)
        v_out[0, 12:13, 0:192] += jnp.sum(low_v.astype(F32), axis=0, keepdims=True)
        through = mm_nt(low_k, aw_ref[:, 192:384]) + mm_nt(low_v, aw_ref[:, 384:576])
        if diagonal:
            flipped = dqt[...] * SCALE
            low_q = flipped.T.astype(BF)
            gt[0:192, :] = mm(flipped.astype(BF), rows)
            v_out[0, 13:14, 0:192] = jnp.sum(low_q.astype(F32), axis=0, keepdims=True)
            through = through + mm_nt(low_q, aw_ref[:, 0:192])
        dnb[index % 3] = through.astype(BF)

    def to_twin(index):
        slot = index % 3
        return tuple(
            remote(
                rows_of(dnb.at[slot], half * 2 + 1 - me.core), far.at[index, half],
                far_send.at[index, half], far_recv.at[index, half], me.twin,
            )
            for half in range(2)
        )

    def x_copy(index):
        return remote(far.at[index, 0], x_in.at[index], x_send.at[index], x_recv.at[index], me.across)

    def y_copy(level):
        return remote(y_out.at[level], y_in.at[level], y_send.at[level], y_recv.at[level], me.beside)

    def down_copy(level):
        return remote(d_out.at[level], d_in.at[level], d_send.at[level], d_recv.at[level], below)

    def with_twin(index):
        slot = index % 3
        all_of(to_twin(index), lambda copy: copy.wait())

        def rows(half):
            own = dnb[slot, pl.ds(pl.multiple_of((half * 2 + me.core) * 192, 192), 192), :]
            return own.astype(F32) + far[index, half].astype(F32)

        keep[index] = rows(me.half)
        far[index, 0] = rows(1 - me.half).astype(BF)
        x_copy(index).start()

    def with_across(index):
        x_copy(index).wait_recv()
        keep[index] += x_in[index].astype(F32)
        level = index // 2

        @pl.when((index % 2 != side))
        def _():
            y_out[level] = keep[index].astype(BF)
            y_copy(level).start()

    def with_beside(level):
        y_copy(level).wait_recv()
        keep[level * 2 + side] += y_in[level].astype(F32)

    def dn_step(step):
        level = step - (top - z)

        @pl.when((level >= 0) & (level < z))
        def _():
            with_beside(level)
            index = level * 2 + side

            @pl.when(z < top)
            def _():
                down_copy(level).wait_recv()
                keep[index] += d_in[level].astype(F32)

            d_out[level] = keep[index].astype(BF)
            down_copy(level).start()

    def done(level, where):
        return (cg_out.at[level * 2 + where], corner_of(pg_out, level, where))

    def along_copies(way, distance):
        level = z - distance if way == 0 else z + distance
        device = above if way == 0 else below
        return tuple(
            remote(ref, ref, u_send.at[way, distance, i], u_recv.at[way, distance, i], device)
            for i, ref in enumerate(done(level, side))
        )

    def side_copies(level, where):
        return tuple(
            remote(ref, ref, w_send.at[level, i], w_recv.at[level, i], me.beside) for i, ref in enumerate(done(level, where))
        )

    def pass_on(distance, way):
        if way != 1:

            @pl.when(z < top)
            def _():
                all_of(along_copies(0, distance), start)

        if way != 0:

            @pl.when(z > 0)
            def _():
                all_of(along_copies(1, distance), start)

        all_of(side_copies(z - distance if way == 0 else z + distance, side), start)

    def arrivals(distance):
        for way in range(2):
            level = z - distance if way == 0 else z + distance

            @pl.when((level >= 0) & (level <= top))
            def _():
                for i, ref in enumerate(done(level, side)):
                    remote(ref, ref, u_send.at[way, distance - 1, i], u_recv.at[way, distance - 1, i], me.twin).wait_recv()
                pass_on(distance, way)

    def e_chunk(where, origin):
        return eg_out.at[pl.ds(pl.multiple_of(where * 96, 96), 96), pl.ds(pl.multiple_of(origin * D, D), D)]

    def a_chunk(where, origin):
        return a_rows.at[where, origin]

    class Rows:
        def __init__(self, moved, chunk, m_send, m_recv, b_send, b_recv, t_send, t_recv):
            self.moved, self.chunk = moved, chunk
            self.m_send, self.m_recv, self.b_send, self.b_recv = m_send, m_recv, b_send, b_recv
            self.t_send, self.t_recv = t_send, t_recv

        def move(self):
            return remote(self.moved, self.chunk(side, mine), self.m_send.at[0], self.m_recv.at[mine], me.at(half=z // 2, core=z % 2))

        def begin(self):
            @pl.when(mine != z)
            def _():
                self.move().start()

            @pl.when(mine == z)
            def _():
                self.chunk(side, mine)[...] = self.moved[...]

        def line(self, way, origin):
            ref = self.chunk(side, origin)
            return remote(ref, ref, self.b_send.at[way, origin], self.b_recv.at[way, origin], below if way == 0 else above)

        def turn(self, origin, where):
            ref = self.chunk(where, origin)
            return remote(ref, ref, self.t_send.at[origin], self.t_recv.at[origin], me.beside)

        def spread(self, origin):
            @pl.when((mine == z) & (mine != origin))
            def _():
                remote(self.moved, self.chunk(side, origin), self.m_send.at[0], self.m_recv.at[origin], me.twin).wait_recv()

            @pl.when(mine > z)
            def _():
                self.line(0, origin).wait_recv()

            @pl.when(mine < z)
            def _():
                self.line(1, origin).wait_recv()

            @pl.when((mine >= z) & (z > 0))
            def _():
                self.line(0, origin).start()

            @pl.when((mine <= z) & (z < top))
            def _():
                self.line(1, origin).start()

            self.turn(origin, side).start()

        def drain(self):
            @pl.when(mine != z)
            def _():
                self.move().wait_send()

            for origin in range(4):

                @pl.when((mine >= z) & (z > 0))
                def _():
                    self.line(0, origin).wait_send()

                @pl.when((mine <= z) & (z < top))
                def _():
                    self.line(1, origin).wait_send()

                self.turn(origin, side).wait_send()

    e_flow = Rows(e_move, e_chunk, me_send, me_recv, be_send, be_recv, te_send, te_recv)
    a_flow = Rows(a_move, a_chunk, ma_send, ma_recv, ba_send, ba_recv, ta_send, ta_recv)

    def finish_rows():
        @pl.when(side == 0)
        def _():
            with_beside(z)

        @pl.when(z < top)
        def _():
            down_copy(z).wait_recv()
            keep[ctx] += d_in[z].astype(F32)

        grad = keep[ctx]
        gain = vec_ref[4:5, :]
        normed, unit, inverse = layer_norm(tok_ref[...].astype(F32), gain, vec_ref[5:6, :])
        scaled = grad * gain
        spread = (
            scaled - jnp.mean(scaled, axis=1, keepdims=True) - unit * jnp.mean(scaled * unit, axis=1, keepdims=True)
        )
        tg_out[...] = (gmid_ref[...] + inverse * spread).astype(BF)
        for part in range(4):

            @pl.when(mine == part)
            def _():
                v_out[0, 0:1, part * 192 : part * 192 + 192] = v_out[0, 13:14, 0:192]
                v_out[0, 1:2, part * 192 : part * 192 + 192] = v_out[0, 12:13, 0:192]
                v_out[0, 8 + part : 9 + part, :] = sums_ref[4:5, :]

        v_out[0, 12:16, :] = jnp.zeros((4, D), F32)
        v_out[0, 2:4, :] = sums_ref[0:2, :]
        v_out[0, 4:5, :] = jnp.sum(grad * unit, axis=0, keepdims=True)
        v_out[0, 5:6, :] = jnp.sum(grad, axis=0, keepdims=True)
        v_out[0, 6:8, :] = sums_ref[2:4, :]

    def v_copy(i):
        return remote(v_out.at[i], v_in.at[i], v_send.at[i], v_recv.at[i], (me.twin, me.across, me.beside)[i])

    def vectors_on(i):
        if i > 0:
            v_copy(i - 1).wait_recv()
            v_out[i] = v_out[i - 1] + v_in[i - 1]
        if i < 3:
            v_copy(i).start()
        else:
            v_in[3 + z] = v_out[3]
            for step in range(1, levels):
                remote(
                    v_out.at[3], v_in.at[3 + z], v_send.at[2 + step], v_recv.at[3 + z], me.at(level=(z + step) % levels)
                ).start()


    def slot_of(name):
        spots = [order.index(name) if name in order else -1 for order in ORDERS]
        spot = jnp.int32(spots[0])
        for level in range(1, levels):
            spot = jnp.where(z == level, jnp.int32(spots[level]), spot)
        return spot

    def spots_of(kind, count):
        return [slot_of(kind + str(i)) for i in range(count)]

    spots = {kind: spots_of(kind, count) for kind, count in (("A", 8), ("W", 8), ("X", 8), ("g", 3), ("d", 3), ("s", 3), ("v", 4))}
    spots["r"] = [slot_of("r" + str(i + 1)) for i in range(3)]
    single = {name: slot_of(name) for name in ("gf", "af", "dn", "E", "a")}

    @pl.loop(0, max(len(order) for order in ORDERS))
    def _(slot):
        def number(kind):
            found = jnp.int32(-1)
            for i, spot in enumerate(spots[kind]):
                found = jnp.where(slot == spot, jnp.int32(i), found)
            return found

        turn = number("A")

        @pl.when((turn >= 0) & (turn <= ctx))
        def _():
            all_of(prefetch(turn), lambda copy: copy.wait())

            @pl.when(turn + 1 <= ctx)
            def _():
                all_of(prefetch(turn + 1), start)

            @pl.when(turn < ctx)
            def _():
                attend(turn, False)

            @pl.when(turn == ctx)
            def _():
                attend(turn, True)
                flipped = gt[...].T.astype(BF)
                for chunk in range(8):
                    a_part[chunk] = flipped[chunk * 96 : chunk * 96 + 96]
                for step in range(levels - 1):
                    attends.steps(step, lambda level, way: attends.beside(level, start))
                attends.beside(z, start)

            all_of(to_twin(turn), start)

        after = number("W")

        @pl.when((after >= 0) & (after <= ctx))
        def _():
            with_twin(after)

        last = number("X")

        @pl.when((last >= 0) & (last <= ctx))
        def _():
            with_across(last)

        for kind, act in (("g", grads.step), ("d", dn_step), ("s", attends.step)):
            step = number(kind)

            @pl.when(step >= 0)
            def _():
                act(step)

        distance = number("r")

        @pl.when(distance >= 0)
        def _():
            arrivals(distance + 1)

        @pl.when(slot == single["gf"])
        def _():
            grads.final((cg_out.at[ctx], e_move, corner_of(pg_out, z, side)))
            e_flow.begin()
            pass_on(0, 2)

        @pl.when(slot == single["af"])
        def _():
            attends.final((a_move,))
            a_flow.begin()

        for name, flow in (("E", e_flow), ("a", a_flow)):

            @pl.when(slot == single[name])
            def _():
                for origin in range(4):
                    flow.spread(origin)

        @pl.when(slot == single["dn"])
        def _():
            finish_rows()

        for i in range(4):

            @pl.when(slot == spots["v"][i])
            def _():
                vectors_on(i)

    for step in range(1, levels):
        level = (z + step) % levels
        remote(v_out.at[3], v_in.at[3 + level], v_send.at[2 + step], v_recv.at[3 + level], me.twin).wait_recv()
    total = v_in[3]
    for level in range(1, levels):
        total = total + v_in[3 + level]
    vec_out[...] = total

    over.wait()
    block_out[...] = (near_ref[...] + BRANCH * over_in[...].astype(F32)).astype(BF)
    for level in range(levels):
        all_of(side_copies(level, 1 - side), wait_recv)
    for flow in (e_flow, a_flow):
        for origin in range(4):
            flow.turn(origin, 1 - side).wait_recv()
    grads.drain()
    attends.drain()
    e_flow.drain()
    a_flow.drain()
    for level in range(levels):
        all_of(side_copies(level, side), wait_send)

        @pl.when((level < z) | ((level == z) & (side == 1)))
        def _():
            y_copy(level).wait_send()

        @pl.when(level < z)
        def _():
            down_copy(level).wait_send()

    @pl.loop(0, 2 * levels)
    def _(index):
        @pl.when(index <= ctx)
        def _():
            x_copy(index).wait_send()

    for distance in range(levels):

        @pl.when((z - distance >= 0) & (z < top))
        def _():
            all_of(along_copies(0, distance), wait_send)

        @pl.when((z + distance <= top) & (z > 0))
        def _():
            all_of(along_copies(1, distance), wait_send)

    for i in range(2 + levels):
        remote(v_out.at[0], v_in.at[0], v_send.at[i], v_recv.at[0], me.twin).wait_send()


def attend_reduce(starts, rows_all, k, v, q, o, lse, g, wp, aw, contract, expand, tokens, grad_middle, vectors, sums, near, over):
    levels = lax.axis_size("ctx") // 2
    rows = tokens.shape[0]
    block = rows * 4
    vmem = pl.BlockSpec(memory_space=pltpu.VMEM)
    anywhere = pl.BlockSpec(memory_space=pl.ANY)
    dma = pltpu.SemaphoreType.DMA
    n = levels

    def buf(*shape):
        return pltpu.VMEM(shape, BF)

    def wide(*shape):
        return pltpu.VMEM(shape, F32)

    return pl.pallas_call(
        functools.partial(attend_reduce_kernel, levels),
        in_specs=[pl.BlockSpec(memory_space=pltpu.SMEM)] + [anywhere] * 3 + [vmem] * 4 + [anywhere] + [vmem] * 3 + [anywhere] + [vmem] * 5,
        out_specs=[vmem] * 7,
        out_shape=[
            jax.ShapeDtypeStruct((rows, D), BF),
            jax.ShapeDtypeStruct((2 * n, 96, D), BF),
            jax.ShapeDtypeStruct((192, 4 * D), BF),
            jax.ShapeDtypeStruct((2, 4, 96, 576), BF),
            jax.ShapeDtypeStruct((192, D), BF),
            jax.ShapeDtypeStruct((16, D), F32),
            jax.ShapeDtypeStruct((rows, D), BF),
        ],
        scratch_shapes=[
            buf(rows, D), buf(192, D), buf(rows, D),
            buf(2, block, D), buf(2, block, 192), buf(2, block, 192), pltpu.VMEM((1, block), jnp.int32),
            buf(3, 128, block), buf(3, 128, block), buf(3, block, 128), buf(3, block, 128),
            wide(8, block), wide(192, block), buf(192, block), wide(block, 192), wide(block, 192), wide(576, D),
            buf(2 * n, 96, 576), buf(192, D),
            buf(3, block, D), buf(2 * n, 2, rows, D), wide(2 * n, rows, D), buf(2 * n, rows, D),
            buf(n, rows, D), buf(n, rows, D), buf(n, rows, D), buf(n, rows, D),
            buf(n, 96, D), buf(n, 96, D), buf(n, 96, 576), buf(n, 48, 384),
            buf(n, 96, D), buf(n, 96, D), buf(n, 96, 576), buf(n, 48, 384),
            buf(n + 1, 96, D), buf(n + 1, 96, D), buf(n + 1, 96, 576), buf(n + 1, 48, 384),
            wide(4, 16, D), wide(3 + n, 16, D), buf(96, D), buf(96, 576),
            dma((2, 3)), dma((2 * n, 2)), dma((2 * n, 2)), dma((2 * n,)), dma((2 * n,)),
            dma((n,)), dma((n,)), dma((n,)), dma((n,)),
            dma((n, 3)), dma((n, 3)), dma((n, 3)), dma((n + 1, 3)),
            dma((n, 1)), dma((n, 1)), dma((n, 1)), dma((n + 1, 1)),
            dma((1,)), dma((4,)), dma((1,)), dma((4,)),
            dma((2, n, 2)), dma((2, n, 2)), dma((n, 2)), dma((n, 2)),
            dma((2, 4)), dma((2, 4)), dma((2, 4)), dma((2, 4)), dma((4,)), dma((4,)), dma((4,)), dma((4,)),
            dma((2 + n,)), dma((3 + n,)), dma((2,)), dma((1,)), dma((1,)),
        ],
        compiler_params=pltpu.CompilerParams(collective_id=5, has_side_effects=True, vmem_limit_bytes=60 << 20),
        name="attend_reduce",
    )(starts, rows_all, k, v, q, o, lse, g, wp, aw, contract, expand, tokens, grad_middle, vectors, sums, near, over)


def finish_kernel(
    tg_ref, c_ref, e_ref, a_ref, p_ref, vec_ref, block_ref,
    block_out, tg_out, a_out, ab_out, p_out, pb_out, e_out, hid_out, c_out, cb_out, gf_out, sf_out, gs_out, ss_out,
):
    mine = lax.axis_index("fsdp")
    block_out[...] = block_ref[...]
    tg_out[...] = tg_ref[...]
    p_out[...] = p_ref[...].astype(F32)
    e_out[...] = e_ref[...].astype(F32)
    for chunk in range(8):
        c_out[chunk * 96 : chunk * 96 + 96, :] = c_ref[chunk].astype(F32)
    for where in range(2):
        for part in range(4):
            for kind in range(3):
                lane = kind * D + part * 192
                a_out[where * 96 : where * 96 + 96, lane : lane + 192] = a_ref[
                    where, part, :, kind * 192 : kind * 192 + 192
                ].astype(F32)
    hid_out[...] = vec_ref[pl.ds(8 + mine, 1), :].reshape(D)
    for part in range(4):

        @pl.when(mine == part)
        def _():
            source, lane = part // 2, (part % 2) * 384
            ab_out[...] = vec_ref[source : source + 1, lane : lane + 384].reshape(384)
            for i, ref in enumerate((pb_out, cb_out, gf_out, sf_out, gs_out, ss_out)):
                ref[...] = vec_ref[2 + i : 3 + i, part * 192 : part * 192 + 192].reshape(192)


def finish(tokens_grad, contract, expand, attend, project, vectors, block_output):
    rows = tokens_grad.shape[0]
    one = jax.ShapeDtypeStruct((192,), F32)
    return pl.pallas_call(
        finish_kernel,
        in_specs=[pl.BlockSpec(memory_space=pltpu.VMEM)] * 7,
        out_shape=[
            jax.ShapeDtypeStruct((rows, D), BF),
            jax.ShapeDtypeStruct((rows, D), BF),
            jax.ShapeDtypeStruct((192, 3 * D), F32),
            jax.ShapeDtypeStruct((384,), F32),
            jax.ShapeDtypeStruct((192, D), F32),
            one,
            jax.ShapeDtypeStruct((192, 4 * D), F32),
            jax.ShapeDtypeStruct((D,), F32),
            jax.ShapeDtypeStruct((D, D), F32),
            one, one, one, one, one,
        ],
        compiler_params=pltpu.CompilerParams(vmem_limit_bytes=58 << 20),
        name="finish",
    )(tokens_grad, contract, expand, attend, project, vectors, block_output)


def normalize(rows_in, gain, shift):
    mean = jnp.mean(rows_in, axis=1, keepdims=True)
    centered = rows_in - mean
    inverse = lax.rsqrt(jnp.mean(centered * centered, axis=1, keepdims=True) + EPS)
    unit = centered * inverse
    return (unit * gain + shift, unit, inverse)


def normalize_back(incoming, unit, inverse, gain):
    scaled = incoming * gain
    spread = (
        scaled
        - jnp.mean(scaled, axis=1, keepdims=True)
        - unit * jnp.mean(scaled * unit, axis=1, keepdims=True)
    )
    return (inverse * spread, jnp.sum(incoming * unit, axis=0), jnp.sum(incoming, axis=0))


def first_position(places, starts):
    below = starts[None, :] <= places[:, None]
    return jnp.max(jnp.where(below, starts[None, :], 0), axis=1)


def forward_plain(
    tokens, document_starts, attend_weight, attend_bias, expand_weight, cotangent, own_vectors
):
    rows = tokens.shape[0]
    ways = lax.axis_size("fsdp")
    block = rows * ways
    ctx = lax.axis_index("ctx")
    part = lax.axis_index("fsdp")
    vectors = lax.dynamic_update_slice(jnp.zeros((6, D), F32), jnp.stack(own_vectors).astype(F32), (0, part * rows))
    biases = lax.dynamic_update_slice(jnp.zeros((2 * D,), F32), attend_bias.astype(F32), (part * 2 * rows,))
    vectors = jnp.concatenate([biases.reshape(2, D), vectors])
    attend_cols = attend_weight.reshape(rows, 3, ways, 192).transpose(2, 0, 1, 3).reshape(ways, rows, 576)
    normed_all, attend_cols, expand_cols, g2, vectors = gather_inputs(
        tokens, vectors, attend_cols, expand_weight, cotangent
    )
    wq, wk, wv = attend_cols[:, :192], attend_cols[:, 192:384], attend_cols[:, 384:]
    bias = lax.dynamic_slice(vectors, (0, part * 192), (2, 192))
    own = lax.dynamic_slice(normed_all, (ctx * block, 0), (block, D))
    where, begins_row = places_of(document_starts, block)
    q, k, v, o, lse = attend_forward(where, normed_all, own, wq, wk, wv, bias, begins_row)
    return normed_all, attend_cols, expand_cols, g2, vectors, q, k, v, o, lse


def places_of(document_starts, block):
    ctx = lax.axis_index("ctx")
    places = ctx * block + jnp.arange(block, dtype=jnp.int32)
    begins = first_position(places, document_starts)
    where = jnp.stack([ctx, begins[0], begins[-1]]).astype(jnp.int32)
    return where, begins.reshape(1, block)


def forward(tokens, document_starts, attend_weight, attend_bias, expand_weight, cotangent, own_vectors):
    rows = tokens.shape[0]
    if lax.axis_size("ctx") != 8:
        return forward_plain(
            tokens, document_starts, attend_weight, attend_bias, expand_weight, cotangent, own_vectors
        )
    return gather_attend(
        document_starts, tokens, attend_weight, expand_weight, cotangent, (attend_bias,) + tuple(own_vectors)
    )


def backward_plain(
    document_starts, normed_all, k, v, q, o, lse, g1, project_weight, attend_cols,
    contract_part, expand_part, tokens, grad_middle, vectors, mlp_sums,
):
    both = ("ctx", "fsdp")
    rows = tokens.shape[0]
    ways = lax.axis_size("fsdp")
    block = rows * ways
    ctx = lax.axis_index("ctx")
    part = lax.axis_index("fsdp")
    gain_one = vectors[4]
    wq, wk, wv = attend_cols[:, :192], attend_cols[:, 192:384], attend_cols[:, 384:]
    where, begins_row = places_of(document_starts, block)
    own = lax.dynamic_slice(normed_all, (ctx * block, 0), (block, D))
    dn, attend_t, project_part, sums = attend_backward(
        where, normed_all, k, v, own, q, o, lse, g1, project_weight, wq, wk, wv, begins_row
    )
    grad_normed = lax.psum_scatter(dn.astype(F32), both, scatter_dimension=0, tiled=True)
    normed, unit_one, inverse_one = normalize(tokens.astype(F32), gain_one, jnp.zeros_like(gain_one))
    first_part, gainone_grad, shiftone_grad = normalize_back(grad_normed, unit_one, inverse_one, gain_one)
    tokens_grad = (grad_middle + first_part).astype(BF)

    def summed(array_in):
        return lax.psum(array_in.astype(BF), "ctx").astype(F32)

    contract_grad = summed(contract_part)
    project_grad = summed(project_part)
    expand_grad = lax.all_to_all(summed(expand_part).reshape(ways, rows, D), "fsdp", 0, 0)
    expand_grad = expand_grad.transpose(1, 0, 2).reshape(rows, ways * D)
    attend_grad = lax.all_to_all(summed(attend_t.T).reshape(ways, rows, 576), "fsdp", 0, 0)
    attend_grad = attend_grad.reshape(ways, rows, 3, 192).transpose(1, 2, 0, 3).reshape(rows, 3 * D)
    spread = lax.dynamic_update_slice(jnp.zeros((2, D), F32), sums[:2], (0, part * 192))
    hidden = lax.dynamic_update_slice(jnp.zeros((4, D), F32), mlp_sums[4:5], (part, 0))
    totals = jnp.concatenate([
        spread, mlp_sums[0:2], gainone_grad[None], shiftone_grad[None], mlp_sums[2:4], hidden
    ])
    totals = lax.psum(totals, both)
    attbias = lax.dynamic_slice(totals[:2].reshape(-1), (part * 2 * rows,), (2 * rows,))
    mine = lax.dynamic_slice(totals, (2, part * rows), (6, rows))
    expbias = lax.dynamic_slice(totals, (8 + part, 0), (1, D)).reshape(D)
    return (
        tokens_grad, attend_grad, attbias, project_grad, mine[0], expand_grad, expbias,
        contract_grad, mine[1], mine[2], mine[3], mine[4], mine[5],
    )


def per_device(
    tokens, document_starts, attend_weight, attend_bias, project_weight, project_bias,
    expand_weight, expand_bias, contract_weight, contract_bias,
    gain_first, shift_first, gain_second, shift_second, cotangent,
):
    both = ("ctx", "fsdp")
    rows = tokens.shape[0]
    ways = lax.axis_size("fsdp")
    block = rows * ways
    ctx = lax.axis_index("ctx")
    part = lax.axis_index("fsdp")

    def whole(array_in):
        return lax.all_gather(array_in, "fsdp", axis=0, tiled=True)

    normed_all, attend_cols, expand_cols, g2, vectors, q, k, v, o, lse = forward(
        tokens, document_starts, attend_weight, attend_bias, expand_weight, cotangent,
        (project_bias, contract_bias, gain_first, shift_first, gain_second, shift_second),
    )
    mlp_args = (o, project_weight, expand_cols, contract_weight, expand_bias, tokens, cotangent, g2, vectors)
    if lax.axis_size("ctx") != 8:
        block_output, grad_middle, g1, contract_part, expand_part, mlp_sums = feed_forward(*mlp_args)
        return (block_output,) + backward_plain(
            document_starts, normed_all, k, v, q, o, lse, g1, project_weight, attend_cols,
            contract_part, expand_part, tokens, grad_middle, vectors, mlp_sums,
        )
    near, over, grad_middle, g1, contract_part, expand_part, mlp_sums = feed_forward_near(*mlp_args)
    reduced = attend_reduce(
        document_starts, normed_all, k, v, q, o, lse, g1, project_weight, attend_cols,
        contract_part.reshape(8, 96, D), expand_part.reshape(8, 96, D), tokens, grad_middle, vectors, mlp_sums, near, over,
    )
    return tuple(finish(*reduced))


def solution(mesh):
    tok, row, vec = P(("ctx", "fsdp"), None), P("fsdp", None), P("fsdp")
    in_specs = (tok, P(), row, vec, row, vec, row, vec, row, vec, vec, vec, vec, vec, tok)
    out_specs = (tok, tok, row, vec, row, vec, row, vec, row, vec, vec, vec, vec, vec)
    return jax.shard_map(per_device, mesh=mesh, in_specs=in_specs, out_specs=out_specs, check_vma=False)
```

```python
import functools
import jax
import jax.numpy as jnp
from jax import lax
from jax.experimental import pallas as pl
from jax.experimental.pallas import tpu as pltpu
from jax.sharding import PartitionSpec as P

D = 768
H = 12
HD = 64
EPS = 1e-05
SCALE = 0.125
BRANCH = 48.0 ** (-0.5)
NEG = -1e30
SUB = 768
STRIP = 256
QS = STRIP
LEAD = 4
BACK_LEAD = 2
BF = jnp.bfloat16
F32 = jnp.float32


def mm(a, b):
    return jnp.dot(a, b, preferred_element_type=F32)


def mm_nt(a, b):
    return lax.dot_general(a, b, (((1,), (1,)), ((), ())), preferred_element_type=F32)


def mm_tn(a, b):
    return lax.dot_general(a, b, (((0,), (0,)), ((), ())), preferred_element_type=F32)


def head_lanes(head):
    return slice(0, 128) if head < 2 else slice(128, 192)


def fill_masked_columns(target, flipped):
    zero = jnp.zeros((HD, flipped.shape[1]), BF)
    target[0, 0:HD, :] = flipped[0:HD]
    target[0, HD : 2 * HD, :] = zero
    target[1, 0:HD, :] = zero
    target[1, HD : 2 * HD, :] = flipped[HD : 2 * HD]
    target[2, 0:HD, :] = flipped[2 * HD : 3 * HD]


def masked_rows(array_in, head):
    if head == 2:
        return array_in[:, 128:192]
    pair = array_in[:, 0:128]
    lane = lax.broadcasted_iota(jnp.int32, pair.shape, 1)
    return jnp.where((lane < HD) if head == 0 else (lane >= HD), pair, jnp.zeros_like(pair))


def allowed_pairs(first_key, first_query, begins, shape):
    key_places = first_key + lax.broadcasted_iota(jnp.int32, shape, 0)
    query_places = first_query + lax.broadcasted_iota(jnp.int32, shape, 1)
    return (key_places <= query_places) & (key_places >= begins)


def attend_forward_kernel(
    where_ref, rows_ref, own_ref, wq_ref, wk_ref, wv_ref, bias_ref, begins_ref,
    q_out, k_out, v_out, o_out, lse_out,
    qm, vt, peak, total, acc,
):
    turn = pl.program_id(0)
    block = own_ref.shape[0]
    mine, begin_low, begin_high = where_ref[0], where_ref[1], where_ref[2]
    first_query = mine * block
    needed = (turn <= mine) & ((turn + 1) * block - 1 >= begin_low)

    @pl.when(turn == 0)
    def _():
        query = (mm(own_ref[...], wq_ref[...]) + bias_ref[0:1, :]).astype(BF)
        q_out[...] = query
        fill_masked_columns(qm, (query.astype(F32) * SCALE).T.astype(BF))
        peak[...] = jnp.full(peak.shape, NEG, F32)
        total[...] = jnp.zeros(total.shape, F32)
        acc[...] = jnp.zeros(acc.shape, F32)

    @pl.when(needed)
    def _():
        rows = rows_ref[...]
        k_out[...] = mm(rows, wk_ref[...]).astype(BF)
        value = (mm(rows, wv_ref[...]) + bias_ref[1:2, :]).astype(BF)
        v_out[...] = value
        vt[...] = value.astype(F32).T.astype(BF)

        def one(step, masked):
            at = pl.ds(pl.multiple_of(step * SUB, SUB), SUB)
            first_key = turn * block + step * SUB
            if masked:
                allowed = allowed_pairs(first_key, first_query, begins_ref[...], (SUB, block))
            strips = [(head, strip) for head in range(3) for strip in range(block // QS)]

            def scored(head, strip):
                depth = 128 if head < 2 else HD
                return mm(k_out[at, head_lanes(head)], qm[head, 0:depth, strip * QS : strip * QS + QS])

            ahead = [scored(*strips[i]) for i in range(LEAD)]
            for i, (head, strip) in enumerate(strips):
                scores = ahead.pop(0)
                if i + LEAD < len(strips):
                    ahead.append(scored(*strips[i + LEAD]))
                lanes = slice(strip * QS, strip * QS + QS)
                if masked:
                    scores = jnp.where(allowed[:, lanes], scores, NEG)
                old = peak[head : head + 1, lanes]
                new = jnp.maximum(old, jnp.max(scores, axis=0, keepdims=True))
                weights = jnp.exp(scores - new)
                if masked:
                    weights = jnp.where(allowed[:, lanes], weights, 0.0)
                factor = jnp.exp(old - new)
                peak[head : head + 1, lanes] = new
                total[head : head + 1, lanes] = total[head : head + 1, lanes] * factor + jnp.sum(
                    weights, axis=0, keepdims=True
                )
                part = slice(head * HD, head * HD + HD)
                acc[part, lanes] = acc[part, lanes] * factor + mm(vt[part, at], weights.astype(BF))

        @pl.loop(0, block // SUB)
        def _(step):
            first_key = turn * block + step * SUB
            inner = (first_key + SUB - 1 <= first_query) & (first_key >= begin_high)
            touched = first_key + SUB - 1 >= begin_low

            @pl.when(inner)
            def _():
                one(step, False)

            @pl.when(jnp.logical_not(inner) & touched)
            def _():
                one(step, True)

    @pl.when(turn == mine)
    def _():
        for head in range(3):
            part = slice(head * HD, head * HD + HD)
            o_out[part, :] = acc[part, :] / total[head : head + 1, :]
        lse_out[...] = peak[...] + jnp.log(jnp.maximum(total[...], 1e-30))


def attend_forward(where, rows_all, own, wq, wk, wv, bias, begins):
    block = own.shape[0]
    count = rows_all.shape[0] // block

    def seen(turn, where_ref):
        return (jnp.minimum(turn, where_ref[0]), 0)

    def fixed(turn, where_ref):
        return (0, 0)

    return pl.pallas_call(
        attend_forward_kernel,
        grid_spec=pltpu.PrefetchScalarGridSpec(
            num_scalar_prefetch=1,
            grid=(count,),
            in_specs=[
                pl.BlockSpec((block, D), seen),
                pl.BlockSpec((block, D), fixed),
                pl.BlockSpec((D, 192), fixed),
                pl.BlockSpec((D, 192), fixed),
                pl.BlockSpec((D, 192), fixed),
                pl.BlockSpec((2, 192), fixed),
                pl.BlockSpec((1, block), fixed),
            ],
            out_specs=[
                pl.BlockSpec((block, 192), fixed),
                pl.BlockSpec((block, 192), seen),
                pl.BlockSpec((block, 192), seen),
                pl.BlockSpec((192, block), fixed),
                pl.BlockSpec((8, block), fixed),
            ],
            scratch_shapes=[
                pltpu.VMEM((3, 128, block), BF),
                pltpu.VMEM((192, block), BF),
                pltpu.VMEM((8, block), F32),
                pltpu.VMEM((8, block), F32),
                pltpu.VMEM((192, block), F32),
            ],
        ),
        out_shape=[
            jax.ShapeDtypeStruct((block, 192), BF),
            jax.ShapeDtypeStruct((block * count, 192), BF),
            jax.ShapeDtypeStruct((block * count, 192), BF),
            jax.ShapeDtypeStruct((192, block), F32),
            jax.ShapeDtypeStruct((8, block), F32),
        ],
        compiler_params=pltpu.CompilerParams(vmem_limit_bytes=48 << 20),
        name="attend_forward",
    )(where, rows_all, own, wq, wk, wv, bias, begins)


def attend_backward_kernel(
    where_ref, rows_ref, k_ref, v_ref, own_ref, q_ref, o_ref, lse_ref, g_ref, wp_ref,
    wq_ref, wk_ref, wv_ref, begins_ref,
    dn_out, grad_out, proj_out, sums_out,
    qm, dm, qn, dn, delta, dqt, kt, dk, dv,
):
    turn = pl.program_id(0)
    block = own_ref.shape[0]
    mine, begin_low, begin_high = where_ref[0], where_ref[1], where_ref[2]
    first_query = mine * block
    needed = (turn <= mine) & ((turn + 1) * block - 1 >= begin_low)

    @pl.when(turn == 0)
    def _():
        grads = g_ref[...]
        exact = o_ref[...]
        proj_out[...] = mm(exact.astype(BF), grads)
        outer = mm_nt(grads, wp_ref[...]).astype(BF)
        flipped = outer.astype(F32).T
        product = flipped * exact
        for head in range(3):
            delta[head : head + 1, :] = jnp.sum(
                product[head * HD : head * HD + HD], axis=0, keepdims=True
            )
        fill_masked_columns(dm, flipped.astype(BF))
        scaled = (q_ref[...].astype(F32) * SCALE)
        fill_masked_columns(qm, scaled.T.astype(BF))
        scaled = scaled.astype(BF)
        for head in range(3):
            depth = 128 if head < 2 else HD
            qn[head, :, 0:depth] = masked_rows(scaled, head)
            dn[head, :, 0:depth] = masked_rows(outer, head)
        dqt[...] = jnp.zeros(dqt.shape, F32)
        grad_out[...] = jnp.zeros(grad_out.shape, F32)
        sums_out[...] = jnp.zeros(sums_out.shape, F32)

    @pl.when(jnp.logical_not(needed))
    def _():
        dn_out[...] = jnp.zeros(dn_out.shape, BF)

    @pl.when(needed)
    def _():
        kt[...] = k_ref[...].astype(F32).T.astype(BF)
        dk[...] = jnp.zeros(dk.shape, F32)
        dv[...] = jnp.zeros(dv.shape, F32)

        def one(step, masked):
            at = pl.ds(pl.multiple_of(step * SUB, SUB), SUB)
            first_key = turn * block + step * SUB
            if masked:
                allowed = allowed_pairs(first_key, first_query, begins_ref[...], (SUB, block))
            for head in range(3):
                depth = 128 if head < 2 else HD
                lanes = head_lanes(head)
                scores = mm(k_ref[at, lanes], qm[head, 0:depth, :])
                probs = jnp.exp(scores - lse_ref[head : head + 1, :])
                if masked:
                    probs = jnp.where(allowed, probs, 0.0)
                outer = mm(v_ref[at, lanes], dm[head, 0:depth, :])
                inner = (probs * (outer - delta[head : head + 1, :])).astype(BF)
                dv[at, lanes] += mm(probs.astype(BF), dn[head, :, 0:depth])
                dk[at, lanes] += mm(inner, qn[head, :, 0:depth])
                part = slice(head * HD, head * HD + HD)
                dqt[part, :] += mm(kt[part, at], inner)

        @pl.loop(0, block // SUB)
        def _(step):
            first_key = turn * block + step * SUB
            inner = (first_key + SUB - 1 <= first_query) & (first_key >= begin_high)
            touched = first_key + SUB - 1 >= begin_low

            @pl.when(inner)
            def _():
                one(step, False)

            @pl.when(jnp.logical_not(inner) & touched)
            def _():
                one(step, True)

        rows = rows_ref[...]
        low_k = dk[...].astype(BF)
        low_v = dv[...].astype(BF)
        grad_out[192:384, :] += mm(low_k.astype(F32).T.astype(BF), rows)
        grad_out[384:576, :] += mm(low_v.astype(F32).T.astype(BF), rows)
        sums_out[1:2, :] += jnp.sum(low_v.astype(F32), axis=0, keepdims=True)
        through = mm_nt(low_k, wk_ref[...]) + mm_nt(low_v, wv_ref[...])

        @pl.when(turn < mine)
        def _():
            dn_out[...] = through.astype(BF)

        @pl.when(turn == mine)
        def _():
            flipped = dqt[...] * SCALE
            low_q = flipped.T.astype(BF)
            grad_out[0:192, :] += mm(flipped.astype(BF), own_ref[...])
            sums_out[0:1, :] += jnp.sum(low_q.astype(F32), axis=0, keepdims=True)
            dn_out[...] = (through + mm_nt(low_q, wq_ref[...])).astype(BF)


def attend_backward(where, rows_all, k, v, own, q, o, lse, g, wp, wq, wk, wv, begins):
    block = own.shape[0]
    count = rows_all.shape[0] // block

    def seen(turn, where_ref):
        return (jnp.minimum(turn, where_ref[0]), 0)

    def each(turn, where_ref):
        return (turn, 0)

    def fixed(turn, where_ref):
        return (0, 0)

    return pl.pallas_call(
        attend_backward_kernel,
        grid_spec=pltpu.PrefetchScalarGridSpec(
            num_scalar_prefetch=1,
            grid=(count,),
            in_specs=[
                pl.BlockSpec((block, D), seen),
                pl.BlockSpec((block, 192), seen),
                pl.BlockSpec((block, 192), seen),
                pl.BlockSpec((block, D), fixed),
                pl.BlockSpec((block, 192), fixed),
                pl.BlockSpec((192, block), fixed),
                pl.BlockSpec((8, block), fixed),
                pl.BlockSpec((block, D), fixed),
                pl.BlockSpec((192, D), fixed),
                pl.BlockSpec((D, 192), fixed),
                pl.BlockSpec((D, 192), fixed),
                pl.BlockSpec((D, 192), fixed),
                pl.BlockSpec((1, block), fixed),
            ],
            out_specs=[
                pl.BlockSpec((block, D), each),
                pl.BlockSpec((576, D), fixed),
                pl.BlockSpec((192, D), fixed),
                pl.BlockSpec((8, 192), fixed),
            ],
            scratch_shapes=[
                pltpu.VMEM((3, 128, block), BF),
                pltpu.VMEM((3, 128, block), BF),
                pltpu.VMEM((3, block, 128), BF),
                pltpu.VMEM((3, block, 128), BF),
                pltpu.VMEM((8, block), F32),
                pltpu.VMEM((192, block), F32),
                pltpu.VMEM((192, block), BF),
                pltpu.VMEM((block, 192), F32),
                pltpu.VMEM((block, 192), F32),
            ],
        ),
        out_shape=[
            jax.ShapeDtypeStruct((block * count, D), BF),
            jax.ShapeDtypeStruct((576, D), F32),
            jax.ShapeDtypeStruct((192, D), F32),
            jax.ShapeDtypeStruct((8, 192), F32),
        ],
        compiler_params=pltpu.CompilerParams(vmem_limit_bytes=48 << 20),
        name="attend_backward",
    )(where, rows_all, k, v, own, q, o, lse, g, wp, wq, wk, wv, begins)


MESH = pl.DeviceIdType.MESH


class Place:
    def __init__(self):
        ctx = lax.axis_index("ctx")
        part = lax.axis_index("fsdp")
        self.levels = lax.axis_size("ctx") // 2
        self.ctx, self.part = ctx, part
        self.level, self.side = ctx // 2, ctx % 2
        self.half, self.core = part // 2, part % 2

    def at(self, level=None, side=None, half=None, core=None):
        level = self.level if level is None else level
        side = self.side if side is None else side
        half = self.half if half is None else half
        core = self.core if core is None else core
        return (level * 2 + side, half * 2 + core)

    @property
    def twin(self):
        return self.at(core=1 - self.core)

    @property
    def across(self):
        return self.at(half=1 - self.half)

    @property
    def corner(self):
        return self.at(half=1 - self.half, core=1 - self.core)

    @property
    def beside(self):
        return self.at(side=1 - self.side)


def remote(source, target, send, recv, device):
    return pltpu.make_async_remote_copy(
        src_ref=source, dst_ref=target, send_sem=send, recv_sem=recv, device_id=device, device_id_type=MESH
    )


def signal(sem, device):
    pl.semaphore_signal(sem, inc=1, device_id=device, device_id_type=MESH)


def piece(ref, ctx, part):
    rows = 192
    return ref.at[pl.ds(pl.multiple_of((ctx * 4 + part) * rows, rows), rows)]


def rows_of(ref, part):
    return ref.at[pl.ds(pl.multiple_of(part * 192, 192), 192)]


def layer_norm(rows_in, gain, shift):
    mean = jnp.mean(rows_in, axis=1, keepdims=True)
    centered = rows_in - mean
    inverse = lax.rsqrt(jnp.mean(centered * centered, axis=1, keepdims=True) + EPS)
    unit = centered * inverse
    return unit * gain + shift, unit, inverse


def gather_kernel(
    levels, tok_ref, vec_ref, acol_ref, ecol_ref, cot_ref,
    all_ref, attend_ref, expand_ref, gtwo_ref, vec_out,
    normed, gtwo, vec_in,
    vec_send, vec_recv, att_send, att_recv, exp_send, exp_recv, two_send, two_recv,
    x_send, x_recv, z_send, z_recv, y_send, y_recv, core_send, core_recv, local_sem,
):
    me = Place()
    mine = me.part
    barrier = pltpu.get_barrier_semaphore()
    for device in (me.twin, me.across, me.corner, me.beside):
        signal(barrier, device)

    @pl.when(me.level > 0)
    def _():
        signal(barrier, me.at(level=me.level - 1))

    @pl.when(me.level < levels - 1)
    def _():
        signal(barrier, me.at(level=me.level + 1))

    ends = (me.level == 0).astype(jnp.int32) + (me.level == levels - 1).astype(jnp.int32)
    pl.semaphore_wait(barrier, 6 - ends)

    peers = (
        (me.twin, me.half * 2 + 1 - me.core),
        (me.across, (1 - me.half) * 2 + me.core),
        (me.corner, (1 - me.half) * 2 + 1 - me.core),
    )
    vecs = [remote(vec_ref, vec_in.at[i], vec_send.at[i], vec_recv.at[i], d) for i, (d, p) in enumerate(peers)]
    for copy in vecs:
        copy.start()
    atts = [
        remote(acol_ref.at[p], rows_of(attend_ref, mine), att_send.at[i], att_recv.at[i], d)
        for i, (d, p) in enumerate(peers)
    ]
    for copy in atts:
        copy.start()
    local = [
        pltpu.make_async_copy(acol_ref.at[mine], rows_of(attend_ref, mine), local_sem.at[0]),
        pltpu.make_async_copy(ecol_ref.at[:, pl.ds(pl.multiple_of(mine * D, D), D)], rows_of(expand_ref, mine), local_sem.at[1]),
    ]
    for copy in local:
        copy.start()
    gtwo[...] = (BRANCH * cot_ref[...].astype(F32)).astype(BF)
    for copy in vecs:
        copy.wait_recv()
    vec_out[...] = vec_ref[...] + vec_in[0] + vec_in[1] + vec_in[2]
    out, unit, inverse = layer_norm(tok_ref[...].astype(F32), vec_out[4:5, :], vec_out[5:6, :])
    normed[...] = out.astype(BF)

    def go(copy):
        copy.start()
        return copy

    ctx = me.ctx
    across = go(remote(normed, piece(all_ref, ctx, mine), x_send.at[0], x_recv.at[0], me.across))
    keep = go(pltpu.make_async_copy(normed, piece(all_ref, ctx, mine), local_sem.at[2]))
    keep_two = go(pltpu.make_async_copy(gtwo, rows_of(gtwo_ref, mine), local_sem.at[3]))
    local += [keep, keep_two]

    def spread_static(source, distance, slot):
        level = me.level - distance
        where = level * 2 + me.side
        half = me.half if slot == 0 else 1 - me.half
        part = half * 2 + me.core

        @pl.when(me.level < levels - 1)
        def _():
            remote(source, piece(all_ref, where, part), z_send.at[distance, slot], z_recv.at[distance + 1, slot], me.at(level=me.level + 1)).start()

        remote(source, piece(all_ref, where, part), y_send.at[distance, slot], y_recv.at[distance, slot], me.beside).start()
        remote(source, piece(all_ref, where, part), core_send.at[distance, 0, slot], core_recv.at[distance, 0, slot], me.twin).start()

    spread_static(normed, 0, 0)
    exps = [
        go(remote(ecol_ref.at[:, pl.ds(pl.multiple_of(p * D, D), D)], rows_of(expand_ref, mine), exp_send.at[i], exp_recv.at[i], d))
        for i, (d, p) in enumerate(peers)
    ]
    two_x = go(remote(gtwo, rows_of(gtwo_ref, mine), two_send.at[0], two_recv.at[0], me.across))
    two_c = go(remote(gtwo, rows_of(gtwo_ref, mine), two_send.at[1], two_recv.at[1], me.twin))

    other = (1 - me.half) * 2 + me.core

    def held(distance, slot, side):
        half = me.half if slot == 0 else 1 - me.half
        return piece(all_ref, (me.level - distance) * 2 + side, half * 2 + me.core)

    def take_y(distance):
        for slot in range(2):
            got = held(distance, slot, 1 - me.side)
            remote(got, got, y_send.at[distance, slot], y_recv.at[distance, slot], me.beside).wait_recv()
            remote(got, got, core_send.at[distance, 1, slot], core_recv.at[distance, 1, slot], me.twin).start()

    got = piece(all_ref, ctx, other)
    remote(normed, got, x_send.at[0], x_recv.at[0], me.across).wait_recv()
    spread_static(got, 0, 1)
    for distance in range(1, levels):

        @pl.when(me.level >= distance)
        def _():
            for slot in range(2):
                got = held(distance, slot, me.side)
                remote(got, got, z_send.at[distance, slot], z_recv.at[distance, slot], me.twin).wait_recv()
                spread_static(got, distance, slot)

        if distance == 1:
            take_y(0)
        else:

            @pl.when(me.level >= distance - 1)
            def _():
                take_y(distance - 1)

    @pl.when(me.level >= levels - 1)
    def _():
        take_y(levels - 1)

    got = rows_of(gtwo_ref, other)
    remote(gtwo, got, two_send.at[0], two_recv.at[0], me.across).wait_recv()
    two_f = go(remote(got, got, two_send.at[2], two_recv.at[2], me.twin))
    for copy in local:
        copy.wait()
    for copy in vecs:
        copy.wait_send()
    for copy in atts + exps + [two_c, two_f]:
        copy.wait()
    two_x.wait_send()
    across.wait_send()
    for distance in range(levels):

        @pl.when(me.level >= distance)
        def _():
            for slot in range(2):
                got = held(distance, slot, me.side)

                @pl.when(me.level < levels - 1)
                def _():
                    remote(got, got, z_send.at[distance, slot], z_recv.at[distance, slot], me.twin).wait_send()

                remote(got, got, y_send.at[distance, slot], y_recv.at[distance, slot], me.beside).wait_send()
                for side in range(2):
                    remote(got, got, core_send.at[distance, side, slot], core_recv.at[distance, side, slot], me.twin).wait()


def gather_inputs(tokens, vectors, attend_cols, expand_weight, cotangent):
    levels = lax.axis_size("ctx") // 2
    rows = tokens.shape[0]
    block = rows * 4
    vmem = pl.BlockSpec(memory_space=pltpu.VMEM)
    anywhere = pl.BlockSpec(memory_space=pl.ANY)
    dma = pltpu.SemaphoreType.DMA
    return pl.pallas_call(
        functools.partial(gather_kernel, levels),
        in_specs=[vmem, vmem, anywhere, anywhere, vmem],
        out_specs=[anywhere, anywhere, anywhere, anywhere, vmem],
        out_shape=[
            jax.ShapeDtypeStruct((block * levels * 2, D), BF),
            jax.ShapeDtypeStruct((D, 576), BF),
            jax.ShapeDtypeStruct((D, D), BF),
            jax.ShapeDtypeStruct((block, D), BF),
            jax.ShapeDtypeStruct((8, D), F32),
        ],
        scratch_shapes=[
            pltpu.VMEM((rows, D), BF),
            pltpu.VMEM((rows, D), BF),
            pltpu.VMEM((3, 8, D), F32),
            dma((3,)), dma((3,)), dma((3,)), dma((3,)), dma((3,)), dma((3,)), dma((3,)), dma((3,)),
            dma((1,)), dma((1,)),
            dma((levels, 2)), dma((levels + 1, 2)),
            dma((levels, 2)), dma((levels, 2)),
            dma((levels, 2, 2)), dma((levels, 2, 2)),
            dma((4,)),
        ],
        compiler_params=pltpu.CompilerParams(collective_id=1, has_side_effects=True, vmem_limit_bytes=16 << 20),
        name="gather_inputs",
    )(tokens, vectors, attend_cols, expand_weight, cotangent)


SHARE = 176


def begins_of(starts_ref, first, count):
    places = first + lax.broadcasted_iota(jnp.int32, (1, count), 1)
    begins = jnp.zeros((1, count), jnp.int32)
    for document in range(8):
        start = starts_ref[document]
        begins = jnp.where(places >= start, jnp.maximum(begins, start), begins)
    return begins


def gather_attend_kernel(
    levels, starts_ref, tok_hbm, aw_hbm, ew_ref, cot_hbm, *rest_refs,
):
    vector_hbm, vector_refs = rest_refs[:7], rest_refs[-7:]
    (
        all_ref, attend_ref, expand_ref, gtwo_ref, vec_out, q_out, k_out, v_out, o_out, lse_out,
        tok_ref, aw_ref, cot_ref, vec_ref, staged, vec_in, begins, qm, vt, acc, peak, total,
        vec_send, vec_recv, att_send, att_recv, exp_send, exp_recv, two_send, two_recv,
        x_send, x_recv, z_send, z_recv, y_send, y_recv, core_send, core_recv, r_send, r_recv, rc_send, rc_recv, local_sem,
    ) = rest_refs[7:-7]
    me = Place()
    mine, z, side = me.part, me.level, me.side
    top = levels - 1
    block = gtwo_ref.shape[0]
    fetched = (
        pltpu.make_async_copy(tok_hbm, tok_ref, local_sem.at[1]),
        pltpu.make_async_copy(aw_hbm, aw_ref, local_sem.at[2]),
        pltpu.make_async_copy(cot_hbm, cot_ref, local_sem.at[3]),
    ) + tuple(
        pltpu.make_async_copy(source, target, local_sem.at[4 + i])
        for i, (source, target) in enumerate(zip(vector_hbm, vector_refs))
    )
    for copy in fetched:
        copy.start()
    barrier = pltpu.get_barrier_semaphore()
    for device in (me.twin, me.across, me.corner, me.beside):
        signal(barrier, device)

    @pl.when(z > 0)
    def _():
        signal(barrier, me.at(level=z - 1))

    @pl.when(z < top)
    def _():
        signal(barrier, me.at(level=z + 1))

    for copy in fetched:
        copy.wait()
    both = vector_refs[0][...].astype(F32).reshape(1, 384)
    vec_ref[0:1, :] = both[:, 0:192]
    vec_ref[1:2, :] = both[:, 192:384]
    for i, ref in enumerate(vector_refs[1:]):
        vec_ref[2 + i : 3 + i, :] = ref[...].astype(F32).reshape(1, 192)
    for part in range(4):
        for kind in range(3):
            staged[part, :, kind * 192 : kind * 192 + 192] = aw_ref[:, kind * D + part * 192 : kind * D + part * 192 + 192]
    ends = (z == 0).astype(jnp.int32) + (z == top).astype(jnp.int32)
    pl.semaphore_wait(barrier, 6 - ends)

    peers = (
        (me.twin, me.half * 2 + 1 - me.core),
        (me.across, (1 - me.half) * 2 + me.core),
        (me.corner, (1 - me.half) * 2 + 1 - me.core),
    )

    def go(copy):
        copy.start()
        return copy

    vecs = [go(remote(vec_ref, vec_in.at[mine], vec_send.at[i], vec_recv.at[i], d)) for i, (d, p) in enumerate(peers)]
    atts = [
        remote(staged.at[p], rows_of(attend_ref, mine), att_send.at[i], att_recv.at[i], d) for i, (d, p) in enumerate(peers)
    ]
    atts[0].start()
    atts[1].start()
    vec_in[mine] = vec_ref[...]
    rows_of(attend_ref, mine)[...] = staged[mine]
    local = [
        go(pltpu.make_async_copy(
            ew_ref.at[:, pl.ds(pl.multiple_of(mine * D, D), D)], rows_of(expand_ref, mine), local_sem.at[0]
        ))
    ]
    own_two = rows_of(gtwo_ref, mine)
    own_two[...] = (BRANCH * cot_ref[...].astype(F32)).astype(BF)
    for i, (d, p) in enumerate(peers):
        remote(vec_ref, vec_in.at[p], vec_send.at[i], vec_recv.at[i], d).wait_recv()
    for part in range(4):
        vec_out[:, part * 192 : part * 192 + 192] = vec_in[part]
    out, unit, inverse = layer_norm(tok_ref[...].astype(F32), vec_out[4:5, :], vec_out[5:6, :])
    own_rows = piece(all_ref, me.ctx, mine)
    own_rows[...] = out.astype(BF)
    across = go(remote(own_rows, own_rows, x_send.at[0], x_recv.at[0], me.across))
    atts[2].start()

    def most(ref):
        return ref.at[pl.ds(0, SHARE)]

    def rest(ref):
        return ref.at[pl.ds(SHARE, 192 - SHARE)]

    def held(distance, slot, where):
        half = me.half + slot * (1 - 2 * me.half)
        return piece(all_ref, (z - distance) * 2 + where, half * 2 + me.core)

    def y_copy(distance, slot, where, whole):
        got = held(distance, slot, where)
        if not whole:
            got = most(got)
        return remote(got, got, y_send.at[distance, slot], y_recv.at[distance, slot], me.beside)

    def rest_up(distance, slot):
        got = rest(held(distance, slot, 1 - side))
        return remote(got, got, r_send.at[distance, slot], r_recv.at[distance + 1, slot], me.at(level=z + 1))

    def rest_twin(distance, slot):
        got = rest(held(distance, slot, 1 - side))
        return remote(got, got, rc_send.at[distance, slot], rc_recv.at[distance, slot], me.twin)

    def spread(distance, slot, first):
        half = me.half + slot * (1 - 2 * me.half)
        got = piece(all_ref, (z - distance) * 2 + side, half * 2 + me.core)

        @pl.when(z < top)
        def _():
            remote(got, got, z_send.at[distance, slot], z_recv.at[distance + 1, slot], me.at(level=z + 1)).start()

        y_copy(distance, slot, side, first).start()
        remote(got, got, core_send.at[distance, 0, slot], core_recv.at[distance, 0, slot], me.twin).start()

    def from_twin(distance, which, where, whole):
        for slot in range(2):
            half = me.half + slot * (1 - 2 * me.half)
            got = piece(all_ref, (z - distance) * 2 + where, half * 2 + 1 - me.core)
            if not whole:
                last = rest(got)
                remote(last, last, rc_send.at[distance, slot], rc_recv.at[distance, slot], me.twin).wait_recv()
                got = most(got)
            remote(got, got, core_send.at[distance, which, slot], core_recv.at[distance, which, slot], me.twin).wait_recv()

    spread(0, 0, True)
    begins[...] = begins_of(starts_ref, me.ctx * block, block)
    got = held(0, 1, side)
    remote(got, got, x_send.at[0], x_recv.at[0], me.across).wait_recv()
    spread(0, 1, True)
    def from_below(distance, slot):
        @pl.when(distance <= z)
        def _():
            got = held(distance, slot, side)
            remote(got, got, z_send.at[distance - 1, slot], z_recv.at[distance, slot], me.twin).wait_recv()
            spread(distance, slot, False)

    from_below(1, 0)
    two_x = go(remote(own_two, own_two, two_send.at[0], two_recv.at[0], me.across))
    two_c = go(remote(own_two, own_two, two_send.at[1], two_recv.at[1], me.twin))
    exps = [
        go(remote(ew_ref.at[:, pl.ds(pl.multiple_of(p * D, D), D)], rows_of(expand_ref, mine), exp_send.at[i], exp_recv.at[i], d))
        for i, (d, p) in enumerate(peers)
    ]
    for copy in atts:
        copy.wait_recv()
    from_twin(0, 0, side, True)

    first_query = me.ctx * block
    bias_q = vec_in[mine // 2, pl.ds(mine % 2, 1), :]
    query = (mm(all_ref[pl.ds(pl.multiple_of(first_query, block), block), :], attend_ref[:, 0:192]) + bias_q).astype(BF)
    q_out[...] = query
    fill_masked_columns(qm, (query.astype(F32) * SCALE).T.astype(BF))
    peak[...] = jnp.full(peak.shape, NEG, F32)
    total[...] = jnp.zeros(total.shape, F32)
    acc[...] = jnp.zeros(acc.shape, F32)

    def attend(ctx, diagonal):
        first_key = ctx * block
        at = pl.ds(pl.multiple_of(first_key, block), block)
        rows = all_ref[at, :]
        key = mm(rows, attend_ref[:, 192:384]).astype(BF)
        k_out[at, :] = key
        value = (mm(rows, attend_ref[:, 384:576]) + vec_in[2 + mine // 2, pl.ds(mine % 2, 1), :]).astype(BF)
        v_out[at, :] = value
        vt[...] = value.astype(F32).T.astype(BF)
        strips = [(head, strip) for head in range(3) for strip in range(block // STRIP)]

        def keys_of(strip):
            return strip * STRIP + STRIP if diagonal else block

        def scored(head, strip):
            depth = 128 if head < 2 else HD
            return mm(key[0 : keys_of(strip), head_lanes(head)], qm[head, 0:depth, strip * STRIP : strip * STRIP + STRIP])

        ahead = [scored(*strips[i]) for i in range(LEAD)]
        for i, (head, strip) in enumerate(strips):
            scores = ahead.pop(0)
            if i + LEAD < len(strips):
                ahead.append(scored(*strips[i + LEAD]))
            lanes = slice(strip * STRIP, strip * STRIP + STRIP)
            count = keys_of(strip)
            places = first_key + lax.broadcasted_iota(jnp.int32, (count, STRIP), 0)
            allowed = places >= begins[:, lanes]
            if diagonal:
                queries = first_query + strip * STRIP + lax.broadcasted_iota(jnp.int32, (count, STRIP), 1)
                allowed = allowed & (places <= queries)
            scores = jnp.where(allowed, scores, NEG)
            old = peak[head : head + 1, lanes]
            new = jnp.maximum(old, jnp.max(scores, axis=0, keepdims=True))
            weights = jnp.exp(scores - new)
            factor = jnp.exp(old - new)
            peak[head : head + 1, lanes] = new
            total[head : head + 1, lanes] = total[head : head + 1, lanes] * factor + jnp.sum(
                weights, axis=0, keepdims=True
            )
            part = slice(head * HD, head * HD + HD)
            acc[part, lanes] = acc[part, lanes] * factor + mm(vt[part, 0:count], weights.astype(BF))

    attend(me.ctx, True)

    def take_side(distance, whole):
        for slot in range(2):
            y_copy(distance, slot, 1 - side, whole).wait_recv()
            got = held(distance, slot, 1 - side)
            if not whole:
                got = most(got)
            remote(got, got, core_send.at[distance, 1, slot], core_recv.at[distance, 1, slot], me.twin).start()

    @pl.loop(1, 2 * levels)
    def _(turn):
        @pl.when(turn < 2 * levels - 2)
        def _():
            from_below(turn // 2 + 1, turn % 2)

        distance = turn // 2

        @pl.when(turn == 1)
        def _():
            take_side(0, True)

            @pl.when(z < top)
            def _():
                for slot in range(2):
                    rest_up(0, slot).start()

            from_twin(0, 1, 1 - side, True)

        @pl.when((turn > 1) & (turn % 2 == 1) & (distance <= z))
        def _():
            take_side(distance, False)
            for slot in range(2):
                got = rest(held(distance, slot, 1 - side))
                remote(got, got, r_send.at[distance - 1, slot], r_recv.at[distance, slot], me.twin).wait_recv()
                rest_twin(distance, slot).start()

                @pl.when(z < top)
                def _():
                    rest_up(distance, slot).start()

            from_twin(distance, 1, 1 - side, False)

        @pl.when((turn % 2 == 0) & (distance <= z))
        def _():
            from_twin(distance, 0, side, True)

        ctx = me.ctx - 2 * distance + (turn % 2) * (1 - 2 * side)

        @pl.when((ctx >= 0) & (ctx < me.ctx))
        def _():
            attend(ctx, False)

    for head in range(3):
        part = slice(head * HD, head * HD + HD)
        o_out[part, :] = acc[part, :] / total[head : head + 1, :]
    lse_out[...] = peak[...] + jnp.log(jnp.maximum(total[...], 1e-30))

    other = (1 - me.half) * 2 + me.core
    got = rows_of(gtwo_ref, other)
    remote(got, got, two_send.at[0], two_recv.at[0], me.across).wait_recv()
    two_f = go(remote(got, got, two_send.at[2], two_recv.at[2], me.twin))
    for copy in local:
        copy.wait()
    for copy in vecs + atts + [two_x, across]:
        copy.wait_send()
    for copy in exps + [two_c, two_f]:
        copy.wait()

    def left(distance, whole):
        for slot in range(2):
            got = held(distance, slot, side)

            @pl.when(z < top)
            def _():
                remote(got, got, z_send.at[distance, slot], z_recv.at[distance, slot], me.twin).wait_send()
                rest_up(distance, slot).wait_send()

            y_copy(distance, slot, side, whole).wait_send()
            remote(got, got, core_send.at[distance, 0, slot], core_recv.at[distance, 0, slot], me.twin).wait_send()
            if not whole:
                rest_twin(distance, slot).wait_send()
                got = most(got)
            remote(got, got, core_send.at[distance, 1, slot], core_recv.at[distance, 1, slot], me.twin).wait_send()

    left(0, True)

    @pl.loop(1, levels)
    def _(step):
        @pl.when(step <= z)
        def _():
            left(step, False)


def gather_attend(starts, tokens, attend_weight, expand_weight, cotangent, vectors):
    levels = lax.axis_size("ctx") // 2
    rows = tokens.shape[0]
    block = rows * 4
    length = block * levels * 2
    vmem = pl.BlockSpec(memory_space=pltpu.VMEM)
    dma = pltpu.SemaphoreType.DMA
    return pl.pallas_call(
        functools.partial(gather_attend_kernel, levels),
        in_specs=[pl.BlockSpec(memory_space=pltpu.SMEM)] + [pl.BlockSpec(memory_space=pl.ANY)] * 11,
        out_specs=[vmem] * 10,
        out_shape=[
            jax.ShapeDtypeStruct((length, D), BF),
            jax.ShapeDtypeStruct((D, 576), BF),
            jax.ShapeDtypeStruct((D, D), BF),
            jax.ShapeDtypeStruct((block, D), BF),
            jax.ShapeDtypeStruct((8, D), F32),
            jax.ShapeDtypeStruct((block, 192), BF),
            jax.ShapeDtypeStruct((length, 192), BF),
            jax.ShapeDtypeStruct((length, 192), BF),
            jax.ShapeDtypeStruct((192, block), F32),
            jax.ShapeDtypeStruct((8, block), F32),
        ],
        scratch_shapes=[
            pltpu.VMEM((rows, D), BF),
            pltpu.VMEM((rows, 3 * D), BF),
            pltpu.VMEM((rows, D), BF),
            pltpu.VMEM((8, 192), F32),
            pltpu.VMEM((4, rows, 576), BF),
            pltpu.VMEM((4, 8, 192), F32),
            pltpu.VMEM((1, block), jnp.int32),
            pltpu.VMEM((3, 128, block), BF),
            pltpu.VMEM((192, block), BF),
            pltpu.VMEM((192, block), F32),
            pltpu.VMEM((8, block), F32),
            pltpu.VMEM((8, block), F32),
            dma((3,)), dma((3,)), dma((3,)), dma((3,)), dma((3,)), dma((3,)), dma((3,)), dma((3,)),
            dma((1,)), dma((1,)),
            dma((levels, 2)), dma((levels + 1, 2)),
            dma((levels, 2)), dma((levels, 2)),
            dma((levels, 2, 2)), dma((levels, 2, 2)),
            dma((levels, 2)), dma((levels + 1, 2)), dma((levels, 2)), dma((levels, 2)),
            dma((11,)),
            pltpu.VMEM((2 * rows,), BF),
        ]
        + [pltpu.VMEM((rows,), BF)] * 6,
        compiler_params=pltpu.CompilerParams(collective_id=4, has_side_effects=True, vmem_limit_bytes=60 << 20),
        name="gather_attend",
    )(starts, tokens, attend_weight, expand_weight, cotangent, *vectors)


def gelu_pair(t):
    slope = 0.7978845608028654
    square = t * t
    bend = jnp.tanh(slope * t * (1.0 + 0.044715 * square))
    half = 0.5 * (1.0 + bend)
    return t * half, half + 0.5 * t * (1.0 - bend * bend) * (slope * (1.0 + 0.134145 * square))


def mlp_kernel(
    o_ref, wp_hbm, expand_ref, contract_hbm, ebias_hbm, tok_hbm, cot_hbm, gtwo_ref, vec_ref,
    block_out, gmid_out, gone_out, cpart_out, epart_out, sums_out,
    wp_ref, contract_ref, tok_ref, cot_ref, ebias_ref, bias_row, o_rows, gact, n2, act, gexp, held, unit,
    c_send_buf, c_recv_buf, x_send_buf, x_recv_buf,
    c_send, c_recv, x_send, x_recv, ag_send, ag_recv, local_sem,
):
    me = Place()
    mine = me.part
    fetched = [
        pltpu.make_async_copy(source, target, local_sem.at[i])
        for i, (source, target) in enumerate(
            ((wp_hbm, wp_ref), (contract_hbm, contract_ref), (tok_hbm, tok_ref), (cot_hbm, cot_ref), (ebias_hbm, ebias_ref))
        )
    ]
    for copy in fetched:
        copy.start()
    o_rows[...] = o_ref[...].T.astype(BF)
    barrier = pltpu.get_barrier_semaphore()
    signal(barrier, me.twin)
    signal(barrier, me.across)
    pl.semaphore_wait(barrier, 2)
    p_across = (1 - me.half) * 2 + me.core
    p_twin = me.half * 2 + 1 - me.core
    p_corner = (1 - me.half) * 2 + 1 - me.core

    def part(ref, p):
        return ref[pl.ds(pl.multiple_of(p * 192, 192), 192), :]

    def to_twin(i, slot, value):
        c_send_buf[i, slot] = value.astype(BF)
        remote(c_send_buf.at[i, slot], c_recv_buf.at[i, slot], c_send.at[i, slot], c_recv.at[i, slot], me.twin).start()

    def from_twin(i, slot):
        remote(c_send_buf.at[i, slot], c_recv_buf.at[i, slot], c_send.at[i, slot], c_recv.at[i, slot], me.twin).wait_recv()
        return c_recv_buf[i, slot].astype(F32)

    def to_across(i, value):
        x_send_buf[i] = value.astype(BF)
        remote(x_send_buf.at[i], x_recv_buf.at[i], x_send.at[i], x_recv.at[i], me.across).start()

    def from_across(i):
        remote(x_send_buf.at[i], x_recv_buf.at[i], x_send.at[i], x_recv.at[i], me.across).wait_recv()
        return x_recv_buf[i].astype(F32)

    def share(i, ref):
        own = rows_of(ref, mine)
        remote(own, own, ag_send.at[i, 0], ag_recv.at[i, 0], me.across).start()
        remote(own, own, ag_send.at[i, 1], ag_recv.at[i, 1], me.twin).start()

    def share_across(i, ref):
        got = rows_of(ref, p_across)
        remote(got, got, ag_send.at[i, 0], ag_recv.at[i, 0], me.across).wait_recv()
        remote(got, got, ag_send.at[i, 2], ag_recv.at[i, 2], me.twin).start()

    def share_twin(i, ref):
        got = rows_of(ref, p_twin)
        remote(got, got, ag_send.at[i, 1], ag_recv.at[i, 1], me.twin).wait_recv()

    def share_corner(i, ref):
        got = rows_of(ref, p_corner)
        remote(got, got, ag_send.at[i, 2], ag_recv.at[i, 2], me.twin).wait_recv()

    fetched[0].wait()
    to_twin(0, 0, mm(part(o_rows, p_corner), wp_ref[...]))
    to_twin(0, 1, mm(part(o_rows, p_twin), wp_ref[...]))
    value = mm(part(o_rows, p_across), wp_ref[...])
    to_across(0, value + from_twin(0, 0))
    for copy in fetched[1:]:
        copy.wait()
    bias_row[...] = ebias_ref[...].astype(F32).reshape(1, D)
    for p in range(4):
        gact[p * 192 : p * 192 + 192, :] = mm_nt(gtwo_ref[p * 192 : p * 192 + 192, :], contract_ref[...])
    value = mm(part(o_rows, mine), wp_ref[...]) + from_twin(0, 1)
    value = value + from_across(0)
    middle = tok_ref[...].astype(F32) + BRANCH * (value + vec_ref[2:3, :])
    out, unit_two, inverse = layer_norm(middle, vec_ref[6:7, :], vec_ref[7:8, :])
    n2[pl.ds(pl.multiple_of(mine * 192, 192), 192), :] = out.astype(BF)
    share(0, n2)
    unit[...] = unit_two
    held[...] = middle

    def through(p):
        at = pl.ds(pl.multiple_of(p * 192, 192), 192)
        expanded = mm(n2[at, :], expand_ref[...]) + bias_row[...]
        activation, slope = gelu_pair(expanded)
        act[at, :] = activation.astype(BF)
        low = (gact[at, :] * slope).astype(BF)
        gexp[at, :] = low
        return mm_nt(low, expand_ref[...])

    own_value = through(mine)
    share_twin(0, n2)
    to_twin(1, 1, through(p_twin))
    share_across(0, n2)
    across_value = through(p_across)
    share_corner(0, n2)
    to_twin(1, 0, through(p_corner))
    to_across(1, across_value + from_twin(1, 0))
    own_value = own_value + from_twin(1, 1)
    to_twin(2, 0, mm(part(act, p_corner), contract_ref[...]))
    to_twin(2, 1, mm(part(act, p_twin), contract_ref[...]))
    to_across(2, mm(part(act, p_across), contract_ref[...]) + from_twin(2, 0))
    cpart_out[...] = mm_tn(act[...], gtwo_ref[...]).astype(BF)
    grad = own_value + from_across(1)
    unit_two = unit[...]
    scaled = grad * vec_ref[6:7, :]
    spread = (
        scaled
        - jnp.mean(scaled, axis=1, keepdims=True)
        - unit_two * jnp.mean(scaled * unit_two, axis=1, keepdims=True)
    )
    grad_middle = cot_ref[...].astype(F32) + inverse * spread
    gmid_out[...] = grad_middle
    low = (BRANCH * grad_middle).astype(BF)
    gone_out[pl.ds(pl.multiple_of(mine * 192, 192), 192), :] = low
    share(1, gone_out)
    sums_out[0:1, :] = jnp.sum(low.astype(F32), axis=0, keepdims=True)
    sums_out[1:2, :] = jnp.sum(part(gtwo_ref, mine).astype(F32), axis=0, keepdims=True)
    sums_out[2:3, :] = jnp.sum(grad * unit_two, axis=0, keepdims=True)
    sums_out[3:4, :] = jnp.sum(grad, axis=0, keepdims=True)
    sums_out[4:5, :] = jnp.sum(gexp[...].astype(F32), axis=0, keepdims=True)
    sums_out[5:8, :] = jnp.zeros((3, D), F32)
    epart_out[...] = mm_tn(n2[...], gexp[...]).astype(BF)
    value = mm(part(act, mine), contract_ref[...]) + from_twin(2, 1)
    value = value + from_across(2)
    block_out[...] = (held[...] + BRANCH * (value + vec_ref[3:4, :])).astype(BF)
    share_across(1, gone_out)
    share_twin(1, gone_out)
    share_corner(1, gone_out)
    for i in range(3):
        for slot in range(2):
            remote(c_send_buf.at[i, slot], c_recv_buf.at[i, slot], c_send.at[i, slot], c_recv.at[i, slot], me.twin).wait_send()
        remote(x_send_buf.at[i], x_recv_buf.at[i], x_send.at[i], x_recv.at[i], me.across).wait_send()
    for i, ref in ((0, n2), (1, gone_out)):
        own = rows_of(ref, mine)
        for j in range(3):
            remote(own, own, ag_send.at[i, j], ag_recv.at[i, j], me.twin).wait_send()


def feed_forward(o, wp, expand, contract, ebias, tokens, cotangent, gtwo, vectors):
    rows = tokens.shape[0]
    block = rows * 4
    vmem = pl.BlockSpec(memory_space=pltpu.VMEM)
    anywhere = pl.BlockSpec(memory_space=pl.ANY)
    dma = pltpu.SemaphoreType.DMA
    return pl.pallas_call(
        mlp_kernel,
        in_specs=[vmem, anywhere, vmem, anywhere, anywhere, anywhere, anywhere, vmem, vmem],
        out_specs=[vmem] * 6,
        out_shape=[
            jax.ShapeDtypeStruct((rows, D), BF),
            jax.ShapeDtypeStruct((rows, D), F32),
            jax.ShapeDtypeStruct((block, D), BF),
            jax.ShapeDtypeStruct((D, D), BF),
            jax.ShapeDtypeStruct((D, D), BF),
            jax.ShapeDtypeStruct((8, D), F32),
        ],
        scratch_shapes=[
            pltpu.VMEM((192, D), BF),
            pltpu.VMEM((D, D), BF),
            pltpu.VMEM((rows, D), BF),
            pltpu.VMEM((rows, D), BF),
            pltpu.VMEM((D,), BF),
            pltpu.VMEM((1, D), F32),
            pltpu.VMEM((block, 192), BF),
            pltpu.VMEM((block, D), F32),
            pltpu.VMEM((block, D), BF),
            pltpu.VMEM((block, D), BF),
            pltpu.VMEM((block, D), BF),
            pltpu.VMEM((rows, D), F32),
            pltpu.VMEM((rows, D), F32),
            pltpu.VMEM((3, 2, rows, D), BF),
            pltpu.VMEM((3, 2, rows, D), BF),
            pltpu.VMEM((3, rows, D), BF),
            pltpu.VMEM((3, rows, D), BF),
            dma((3, 2)), dma((3, 2)), dma((3,)), dma((3,)), dma((2, 3)), dma((2, 3)), dma((5,)),
        ],
        compiler_params=pltpu.CompilerParams(collective_id=2, has_side_effects=True, vmem_limit_bytes=58 << 20),
        name="feed_forward",
    )(o, wp, expand, contract, ebias, tokens, cotangent, gtwo, vectors)


def mlp_near_kernel(
    o_ref, wp_hbm, expand_ref, contract_hbm, ebias_hbm, tok_hbm, cot_hbm, gtwo_ref, vec_ref,
    block_out, over_out, gmid_out, gone_out, cpart_out, epart_out, sums_out,
    wp_ref, contract_ref, tok_ref, cot_ref, ebias_ref, bias_row, o_rows, gact, n2, act, gexp, held, unit,
    c_send_buf, c_recv_buf, x_send_buf, x_recv_buf,
    c_send, c_recv, x_send, x_recv, ag_send, ag_recv, local_sem,
):
    me = Place()
    mine = me.part
    fetched = [
        pltpu.make_async_copy(source, target, local_sem.at[i])
        for i, (source, target) in enumerate(
            ((wp_hbm, wp_ref), (contract_hbm, contract_ref), (tok_hbm, tok_ref), (cot_hbm, cot_ref), (ebias_hbm, ebias_ref))
        )
    ]
    for copy in fetched:
        copy.start()
    o_rows[...] = o_ref[...].T.astype(BF)
    barrier = pltpu.get_barrier_semaphore()
    signal(barrier, me.twin)
    signal(barrier, me.across)
    pl.semaphore_wait(barrier, 2)
    p_across = (1 - me.half) * 2 + me.core
    p_twin = me.half * 2 + 1 - me.core
    p_corner = (1 - me.half) * 2 + 1 - me.core

    def part(ref, p):
        return ref[pl.ds(pl.multiple_of(p * 192, 192), 192), :]

    def to_twin(i, slot, value):
        c_send_buf[i, slot] = value.astype(BF)
        remote(c_send_buf.at[i, slot], c_recv_buf.at[i, slot], c_send.at[i, slot], c_recv.at[i, slot], me.twin).start()

    def from_twin(i, slot):
        remote(c_send_buf.at[i, slot], c_recv_buf.at[i, slot], c_send.at[i, slot], c_recv.at[i, slot], me.twin).wait_recv()
        return c_recv_buf[i, slot].astype(F32)

    def to_across(i, value):
        x_send_buf[i] = value.astype(BF)
        remote(x_send_buf.at[i], x_recv_buf.at[i], x_send.at[i], x_recv.at[i], me.across).start()

    def from_across(i):
        remote(x_send_buf.at[i], x_recv_buf.at[i], x_send.at[i], x_recv.at[i], me.across).wait_recv()
        return x_recv_buf[i].astype(F32)

    def share(i, ref):
        own = rows_of(ref, mine)
        remote(own, own, ag_send.at[i, 0], ag_recv.at[i, 0], me.across).start()
        remote(own, own, ag_send.at[i, 1], ag_recv.at[i, 1], me.twin).start()

    def share_across(i, ref):
        got = rows_of(ref, p_across)
        remote(got, got, ag_send.at[i, 0], ag_recv.at[i, 0], me.across).wait_recv()
        remote(got, got, ag_send.at[i, 2], ag_recv.at[i, 2], me.twin).start()

    def share_twin(i, ref):
        got = rows_of(ref, p_twin)
        remote(got, got, ag_send.at[i, 1], ag_recv.at[i, 1], me.twin).wait_recv()

    def share_corner(i, ref):
        got = rows_of(ref, p_corner)
        remote(got, got, ag_send.at[i, 2], ag_recv.at[i, 2], me.twin).wait_recv()

    fetched[0].wait()
    to_twin(0, 0, mm(part(o_rows, p_corner), wp_ref[...]))
    to_twin(0, 1, mm(part(o_rows, p_twin), wp_ref[...]))
    value = mm(part(o_rows, p_across), wp_ref[...])
    to_across(0, value + from_twin(0, 0))
    for copy in fetched[1:]:
        copy.wait()
    bias_row[...] = ebias_ref[...].astype(F32).reshape(1, D)
    for p in range(4):
        gact[p * 192 : p * 192 + 192, :] = mm_nt(gtwo_ref[p * 192 : p * 192 + 192, :], contract_ref[...])
    value = mm(part(o_rows, mine), wp_ref[...]) + from_twin(0, 1)
    value = value + from_across(0)
    middle = tok_ref[...].astype(F32) + BRANCH * (value + vec_ref[2:3, :])
    out, unit_two, inverse = layer_norm(middle, vec_ref[6:7, :], vec_ref[7:8, :])
    n2[pl.ds(pl.multiple_of(mine * 192, 192), 192), :] = out.astype(BF)
    share(0, n2)
    unit[...] = unit_two
    held[...] = middle

    def through(p):
        at = pl.ds(pl.multiple_of(p * 192, 192), 192)
        expanded = mm(n2[at, :], expand_ref[...]) + bias_row[...]
        activation, slope = gelu_pair(expanded)
        act[at, :] = activation.astype(BF)
        low = (gact[at, :] * slope).astype(BF)
        gexp[at, :] = low
        return mm_nt(low, expand_ref[...])

    own_value = through(mine)
    share_twin(0, n2)
    to_twin(1, 1, through(p_twin))
    share_across(0, n2)
    across_value = through(p_across)
    share_corner(0, n2)
    to_twin(1, 0, through(p_corner))
    to_across(1, across_value + from_twin(1, 0))
    own_value = own_value + from_twin(1, 1)
    to_twin(2, 0, mm(part(act, p_corner), contract_ref[...]))
    to_twin(2, 1, mm(part(act, p_twin), contract_ref[...]))
    cpart_out[...] = mm_tn(act[...], gtwo_ref[...]).astype(BF)
    grad = own_value + from_across(1)
    unit_two = unit[...]
    scaled = grad * vec_ref[6:7, :]
    spread = (
        scaled
        - jnp.mean(scaled, axis=1, keepdims=True)
        - unit_two * jnp.mean(scaled * unit_two, axis=1, keepdims=True)
    )
    grad_middle = cot_ref[...].astype(F32) + inverse * spread
    gmid_out[...] = grad_middle
    low = (BRANCH * grad_middle).astype(BF)
    gone_out[pl.ds(pl.multiple_of(mine * 192, 192), 192), :] = low
    share(1, gone_out)
    sums_out[0:1, :] = jnp.sum(low.astype(F32), axis=0, keepdims=True)
    sums_out[1:2, :] = jnp.sum(part(gtwo_ref, mine).astype(F32), axis=0, keepdims=True)
    sums_out[2:3, :] = jnp.sum(grad * unit_two, axis=0, keepdims=True)
    sums_out[3:4, :] = jnp.sum(grad, axis=0, keepdims=True)
    sums_out[4:5, :] = jnp.sum(gexp[...].astype(F32), axis=0, keepdims=True)
    sums_out[5:8, :] = jnp.zeros((3, D), F32)
    epart_out[...] = mm_tn(n2[...], gexp[...]).astype(BF)
    value = mm(part(act, mine), contract_ref[...]) + from_twin(2, 1)
    block_out[...] = held[...] + BRANCH * (value + vec_ref[3:4, :])
    over_out[...] = (mm(part(act, p_across), contract_ref[...]) + from_twin(2, 0)).astype(BF)
    share_across(1, gone_out)
    share_twin(1, gone_out)
    share_corner(1, gone_out)
    for i in range(3):
        for slot in range(2):
            remote(c_send_buf.at[i, slot], c_recv_buf.at[i, slot], c_send.at[i, slot], c_recv.at[i, slot], me.twin).wait_send()
    for i in range(2):
        remote(x_send_buf.at[i], x_recv_buf.at[i], x_send.at[i], x_recv.at[i], me.across).wait_send()
    for i, ref in ((0, n2), (1, gone_out)):
        own = rows_of(ref, mine)
        for j in range(3):
            remote(own, own, ag_send.at[i, j], ag_recv.at[i, j], me.twin).wait_send()


def feed_forward_near(o, wp, expand, contract, ebias, tokens, cotangent, gtwo, vectors):
    rows = tokens.shape[0]
    block = rows * 4
    vmem = pl.BlockSpec(memory_space=pltpu.VMEM)
    anywhere = pl.BlockSpec(memory_space=pl.ANY)
    dma = pltpu.SemaphoreType.DMA
    return pl.pallas_call(
        mlp_near_kernel,
        in_specs=[vmem, anywhere, vmem, anywhere, anywhere, anywhere, anywhere, vmem, vmem],
        out_specs=[vmem] * 7,
        out_shape=[
            jax.ShapeDtypeStruct((rows, D), F32),
            jax.ShapeDtypeStruct((rows, D), BF),
            jax.ShapeDtypeStruct((rows, D), F32),
            jax.ShapeDtypeStruct((block, D), BF),
            jax.ShapeDtypeStruct((D, D), BF),
            jax.ShapeDtypeStruct((D, D), BF),
            jax.ShapeDtypeStruct((8, D), F32),
        ],
        scratch_shapes=[
            pltpu.VMEM((192, D), BF),
            pltpu.VMEM((D, D), BF),
            pltpu.VMEM((rows, D), BF),
            pltpu.VMEM((rows, D), BF),
            pltpu.VMEM((D,), BF),
            pltpu.VMEM((1, D), F32),
            pltpu.VMEM((block, 192), BF),
            pltpu.VMEM((block, D), F32),
            pltpu.VMEM((block, D), BF),
            pltpu.VMEM((block, D), BF),
            pltpu.VMEM((block, D), BF),
            pltpu.VMEM((rows, D), F32),
            pltpu.VMEM((rows, D), F32),
            pltpu.VMEM((3, 2, rows, D), BF),
            pltpu.VMEM((3, 2, rows, D), BF),
            pltpu.VMEM((2, rows, D), BF),
            pltpu.VMEM((2, rows, D), BF),
            dma((3, 2)), dma((3, 2)), dma((2,)), dma((2,)), dma((2, 3)), dma((2, 3)), dma((5,)),
        ],
        compiler_params=pltpu.CompilerParams(collective_id=7, has_side_effects=True, vmem_limit_bytes=58 << 20),
        name="feed_forward_near",
    )(o, wp, expand, contract, ebias, tokens, cotangent, gtwo, vectors)


ORDERS = (
    (
        "g0", "A0", "A1", "g1", "g2", "W0", "d0", "X0", "d1", "s0", "s1", "W1",
        "gf", "X1", "E", "d2", "dn", "s2", "v0", "r1", "v1", "af", "r2", "v2",
        "r3", "a", "v3",
    ),
    (
        "A0", "g0", "d0", "A1", "W0", "d1", "A2", "W1", "A3", "g1", "W2", "X0",
        "g2", "X1", "gf", "s0", "r1", "X2", "W3", "X3", "d2", "s1", "E", "s2",
        "r2", "dn", "af", "a", "v0", "v1", "v2", "r3", "v3",
    ),
    (
        "A0", "A1", "W0", "W1", "A2", "g0", "W2", "A3", "X0", "g1", "X1", "W3",
        "X2", "d0", "g2", "A4", "gf", "A5", "s0", "d1", "r1", "W4", "X3", "X4",
        "W5", "E", "d2", "r2", "r3", "s1", "s2", "X5", "af", "dn", "v0", "a",
        "v1", "v2", "v3",
    ),
    (
        "A0", "A1", "W0", "g0", "A2", "X0", "W1", "A3", "X1", "g1", "W2", "A4",
        "W3", "g2", "d0", "X2", "A5", "W4", "X3", "gf", "A6", "W5", "X4", "A7",
        "W6", "d1", "W7", "s0", "X5", "X6", "E", "s1", "d2", "X7", "s2", "dn",
        "v0", "r1", "r2", "af", "v1", "r3", "v2", "a", "v3",
    ),
)


class Exchange:
    def __init__(self, me, levels, items, y_send, y_recv, z_send, z_recv):
        self.me, self.top, self.items = me, levels - 1, items
        self.y_send, self.y_recv, self.z_send, self.z_recv = y_send, y_recv, z_send, z_recv

    def beside(self, level, act, only=None):
        for i, (chunk, y_in, z_out, z_in) in enumerate(self.items):
            if only is None or i in only:
                act(remote(chunk(level, 1 - self.me.side), y_in.at[level], self.y_send.at[level, i], self.y_recv.at[level, i], self.me.beside))

    def steps(self, step, act):
        z, top = self.me.level, self.top
        down = step - (top - z)
        up = top - (step - z)

        @pl.when((down >= 0) & (down < z))
        def _():
            act(down, 0)

        @pl.when((up <= top) & (up > z))
        def _():
            act(up, 1)

    def along(self, level, way, act):
        device = self.me.at(level=self.me.level - 1) if way == 0 else self.me.at(level=self.me.level + 1)
        last = level == (self.me.level - 1 if way == 0 else self.me.level + 1)
        spot = level if way == 0 else jnp.where(last, self.top + 1, level)
        for i, (chunk, y_in, z_out, z_in) in enumerate(self.items):
            act(remote(z_out.at[level], z_in.at[spot], self.z_send.at[level, i], self.z_recv.at[spot, i], device))

    def arrived(self, level, way):
        spot = level if way == 0 else jnp.where(level == self.me.level, self.top + 1, level)
        for i, (chunk, y_in, z_out, z_in) in enumerate(self.items):
            remote(z_out.at[level], z_in.at[spot], self.z_send.at[level, i], self.z_recv.at[spot, i], self.me.twin).wait_recv()
        return spot

    def step(self, step):
        z, top, side = self.me.level, self.top, self.me.side

        def act(level, way):
            self.beside(level, lambda copy: copy.wait_recv())
            inner = (z < top) if way == 0 else (z > 0)

            @pl.when(inner)
            def _():
                spot = self.arrived(level, way)
                for chunk, y_in, z_out, z_in in self.items:
                    z_out[level] = (
                        chunk(level, side)[...].astype(F32) + y_in[level].astype(F32) + z_in[spot].astype(F32)
                    ).astype(BF)

            @pl.when(jnp.logical_not(inner))
            def _():
                for chunk, y_in, z_out, z_in in self.items:
                    z_out[level] = (chunk(level, side)[...].astype(F32) + y_in[level].astype(F32)).astype(BF)

            self.along(level, way, lambda copy: copy.start())

        self.steps(step, act)

    def final(self, targets):
        z, top, side = self.me.level, self.top, self.me.side
        self.beside(z, lambda copy: copy.wait_recv())

        def add(spots):
            for (chunk, y_in, z_out, z_in), target in zip(self.items, targets):
                sum_of = chunk(z, side)[...].astype(F32) + y_in[z].astype(F32)
                for spot in spots:
                    sum_of = sum_of + z_in[spot].astype(F32)
                target[...] = sum_of.astype(BF)

        @pl.when(z < top)
        def _():
            self.arrived(z, 0)

        @pl.when(z > 0)
        def _():
            self.arrived(z, 1)

        @pl.when(z == 0)
        def _():
            add((z,))

        @pl.when(z == top)
        def _():
            add((top + 1,))

        @pl.when((z > 0) & (z < top))
        def _():
            add((z, top + 1))

    def drain(self):
        for level in range(self.top + 1):
            self.beside(level, lambda copy: copy.wait_send())

            @pl.when(level != self.me.level)
            def _():
                for i, (chunk, y_in, z_out, z_in) in enumerate(self.items):
                    remote(z_out.at[level], z_in.at[level], self.z_send.at[level, i], self.z_recv.at[level, i], self.me.twin).wait_send()


def attend_reduce_kernel(
    levels, starts_ref, all_ref, k_ref, v_ref, q_ref, o_ref, lse_ref, g_ref, wp_hbm, aw_ref,
    c_ref, e_ref, tok_hbm, gmid_ref, vec_ref, sums_ref, near_ref, over_ref,
    tg_out, cg_out, eg_out, a_rows, pg_out, vec_out, block_out,
    over_in, wp_ref, tok_ref, rows_in, keys_in, values_in, begins, qm, dm, qn, dn, delta, dqt, kt, dk, dv, gt, a_part, p_part,
    dnb, far, keep, x_in, y_out, y_in, d_out, d_in,
    yc, ye, ya, yp, zc_out, ze_out, za_out, zp_out, zc_in, ze_in, za_in, zp_in, v_out, v_in, e_move, a_move,
    pre_sem, far_send, far_recv, x_send, x_recv, y_send, y_recv, d_send, d_recv,
    gy_send, gy_recv, gz_send, gz_recv, ay_send, ay_recv, az_send, az_recv,
    me_send, me_recv, ma_send, ma_recv, u_send, u_recv, w_send, w_recv,
    be_send, be_recv, ba_send, ba_recv, te_send, te_recv, ta_send, ta_recv, v_send, v_recv, local_sem, o_send, o_recv,
):
    me = Place()
    z, side, mine, ctx = me.level, me.side, me.part, me.ctx
    top = levels - 1
    block = g_ref.shape[0]
    barrier = pltpu.get_barrier_semaphore()
    for device in (me.twin, me.across, me.corner, me.beside):
        signal(barrier, device)
    for step in range(1, levels):
        signal(barrier, me.at(level=(z + step) % levels))
    below, above = me.at(level=z - 1), me.at(level=z + 1)
    start = lambda copy: copy.start()
    wait_recv = lambda copy: copy.wait_recv()
    wait_send = lambda copy: copy.wait_send()

    def prefetch(index):
        slot = index % 2
        at = pl.ds(pl.multiple_of(index * block, block), block)
        return (
            pltpu.make_async_copy(all_ref.at[at], rows_in.at[slot], pre_sem.at[slot, 0]),
            pltpu.make_async_copy(k_ref.at[at], keys_in.at[slot], pre_sem.at[slot, 1]),
            pltpu.make_async_copy(v_ref.at[at], values_in.at[slot], pre_sem.at[slot, 2]),
        )

    def all_of(copies, act):
        for copy in copies:
            act(copy)

    all_of(prefetch(0), start)
    fetched = (
        pltpu.make_async_copy(wp_hbm, wp_ref, local_sem.at[0]),
        pltpu.make_async_copy(tok_hbm, tok_ref, local_sem.at[1]),
    )
    all_of(fetched, start)

    def corner_of(ref, level, where):
        return ref.at[pl.ds(pl.multiple_of(level * 48, 48), 48), pl.ds(pl.multiple_of(where * 384, 128), 384)]

    grads = Exchange(
        me, levels,
        (
            (lambda level, where: c_ref.at[level * 2 + where], yc, zc_out, zc_in),
            (lambda level, where: e_ref.at[level * 2 + where], ye, ze_out, ze_in),
            (lambda level, where: corner_of(p_part, level, where), yp, zp_out, zp_in),
        ),
        gy_send, gy_recv, gz_send, gz_recv,
    )
    attends = Exchange(
        me, levels, ((lambda level, where: a_part.at[level * 2 + where], ya, za_out, za_in),), ay_send, ay_recv, az_send, az_recv
    )
    grads_in = g_ref[...]
    exact = o_ref[...]
    p_part[...] = mm(exact.astype(BF), grads_in).astype(BF)
    all_of(fetched, lambda copy: copy.wait())
    outer = mm_nt(grads_in, wp_ref[...]).astype(BF)
    pl.semaphore_wait(barrier, levels + 3)
    over = remote(over_ref, over_in, o_send.at[0], o_recv.at[0], me.across)
    over.start()
    for step in range(levels - 1):
        grads.steps(step, lambda level, way: grads.beside(level, start))
    grads.beside(z, start)
    flipped = outer.astype(F32).T
    product = flipped * exact
    for head in range(3):
        delta[head : head + 1, :] = jnp.sum(product[head * HD : head * HD + HD], axis=0, keepdims=True)
    fill_masked_columns(dm, flipped.astype(BF))
    scaled = q_ref[...].astype(F32) * SCALE
    fill_masked_columns(qm, scaled.T.astype(BF))
    scaled = scaled.astype(BF)
    for head in range(3):
        depth = 128 if head < 2 else HD
        qn[head, :, 0:depth] = masked_rows(scaled, head)
        dn[head, :, 0:depth] = masked_rows(outer, head)
    dqt[...] = jnp.zeros(dqt.shape, F32)
    gt[...] = jnp.zeros(gt.shape, F32)
    first_query = ctx * block
    begins[...] = begins_of(starts_ref, first_query, block)
    v_out[0] = jnp.zeros(v_out.shape[1:], F32)

    def attend(index, diagonal):
        slot = index % 2
        first_key = index * block
        kt[...] = keys_in[slot].astype(F32).T.astype(BF)
        dk[...] = jnp.zeros(dk.shape, F32)
        dv[...] = jnp.zeros(dv.shape, F32)
        strips = [(head, strip) for head in range(3) for strip in range(block // STRIP)]

        def keys_of(strip):
            return strip * STRIP + STRIP if diagonal else block

        def scored(head, strip):
            depth = 128 if head < 2 else HD
            lanes = head_lanes(head)
            cols = slice(strip * STRIP, strip * STRIP + STRIP)
            count = keys_of(strip)
            return (
                mm(keys_in[slot, 0:count, lanes], qm[head, 0:depth, cols]),
                mm(values_in[slot, 0:count, lanes], dm[head, 0:depth, cols]),
            )

        ahead = [scored(*strips[i]) for i in range(BACK_LEAD)]
        for i, (head, strip) in enumerate(strips):
            scores, outer = ahead.pop(0)
            if i + BACK_LEAD < len(strips):
                ahead.append(scored(*strips[i + BACK_LEAD]))
            depth = 128 if head < 2 else HD
            lanes = head_lanes(head)
            cols = slice(strip * STRIP, strip * STRIP + STRIP)
            count = keys_of(strip)
            places = first_key + lax.broadcasted_iota(jnp.int32, (count, STRIP), 0)
            allowed = places >= begins[:, cols]
            if diagonal:
                queries = first_query + strip * STRIP + lax.broadcasted_iota(jnp.int32, (count, STRIP), 1)
                allowed = allowed & (places <= queries)
            probs = jnp.where(allowed, jnp.exp(scores - lse_ref[head : head + 1, cols]), 0.0)
            inner = (probs * (outer - delta[head : head + 1, cols])).astype(BF)
            dv[0:count, lanes] += mm(probs.astype(BF), dn[head, cols, 0:depth])
            dk[0:count, lanes] += mm(inner, qn[head, cols, 0:depth])
            part = slice(head * HD, head * HD + HD)
            dqt[part, cols] += mm(kt[part, 0:count], inner)
        rows = rows_in[slot]
        low_k = dk[...].astype(BF)
        low_v = dv[...].astype(BF)
        gt[192:384, :] += mm(low_k.astype(F32).T.astype(BF), rows)
        gt[384:576, :] += mm(low_v.astype(F32).T.astype(BF), rows)
        v_out[0, 12:13, 0:192] += jnp.sum(low_v.astype(F32), axis=0, keepdims=True)
        through = mm_nt(low_k, aw_ref[:, 192:384]) + mm_nt(low_v, aw_ref[:, 384:576])
        if diagonal:
            flipped = dqt[...] * SCALE
            low_q = flipped.T.astype(BF)
            gt[0:192, :] = mm(flipped.astype(BF), rows)
            v_out[0, 13:14, 0:192] = jnp.sum(low_q.astype(F32), axis=0, keepdims=True)
            through = through + mm_nt(low_q, aw_ref[:, 0:192])
        dnb[index % 3] = through.astype(BF)

    def to_twin(index):
        slot = index % 3
        return tuple(
            remote(
                rows_of(dnb.at[slot], half * 2 + 1 - me.core), far.at[index, half],
                far_send.at[index, half], far_recv.at[index, half], me.twin,
            )
            for half in range(2)
        )

    def x_copy(index):
        return remote(far.at[index, 0], x_in.at[index], x_send.at[index], x_recv.at[index], me.across)

    def y_copy(level):
        return remote(y_out.at[level], y_in.at[level], y_send.at[level], y_recv.at[level], me.beside)

    def down_copy(level):
        return remote(d_out.at[level], d_in.at[level], d_send.at[level], d_recv.at[level], below)

    def with_twin(index):
        slot = index % 3
        all_of(to_twin(index), lambda copy: copy.wait())

        def rows(half):
            own = dnb[slot, pl.ds(pl.multiple_of((half * 2 + me.core) * 192, 192), 192), :]
            return own.astype(F32) + far[index, half].astype(F32)

        keep[index] = rows(me.half)
        far[index, 0] = rows(1 - me.half).astype(BF)
        x_copy(index).start()

    def with_across(index):
        x_copy(index).wait_recv()
        keep[index] += x_in[index].astype(F32)
        level = index // 2

        @pl.when((index % 2 != side))
        def _():
            y_out[level] = keep[index].astype(BF)
            y_copy(level).start()

    def with_beside(level):
        y_copy(level).wait_recv()
        keep[level * 2 + side] += y_in[level].astype(F32)

    def dn_step(step):
        level = step - (top - z)

        @pl.when((level >= 0) & (level < z))
        def _():
            with_beside(level)
            index = level * 2 + side

            @pl.when(z < top)
            def _():
                down_copy(level).wait_recv()
                keep[index] += d_in[level].astype(F32)

            d_out[level] = keep[index].astype(BF)
            down_copy(level).start()

    def done(level, where):
        return (cg_out.at[level * 2 + where], corner_of(pg_out, level, where))

    def along_copies(way, distance):
        level = z - distance if way == 0 else z + distance
        device = above if way == 0 else below
        return tuple(
            remote(ref, ref, u_send.at[way, distance, i], u_recv.at[way, distance, i], device)
            for i, ref in enumerate(done(level, side))
        )

    def side_copies(level, where):
        return tuple(
            remote(ref, ref, w_send.at[level, i], w_recv.at[level, i], me.beside) for i, ref in enumerate(done(level, where))
        )

    def pass_on(distance, way):
        if way != 1:

            @pl.when(z < top)
            def _():
                all_of(along_copies(0, distance), start)

        if way != 0:

            @pl.when(z > 0)
            def _():
                all_of(along_copies(1, distance), start)

        all_of(side_copies(z - distance if way == 0 else z + distance, side), start)

    def arrivals(distance):
        for way in range(2):
            level = z - distance if way == 0 else z + distance

            @pl.when((level >= 0) & (level <= top))
            def _():
                for i, ref in enumerate(done(level, side)):
                    remote(ref, ref, u_send.at[way, distance - 1, i], u_recv.at[way, distance - 1, i], me.twin).wait_recv()
                pass_on(distance, way)

    def e_chunk(where, origin):
        return eg_out.at[pl.ds(pl.multiple_of(where * 96, 96), 96), pl.ds(pl.multiple_of(origin * D, D), D)]

    def a_chunk(where, origin):
        return a_rows.at[where, origin]

    class Rows:
        def __init__(self, moved, chunk, m_send, m_recv, b_send, b_recv, t_send, t_recv):
            self.moved, self.chunk = moved, chunk
            self.m_send, self.m_recv, self.b_send, self.b_recv = m_send, m_recv, b_send, b_recv
            self.t_send, self.t_recv = t_send, t_recv

        def move(self):
            return remote(self.moved, self.chunk(side, mine), self.m_send.at[0], self.m_recv.at[mine], me.at(half=z // 2, core=z % 2))

        def begin(self):
            @pl.when(mine != z)
            def _():
                self.move().start()

            @pl.when(mine == z)
            def _():
                self.chunk(side, mine)[...] = self.moved[...]

        def line(self, way, origin):
            ref = self.chunk(side, origin)
            return remote(ref, ref, self.b_send.at[way, origin], self.b_recv.at[way, origin], below if way == 0 else above)

        def turn(self, origin, where):
            ref = self.chunk(where, origin)
            return remote(ref, ref, self.t_send.at[origin], self.t_recv.at[origin], me.beside)

        def spread(self, origin):
            @pl.when((mine == z) & (mine != origin))
            def _():
                remote(self.moved, self.chunk(side, origin), self.m_send.at[0], self.m_recv.at[origin], me.twin).wait_recv()

            @pl.when(mine > z)
            def _():
                self.line(0, origin).wait_recv()

            @pl.when(mine < z)
            def _():
                self.line(1, origin).wait_recv()

            @pl.when((mine >= z) & (z > 0))
            def _():
                self.line(0, origin).start()

            @pl.when((mine <= z) & (z < top))
            def _():
                self.line(1, origin).start()

            self.turn(origin, side).start()

        def drain(self):
            @pl.when(mine != z)
            def _():
                self.move().wait_send()

            for origin in range(4):

                @pl.when((mine >= z) & (z > 0))
                def _():
                    self.line(0, origin).wait_send()

                @pl.when((mine <= z) & (z < top))
                def _():
                    self.line(1, origin).wait_send()

                self.turn(origin, side).wait_send()

    e_flow = Rows(e_move, e_chunk, me_send, me_recv, be_send, be_recv, te_send, te_recv)
    a_flow = Rows(a_move, a_chunk, ma_send, ma_recv, ba_send, ba_recv, ta_send, ta_recv)

    def finish_rows():
        @pl.when(side == 0)
        def _():
            with_beside(z)

        @pl.when(z < top)
        def _():
            down_copy(z).wait_recv()
            keep[ctx] += d_in[z].astype(F32)

        grad = keep[ctx]
        gain = vec_ref[4:5, :]
        normed, unit, inverse = layer_norm(tok_ref[...].astype(F32), gain, vec_ref[5:6, :])
        scaled = grad * gain
        spread = (
            scaled - jnp.mean(scaled, axis=1, keepdims=True) - unit * jnp.mean(scaled * unit, axis=1, keepdims=True)
        )
        tg_out[...] = (gmid_ref[...] + inverse * spread).astype(BF)
        for part in range(4):

            @pl.when(mine == part)
            def _():
                v_out[0, 0:1, part * 192 : part * 192 + 192] = v_out[0, 13:14, 0:192]
                v_out[0, 1:2, part * 192 : part * 192 + 192] = v_out[0, 12:13, 0:192]
                v_out[0, 8 + part : 9 + part, :] = sums_ref[4:5, :]

        v_out[0, 12:16, :] = jnp.zeros((4, D), F32)
        v_out[0, 2:4, :] = sums_ref[0:2, :]
        v_out[0, 4:5, :] = jnp.sum(grad * unit, axis=0, keepdims=True)
        v_out[0, 5:6, :] = jnp.sum(grad, axis=0, keepdims=True)
        v_out[0, 6:8, :] = sums_ref[2:4, :]

    def v_copy(i):
        return remote(v_out.at[i], v_in.at[i], v_send.at[i], v_recv.at[i], (me.twin, me.across, me.beside)[i])

    def vectors_on(i):
        if i > 0:
            v_copy(i - 1).wait_recv()
            v_out[i] = v_out[i - 1] + v_in[i - 1]
        if i < 3:
            v_copy(i).start()
        else:
            v_in[3 + z] = v_out[3]
            for step in range(1, levels):
                remote(
                    v_out.at[3], v_in.at[3 + z], v_send.at[2 + step], v_recv.at[3 + z], me.at(level=(z + step) % levels)
                ).start()


    def slot_of(name):
        spots = [order.index(name) if name in order else -1 for order in ORDERS]
        spot = jnp.int32(spots[0])
        for level in range(1, levels):
            spot = jnp.where(z == level, jnp.int32(spots[level]), spot)
        return spot

    def spots_of(kind, count):
        return [slot_of(kind + str(i)) for i in range(count)]

    spots = {kind: spots_of(kind, count) for kind, count in (("A", 8), ("W", 8), ("X", 8), ("g", 3), ("d", 3), ("s", 3), ("v", 4))}
    spots["r"] = [slot_of("r" + str(i + 1)) for i in range(3)]
    single = {name: slot_of(name) for name in ("gf", "af", "dn", "E", "a")}

    @pl.loop(0, max(len(order) for order in ORDERS))
    def _(slot):
        def number(kind):
            found = jnp.int32(-1)
            for i, spot in enumerate(spots[kind]):
                found = jnp.where(slot == spot, jnp.int32(i), found)
            return found

        turn = number("A")

        @pl.when((turn >= 0) & (turn <= ctx))
        def _():
            all_of(prefetch(turn), lambda copy: copy.wait())

            @pl.when(turn + 1 <= ctx)
            def _():
                all_of(prefetch(turn + 1), start)

            @pl.when(turn < ctx)
            def _():
                attend(turn, False)

            @pl.when(turn == ctx)
            def _():
                attend(turn, True)
                flipped = gt[...].T.astype(BF)
                for chunk in range(8):
                    a_part[chunk] = flipped[chunk * 96 : chunk * 96 + 96]
                for step in range(levels - 1):
                    attends.steps(step, lambda level, way: attends.beside(level, start))
                attends.beside(z, start)

            all_of(to_twin(turn), start)

        after = number("W")

        @pl.when((after >= 0) & (after <= ctx))
        def _():
            with_twin(after)

        last = number("X")

        @pl.when((last >= 0) & (last <= ctx))
        def _():
            with_across(last)

        for kind, act in (("g", grads.step), ("d", dn_step), ("s", attends.step)):
            step = number(kind)

            @pl.when(step >= 0)
            def _():
                act(step)

        distance = number("r")

        @pl.when(distance >= 0)
        def _():
            arrivals(distance + 1)

        @pl.when(slot == single["gf"])
        def _():
            grads.final((cg_out.at[ctx], e_move, corner_of(pg_out, z, side)))
            e_flow.begin()
            pass_on(0, 2)

        @pl.when(slot == single["af"])
        def _():
            attends.final((a_move,))
            a_flow.begin()

        for name, flow in (("E", e_flow), ("a", a_flow)):

            @pl.when(slot == single[name])
            def _():
                for origin in range(4):
                    flow.spread(origin)

        @pl.when(slot == single["dn"])
        def _():
            finish_rows()

        for i in range(4):

            @pl.when(slot == spots["v"][i])
            def _():
                vectors_on(i)

    for step in range(1, levels):
        level = (z + step) % levels
        remote(v_out.at[3], v_in.at[3 + level], v_send.at[2 + step], v_recv.at[3 + level], me.twin).wait_recv()
    total = v_in[3]
    for level in range(1, levels):
        total = total + v_in[3 + level]
    vec_out[...] = total

    over.wait()
    block_out[...] = (near_ref[...] + BRANCH * over_in[...].astype(F32)).astype(BF)
    for level in range(levels):
        all_of(side_copies(level, 1 - side), wait_recv)
    for flow in (e_flow, a_flow):
        for origin in range(4):
            flow.turn(origin, 1 - side).wait_recv()
    grads.drain()
    attends.drain()
    e_flow.drain()
    a_flow.drain()
    for level in range(levels):
        all_of(side_copies(level, side), wait_send)

        @pl.when((level < z) | ((level == z) & (side == 1)))
        def _():
            y_copy(level).wait_send()

        @pl.when(level < z)
        def _():
            down_copy(level).wait_send()

    @pl.loop(0, 2 * levels)
    def _(index):
        @pl.when(index <= ctx)
        def _():
            x_copy(index).wait_send()

    for distance in range(levels):

        @pl.when((z - distance >= 0) & (z < top))
        def _():
            all_of(along_copies(0, distance), wait_send)

        @pl.when((z + distance <= top) & (z > 0))
        def _():
            all_of(along_copies(1, distance), wait_send)

    for i in range(2 + levels):
        remote(v_out.at[0], v_in.at[0], v_send.at[i], v_recv.at[0], me.twin).wait_send()


def attend_reduce(starts, rows_all, k, v, q, o, lse, g, wp, aw, contract, expand, tokens, grad_middle, vectors, sums, near, over):
    levels = lax.axis_size("ctx") // 2
    rows = tokens.shape[0]
    block = rows * 4
    vmem = pl.BlockSpec(memory_space=pltpu.VMEM)
    anywhere = pl.BlockSpec(memory_space=pl.ANY)
    dma = pltpu.SemaphoreType.DMA
    n = levels

    def buf(*shape):
        return pltpu.VMEM(shape, BF)

    def wide(*shape):
        return pltpu.VMEM(shape, F32)

    return pl.pallas_call(
        functools.partial(attend_reduce_kernel, levels),
        in_specs=[pl.BlockSpec(memory_space=pltpu.SMEM)] + [anywhere] * 3 + [vmem] * 4 + [anywhere] + [vmem] * 3 + [anywhere] + [vmem] * 5,
        out_specs=[vmem] * 7,
        out_shape=[
            jax.ShapeDtypeStruct((rows, D), BF),
            jax.ShapeDtypeStruct((2 * n, 96, D), BF),
            jax.ShapeDtypeStruct((192, 4 * D), BF),
            jax.ShapeDtypeStruct((2, 4, 96, 576), BF),
            jax.ShapeDtypeStruct((192, D), BF),
            jax.ShapeDtypeStruct((16, D), F32),
            jax.ShapeDtypeStruct((rows, D), BF),
        ],
        scratch_shapes=[
            buf(rows, D), buf(192, D), buf(rows, D),
            buf(2, block, D), buf(2, block, 192), buf(2, block, 192), pltpu.VMEM((1, block), jnp.int32),
            buf(3, 128, block), buf(3, 128, block), buf(3, block, 128), buf(3, block, 128),
            wide(8, block), wide(192, block), buf(192, block), wide(block, 192), wide(block, 192), wide(576, D),
            buf(2 * n, 96, 576), buf(192, D),
            buf(3, block, D), buf(2 * n, 2, rows, D), wide(2 * n, rows, D), buf(2 * n, rows, D),
            buf(n, rows, D), buf(n, rows, D), buf(n, rows, D), buf(n, rows, D),
            buf(n, 96, D), buf(n, 96, D), buf(n, 96, 576), buf(n, 48, 384),
            buf(n, 96, D), buf(n, 96, D), buf(n, 96, 576), buf(n, 48, 384),
            buf(n + 1, 96, D), buf(n + 1, 96, D), buf(n + 1, 96, 576), buf(n + 1, 48, 384),
            wide(4, 16, D), wide(3 + n, 16, D), buf(96, D), buf(96, 576),
            dma((2, 3)), dma((2 * n, 2)), dma((2 * n, 2)), dma((2 * n,)), dma((2 * n,)),
            dma((n,)), dma((n,)), dma((n,)), dma((n,)),
            dma((n, 3)), dma((n, 3)), dma((n, 3)), dma((n + 1, 3)),
            dma((n, 1)), dma((n, 1)), dma((n, 1)), dma((n + 1, 1)),
            dma((1,)), dma((4,)), dma((1,)), dma((4,)),
            dma((2, n, 2)), dma((2, n, 2)), dma((n, 2)), dma((n, 2)),
            dma((2, 4)), dma((2, 4)), dma((2, 4)), dma((2, 4)), dma((4,)), dma((4,)), dma((4,)), dma((4,)),
            dma((2 + n,)), dma((3 + n,)), dma((2,)), dma((1,)), dma((1,)),
        ],
        compiler_params=pltpu.CompilerParams(collective_id=5, has_side_effects=True, vmem_limit_bytes=60 << 20),
        name="attend_reduce",
    )(starts, rows_all, k, v, q, o, lse, g, wp, aw, contract, expand, tokens, grad_middle, vectors, sums, near, over)


def finish_kernel(
    tg_ref, c_ref, e_ref, a_ref, p_ref, vec_ref, block_ref,
    block_out, tg_out, a_out, ab_out, p_out, pb_out, e_out, hid_out, c_out, cb_out, gf_out, sf_out, gs_out, ss_out,
):
    mine = lax.axis_index("fsdp")
    block_out[...] = block_ref[...]
    tg_out[...] = tg_ref[...]
    p_out[...] = p_ref[...].astype(F32)
    e_out[...] = e_ref[...].astype(F32)
    for chunk in range(8):
        c_out[chunk * 96 : chunk * 96 + 96, :] = c_ref[chunk].astype(F32)
    for where in range(2):
        for part in range(4):
            for kind in range(3):
                lane = kind * D + part * 192
                a_out[where * 96 : where * 96 + 96, lane : lane + 192] = a_ref[
                    where, part, :, kind * 192 : kind * 192 + 192
                ].astype(F32)
    hid_out[...] = vec_ref[pl.ds(8 + mine, 1), :].reshape(D)
    for part in range(4):

        @pl.when(mine == part)
        def _():
            source, lane = part // 2, (part % 2) * 384
            ab_out[...] = vec_ref[source : source + 1, lane : lane + 384].reshape(384)
            for i, ref in enumerate((pb_out, cb_out, gf_out, sf_out, gs_out, ss_out)):
                ref[...] = vec_ref[2 + i : 3 + i, part * 192 : part * 192 + 192].reshape(192)


def finish(tokens_grad, contract, expand, attend, project, vectors, block_output):
    rows = tokens_grad.shape[0]
    one = jax.ShapeDtypeStruct((192,), F32)
    return pl.pallas_call(
        finish_kernel,
        in_specs=[pl.BlockSpec(memory_space=pltpu.VMEM)] * 7,
        out_shape=[
            jax.ShapeDtypeStruct((rows, D), BF),
            jax.ShapeDtypeStruct((rows, D), BF),
            jax.ShapeDtypeStruct((192, 3 * D), F32),
            jax.ShapeDtypeStruct((384,), F32),
            jax.ShapeDtypeStruct((192, D), F32),
            one,
            jax.ShapeDtypeStruct((192, 4 * D), F32),
            jax.ShapeDtypeStruct((D,), F32),
            jax.ShapeDtypeStruct((D, D), F32),
            one, one, one, one, one,
        ],
        compiler_params=pltpu.CompilerParams(vmem_limit_bytes=58 << 20),
        name="finish",
    )(tokens_grad, contract, expand, attend, project, vectors, block_output)


def normalize(rows_in, gain, shift):
    mean = jnp.mean(rows_in, axis=1, keepdims=True)
    centered = rows_in - mean
    inverse = lax.rsqrt(jnp.mean(centered * centered, axis=1, keepdims=True) + EPS)
    unit = centered * inverse
    return (unit * gain + shift, unit, inverse)


def normalize_back(incoming, unit, inverse, gain):
    scaled = incoming * gain
    spread = (
        scaled
        - jnp.mean(scaled, axis=1, keepdims=True)
        - unit * jnp.mean(scaled * unit, axis=1, keepdims=True)
    )
    return (inverse * spread, jnp.sum(incoming * unit, axis=0), jnp.sum(incoming, axis=0))


def first_position(places, starts):
    below = starts[None, :] <= places[:, None]
    return jnp.max(jnp.where(below, starts[None, :], 0), axis=1)


def forward_plain(
    tokens, document_starts, attend_weight, attend_bias, expand_weight, cotangent, own_vectors
):
    rows = tokens.shape[0]
    ways = lax.axis_size("fsdp")
    block = rows * ways
    ctx = lax.axis_index("ctx")
    part = lax.axis_index("fsdp")
    vectors = lax.dynamic_update_slice(jnp.zeros((6, D), F32), jnp.stack(own_vectors).astype(F32), (0, part * rows))
    biases = lax.dynamic_update_slice(jnp.zeros((2 * D,), F32), attend_bias.astype(F32), (part * 2 * rows,))
    vectors = jnp.concatenate([biases.reshape(2, D), vectors])
    attend_cols = attend_weight.reshape(rows, 3, ways, 192).transpose(2, 0, 1, 3).reshape(ways, rows, 576)
    normed_all, attend_cols, expand_cols, g2, vectors = gather_inputs(
        tokens, vectors, attend_cols, expand_weight, cotangent
    )
    wq, wk, wv = attend_cols[:, :192], attend_cols[:, 192:384], attend_cols[:, 384:]
    bias = lax.dynamic_slice(vectors, (0, part * 192), (2, 192))
    own = lax.dynamic_slice(normed_all, (ctx * block, 0), (block, D))
    where, begins_row = places_of(document_starts, block)
    q, k, v, o, lse = attend_forward(where, normed_all, own, wq, wk, wv, bias, begins_row)
    return normed_all, attend_cols, expand_cols, g2, vectors, q, k, v, o, lse


def places_of(document_starts, block):
    ctx = lax.axis_index("ctx")
    places = ctx * block + jnp.arange(block, dtype=jnp.int32)
    begins = first_position(places, document_starts)
    where = jnp.stack([ctx, begins[0], begins[-1]]).astype(jnp.int32)
    return where, begins.reshape(1, block)


def forward(tokens, document_starts, attend_weight, attend_bias, expand_weight, cotangent, own_vectors):
    rows = tokens.shape[0]
    if lax.axis_size("ctx") != 8:
        return forward_plain(
            tokens, document_starts, attend_weight, attend_bias, expand_weight, cotangent, own_vectors
        )
    return gather_attend(
        document_starts, tokens, attend_weight, expand_weight, cotangent, (attend_bias,) + tuple(own_vectors)
    )


def backward_plain(
    document_starts, normed_all, k, v, q, o, lse, g1, project_weight, attend_cols,
    contract_part, expand_part, tokens, grad_middle, vectors, mlp_sums,
):
    both = ("ctx", "fsdp")
    rows = tokens.shape[0]
    ways = lax.axis_size("fsdp")
    block = rows * ways
    ctx = lax.axis_index("ctx")
    part = lax.axis_index("fsdp")
    gain_one = vectors[4]
    wq, wk, wv = attend_cols[:, :192], attend_cols[:, 192:384], attend_cols[:, 384:]
    where, begins_row = places_of(document_starts, block)
    own = lax.dynamic_slice(normed_all, (ctx * block, 0), (block, D))
    dn, attend_t, project_part, sums = attend_backward(
        where, normed_all, k, v, own, q, o, lse, g1, project_weight, wq, wk, wv, begins_row
    )
    grad_normed = lax.psum_scatter(dn.astype(F32), both, scatter_dimension=0, tiled=True)
    normed, unit_one, inverse_one = normalize(tokens.astype(F32), gain_one, jnp.zeros_like(gain_one))
    first_part, gainone_grad, shiftone_grad = normalize_back(grad_normed, unit_one, inverse_one, gain_one)
    tokens_grad = (grad_middle + first_part).astype(BF)

    def summed(array_in):
        return lax.psum(array_in.astype(BF), "ctx").astype(F32)

    contract_grad = summed(contract_part)
    project_grad = summed(project_part)
    expand_grad = lax.all_to_all(summed(expand_part).reshape(ways, rows, D), "fsdp", 0, 0)
    expand_grad = expand_grad.transpose(1, 0, 2).reshape(rows, ways * D)
    attend_grad = lax.all_to_all(summed(attend_t.T).reshape(ways, rows, 576), "fsdp", 0, 0)
    attend_grad = attend_grad.reshape(ways, rows, 3, 192).transpose(1, 2, 0, 3).reshape(rows, 3 * D)
    spread = lax.dynamic_update_slice(jnp.zeros((2, D), F32), sums[:2], (0, part * 192))
    hidden = lax.dynamic_update_slice(jnp.zeros((4, D), F32), mlp_sums[4:5], (part, 0))
    totals = jnp.concatenate([
        spread, mlp_sums[0:2], gainone_grad[None], shiftone_grad[None], mlp_sums[2:4], hidden
    ])
    totals = lax.psum(totals, both)
    attbias = lax.dynamic_slice(totals[:2].reshape(-1), (part * 2 * rows,), (2 * rows,))
    mine = lax.dynamic_slice(totals, (2, part * rows), (6, rows))
    expbias = lax.dynamic_slice(totals, (8 + part, 0), (1, D)).reshape(D)
    return (
        tokens_grad, attend_grad, attbias, project_grad, mine[0], expand_grad, expbias,
        contract_grad, mine[1], mine[2], mine[3], mine[4], mine[5],
    )


def per_device(
    tokens, document_starts, attend_weight, attend_bias, project_weight, project_bias,
    expand_weight, expand_bias, contract_weight, contract_bias,
    gain_first, shift_first, gain_second, shift_second, cotangent,
):
    both = ("ctx", "fsdp")
    rows = tokens.shape[0]
    ways = lax.axis_size("fsdp")
    block = rows * ways
    ctx = lax.axis_index("ctx")
    part = lax.axis_index("fsdp")

    def whole(array_in):
        return lax.all_gather(array_in, "fsdp", axis=0, tiled=True)

    normed_all, attend_cols, expand_cols, g2, vectors, q, k, v, o, lse = forward(
        tokens, document_starts, attend_weight, attend_bias, expand_weight, cotangent,
        (project_bias, contract_bias, gain_first, shift_first, gain_second, shift_second),
    )
    mlp_args = (o, project_weight, expand_cols, contract_weight, expand_bias, tokens, cotangent, g2, vectors)
    if lax.axis_size("ctx") != 8:
        block_output, grad_middle, g1, contract_part, expand_part, mlp_sums = feed_forward(*mlp_args)
        return (block_output,) + backward_plain(
            document_starts, normed_all, k, v, q, o, lse, g1, project_weight, attend_cols,
            contract_part, expand_part, tokens, grad_middle, vectors, mlp_sums,
        )
    near, over, grad_middle, g1, contract_part, expand_part, mlp_sums = feed_forward_near(*mlp_args)
    reduced = attend_reduce(
        document_starts, normed_all, k, v, q, o, lse, g1, project_weight, attend_cols,
        contract_part.reshape(8, 96, D), expand_part.reshape(8, 96, D), tokens, grad_middle, vectors, mlp_sums, near, over,
    )
    return tuple(finish(*reduced))


def solution(mesh):
    tok, row, vec = P(("ctx", "fsdp"), None), P("fsdp", None), P("fsdp")
    in_specs = (tok, P(), row, vec, row, vec, row, vec, row, vec, vec, vec, vec, vec, tok)
    out_specs = (tok, tok, row, vec, row, vec, row, vec, row, vec, vec, vec, vec, vec)
    return jax.shard_map(per_device, mesh=mesh, in_specs=in_specs, out_specs=out_specs, check_vma=False)
```
